32 devices in a mesh: seq: 8 (over z, y), head: 4 (over x, core).
Axes of the slice: x: 2, y: 2, z: 4, core: 2. Of those that a mesh axis runs over, the one named last changes fastest.
Arguments:
- hidden_states: bfloat16 [2048, 2048], P('seq', 'head'), may hold values from -0.375 to 0.375
- w_lambda: bfloat16 [2048, 384], P('head'), may hold values from -2 to 2
- queries: bfloat16 [2048, 2048], P('seq', 'head'), may hold values from -6 to 6
- keys: bfloat16 [2048, 2048], P('seq', 'head'), may hold values from -0.046875 to 0.046875
- values: bfloat16 [2048, 4096], P('seq', 'head'), may hold values from -6 to 6
- d_out: bfloat16 [2048, 4096], P('seq', 'head'), may hold values from -0.75 to 0.75
- d_state: float32 [32, 64, 128], P('head'), may hold values from -6 to 6
Outputs:
- out: bfloat16 [2048, 4096], P('seq', 'head')
- d_queries: bfloat16 [2048, 2048], P('seq', 'head')
- d_keys: bfloat16 [2048, 2048], P('seq', 'head')
- d_values: bfloat16 [2048, 4096], P('seq', 'head')
- d_hidden: bfloat16 [2048, 2048], P('seq', 'head')
- d_w_lambda: float32 [2048, 384], P(('head', 'seq'))
The draws below stay inside these ranges and needn't reach their ends.
All inputs are finite; a program needn't handle non-finite values.
Results may differ from the reference program's by a relative error of at most 0.0049.
Values may be sent and summed in bfloat16 or wider, within the bound.
No kernel may reach another device: no remote copies, remote signals or barrier semaphores. Data moves between devices by JAX's collectives and lax.ppermute only.
A program may use at most 64 MiB of HBM per device.

```python
import jax
import jax.numpy as jnp
from jax import lax

D = 2048
H = 32
DK = 64
DV = 128
TOK_DEV = 256
TOKENS = 2048
TOK_BITS = 8
SEQ_BITS = 3
LEVELS = 12
N_SEQ = 8
N_HEAD = 4


def block_scale(key, dims, cuts, smallest, top_value):
    def one(axis_at, parts):
        heights = jax.random.uniform(jax.random.fold_in(jax.random.fold_in(key, 6), axis_at), (parts,), jnp.float32, smallest / len(cuts), top_value / len(cuts))
        return jnp.repeat(jnp.exp(heights), dims[axis_at] // parts).reshape((-1,) + (1,) * (len(dims) - axis_at - 1))

    loudness = one(*cuts[0])
    for cut in cuts[1:]:
        loudness = loudness * one(*cut)
    return loudness


def noise(rng, extent, scale, bound, pieces=(), held_as=jnp.bfloat16):
    array = scale * jax.random.normal(rng, extent, jnp.float32)
    if pieces:
        array = array * block_scale(rng, extent, pieces, -0.22, 0.18)
    return jnp.clip(array, -bound, bound).astype(held_as)


def setup_inputs(seed: int = 0) -> dict:
    streams_of = jax.random.split(jax.random.key(seed), 8)
    return {
        "hidden_states": noise(streams_of[0], (TOKENS, D), 0.0625, 0.375, ((0, 8), (1, 4))),
        "w_lambda": noise(streams_of[1], (D, H * LEVELS), (D // 256) ** -0.5, 2.0, ((0, 4),)),
        "queries": noise(streams_of[2], (TOKENS, H * DK), 1.0, 6.0, ((0, 8), (1, 4))),
        "keys": noise(streams_of[3], (TOKENS, H * DK), (DK * TOKENS // 8) ** -0.5, 0.046875, ((0, 8), (1, 4))),
        "values": noise(streams_of[4], (TOKENS, H * DV), 1.0, 6.0, ((0, 8), (1, 4))),
        "d_out": noise(streams_of[5], (TOKENS, H * DV), 0.125, 0.75, ((0, 8), (1, 4))),
        "d_state": noise(streams_of[6], (H, DK, DV), 1.0, 6.0, ((0, 4),), jnp.float32),
    }


PRECISE = lax.Precision.HIGHEST


def digit_count(values, width):
    total = jnp.zeros_like(values)
    for shift in range(width):
        total = total + ((values >> shift) > 0).astype(jnp.int32)
    return total


def level_table(row_count, width, levels):
    later = jnp.arange(row_count, dtype=jnp.int32)[:, None]
    earlier = jnp.arange(row_count, dtype=jnp.int32)[None, :]
    depth = digit_count(jnp.bitwise_xor(later, earlier), width)
    keep = earlier <= later
    grid = jnp.arange(levels, dtype=jnp.int32)[:, None, None]
    return jnp.where((depth[None] == grid) & keep[None], 1.0, 0.0).astype(jnp.float32)


def pick_table(width, seq_bits, levels):
    wanted = width + 1 + jnp.arange(seq_bits, dtype=jnp.int32)
    return jnp.where(jnp.arange(levels, dtype=jnp.int32)[None, :] == wanted[:, None], 1.0, 0.0).astype(jnp.float32)


def swap_blocks(stack, bit):
    count = stack.shape[0]
    folded = stack.reshape((count >> (bit + 1), 2, 1 << bit) + stack.shape[1:])
    return folded[:, ::-1].reshape(stack.shape)


def local_pass(query_heads, key_heads, value_heads, level_weights, table, states, picks, grad_heads):
    query_wide = query_heads.astype(jnp.float32)
    key_wide = key_heads.astype(jnp.float32)
    value_wide = value_heads.astype(jnp.float32)
    grad_wide = grad_heads.astype(jnp.float32)
    scores = jnp.einsum('thd,shd->hts', query_wide, key_wide, precision=PRECISE)
    spread = jnp.einsum('thl,lts->hts', level_weights, table, precision=PRECISE)
    mixed = lax.optimization_barrier((scores * spread).astype(jnp.bfloat16))
    mixed_wide = mixed.astype(jnp.float32)
    local_out = jnp.einsum('hts,shv->thv', mixed_wide, value_wide, precision=PRECISE)
    chosen = jnp.einsum('thl,kl->thk', level_weights, picks, precision=PRECISE)
    scaled = chosen[:, :, :, None] * query_wide[:, :, None, :]
    carried = jnp.einsum('thkd,khdv->thv', scaled, states, precision=PRECISE)
    result = (local_out + carried).astype(jnp.bfloat16)
    grad_mixed = jnp.einsum('thv,shv->hts', grad_wide, value_wide, precision=PRECISE)
    grad_values = jnp.einsum('hts,thv->shv', mixed_wide, grad_wide, precision=PRECISE)
    grad_scores = lax.optimization_barrier((grad_mixed * spread).astype(jnp.bfloat16)).astype(jnp.float32)
    grad_weights = jnp.einsum('hts,lts->thl', grad_mixed * scores, table, precision=PRECISE)
    grad_queries = jnp.einsum('hts,shd->thd', grad_scores, key_wide, precision=PRECISE)
    grad_keys = jnp.einsum('hts,thd->shd', grad_scores, query_wide, precision=PRECISE)
    grad_scaled = jnp.einsum('thv,khdv->thkd', grad_wide, states, precision=PRECISE)
    grad_queries = grad_queries + jnp.einsum('thk,thkd->thd', chosen, grad_scaled, precision=PRECISE)
    grad_chosen = jnp.einsum('thkd,thd->thk', grad_scaled, query_wide, precision=PRECISE)
    grad_weights = grad_weights + jnp.einsum('thk,kl->thl', grad_chosen, picks, precision=PRECISE)
    grad_states = jnp.einsum('thkd,thv->khdv', scaled, grad_wide, precision=PRECISE)
    return result, grad_queries, grad_keys, grad_values, grad_weights, grad_states


def reference(hidden_states, w_lambda, queries, keys, values, d_out, d_state):
    projected = jnp.dot(hidden_states, w_lambda, preferred_element_type=jnp.float32)
    weight_all = jax.nn.softplus(projected).reshape(N_SEQ, TOK_DEV, H, LEVELS)
    table = level_table(TOK_DEV, TOK_BITS, LEVELS)
    picks = pick_table(TOK_BITS, SEQ_BITS, LEVELS)
    block_ids = jnp.arange(N_SEQ, dtype=jnp.int32)
    group = H // N_HEAD
    query_all = queries.reshape(N_SEQ, TOK_DEV, H, DK)
    key_all = keys.reshape(N_SEQ, TOK_DEV, H, DK)
    value_all = values.reshape(N_SEQ, TOK_DEV, H, DV)
    grad_all = d_out.reshape(N_SEQ, TOK_DEV, H, DV)
    collected = []
    for start in range(0, H, group):
        query_group = query_all[:, :, start:start + group]
        key_group = key_all[:, :, start:start + group]
        value_group = value_all[:, :, start:start + group]
        weight_group = weight_all[:, :, start:start + group]
        grad_group = grad_all[:, :, start:start + group]
        state_seed = d_state[start:start + group]
        key_wide = key_group.astype(jnp.float32)
        value_wide = value_group.astype(jnp.float32)
        kv_state = jnp.einsum('bthd,bthv->bhdv', key_wide, value_wide, precision=PRECISE)
        total = kv_state
        uppers = []
        for bit in range(SEQ_BITS):
            partner = swap_blocks(total, bit)
            is_upper = ((block_ids >> bit) & 1) == 1
            uppers.append(jnp.where(is_upper[:, None, None, None], partner, 0.0))
            total = total + partner
        states = jnp.stack(uppers, axis=1)

        def one_block(items):
            return local_pass(items[0], items[1], items[2], items[3], table, items[4], picks, items[5])

        result, query_grads, key_grads, value_grads, weight_grads, state_grads = lax.map(
            one_block, (query_group, key_group, value_group, weight_group, states, grad_group))
        adjoint = jnp.zeros_like(kv_state)
        for bit in reversed(range(SEQ_BITS)):
            is_upper = ((block_ids >> bit) & 1) == 1
            pending = adjoint + jnp.where(is_upper[:, None, None, None], state_grads[:, bit], 0.0)
            adjoint = adjoint + swap_blocks(pending, bit)
        adjoint = adjoint + state_seed[None]
        key_grads = key_grads + jnp.einsum('bthv,bhdv->bthd', value_wide, adjoint, precision=PRECISE)
        value_grads = value_grads + jnp.einsum('bthd,bhdv->bthv', key_wide, adjoint, precision=PRECISE)
        collected.append((result, query_grads, key_grads, value_grads, weight_grads))
    joined = [jnp.concatenate([entry[place] for entry in collected], axis=2) for place in range(5)]
    out = joined[0].reshape(TOKENS, H * DV)
    d_queries = joined[1].reshape(TOKENS, H * DK).astype(jnp.bfloat16)
    d_keys = joined[2].reshape(TOKENS, H * DK).astype(jnp.bfloat16)
    d_values = joined[3].reshape(TOKENS, H * DV).astype(jnp.bfloat16)
    grad_level = joined[4].reshape(TOKENS, H * LEVELS)
    grad_projected = (grad_level * jax.nn.sigmoid(projected)).astype(jnp.bfloat16)
    d_hidden = jnp.dot(grad_projected, w_lambda.T, preferred_element_type=jnp.float32).astype(jnp.bfloat16)
    d_w_lambda = jnp.dot(hidden_states.T, grad_projected, preferred_element_type=jnp.float32)
    return (out, d_queries, d_keys, d_values, d_hidden, d_w_lambda)
```

```python
import functools

import jax
import jax.numpy as jnp
from jax import lax
from jax.experimental import pallas as pl
from jax.experimental.pallas import tpu as pltpu
from jax.sharding import PartitionSpec as P

F32 = jnp.float32
BF16 = jnp.bfloat16
LANES = 128
SUB = 8
VM = pl.BlockSpec(memory_space=pltpu.VMEM)
SM = pl.BlockSpec(memory_space=pltpu.SMEM)


def nn(a, b):
    return lax.dot_general(a, b, (((1,), (0,)), ((), ())), preferred_element_type=F32)


def nt(a, b):
    return lax.dot_general(a, b, (((1,), (1,)), ((), ())), preferred_element_type=F32)


def tn(a, b):
    return lax.dot_general(a, b, (((0,), (0,)), ((), ())), preferred_element_type=F32)


def call(kernel, outs, specs, flops, name, **kwargs):
    size = sum(o.size * o.dtype.itemsize for o in outs)
    return pl.pallas_call(
        kernel,
        out_shape=outs,
        in_specs=specs,
        compiler_params=pltpu.CompilerParams(vmem_limit_bytes=24 << 20),
        cost_estimate=pl.CostEstimate(flops=flops, bytes_accessed=2 * size, transcendentals=0),
        name=name,
        **kwargs,
    )


def swap(value, axis, bit):
    mask = 1 << bit
    pairs = [(source, source ^ mask) for source in range(lax.axis_size(axis))]
    return lax.ppermute(value, axis, pairs)


def state_kernel(dims, k_ref, v_ref, kv_ref, kvb_ref):
    nh, dk, dv = dims
    for pair in range(nh // 2):
        turned = k_ref[:, pair * 2 * dk:(pair + 1) * 2 * dk].T
        for j in range(2):
            h = 2 * pair + j
            kv = nn(turned[j * dk:(j + 1) * dk], v_ref[:, h * dv:(h + 1) * dv])
            kv_ref[h * dk:(h + 1) * dk, :] = kv
            kvb_ref[h * dk:(h + 1) * dk, :] = kv.astype(BF16)


def project_kernel(w_ref, x_ref, p_ref):
    p_ref[...] = lax.dot_general(
        w_ref[...], x_ref[...], (((0,), (1,)), ((), ())), preferred_element_type=F32)


def weight_kernel(dims, levels, first, count, keep_ref, got_ref, q_ref, g_ref,
                  proj_ref, lw_ref, qt_ref, gu_ref):
    nh, dk, dv = dims
    proj = keep_ref[...] + got_ref[...].astype(F32)
    proj_ref[...] = proj
    lw_ref[...] = jnp.maximum(proj, 0.0) + jnp.log1p(jnp.exp(-jnp.abs(proj)))
    for pair in range(nh // 2):
        turned = q_ref[:, pair * 2 * dk:(pair + 1) * 2 * dk].T
        qt_ref[pair * 2 * dk:(pair + 1) * 2 * dk, :] = turned
        wide = turned.astype(F32)
        for j in range(2):
            h = 2 * pair + j
            scaled = jnp.concatenate(
                [wide[j * dk:(j + 1) * dk] * lw_ref[h * levels + first + m:h * levels + first + m + 1, :]
                 for m in range(count)], axis=0)
            grad = nn(scaled.astype(BF16), g_ref[:, h * dv:(h + 1) * dv])
            for m in range(count):
                gu_ref[m, h * dk:(h + 1) * dk, :] = grad[m * dk:(m + 1) * dk]


def spread_half(rows, lane, low, t_low):
    digits = (low ^ t_low)
    near = jnp.where(digits == 0, rows[0], jnp.where(digits < 2, rows[1], jnp.where(digits < 4, rows[2], rows[3])))
    near = jnp.where(low <= t_low, near, 0.0)
    parts = []
    for a in range(LANES // SUB):
        value = None
        for l in reversed(range(4, 8)):
            if (a >> (l - 4)) & 1 == 0:
                end = (((a >> (l - 3)) + 1) << (l - 3)) * SUB
                value = rows[l] if value is None else jnp.where(lane < end, rows[l], value)
        value = near if value is None else jnp.where(lane < (a + 1) * SUB, near, value)
        if a:
            value = jnp.where(lane < a * SUB, 0.0, value)
        parts.append(value)
    return jnp.concatenate(parts, axis=0)


def level_sums(prod, lane, low, t_low):
    count = LANES // SUB
    group = lane // SUB
    cur = [prod[a * SUB:(a + 1) * SUB] for a in range(count)]
    near = jnp.zeros_like(cur[0])
    for a in range(count):
        near = jnp.where(group == a, cur[a], near)
    near = jnp.where(low <= t_low, near, 0.0)
    digits = low ^ t_low
    sums = []
    for l in range(4):
        lo, hi = (0, 1) if l == 0 else (1 << (l - 1), 1 << l)
        sums.append(jnp.where((digits >= lo) & (digits < hi), near, 0.0))
    for l in range(4, 8):
        total = jnp.zeros_like(near)
        for a in range(0, len(cur), 2):
            total = jnp.where((lane >> (l - 1)) == a + 1, cur[a], total)
        sums.append(total)
        cur = [cur[a] + cur[a + 1] for a in range(0, len(cur), 2)]
    return [jnp.sum(s, axis=0, keepdims=True) for s in sums]


def local_kernel(dims, levels, k_ref, q_ref, v_ref, g_ref, lw_ref, out_ref, dq_ref, dk_ref, dv_ref, gl_ref):
    nh, dk, dv = dims
    kp, qp = k_ref[...], q_ref[...]
    kt, qt = kp.T, qp.T
    zero = jnp.zeros_like(qt[:dk])
    lane = lax.broadcasted_iota(jnp.int32, (SUB, LANES), 1)
    low = lax.broadcasted_iota(jnp.int32, (SUB, LANES), 0)
    t_low = lane % SUB
    wide_lane = lax.broadcasted_iota(jnp.int32, qp.shape, 1)
    gl_ref[...] = jnp.zeros_like(gl_ref)
    dk_sum = None
    for j in range(2):
        vj = v_ref[:, j * dv:(j + 1) * dv]
        gj = g_ref[:, j * dv:(j + 1) * dv]
        qz = jnp.concatenate([qt[:dk], zero] if j == 0 else [zero, qt[dk:]], axis=0)
        scores = nn(kp, qz)
        grads = nt(vj, gj)
        base = j * levels
        cross = lw_ref[base + 8:base + 9, LANES:]
        halves = []
        for x in range(2):
            rows = [jnp.broadcast_to(lw_ref[base + l:base + l + 1, x * LANES:(x + 1) * LANES], (SUB, LANES))
                    for l in range(8)]
            halves.append(spread_half(rows, lane, low, t_low))

        def weigh(full):
            top = jnp.concatenate([full[:LANES, :LANES] * halves[0], full[:LANES, LANES:] * cross], axis=1)
            bottom = full[LANES:, LANES:] * halves[1]
            bottom = jnp.concatenate([jnp.zeros_like(bottom), bottom], axis=1)
            return jnp.concatenate([top, bottom], axis=0).astype(BF16)

        mixed = weigh(scores)
        grad_scores = weigh(grads)
        for x in range(2):
            part = slice(x * LANES, (x + 1) * LANES)
            sums = level_sums(scores[part, part] * grads[part, part], lane, low, t_low)
            for l in range(8):
                gl_ref[base + l:base + l + 1, part] = sums[l]
        crossed = scores[:LANES, LANES:] * grads[:LANES, LANES:]
        gl_ref[base + 8:base + 9, LANES:] = jnp.sum(crossed, axis=0, keepdims=True)
        out_ref[j * dv:(j + 1) * dv, :] = tn(vj, mixed)
        dq_ref[j * dk:(j + 1) * dk, :] = nn(kt[j * dk:(j + 1) * dk], grad_scores)
        dv_ref[:, j * dv:(j + 1) * dv] = nn(mixed, gj)
        mine = (wide_lane < dk) if j == 0 else (wide_lane >= dk)
        term = nn(grad_scores, jnp.where(mine, qp, jnp.zeros_like(qp)))
        dk_sum = term if dk_sum is None else dk_sum + term
    dk_ref[...] = dk_sum


def carry_kernel(dims, levels, first, count, idx_ref, *refs):
    nh, dk, dv = dims
    ups = refs[:count]
    g_ref, qt_ref, lw_ref, proj_ref, gl_ref, dql_ref, gp_ref, dq_ref = refs[count:]
    index = idx_ref[0]
    for pair in range(nh // 2):
        halves = []
        for j in range(2):
            h = 2 * pair + j
            rows = slice(h * dk, (h + 1) * dk)
            gj = g_ref[:, h * dv:(h + 1) * dv]
            wide = qt_ref[rows, :].astype(F32)
            total = dql_ref[rows, :]
            for m in range(count):
                r = h * levels + first + m
                up = ((index >> m) & 1).astype(F32)
                x = nt(ups[m][rows, :], gj) * up
                total = total + x * lw_ref[r:r + 1, :]
                gl_ref_row = jnp.sum(x * wide, axis=0, keepdims=True)
                gp_ref[r:r + 1, :] = gl_ref_row
            halves.append(total)
        dq_ref[:, pair * 2 * dk:(pair + 1) * 2 * dk] = jnp.concatenate(halves, axis=0).T.astype(BF16)
        for j in range(2):
            r = (2 * pair + j) * levels
            gp_ref[r:r + first, :] = gl_ref[r:r + first, :]


def out_kernel(dims, levels, first, count, idx_ref, *refs):
    nh, dk, dv = dims
    ups = refs[:count]
    qt_ref, lw_ref, outl_ref, out_ref = refs[count:]
    index = idx_ref[0]
    for h in range(nh):
        rows = slice(h * dk, (h + 1) * dk)
        total = outl_ref[h * dv:(h + 1) * dv, :]
        for m in range(count):
            r = h * levels + first + m
            up = ((index >> m) & 1).astype(F32)
            total = total + tn(ups[m][rows, :], qt_ref[rows, :]) * (lw_ref[r:r + 1, :] * up)
        out_ref[:, h * dv:(h + 1) * dv] = total.T.astype(BF16)


def wgrad_kernel(gp_ref, x_ref, dw_ref):
    dw_ref[...] = lax.dot_general(
        x_ref[...], gp_ref[...], (((0,), (1,)), ((), ())), preferred_element_type=F32)


def hidden_kernel(gp_ref, w_ref, dx_ref):
    dx_ref[...] = lax.dot_general(
        gp_ref[...], w_ref[...], (((0,), (1,)), ((), ())), preferred_element_type=F32).astype(BF16)


def final_kernel(dims, adj_ref, ds_ref, k_ref, v_ref, dkl_ref, dvl_ref, dk_ref, dv_ref):
    nh, dk, dv = dims
    zero = jnp.zeros((dk, dv), BF16)
    for pair in range(nh // 2):
        adj = [(adj_ref[h * dk:(h + 1) * dk, :] + ds_ref[h * dk:(h + 1) * dk, :]).astype(BF16)
               for h in (2 * pair, 2 * pair + 1)]
        kp = k_ref[:, pair * 2 * dk:(pair + 1) * 2 * dk]
        total = dkl_ref[:, pair * 2 * dk:(pair + 1) * 2 * dk]
        for j in range(2):
            h = 2 * pair + j
            padded = jnp.concatenate([adj[j], zero] if j == 0 else [zero, adj[j]], axis=0)
            cols = slice(h * dv, (h + 1) * dv)
            total = total + nt(v_ref[:, cols], padded)
            dv_ref[:, cols] = (dvl_ref[:, cols] + nn(kp, padded)).astype(BF16)
        dk_ref[:, pair * 2 * dk:(pair + 1) * 2 * dk] = total.astype(BF16)


def body(hidden, w, queries, keys, values, d_out, d_state):
    tokens, width = hidden.shape
    dims = d_state.shape
    nh, dk, dv = dims
    n_seq, n_head = lax.axis_size("seq"), lax.axis_size("head")
    seq_bits, head_bits = n_seq.bit_length() - 1, n_head.bit_length() - 1
    cols = w.shape[1]
    levels = cols // (nh * n_head)
    own = nh * levels
    first = tokens.bit_length()
    si, hi = lax.axis_index("seq"), lax.axis_index("head")
    idx = jnp.reshape(si, (1,)).astype(jnp.int32)
    S = jax.ShapeDtypeStruct
    rows = nh * dk

    kv, kvb = call(functools.partial(state_kernel, dims), [S((rows, dv), F32), S((rows, dv), BF16)],
                   [VM, VM], 2 * tokens * rows * dv, "kv_state")(keys, values)
    partial = call(project_kernel, [S((cols, tokens), F32)], [VM, VM], 2 * tokens * width * cols, "project")(w, hidden)[0]

    keep = partial
    got = None
    for bit in reversed(range(head_bits)):
        pair = keep.reshape(2, keep.shape[0] // 2, tokens)
        mine = (hi >> bit) & 1
        send = lax.dynamic_index_in_dim(pair, 1 - mine, 0, keepdims=False).astype(BF16)
        keep = lax.dynamic_index_in_dim(pair, mine, 0, keepdims=False)
        got = swap(send, "head", bit)
        if bit:
            keep = keep + got.astype(F32)
    proj, lw, qt, gu = call(
        functools.partial(weight_kernel, dims, levels, first, seq_bits),
        [S((own, tokens), F32), S((own, tokens), F32), S((rows, tokens), BF16), S((seq_bits, rows, dv), F32)],
        [VM] * 4, 2 * tokens * rows * dv * seq_bits, "level_weights")(keep, got, queries, d_out)

    top = seq_bits - 1
    total, send = kv, kvb
    ups = []
    for bit in range(top):
        partner = swap(send, "seq", bit)
        ups.append(partner)
        total = total + partner.astype(F32)
        send = total.astype(BF16)
    upper_top = ((si >> top) & 1) == 1
    partner = swap(jnp.where(upper_top, gu[top].astype(BF16), send), "seq", top)
    ups.append(partner)
    adjoint = jnp.where(upper_top, 0.0, partner.astype(F32))
    for bit in reversed(range(top)):
        pending = adjoint + jnp.where(((si >> bit) & 1) == 1, gu[bit], 0.0)
        adjoint = adjoint + swap(pending.astype(BF16), "seq", bit).astype(F32)

    pair_spec = lambda n: pl.BlockSpec((tokens, n), lambda p: (0, p))
    row_spec = lambda n: pl.BlockSpec((n, tokens), lambda p: (p, 0))
    out_l, dq_l, dk_l, dv_l, gl = call(
        functools.partial(local_kernel, dims, levels),
        [S((nh * dv, tokens), F32), S((rows, tokens), F32), S((tokens, rows), F32), S((tokens, nh * dv), F32),
         S((own, tokens), F32)],
        [pair_spec(2 * dk), pair_spec(2 * dk), pair_spec(2 * dv), pair_spec(2 * dv), row_spec(2 * levels)],
        2 * tokens * tokens * nh * (3 * dk + 3 * dv), "local", grid=(nh // 2,),
        out_specs=[row_spec(2 * dv), row_spec(2 * dk), pair_spec(2 * dk), pair_spec(2 * dv), row_spec(2 * levels)],
    )(keys, queries, values, d_out, lw)

    grad_level, d_queries = call(
        functools.partial(carry_kernel, dims, levels, first, seq_bits),
        [S((own, tokens), F32), S((tokens, rows), BF16)],
        [SM] + [VM] * (seq_bits + 6), 2 * tokens * rows * dv * seq_bits, "carry")(
            idx, *ups, d_out, qt, lw, proj, gl, dq_l)
    out = call(
        functools.partial(out_kernel, dims, levels, first, seq_bits),
        [S((tokens, nh * dv), BF16)],
        [SM] + [VM] * (seq_bits + 3), 2 * tokens * rows * dv * seq_bits, "out")(idx, *ups, qt, lw, out_l)[0]
    gp = (grad_level * jax.nn.sigmoid(proj)).astype(BF16)

    full = gp[None]
    for bit in reversed(range(head_bits)):
        other = swap(full, "head", bit)
        mine = (hi >> bit) & 1
        full = jnp.where(mine == 0, jnp.stack([full, other]), jnp.stack([other, full]))
        full = full.reshape((-1,) + full.shape[2:]) if bit == head_bits - 1 else full
    full = full.reshape((2,) * head_bits + (own, tokens))
    full = full.transpose(tuple(reversed(range(head_bits))) + (head_bits, head_bits + 1))
    gathered = full.reshape(cols, tokens)
    partial_w = call(wgrad_kernel, [S((width, cols), F32)], [VM, VM], 2 * tokens * width * cols, "wgrad")(gathered, hidden)[0]
    d_hidden = call(hidden_kernel, [S((tokens, width), BF16)], [VM, VM], 2 * tokens * width * cols, "hgrad")(gathered, w)[0]

    keep = partial_w.reshape(n_seq, width // n_seq, cols)
    for bit in range(seq_bits):
        pair = keep.reshape(keep.shape[0] // 2, 2, keep.shape[1], cols)
        mine = (si >> bit) & 1
        send = lax.dynamic_index_in_dim(pair, 1 - mine, 1, keepdims=False).astype(BF16)
        got = swap(send, "seq", bit)
        keep = lax.dynamic_index_in_dim(pair, mine, 1, keepdims=False) + got.astype(F32)
    d_w = keep.reshape(width // n_seq, cols)

    d_keys, d_values = call(
        functools.partial(final_kernel, dims),
        [S((tokens, rows), BF16), S((tokens, nh * dv), BF16)], [VM] * 6, 4 * tokens * rows * dv, "final")(
            adjoint, d_state.reshape(rows, dv), keys, values, dk_l, dv_l)
    return (out, d_queries, d_keys, d_values, d_hidden, d_w)


def solution(mesh):
    two = P("seq", "head")
    return jax.shard_map(
        body, mesh=mesh,
        in_specs=(two, P("head", None), two, two, two, two, P("head", None, None)),
        out_specs=(two, two, two, two, two, P(("head", "seq"), None)),
        check_vma=False)
```

```python
import functools

import jax
import jax.numpy as jnp
from jax import lax
from jax.experimental import pallas as pl
from jax.experimental.pallas import tpu as pltpu
from jax.sharding import PartitionSpec as P

F32 = jnp.float32
BF16 = jnp.bfloat16
LANES = 128
SUB = 8
VM = pl.BlockSpec(memory_space=pltpu.VMEM)
SM = pl.BlockSpec(memory_space=pltpu.SMEM)


def nn(a, b):
    return lax.dot_general(a, b, (((1,), (0,)), ((), ())), preferred_element_type=F32)


def nt(a, b):
    return lax.dot_general(a, b, (((1,), (1,)), ((), ())), preferred_element_type=F32)


def tn(a, b):
    return lax.dot_general(a, b, (((0,), (0,)), ((), ())), preferred_element_type=F32)


def call(kernel, outs, specs, flops, name, **kwargs):
    size = sum(o.size * o.dtype.itemsize for o in outs)
    return pl.pallas_call(
        kernel,
        out_shape=outs,
        in_specs=specs,
        compiler_params=pltpu.CompilerParams(vmem_limit_bytes=16 << 20),
        cost_estimate=pl.CostEstimate(flops=flops, bytes_accessed=2 * size, transcendentals=0),
        name=name,
        **kwargs,
    )


def swap(value, axis, bit, name):
    mask = 1 << bit
    pairs = [(source, source ^ mask) for source in range(lax.axis_size(axis))]
    with jax.named_scope(f"{name}_{axis}{bit}"):
        return lax.ppermute(value, axis, pairs)


def front_kernel(dims, k_hbm, v_hbm, w_hbm, x_hbm, kv_ref, kvb_ref, p_ref, xt_ref,
                 k_ref, v_ref, w_ref, x_ref, sems):
    nh, dk, dv = dims
    copies = [pltpu.make_async_copy(src, dst, sems.at[n]) for n, (src, dst) in enumerate(
        ((k_hbm, k_ref), (v_hbm, v_ref), (x_hbm, x_ref), (w_hbm, w_ref)))]
    for copy in copies:
        copy.start()
    copies[0].wait()
    copies[1].wait()
    for pair in range(nh // 2):
        turned = k_ref[:, pair * 2 * dk:(pair + 1) * 2 * dk].T
        for j in range(2):
            h = 2 * pair + j
            kv = nn(turned[j * dk:(j + 1) * dk], v_ref[:, h * dv:(h + 1) * dv])
            kv_ref[h * dk:(h + 1) * dk, :] = kv
            kvb_ref[h * dk:(h + 1) * dk, :] = kv.astype(BF16)
    copies[2].wait()
    xt = x_ref[...].T
    xt_ref[...] = xt
    copies[3].wait()
    p_ref[...] = tn(w_ref[...], xt)


def weight_kernel(dims, levels, first, count, keep_ref, got_ref, gl_ref, q_ref, g_ref,
                  sig_ref, lw_ref, near_ref, qt_ref, gu_ref):
    nh, dk, dv = dims
    proj = keep_ref[...] + got_ref[...].astype(F32)
    sig = jax.nn.sigmoid(proj)
    sig_ref[...] = sig
    near_ref[...] = (gl_ref[...] * sig).astype(BF16)
    lw_ref[...] = jnp.maximum(proj, 0.0) + jnp.log1p(jnp.exp(-jnp.abs(proj)))
    for pair in range(nh // 2):
        turned = q_ref[:, pair * 2 * dk:(pair + 1) * 2 * dk].T
        qt_ref[pair * 2 * dk:(pair + 1) * 2 * dk, :] = turned
        wide = turned.astype(F32)
        for j in range(2):
            h = 2 * pair + j
            scaled = jnp.concatenate(
                [wide[j * dk:(j + 1) * dk] * lw_ref[h * levels + first + m:h * levels + first + m + 1, :]
                 for m in range(count)], axis=0)
            grad = nn(scaled.astype(BF16), g_ref[:, h * dv:(h + 1) * dv])
            for m in range(count):
                gu_ref[m, h * dk:(h + 1) * dk, :] = grad[m * dk:(m + 1) * dk].astype(BF16)


def spread_half(rows, lane, low, t_low):
    digits = (low ^ t_low)
    near = jnp.where(digits == 0, rows[0], jnp.where(digits < 2, rows[1], jnp.where(digits < 4, rows[2], rows[3])))
    near = jnp.where(low <= t_low, near, 0.0)
    parts = []
    for a in range(LANES // SUB):
        value = None
        for l in reversed(range(4, 8)):
            if (a >> (l - 4)) & 1 == 0:
                end = (((a >> (l - 3)) + 1) << (l - 3)) * SUB
                value = rows[l] if value is None else jnp.where(lane < end, rows[l], value)
        value = near if value is None else jnp.where(lane < (a + 1) * SUB, near, value)
        if a:
            value = jnp.where(lane < a * SUB, 0.0, value)
        parts.append(value)
    return jnp.concatenate(parts, axis=0)


def level_sums(prod, lane, low, t_low):
    count = LANES // SUB
    group = lane // SUB
    cur = [prod[a * SUB:(a + 1) * SUB] for a in range(count)]
    near = jnp.zeros_like(cur[0])
    for a in range(count):
        near = jnp.where(group == a, cur[a], near)
    near = jnp.where(low <= t_low, near, 0.0)
    digits = low ^ t_low
    sums = []
    for l in range(4):
        lo, hi = (0, 1) if l == 0 else (1 << (l - 1), 1 << l)
        sums.append(jnp.where((digits >= lo) & (digits < hi), near, 0.0))
    for l in range(4, 8):
        total = jnp.zeros_like(near)
        for a in range(0, len(cur), 2):
            total = jnp.where((lane >> (l - 1)) == a + 1, cur[a], total)
        sums.append(total)
        cur = [cur[a] + cur[a + 1] for a in range(0, len(cur), 2)]
    return [jnp.sum(s, axis=0, keepdims=True) for s in sums]


def level_kernel(dims, levels, k_ref, q_ref, v_ref, g_ref, gl_ref):
    nh, dk, dv = dims
    kp = k_ref[...]
    qt = q_ref[...].T
    zero = jnp.zeros_like(qt[:dk])
    lane = lax.broadcasted_iota(jnp.int32, (SUB, LANES), 1)
    low = lax.broadcasted_iota(jnp.int32, (SUB, LANES), 0)
    t_low = lane % SUB
    gl_ref[...] = jnp.zeros_like(gl_ref)
    for j in range(2):
        base = j * levels
        qz = jnp.concatenate([qt[:dk], zero] if j == 0 else [zero, qt[dk:]], axis=0)
        prod = nn(kp, qz) * nt(v_ref[:, j * dv:(j + 1) * dv], g_ref[:, j * dv:(j + 1) * dv])
        for x in range(2):
            part = slice(x * LANES, (x + 1) * LANES)
            sums = level_sums(prod[part, part], lane, low, t_low)
            for l in range(8):
                gl_ref[base + l:base + l + 1, part] = sums[l]
        gl_ref[base + 8:base + 9, LANES:] = jnp.sum(prod[:LANES, LANES:], axis=0, keepdims=True)


def local_kernel(dims, levels, k_ref, q_ref, v_ref, g_ref, lw_ref, out_ref, dq_ref, dk_ref, dv_ref):
    nh, dk, dv = dims
    kp, qp = k_ref[...], q_ref[...]
    kt, qt = kp.T, qp.T
    zero = jnp.zeros_like(qt[:dk])
    lane = lax.broadcasted_iota(jnp.int32, (SUB, LANES), 1)
    low = lax.broadcasted_iota(jnp.int32, (SUB, LANES), 0)
    t_low = lane % SUB
    wide_lane = lax.broadcasted_iota(jnp.int32, qp.shape, 1)
    dk_sum = None
    for j in range(2):
        vj = v_ref[:, j * dv:(j + 1) * dv]
        gj = g_ref[:, j * dv:(j + 1) * dv]
        qz = jnp.concatenate([qt[:dk], zero] if j == 0 else [zero, qt[dk:]], axis=0)
        base = j * levels
        cross = lw_ref[base + 8:base + 9, LANES:]
        halves = []
        for x in range(2):
            rows = [jnp.broadcast_to(lw_ref[base + l:base + l + 1, x * LANES:(x + 1) * LANES], (SUB, LANES))
                    for l in range(8)]
            halves.append(spread_half(rows, lane, low, t_low))

        def weigh(full):
            top = jnp.concatenate([full[:LANES, :LANES] * halves[0], full[:LANES, LANES:] * cross], axis=1)
            bottom = full[LANES:, LANES:] * halves[1]
            bottom = jnp.concatenate([jnp.zeros_like(bottom), bottom], axis=1)
            return jnp.concatenate([top, bottom], axis=0).astype(BF16)

        mixed = weigh(nn(kp, qz))
        grad_scores = weigh(nt(vj, gj))
        out_ref[j * dv:(j + 1) * dv, :] = tn(vj, mixed)
        dq_ref[j * dk:(j + 1) * dk, :] = nn(kt[j * dk:(j + 1) * dk], grad_scores)
        dv_ref[:, j * dv:(j + 1) * dv] = nn(mixed, gj)
        mine = (wide_lane < dk) if j == 0 else (wide_lane >= dk)
        term = nn(grad_scores, jnp.where(mine, qp, jnp.zeros_like(qp)))
        dk_sum = term if dk_sum is None else dk_sum + term
    dk_ref[...] = dk_sum


def carry_kernel(dims, levels, first, count, idx_ref, *refs):
    nh, dk, dv = dims
    ups = refs[:count]
    g_ref, qt_ref, sig_ref, far_ref = refs[count:]
    index = idx_ref[0]
    for m in range(count):
        up = ((index >> m) & 1).astype(F32)
        found = []
        for h in range(nh):
            rows = slice(h * dk, (h + 1) * dk)
            r = h * levels + first + m
            x = nt(ups[m][rows, :], g_ref[:, h * dv:(h + 1) * dv])
            row = jnp.sum(x * qt_ref[rows, :].astype(F32), axis=0, keepdims=True)
            found.append(row * (sig_ref[r:r + 1, :] * up))
        far_ref[m * nh:(m + 1) * nh, :] = jnp.concatenate(found, axis=0).astype(BF16)


def query_kernel(dims, levels, first, count, idx_ref, *refs):
    nh, dk, dv = dims
    ups = refs[:count]
    g_ref, lw_ref, low_ref, high_ref, dq_ref = refs[count:]
    index = idx_ref[0]
    for pair in range(nh // 2):
        halves = []
        for j in range(2):
            h = 2 * pair + j
            local_ref, n = (low_ref, h) if h < nh // 2 else (high_ref, h - nh // 2)
            total = local_ref[n * dk:(n + 1) * dk, :]
            for m in range(count):
                r = h * levels + first + m
                up = ((index >> m) & 1).astype(F32)
                x = nt(ups[m][h * dk:(h + 1) * dk, :], g_ref[:, h * dv:(h + 1) * dv])
                total = total + x * (lw_ref[r:r + 1, :] * up)
            halves.append(total)
        dq_ref[:, pair * 2 * dk:(pair + 1) * 2 * dk] = jnp.concatenate(halves, axis=0).T.astype(BF16)


def out_kernel(dims, levels, first, count, idx_ref, *refs):
    nh, dk, dv = dims
    ups = refs[:count]
    qt_ref, lw_ref, low_ref, high_ref, out_ref = refs[count:]
    index = idx_ref[0]
    for h in range(nh):
        rows = slice(h * dk, (h + 1) * dk)
        local_ref, n = (low_ref, h) if h < nh // 2 else (high_ref, h - nh // 2)
        total = local_ref[n * dv:(n + 1) * dv, :]
        for m in range(count):
            r = h * levels + first + m
            up = ((index >> m) & 1).astype(F32)
            total = total + tn(ups[m][rows, :], qt_ref[rows, :]) * (lw_ref[r:r + 1, :] * up)
        out_ref[:, h * dv:(h + 1) * dv] = total.T.astype(BF16)


def wgrad_kernel(xt_ref, gp_ref, dw_ref):
    dw_ref[...] = nt(xt_ref[...], gp_ref[...])


def merge_kernel(half, idx_ref, near_ref, far_ref, place_ref, send_ref, keep_ref):
    total = near_ref[...] + lax.dot_general(
        far_ref[...], place_ref[...], (((1,), (0,)), ((), ())),
        preferred_element_type=F32, precision=lax.Precision.HIGHEST)
    upper = ((idx_ref[0] >> half) & 1) == 1
    n = total.shape[0] // 2
    low, high = total[:n], total[n:]
    keep_ref[...] = jnp.where(upper, high, low)
    send_ref[...] = jnp.where(upper, low, high).astype(BF16)


def hidden_kernel(near_ref, far_ref, place_ref, w_ref, dx_ref):
    gp = near_ref[...].astype(F32) + tn(place_ref[...].astype(BF16), far_ref[...])
    dx_ref[...] = lax.dot_general(
        gp.astype(BF16), w_ref[...], (((0,), (1,)), ((), ())), preferred_element_type=F32).astype(BF16)


def join_kernel(top, count, idx_ref, kv_ref, *refs):
    ups = refs[:count]
    gu_ref, send_ref = refs[count:]
    upper = ((idx_ref[0] >> top) & 1) == 1

    @pl.when(upper)
    def _():
        send_ref[...] = gu_ref[top]

    @pl.when(jnp.logical_not(upper))
    def _():
        total = kv_ref[...]
        for up in ups:
            total = total + up[...].astype(F32)
        send_ref[...] = total.astype(BF16)


def final_kernel(dims, adj_ref, ds_ref, k_ref, v_ref, low_k, high_k, low_v, high_v, dk_ref, dv_ref):
    nh, dk, dv = dims
    zero = jnp.zeros((dk, dv), BF16)
    for pair in range(nh // 2):
        adj = [(adj_ref[h * dk:(h + 1) * dk, :] + ds_ref[h * dk:(h + 1) * dk, :]).astype(BF16)
               for h in (2 * pair, 2 * pair + 1)]
        kp = k_ref[:, pair * 2 * dk:(pair + 1) * 2 * dk]
        dkl_ref, dvl_ref, p = (low_k, low_v, pair) if pair < nh // 4 else (high_k, high_v, pair - nh // 4)
        total = dkl_ref[:, p * 2 * dk:(p + 1) * 2 * dk]
        for j in range(2):
            h = 2 * pair + j
            padded = jnp.concatenate([adj[j], zero] if j == 0 else [zero, adj[j]], axis=0)
            cols = slice(h * dv, (h + 1) * dv)
            total = total + nt(v_ref[:, cols], padded)
            near = dvl_ref[:, (2 * p + j) * dv:(2 * p + j + 1) * dv]
            dv_ref[:, cols] = (near + nn(kp, padded)).astype(BF16)
        dk_ref[:, pair * 2 * dk:(pair + 1) * 2 * dk] = total.astype(BF16)


def gather_heads(value, hi, head_bits, name):
    full = value[None]
    for bit in reversed(range(head_bits)):
        other = swap(full, "head", bit, name)
        mine = (hi >> bit) & 1
        full = jnp.where(mine == 0, jnp.stack([full, other]), jnp.stack([other, full]))
        full = full.reshape((-1,) + full.shape[2:]) if bit == head_bits - 1 else full
    full = full.reshape((2,) * head_bits + value.shape)
    full = full.transpose(tuple(reversed(range(head_bits))) + (head_bits, head_bits + 1))
    return full.reshape((-1,) + value.shape[1:])


def halve(keep, si, bit, name):
    pair = keep.reshape(keep.shape[0] // 2, 2, *keep.shape[1:])
    mine = (si >> bit) & 1
    send = lax.dynamic_index_in_dim(pair, 1 - mine, 1, keepdims=False).astype(BF16)
    got = swap(send, "seq", bit, name)
    return lax.dynamic_index_in_dim(pair, mine, 1, keepdims=False) + got.astype(F32)


def body(hidden, w, queries, keys, values, d_out, d_state):
    tokens, width = hidden.shape
    dims = d_state.shape
    nh, dk, dv = dims
    n_seq, n_head = lax.axis_size("seq"), lax.axis_size("head")
    seq_bits, head_bits = n_seq.bit_length() - 1, n_head.bit_length() - 1
    cols = w.shape[1]
    levels = cols // (nh * n_head)
    own = nh * levels
    far = nh * seq_bits
    first = tokens.bit_length()
    si, hi = lax.axis_index("seq"), lax.axis_index("head")
    idx = jnp.reshape(si, (1,)).astype(jnp.int32)
    S = jax.ShapeDtypeStruct
    rows = nh * dk

    hbm = pl.BlockSpec(memory_space=pltpu.HBM)
    kv, kvb, partial, xt = call(
        functools.partial(front_kernel, dims),
        [S((rows, dv), F32), S((rows, dv), BF16), S((cols, tokens), F32), S((width, tokens), BF16)],
        [hbm] * 4, 2 * tokens * (rows * dv + width * cols), "front",
        scratch_shapes=[pltpu.VMEM((tokens, rows), BF16), pltpu.VMEM((tokens, nh * dv), BF16),
                        pltpu.VMEM((width, cols), BF16), pltpu.VMEM((tokens, width), BF16),
                        pltpu.SemaphoreType.DMA((4,))])(
                            *[pltpu.with_memory_space_constraint(a, pltpu.HBM) for a in (keys, values, w, hidden)])

    top = seq_bits - 1
    total, send = kv, kvb
    ups = []
    for bit in range(top):
        partner = swap(send, "seq", bit, "up")
        ups.append(partner)
        if bit < top - 1:
            total = total + partner.astype(F32)
            send = total.astype(BF16)

    keep = partial
    got = None
    for bit in reversed(range(head_bits)):
        pair = keep.reshape(2, keep.shape[0] // 2, tokens)
        mine = (hi >> bit) & 1
        send = lax.dynamic_index_in_dim(pair, 1 - mine, 0, keepdims=False).astype(BF16)
        keep = lax.dynamic_index_in_dim(pair, mine, 0, keepdims=False)
        got = swap(send, "head", bit, "proj")
        if bit:
            keep = keep + got.astype(F32)

    pair_spec = lambda n: pl.BlockSpec((tokens, n), lambda p: (0, p))
    row_spec = lambda n: pl.BlockSpec((n, tokens), lambda p: (p, 0))
    gl = call(
        functools.partial(level_kernel, dims, levels), [S((own, tokens), F32)],
        [pair_spec(2 * dk), pair_spec(2 * dk), pair_spec(2 * dv), pair_spec(2 * dv)],
        2 * tokens * tokens * nh * (dk + dv), "near_levels", grid=(nh // 2,),
        out_specs=[row_spec(2 * levels)])(keys, queries, values, d_out)[0]
    sig, lw, near, qt, gu = call(
        functools.partial(weight_kernel, dims, levels, first, seq_bits),
        [S((own, tokens), F32), S((own, tokens), F32), S((own, tokens), BF16), S((rows, tokens), BF16),
         S((seq_bits, rows, dv), BF16)],
        [VM] * 5, 2 * tokens * rows * dv * seq_bits, "level_weights")(keep, got, gl, queries, d_out)

    send = call(functools.partial(join_kernel, top, top), [S((rows, dv), BF16)], [SM] + [VM] * (top + 2),
                rows * dv, "join")(idx, kv, *ups, gu)[0]
    partner = swap(send, "seq", top, "up")
    ups.append(partner)
    far_rows = call(
        functools.partial(carry_kernel, dims, levels, first, seq_bits), [S((far, tokens), BF16)],
        [SM] + [VM] * (seq_bits + 3), 2 * tokens * rows * dv * seq_bits, "carry")(idx, *ups, d_out, qt, sig)[0]
    upper_top = ((si >> top) & 1) == 1
    adjoint = jnp.where(upper_top, 0.0, partner.astype(F32))
    for bit in reversed(range(top)):
        pending = adjoint + jnp.where(((si >> bit) & 1) == 1, gu[bit].astype(F32), 0.0)
        adjoint = adjoint + swap(pending.astype(BF16), "seq", bit, "down").astype(F32)

    per = width // n_seq
    near_all = gather_heads(near, hi, head_bits, "near")
    near_w = call(wgrad_kernel, [S((width, cols), F32)], [VM, VM], 2 * tokens * width * cols, "near_wgrad")(
        xt, near_all)[0].reshape(n_seq, per, cols)
    for bit in range(top):
        near_w = halve(near_w, si, bit, "near")

    far_all = gather_heads(far_rows, hi, head_bits, "far")
    far_cols = far * n_head
    far_w = call(wgrad_kernel, [S((width, far_cols), F32)], [VM, VM], 2 * tokens * width * far_cols, "far_wgrad")(
        xt, far_all)[0].reshape(n_seq, per, far_cols)
    for bit in range(top):
        far_w = halve(far_w, si, bit, "far")
    col = jnp.arange(cols, dtype=jnp.int32)[None, :]
    row = jnp.arange(far_cols, dtype=jnp.int32)[:, None]
    at = (row // far * nh + row % nh) * levels + first + row % far // nh
    place = (at == col).astype(F32)
    send, keep = call(
        functools.partial(merge_kernel, top), [S((per, cols), BF16), S((per, cols), F32)], [SM] + [VM] * 3,
        4 * per * far_cols * cols, "merge")(
            idx, near_w.reshape(2 * per, cols), far_w.reshape(2 * per, far_cols), place)
    d_w = keep + swap(send, "seq", top, "last").astype(F32)

    half = nh // 4
    local = []
    for part in range(2):
        shift = part * half
        at_col = lambda n, shift=shift: pl.BlockSpec((tokens, n), lambda p: (0, p + shift))
        local.append(call(
            functools.partial(local_kernel, dims, levels),
            [S((nh * dv // 2, tokens), F32), S((rows // 2, tokens), F32), S((tokens, rows // 2), F32),
             S((tokens, nh * dv // 2), F32)],
            [at_col(2 * dk), at_col(2 * dk), at_col(2 * dv), at_col(2 * dv),
             pl.BlockSpec((2 * levels, tokens), lambda p, shift=shift: (p + shift, 0))],
            tokens * tokens * nh * (3 * dk + 3 * dv), "local", grid=(half,),
            out_specs=[row_spec(2 * dv), row_spec(2 * dk), pair_spec(2 * dk), pair_spec(2 * dv)],
        )(keys, queries, values, d_out, lw))
    out_l, dq_l, dk_l, dv_l = [(local[0][n], local[1][n]) for n in range(4)]
    d_queries = call(
        functools.partial(query_kernel, dims, levels, first, seq_bits), [S((tokens, rows), BF16)],
        [SM] + [VM] * (seq_bits + 4), 2 * tokens * rows * dv * seq_bits, "queries")(idx, *ups, d_out, lw, *dq_l)[0]
    out = call(
        functools.partial(out_kernel, dims, levels, first, seq_bits),
        [S((tokens, nh * dv), BF16)],
        [SM] + [VM] * (seq_bits + 4), 2 * tokens * rows * dv * seq_bits, "out")(idx, *ups, qt, lw, *out_l)[0]
    d_hidden = call(hidden_kernel, [S((tokens, width), BF16)], [VM] * 4, 2 * tokens * width * cols, "hgrad")(
        near_all, far_all, place, w)[0]
    d_keys, d_values = call(
        functools.partial(final_kernel, dims),
        [S((tokens, rows), BF16), S((tokens, nh * dv), BF16)], [VM] * 8, 4 * tokens * rows * dv, "final")(
            adjoint, d_state.reshape(rows, dv), keys, values, *dk_l, *dv_l)
    return (out, d_queries, d_keys, d_values, d_hidden, d_w)


def solution(mesh):
    two = P("seq", "head")
    return jax.shard_map(
        body, mesh=mesh,
        in_specs=(two, P("head", None), two, two, two, two, P("head", None, None)),
        out_specs=(two, two, two, two, two, P(("head", "seq"), None)),
        check_vma=False)
```

```python
import functools

import jax
import jax.numpy as jnp
from jax import lax
from jax.experimental import pallas as pl
from jax.experimental.pallas import tpu as pltpu
from jax.sharding import PartitionSpec as P


F32 = jnp.float32
BF16 = jnp.bfloat16
LANES = 128
SUB = 8
VM = pl.BlockSpec(memory_space=pltpu.VMEM)
SM = pl.BlockSpec(memory_space=pltpu.SMEM)


def nn(a, b):
    return lax.dot_general(a, b, (((1,), (0,)), ((), ())), preferred_element_type=F32)


def nt(a, b):
    return lax.dot_general(a, b, (((1,), (1,)), ((), ())), preferred_element_type=F32)


def tn(a, b):
    return lax.dot_general(a, b, (((0,), (0,)), ((), ())), preferred_element_type=F32)


def call(kernel, outs, specs, flops, **kwargs):
    size = sum(o.size * o.dtype.itemsize for o in outs)
    return pl.pallas_call(
        kernel,
        out_shape=outs,
        in_specs=specs,
        compiler_params=pltpu.CompilerParams(vmem_limit_bytes=16 << 20),
        cost_estimate=pl.CostEstimate(flops=flops, bytes_accessed=2 * size, transcendentals=0),
        **kwargs,
    )


def swap(value, axis, bit):
    mask = 1 << bit
    pairs = [(source, source ^ mask) for source in range(lax.axis_size(axis))]
    return lax.ppermute(value, axis, pairs)


def state_kernel(dims, idx_ref, k_hbm, v_hbm, w_hbm, x_hbm, kv_ref, kvb_ref, w_ref, x_ref, k_ref, v_ref, sems):
    nh, dk, dv = dims
    copies = [pltpu.make_async_copy(src, dst, sems.at[n]) for n, (src, dst) in enumerate(
        ((k_hbm, k_ref), (v_hbm, v_ref), (w_hbm, w_ref), (x_hbm, x_ref)))]
    for copy in copies:
        copy.start()
    copies[0].wait()
    copies[1].wait()
    for pair in range(nh // 2):
        turned = k_ref[:, pair * 2 * dk:(pair + 1) * 2 * dk].T
        for j in range(2):
            h = 2 * pair + j
            kv = nn(turned[j * dk:(j + 1) * dk], v_ref[:, h * dv:(h + 1) * dv])
            kv_ref[h * dk:(h + 1) * dk, :] = kv
            kvb_ref[h * dk:(h + 1) * dk, :] = kv.astype(BF16)
    copies[2].wait()
    copies[3].wait()


def part_ways(entries, upper, send_ref, keep_ref, inner):
    n = entries.shape[0] // inner
    for e in range(n // 2):
        low = entries[2 * e * inner:(2 * e + 1) * inner]
        high = entries[(2 * e + 1) * inner:(2 * e + 2) * inner]
        out = slice(e * inner, (e + 1) * inner)
        send_ref[out, :] = jnp.where(upper, low, high).astype(BF16)
        keep_ref[out, :] = jnp.where(upper, high, low)


def project_kernel(bit, idx_ref, w_ref, x_ref, send_ref, keep_ref, xt_ref):
    xt = x_ref[...].T
    xt_ref[...] = xt
    upper = ((idx_ref[1] >> bit) & 1) == 1
    part_ways(tn(w_ref[...], xt), upper, send_ref, keep_ref, keep_ref.shape[0])


def fold_kernel(bit, axis, inner, idx_ref, keep_in, got_ref, send_ref, keep_ref):
    upper = ((idx_ref[axis] >> bit) & 1) == 1
    part_ways(keep_in[...] + got_ref[...].astype(F32), upper, send_ref, keep_ref, inner)


def weight_kernel(dims, levels, first, count, keep_ref, got_ref, gl_ref, q_ref, g_ref,
                  sig_ref, lw_ref, near_ref, qt_ref, gu_ref):
    nh, dk, dv = dims
    proj = keep_ref[...] + got_ref[...].astype(F32)
    sig = jax.nn.sigmoid(proj)
    sig_ref[...] = sig
    near_ref[...] = (gl_ref[...] * sig).astype(BF16)
    lw_ref[...] = jnp.maximum(proj, 0.0) + jnp.log1p(jnp.exp(-jnp.abs(proj)))
    for pair in range(nh // 2):
        turned = q_ref[:, pair * 2 * dk:(pair + 1) * 2 * dk].T
        qt_ref[pair * 2 * dk:(pair + 1) * 2 * dk, :] = turned
        wide = turned.astype(F32)
        for j in range(2):
            h = 2 * pair + j
            scaled = jnp.concatenate(
                [wide[j * dk:(j + 1) * dk] * lw_ref[h * levels + first + m:h * levels + first + m + 1, :]
                 for m in range(count)], axis=0)
            grad = nn(scaled.astype(BF16), g_ref[:, h * dv:(h + 1) * dv])
            for m in range(count):
                gu_ref[m, h * dk:(h + 1) * dk, :] = grad[m * dk:(m + 1) * dk].astype(BF16)


def spread_half(rows, lane, low, t_low):
    digits = (low ^ t_low)
    near = jnp.where(digits == 0, rows[0], jnp.where(digits < 2, rows[1], jnp.where(digits < 4, rows[2], rows[3])))
    near = jnp.where(low <= t_low, near, 0.0)
    parts = []
    for a in range(LANES // SUB):
        value = None
        for l in reversed(range(4, 8)):
            if (a >> (l - 4)) & 1 == 0:
                end = (((a >> (l - 3)) + 1) << (l - 3)) * SUB
                value = rows[l] if value is None else jnp.where(lane < end, rows[l], value)
        value = near if value is None else jnp.where(lane < (a + 1) * SUB, near, value)
        if a:
            value = jnp.where(lane < a * SUB, 0.0, value)
        parts.append(value)
    return jnp.concatenate(parts, axis=0)


def level_sums(prod, lane, low, t_low):
    count = LANES // SUB
    group = lane // SUB
    cur = [prod[a * SUB:(a + 1) * SUB] for a in range(count)]
    near = jnp.zeros_like(cur[0])
    for a in range(count):
        near = jnp.where(group == a, cur[a], near)
    near = jnp.where(low <= t_low, near, 0.0)
    digits = low ^ t_low
    sums = []
    for l in range(4):
        lo, hi = (0, 1) if l == 0 else (1 << (l - 1), 1 << l)
        sums.append(jnp.where((digits >= lo) & (digits < hi), near, 0.0))
    for l in range(4, 8):
        total = jnp.zeros_like(near)
        for a in range(0, len(cur), 2):
            total = jnp.where((lane >> (l - 1)) == a + 1, cur[a], total)
        sums.append(total)
        cur = [cur[a] + cur[a + 1] for a in range(0, len(cur), 2)]
    return [jnp.sum(s, axis=0, keepdims=True) for s in sums]


def level_kernel(dims, levels, k_ref, q_ref, v_ref, g_ref, gl_ref):
    _, dk, dv = dims
    kp = k_ref[...]
    qt = q_ref[...].T
    zero = jnp.zeros_like(qt[:dk])
    lane = lax.broadcasted_iota(jnp.int32, (SUB, LANES), 1)
    low = lax.broadcasted_iota(jnp.int32, (SUB, LANES), 0)
    t_low = lane % SUB
    gl_ref[...] = jnp.zeros_like(gl_ref)
    for j in range(2):
        base = j * levels
        qz = jnp.concatenate([qt[:dk], zero] if j == 0 else [zero, qt[dk:]], axis=0)
        prod = nn(kp, qz) * nt(v_ref[:, j * dv:(j + 1) * dv], g_ref[:, j * dv:(j + 1) * dv])
        for x in range(2):
            part = slice(x * LANES, (x + 1) * LANES)
            sums = level_sums(prod[part, part], lane, low, t_low)
            for l in range(8):
                gl_ref[base + l:base + l + 1, part] = sums[l]
        gl_ref[base + 8:base + 9, LANES:] = jnp.sum(prod[:LANES, LANES:], axis=0, keepdims=True)


def local_kernel(dims, levels, k_ref, q_ref, v_ref, g_ref, lw_ref, out_ref, dq_ref, dk_ref, dv_ref):
    _, dk, dv = dims
    kp, qp = k_ref[...], q_ref[...]
    kt, qt = kp.T, qp.T
    zero = jnp.zeros_like(qt[:dk])
    lane = lax.broadcasted_iota(jnp.int32, (SUB, LANES), 1)
    low = lax.broadcasted_iota(jnp.int32, (SUB, LANES), 0)
    t_low = lane % SUB
    wide_lane = lax.broadcasted_iota(jnp.int32, qp.shape, 1)
    dk_sum = None
    for j in range(2):
        vj = v_ref[:, j * dv:(j + 1) * dv]
        gj = g_ref[:, j * dv:(j + 1) * dv]
        qz = jnp.concatenate([qt[:dk], zero] if j == 0 else [zero, qt[dk:]], axis=0)
        base = j * levels
        cross = lw_ref[base + 8:base + 9, LANES:]
        halves = []
        for x in range(2):
            rows = [jnp.broadcast_to(lw_ref[base + l:base + l + 1, x * LANES:(x + 1) * LANES], (SUB, LANES))
                    for l in range(8)]
            halves.append(spread_half(rows, lane, low, t_low))

        def weigh(full):
            top = jnp.concatenate([full[:LANES, :LANES] * halves[0], full[:LANES, LANES:] * cross], axis=1)
            bottom = full[LANES:, LANES:] * halves[1]
            bottom = jnp.concatenate([jnp.zeros_like(bottom), bottom], axis=1)
            return jnp.concatenate([top, bottom], axis=0).astype(BF16)

        mixed = weigh(nn(kp, qz))
        grad_scores = weigh(nt(vj, gj))
        out_ref[j * dv:(j + 1) * dv, :] = tn(vj, mixed)
        dq_ref[j * dk:(j + 1) * dk, :] = nn(kt[j * dk:(j + 1) * dk], grad_scores)
        dv_ref[:, j * dv:(j + 1) * dv] = nn(mixed, gj)
        mine = (wide_lane < dk) if j == 0 else (wide_lane >= dk)
        term = nn(grad_scores, jnp.where(mine, qp, jnp.zeros_like(qp)))
        dk_sum = term if dk_sum is None else dk_sum + term
    dk_ref[...] = dk_sum


def carry_kernel(dims, levels, first, count, idx_ref, *refs):
    nh, dk, dv = dims
    ups = refs[:count]
    g_ref, qt_ref, sig_ref, far_ref = refs[count:]
    index = idx_ref[0]
    far_ref[...] = jnp.zeros_like(far_ref)
    for m in range(count):
        up = ((index >> m) & 1).astype(F32)
        found = []
        for h in range(nh):
            rows = slice(h * dk, (h + 1) * dk)
            r = h * levels + first + m
            x = nt(ups[m][rows, :], g_ref[:, h * dv:(h + 1) * dv])
            row = jnp.sum(x * qt_ref[rows, :].astype(F32), axis=0, keepdims=True)
            found.append(row * (sig_ref[r:r + 1, :] * up))
        far_ref[m * nh:(m + 1) * nh, :] = jnp.concatenate(found, axis=0).astype(BF16)


def query_kernel(dims, levels, first, count, idx_ref, *refs):
    nh, dk, dv = dims
    ups = refs[:count]
    g_ref, lw_ref, low_ref, high_ref, dq_ref = refs[count:]
    index = idx_ref[0]
    for pair in range(nh // 2):
        halves = []
        for j in range(2):
            h = 2 * pair + j
            local_ref, n = (low_ref, h) if h < nh // 2 else (high_ref, h - nh // 2)
            total = local_ref[n * dk:(n + 1) * dk, :]
            for m in range(count):
                r = h * levels + first + m
                up = ((index >> m) & 1).astype(F32)
                x = nt(ups[m][h * dk:(h + 1) * dk, :], g_ref[:, h * dv:(h + 1) * dv])
                total = total + x * (lw_ref[r:r + 1, :] * up)
            halves.append(total)
        dq_ref[:, pair * 2 * dk:(pair + 1) * 2 * dk] = jnp.concatenate(halves, axis=0).T.astype(BF16)


def out_kernel(dims, levels, first, count, idx_ref, *refs):
    nh, dk, dv = dims
    ups = refs[:count]
    qt_ref, lw_ref, low_ref, high_ref, out_ref = refs[count:]
    index = idx_ref[0]
    for h in range(nh):
        rows = slice(h * dk, (h + 1) * dk)
        local_ref, n = (low_ref, h) if h < nh // 2 else (high_ref, h - nh // 2)
        total = local_ref[n * dv:(n + 1) * dv, :]
        for m in range(count):
            r = h * levels + first + m
            up = ((index >> m) & 1).astype(F32)
            total = total + tn(ups[m][rows, :], qt_ref[rows, :]) * (lw_ref[r:r + 1, :] * up)
        out_ref[:, h * dv:(h + 1) * dv] = total.T.astype(BF16)


def wgrad_kernel(bits, inner, idx_ref, xt_ref, gp_ref, send_ref, keep_ref, sorted_ref):
    count = 1 << bits
    own = gp_ref.shape[0] // count
    for n in range(count):
        away = sum(((n >> k) & 1) << (bits - 1 - k) for k in range(bits))
        at = pl.multiple_of((idx_ref[1] ^ away) * own, 16)
        sorted_ref[pl.ds(at, own), :] = gp_ref[n * own:(n + 1) * own, :]
    part_ways(nt(xt_ref[...], sorted_ref[...]), (idx_ref[0] & 1) == 1, send_ref, keep_ref, inner)


def merge_kernel(bit, idx_ref, near_ref, near_got, far_ref, far_got, place_ref, send_ref, keep_ref):
    total = near_ref[...] + near_got[...].astype(F32) + lax.dot_general(
        far_ref[...] + far_got[...].astype(F32), place_ref[...], (((1,), (0,)), ((), ())),
        preferred_element_type=F32, precision=lax.Precision.HIGHEST)
    part_ways(total, ((idx_ref[0] >> bit) & 1) == 1, send_ref, keep_ref, keep_ref.shape[0])


def hidden_kernel(near_ref, far_ref, place_ref, w_ref, dx_ref):
    gp = near_ref[...].astype(F32) + tn(place_ref[...].astype(BF16), far_ref[...])
    dx_ref[...] = lax.dot_general(
        gp.astype(BF16), w_ref[...], (((0,), (1,)), ((), ())), preferred_element_type=F32).astype(BF16)


def join_kernel(top, count, idx_ref, kv_ref, *refs):
    ups = refs[:count]
    gu_ref, send_ref = refs[count:]
    upper = ((idx_ref[0] >> top) & 1) == 1

    @pl.when(upper)
    def _():
        send_ref[...] = gu_ref[top]

    @pl.when(jnp.logical_not(upper))
    def _():
        total = kv_ref[...]
        for up in ups:
            total = total + up[...].astype(F32)
        send_ref[...] = total.astype(BF16)


def pend_kernel(bit, top, idx_ref, *refs):
    gots, (gu_ref, send_ref) = refs[:-2], refs[-2:]
    index = idx_ref[0]
    total = jnp.where(((index >> top) & 1) == 1, 0.0, gots[0][...].astype(F32))
    for got in gots[1:]:
        total = total + got[...].astype(F32)
    send_ref[...] = (total + jnp.where(((index >> bit) & 1) == 1, gu_ref[bit].astype(F32), 0.0)).astype(BF16)


def final_kernel(dims, top, idx_ref, *refs):
    nh, dk, dv = dims
    gots = refs[:top + 1]
    ds_ref, k_ref, v_ref, low_k, high_k, low_v, high_v, dk_ref, dv_ref = refs[top + 1:]
    upper = ((idx_ref[0] >> top) & 1) == 1
    zero = jnp.zeros((dk, dv), BF16)
    for pair in range(nh // 2):
        pair_rows = slice(pair * 2 * dk, (pair + 1) * 2 * dk)
        total = ds_ref[pair_rows, :] + jnp.where(upper, 0.0, gots[0][pair_rows, :].astype(F32))
        for got in gots[1:]:
            total = total + got[pair_rows, :].astype(F32)
        adj = [total[:dk].astype(BF16), total[dk:].astype(BF16)]
        kp = k_ref[:, pair * 2 * dk:(pair + 1) * 2 * dk]
        dkl_ref, dvl_ref, p = (low_k, low_v, pair) if pair < nh // 4 else (high_k, high_v, pair - nh // 4)
        total = dkl_ref[:, p * 2 * dk:(p + 1) * 2 * dk]
        for j in range(2):
            h = 2 * pair + j
            padded = jnp.concatenate([adj[j], zero] if j == 0 else [zero, adj[j]], axis=0)
            cols = slice(h * dv, (h + 1) * dv)
            total = total + nt(v_ref[:, cols], padded)
            near = dvl_ref[:, (2 * p + j) * dv:(2 * p + j + 1) * dv]
            dv_ref[:, cols] = (near + nn(kp, padded)).astype(BF16)
        dk_ref[:, pair * 2 * dk:(pair + 1) * 2 * dk] = total.astype(BF16)


def gather_heads(value, head_bits):
    full = value
    for bit in reversed(range(head_bits)):
        full = jnp.concatenate([full, swap(full, "head", bit)], axis=0)
    return full


def body(hidden, w, queries, keys, values, d_out, d_state):
    tokens, width = hidden.shape
    dims = d_state.shape
    nh, dk, dv = dims
    n_seq, n_head = lax.axis_size("seq"), lax.axis_size("head")
    seq_bits, head_bits = n_seq.bit_length() - 1, n_head.bit_length() - 1
    top = seq_bits - 1
    cols = w.shape[1]
    levels = cols // (nh * n_head)
    own = nh * levels
    far = nh * seq_bits
    far_own = -(-far // 16) * 16
    far_cols = far_own * n_head
    first = tokens.bit_length()
    per = width // n_seq
    rows = nh * dk
    S = jax.ShapeDtypeStruct
    idx = jnp.stack([lax.axis_index("seq"), lax.axis_index("head")]).astype(jnp.int32)

    hbm = pl.BlockSpec(memory_space=pltpu.HBM)
    kv, kvb, w_near, x_near = call(
        functools.partial(state_kernel, dims),
        [S((rows, dv), F32), S((rows, dv), BF16), S(w.shape, BF16), S(hidden.shape, BF16)],
        [SM] + [hbm] * 4, 2 * tokens * rows * dv,
        scratch_shapes=[pltpu.VMEM((tokens, rows), BF16), pltpu.VMEM((tokens, nh * dv), BF16),
                        pltpu.SemaphoreType.DMA((4,))])(
                            idx, *[pltpu.with_memory_space_constraint(a, pltpu.HBM) for a in (keys, values, w, hidden)])
    send, keep, xt = call(
        functools.partial(project_kernel, head_bits - 1),
        [S((cols // 2, tokens), BF16), S((cols // 2, tokens), F32), S((width, tokens), BF16)], [SM] + [VM] * 2,
        2 * tokens * width * cols)(idx, w_near, x_near)

    total, up = kv, kvb
    ups = []
    for bit in range(top):
        partner = swap(up, "seq", bit)
        ups.append(partner)
        if bit < top - 1:
            total = total + partner.astype(F32)
            up = total.astype(BF16)

    got = swap(send, "head", head_bits - 1)
    for bit in reversed(range(head_bits - 1)):
        n = keep.shape[0] // 2
        send, keep = call(
            functools.partial(fold_kernel, bit, 1, n), [S((n, tokens), BF16), S((n, tokens), F32)],
            [SM] + [VM] * 2, n * tokens)(idx, keep, got)
        got = swap(send, "head", bit)

    pair_spec = lambda n: pl.BlockSpec((tokens, n), lambda p: (0, p))
    row_spec = lambda n: pl.BlockSpec((n, tokens), lambda p: (p, 0))
    gl = call(
        functools.partial(level_kernel, dims, levels), [S((own, tokens), F32)],
        [pair_spec(2 * dk), pair_spec(2 * dk), pair_spec(2 * dv), pair_spec(2 * dv)],
        2 * tokens * tokens * nh * (dk + dv), grid=(nh // 2,),
        out_specs=[row_spec(2 * levels)])(keys, queries, values, d_out)[0]
    sig, lw, near, qt, gu = call(
        functools.partial(weight_kernel, dims, levels, first, seq_bits),
        [S((own, tokens), F32), S((own, tokens), F32), S((own, tokens), BF16), S((rows, tokens), BF16),
         S((seq_bits, rows, dv), BF16)],
        [VM] * 5, 2 * tokens * rows * dv * seq_bits)(keep, got, gl, queries, d_out)

    up = call(functools.partial(join_kernel, top, top), [S((rows, dv), BF16)], [SM] + [VM] * (top + 2),
              rows * dv)(idx, kv, *ups, gu)[0]
    partner = swap(up, "seq", top)
    ups.append(partner)
    far_rows = call(
        functools.partial(carry_kernel, dims, levels, first, seq_bits), [S((far_own, tokens), BF16)],
        [SM] + [VM] * (seq_bits + 3), 2 * tokens * rows * dv * seq_bits)(idx, *ups, d_out, qt, sig)[0]
    gots = [partner]
    for bit in reversed(range(top)):
        down = call(functools.partial(pend_kernel, bit, top), [S((rows, dv), BF16)], [SM] + [VM] * (len(gots) + 1),
                    rows * dv)(idx, *gots, gu)[0]
        gots.append(swap(down, "seq", bit))

    def reduce(gathered, n_cols):
        send, keep, ordered = call(
            functools.partial(wgrad_kernel, head_bits, per),
            [S((width // 2, n_cols), BF16), S((width // 2, n_cols), F32), S((n_cols, tokens), BF16)],
            [SM] + [VM] * 2, 2 * tokens * width * n_cols)(idx, xt, gathered)
        got = swap(send, "seq", 0)
        for bit in range(1, top):
            n = keep.shape[0] // 2
            send, keep = call(
                functools.partial(fold_kernel, bit, 0, per), [S((n, n_cols), BF16), S((n, n_cols), F32)],
                [SM] + [VM] * 2, n * n_cols)(idx, keep, got)
            got = swap(send, "seq", bit)
        return keep, got, ordered

    near_w, near_got, near_all = reduce(gather_heads(near, head_bits), cols)
    far_w, far_got, far_all = reduce(gather_heads(far_rows, head_bits), far_cols)
    col = jnp.arange(cols, dtype=jnp.int32)[None, :]
    row = jnp.arange(far_cols, dtype=jnp.int32)[:, None]
    within = row % far_own
    at = (row // far_own * nh + within % nh) * levels + first + within // nh
    place = ((at == col) & (within < far)).astype(F32)
    send, keep = call(
        functools.partial(merge_kernel, top), [S((per, cols), BF16), S((per, cols), F32)], [SM] + [VM] * 5,
        4 * per * far_cols * cols)(idx, near_w, near_got, far_w, far_got, place)
    d_w = keep + swap(send, "seq", top).astype(F32)

    half = nh // 4
    local = []
    for part in range(2):
        shift = part * half
        at_col = lambda n, shift=shift: pl.BlockSpec((tokens, n), lambda p: (0, p + shift))
        local.append(call(
            functools.partial(local_kernel, dims, levels),
            [S((nh * dv // 2, tokens), F32), S((rows // 2, tokens), F32), S((tokens, rows // 2), F32),
             S((tokens, nh * dv // 2), F32)],
            [at_col(2 * dk), at_col(2 * dk), at_col(2 * dv), at_col(2 * dv),
             pl.BlockSpec((2 * levels, tokens), lambda p, shift=shift: (p + shift, 0))],
            tokens * tokens * nh * (3 * dk + 3 * dv), grid=(half,),
            out_specs=[row_spec(2 * dv), row_spec(2 * dk), pair_spec(2 * dk), pair_spec(2 * dv)],
        )(keys, queries, values, d_out, lw))
    out_l, dq_l, dk_l, dv_l = [(local[0][n], local[1][n]) for n in range(4)]
    d_queries = call(
        functools.partial(query_kernel, dims, levels, first, seq_bits), [S((tokens, rows), BF16)],
        [SM] + [VM] * (seq_bits + 4), 2 * tokens * rows * dv * seq_bits)(idx, *ups, d_out, lw, *dq_l)[0]
    out = call(
        functools.partial(out_kernel, dims, levels, first, seq_bits),
        [S((tokens, nh * dv), BF16)],
        [SM] + [VM] * (seq_bits + 4), 2 * tokens * rows * dv * seq_bits)(idx, *ups, qt, lw, *out_l)[0]
    d_hidden = call(hidden_kernel, [S((tokens, width), BF16)], [VM] * 4, 2 * tokens * width * cols)(
        near_all, far_all, place, w_near)[0]
    d_keys, d_values = call(
        functools.partial(final_kernel, dims, top),
        [S((tokens, rows), BF16), S((tokens, nh * dv), BF16)], [SM] + [VM] * (top + 8), 4 * tokens * rows * dv)(idx, *gots, d_state.reshape(rows, dv), keys, values, *dk_l, *dv_l)
    return (out, d_queries, d_keys, d_values, d_hidden, d_w)


def solution(mesh):
    two = P("seq", "head")
    return jax.shard_map(
        body, mesh=mesh,
        in_specs=(two, P("head", None), two, two, two, two, P("head", None, None)),
        out_specs=(two, two, two, two, two, P(("head", "seq"), None)),
        check_vma=False)
```

```python
import functools

import jax
import jax.numpy as jnp
from jax import lax
from jax.experimental import pallas as pl
from jax.experimental.pallas import tpu as pltpu
from jax.sharding import PartitionSpec as P


F32 = jnp.float32
BF16 = jnp.bfloat16
LANES = 128
SUB = 8
VM = pl.BlockSpec(memory_space=pltpu.VMEM)
SM = pl.BlockSpec(memory_space=pltpu.SMEM)


def nn(a, b):
    return lax.dot_general(a, b, (((1,), (0,)), ((), ())), preferred_element_type=F32)


def nt(a, b):
    return lax.dot_general(a, b, (((1,), (1,)), ((), ())), preferred_element_type=F32)


def tn(a, b):
    return lax.dot_general(a, b, (((0,), (0,)), ((), ())), preferred_element_type=F32)


def call(kernel, outs, specs, flops, **kwargs):
    size = sum(o.size * o.dtype.itemsize for o in outs)
    return pl.pallas_call(
        kernel,
        out_shape=outs,
        in_specs=specs,
        compiler_params=pltpu.CompilerParams(vmem_limit_bytes=16 << 20),
        cost_estimate=pl.CostEstimate(flops=flops, bytes_accessed=2 * size, transcendentals=0),
        **kwargs,
    )


def swap(value, axis, bit):
    mask = 1 << bit
    pairs = [(source, source ^ mask) for source in range(lax.axis_size(axis))]
    return lax.ppermute(value, axis, pairs)


def state_kernel(dims, idx_ref, head_ref, k_hbm, v_hbm, w_hbm, x_hbm, kv_ref, kvb_ref, w_ref, x_ref, k_ref, v_ref, sems):
    nh, dk, dv = dims
    copies = [pltpu.make_async_copy(src, dst, sems.at[n]) for n, (src, dst) in enumerate(
        ((k_hbm, k_ref), (v_hbm, v_ref), (w_hbm, w_ref), (x_hbm, x_ref)))]
    for copy in copies:
        copy.start()
    copies[0].wait()
    copies[1].wait()
    for pair in range(nh // 2):
        turned = k_ref[:, pair * 2 * dk:(pair + 1) * 2 * dk].T
        for j in range(2):
            h = 2 * pair + j
            kv = nn(turned[j * dk:(j + 1) * dk], v_ref[:, h * dv:(h + 1) * dv])
            kv_ref[h * dk:(h + 1) * dk, :] = kv
            kvb_ref[h * dk:(h + 1) * dk, :] = kv.astype(BF16)
    copies[2].wait()
    copies[3].wait()


def part_ways(entries, upper, send_ref, keep_ref, inner):
    n = entries.shape[0] // inner
    for e in range(n // 2):
        low = entries[2 * e * inner:(2 * e + 1) * inner]
        high = entries[(2 * e + 1) * inner:(2 * e + 2) * inner]
        out = slice(e * inner, (e + 1) * inner)
        send_ref[out, :] = jnp.where(upper, low, high).astype(BF16)
        keep_ref[out, :] = jnp.where(upper, high, low)


def project_kernel(bit, idx_ref, w_ref, x_ref, send_ref, keep_ref, xt_ref):
    xt = x_ref[...].T
    xt_ref[...] = xt
    upper = ((idx_ref[0] >> bit) & 1) == 1
    part_ways(tn(w_ref[...], xt), upper, send_ref, keep_ref, keep_ref.shape[0])


def fold_kernel(bit, inner, idx_ref, keep_in, got_ref, send_ref, keep_ref):
    upper = ((idx_ref[0] >> bit) & 1) == 1
    part_ways(keep_in[...] + got_ref[...].astype(F32), upper, send_ref, keep_ref, inner)


def weight_kernel(dims, levels, first, count, keep_ref, got_ref, gl_ref, q_ref, g_ref,
                  sig_ref, lw_ref, near_ref, qt_ref, gu_ref):
    nh, dk, dv = dims
    proj = keep_ref[...] + got_ref[...].astype(F32)
    sig = jax.nn.sigmoid(proj)
    sig_ref[...] = sig
    near_ref[...] = (gl_ref[...] * sig).astype(BF16)
    lw_ref[...] = jnp.maximum(proj, 0.0) + jnp.log1p(jnp.exp(-jnp.abs(proj)))
    for pair in range(nh // 2):
        turned = q_ref[:, pair * 2 * dk:(pair + 1) * 2 * dk].T
        qt_ref[pair * 2 * dk:(pair + 1) * 2 * dk, :] = turned
        wide = turned.astype(F32)
        for j in range(2):
            h = 2 * pair + j
            scaled = jnp.concatenate(
                [wide[j * dk:(j + 1) * dk] * lw_ref[h * levels + first + m:h * levels + first + m + 1, :]
                 for m in range(count)], axis=0)
            grad = nn(scaled.astype(BF16), g_ref[:, h * dv:(h + 1) * dv])
            for m in range(count):
                gu_ref[m, h * dk:(h + 1) * dk, :] = grad[m * dk:(m + 1) * dk].astype(BF16)


def spread_half(rows, lane, low, t_low):
    digits = (low ^ t_low)
    near = jnp.where(digits == 0, rows[0], jnp.where(digits < 2, rows[1], jnp.where(digits < 4, rows[2], rows[3])))
    near = jnp.where(low <= t_low, near, 0.0)
    parts = []
    for a in range(LANES // SUB):
        value = None
        for l in reversed(range(4, 8)):
            if (a >> (l - 4)) & 1 == 0:
                end = (((a >> (l - 3)) + 1) << (l - 3)) * SUB
                value = rows[l] if value is None else jnp.where(lane < end, rows[l], value)
        value = near if value is None else jnp.where(lane < (a + 1) * SUB, near, value)
        if a:
            value = jnp.where(lane < a * SUB, 0.0, value)
        parts.append(value)
    return jnp.concatenate(parts, axis=0)


def level_sums(prod, lane, low, t_low):
    count = LANES // SUB
    group = lane // SUB
    cur = [prod[a * SUB:(a + 1) * SUB] for a in range(count)]
    near = jnp.zeros_like(cur[0])
    for a in range(count):
        near = jnp.where(group == a, cur[a], near)
    near = jnp.where(low <= t_low, near, 0.0)
    digits = low ^ t_low
    sums = []
    for l in range(4):
        lo, hi = (0, 1) if l == 0 else (1 << (l - 1), 1 << l)
        sums.append(jnp.where((digits >= lo) & (digits < hi), near, 0.0))
    for l in range(4, 8):
        total = jnp.zeros_like(near)
        for a in range(0, len(cur), 2):
            total = jnp.where((lane >> (l - 1)) == a + 1, cur[a], total)
        sums.append(total)
        cur = [cur[a] + cur[a + 1] for a in range(0, len(cur), 2)]
    return [jnp.sum(s, axis=0, keepdims=True) for s in sums]


def level_kernel(dims, levels, k_ref, q_ref, v_ref, g_ref, gl_ref):
    _, dk, dv = dims
    kp = k_ref[...]
    qt = q_ref[...].T
    zero = jnp.zeros_like(qt[:dk])
    lane = lax.broadcasted_iota(jnp.int32, (SUB, LANES), 1)
    low = lax.broadcasted_iota(jnp.int32, (SUB, LANES), 0)
    t_low = lane % SUB
    gl_ref[...] = jnp.zeros_like(gl_ref)
    for j in range(2):
        base = j * levels
        qz = jnp.concatenate([qt[:dk], zero] if j == 0 else [zero, qt[dk:]], axis=0)
        prod = nn(kp, qz) * nt(v_ref[:, j * dv:(j + 1) * dv], g_ref[:, j * dv:(j + 1) * dv])
        for x in range(2):
            part = slice(x * LANES, (x + 1) * LANES)
            sums = level_sums(prod[part, part], lane, low, t_low)
            for l in range(8):
                gl_ref[base + l:base + l + 1, part] = sums[l]
        gl_ref[base + 8:base + 9, LANES:] = jnp.sum(prod[:LANES, LANES:], axis=0, keepdims=True)


def local_kernel(dims, levels, k_ref, q_ref, v_ref, g_ref, lw_ref, out_ref, dq_ref, dk_ref, dv_ref):
    _, dk, dv = dims
    kp, qp = k_ref[...], q_ref[...]
    kt, qt = kp.T, qp.T
    zero = jnp.zeros_like(qt[:dk])
    lane = lax.broadcasted_iota(jnp.int32, (SUB, LANES), 1)
    low = lax.broadcasted_iota(jnp.int32, (SUB, LANES), 0)
    t_low = lane % SUB
    wide_lane = lax.broadcasted_iota(jnp.int32, qp.shape, 1)
    dk_sum = None
    for j in range(2):
        vj = v_ref[:, j * dv:(j + 1) * dv]
        gj = g_ref[:, j * dv:(j + 1) * dv]
        qz = jnp.concatenate([qt[:dk], zero] if j == 0 else [zero, qt[dk:]], axis=0)
        base = j * levels
        cross = lw_ref[base + 8:base + 9, LANES:]
        halves = []
        for x in range(2):
            rows = [jnp.broadcast_to(lw_ref[base + l:base + l + 1, x * LANES:(x + 1) * LANES], (SUB, LANES))
                    for l in range(8)]
            halves.append(spread_half(rows, lane, low, t_low))

        def weigh(full):
            top = jnp.concatenate([full[:LANES, :LANES] * halves[0], full[:LANES, LANES:] * cross], axis=1)
            bottom = full[LANES:, LANES:] * halves[1]
            bottom = jnp.concatenate([jnp.zeros_like(bottom), bottom], axis=1)
            return jnp.concatenate([top, bottom], axis=0).astype(BF16)

        mixed = weigh(nn(kp, qz))
        grad_scores = weigh(nt(vj, gj))
        out_ref[j * dv:(j + 1) * dv, :] = tn(vj, mixed)
        dq_ref[j * dk:(j + 1) * dk, :] = nn(kt[j * dk:(j + 1) * dk], grad_scores)
        dv_ref[:, j * dv:(j + 1) * dv] = nn(mixed, gj)
        mine = (wide_lane < dk) if j == 0 else (wide_lane >= dk)
        term = nn(grad_scores, jnp.where(mine, qp, jnp.zeros_like(qp)))
        dk_sum = term if dk_sum is None else dk_sum + term
    dk_ref[...] = dk_sum


def carry_kernel(dims, levels, first, count, idx_ref, *refs):
    nh, dk, dv = dims
    ups = refs[:count]
    g_ref, qt_ref, sig_ref, far_ref = refs[count:]
    index = idx_ref[0]
    far_ref[...] = jnp.zeros_like(far_ref)
    for m in range(count):
        up = ((index >> m) & 1).astype(F32)
        found = []
        for h in range(nh):
            rows = slice(h * dk, (h + 1) * dk)
            r = h * levels + first + m
            x = nt(ups[m][rows, :], g_ref[:, h * dv:(h + 1) * dv])
            row = jnp.sum(x * qt_ref[rows, :].astype(F32), axis=0, keepdims=True)
            found.append(row * (sig_ref[r:r + 1, :] * up))
        far_ref[m * nh:(m + 1) * nh, :] = jnp.concatenate(found, axis=0).astype(BF16)


def query_kernel(dims, levels, first, count, idx_ref, *refs):
    nh, dk, dv = dims
    ups = refs[:count]
    g_ref, lw_ref, low_ref, high_ref, dq_ref = refs[count:]
    index = idx_ref[0]
    for pair in range(nh // 2):
        halves = []
        for j in range(2):
            h = 2 * pair + j
            local_ref, n = (low_ref, h) if h < nh // 2 else (high_ref, h - nh // 2)
            total = local_ref[n * dk:(n + 1) * dk, :]
            for m in range(count):
                r = h * levels + first + m
                up = ((index >> m) & 1).astype(F32)
                x = nt(ups[m][h * dk:(h + 1) * dk, :], g_ref[:, h * dv:(h + 1) * dv])
                total = total + x * (lw_ref[r:r + 1, :] * up)
            halves.append(total)
        dq_ref[:, pair * 2 * dk:(pair + 1) * 2 * dk] = jnp.concatenate(halves, axis=0).T.astype(BF16)


def out_kernel(dims, levels, first, count, idx_ref, *refs):
    nh, dk, dv = dims
    ups = refs[:count]
    qt_ref, lw_ref, low_ref, high_ref, out_ref = refs[count:]
    index = idx_ref[0]
    for h in range(nh):
        rows = slice(h * dk, (h + 1) * dk)
        local_ref, n = (low_ref, h) if h < nh // 2 else (high_ref, h - nh // 2)
        total = local_ref[n * dv:(n + 1) * dv, :]
        for m in range(count):
            r = h * levels + first + m
            up = ((index >> m) & 1).astype(F32)
            total = total + tn(ups[m][rows, :], qt_ref[rows, :]) * (lw_ref[r:r + 1, :] * up)
        out_ref[:, h * dv:(h + 1) * dv] = total.T.astype(BF16)


def wgrad_kernel(bits, inner, idx_ref, head_ref, xt_ref, gp_ref, send_ref, keep_ref, sorted_ref):
    count = 1 << bits
    own = gp_ref.shape[0] // count
    for n in range(count):
        away = sum(((n >> k) & 1) << (bits - 1 - k) for k in range(bits))
        at = pl.multiple_of((head_ref[0] ^ away) * own, 16)
        sorted_ref[pl.ds(at, own), :] = gp_ref[n * own:(n + 1) * own, :]
    part_ways(nt(xt_ref[...], sorted_ref[...]), (idx_ref[0] & 1) == 1, send_ref, keep_ref, inner)


def merge_kernel(bit, idx_ref, near_ref, near_got, far_ref, far_got, place_ref, send_ref, keep_ref):
    total = near_ref[...] + near_got[...].astype(F32) + lax.dot_general(
        far_ref[...] + far_got[...].astype(F32), place_ref[...], (((1,), (0,)), ((), ())),
        preferred_element_type=F32, precision=lax.Precision.HIGHEST)
    part_ways(total, ((idx_ref[0] >> bit) & 1) == 1, send_ref, keep_ref, keep_ref.shape[0])


def hidden_kernel(near_ref, far_ref, place_ref, w_ref, dx_ref):
    gp = near_ref[...].astype(F32) + tn(place_ref[...].astype(BF16), far_ref[...])
    dx_ref[...] = lax.dot_general(
        gp.astype(BF16), w_ref[...], (((0,), (1,)), ((), ())), preferred_element_type=F32).astype(BF16)


def join_kernel(top, count, idx_ref, kv_ref, *refs):
    ups = refs[:count]
    gu_ref, send_ref = refs[count:]
    upper = ((idx_ref[0] >> top) & 1) == 1

    @pl.when(upper)
    def _():
        send_ref[...] = gu_ref[top]

    @pl.when(jnp.logical_not(upper))
    def _():
        total = kv_ref[...]
        for up in ups:
            total = total + up[...].astype(F32)
        send_ref[...] = total.astype(BF16)


def pend_kernel(bit, top, idx_ref, *refs):
    gots, (gu_ref, send_ref) = refs[:-2], refs[-2:]
    index = idx_ref[0]
    total = jnp.where(((index >> top) & 1) == 1, 0.0, gots[0][...].astype(F32))
    for got in gots[1:]:
        total = total + got[...].astype(F32)
    send_ref[...] = (total + jnp.where(((index >> bit) & 1) == 1, gu_ref[bit].astype(F32), 0.0)).astype(BF16)


def final_kernel(dims, top, idx_ref, *refs):
    nh, dk, dv = dims
    gots = refs[:top + 1]
    ds_ref, k_ref, v_ref, low_k, high_k, low_v, high_v, dk_ref, dv_ref = refs[top + 1:]
    upper = ((idx_ref[0] >> top) & 1) == 1
    zero = jnp.zeros((dk, dv), BF16)
    for pair in range(nh // 2):
        pair_rows = slice(pair * 2 * dk, (pair + 1) * 2 * dk)
        total = ds_ref[pair_rows, :] + jnp.where(upper, 0.0, gots[0][pair_rows, :].astype(F32))
        for got in gots[1:]:
            total = total + got[pair_rows, :].astype(F32)
        adj = [total[:dk].astype(BF16), total[dk:].astype(BF16)]
        kp = k_ref[:, pair * 2 * dk:(pair + 1) * 2 * dk]
        dkl_ref, dvl_ref, p = (low_k, low_v, pair) if pair < nh // 4 else (high_k, high_v, pair - nh // 4)
        total = dkl_ref[:, p * 2 * dk:(p + 1) * 2 * dk]
        for j in range(2):
            h = 2 * pair + j
            padded = jnp.concatenate([adj[j], zero] if j == 0 else [zero, adj[j]], axis=0)
            cols = slice(h * dv, (h + 1) * dv)
            total = total + nt(v_ref[:, cols], padded)
            near = dvl_ref[:, (2 * p + j) * dv:(2 * p + j + 1) * dv]
            dv_ref[:, cols] = (near + nn(kp, padded)).astype(BF16)
        dk_ref[:, pair * 2 * dk:(pair + 1) * 2 * dk] = total.astype(BF16)


def gather_heads(value, head_bits):
    full = value
    for bit in reversed(range(head_bits)):
        full = jnp.concatenate([full, swap(full, "head", bit)], axis=0)
    return full


def body(hidden, w, queries, keys, values, d_out, d_state):
    tokens, width = hidden.shape
    dims = d_state.shape
    nh, dk, dv = dims
    n_seq, n_head = lax.axis_size("seq"), lax.axis_size("head")
    seq_bits, head_bits = n_seq.bit_length() - 1, n_head.bit_length() - 1
    top = seq_bits - 1
    cols = w.shape[1]
    levels = cols // (nh * n_head)
    own = nh * levels
    far = nh * seq_bits
    far_own = -(-far // 16) * 16
    far_cols = far_own * n_head
    first = tokens.bit_length()
    per = width // n_seq
    rows = nh * dk
    S = jax.ShapeDtypeStruct
    idx, head_idx = [jnp.reshape(lax.axis_index(axis), (1,)) for axis in ("seq", "head")]

    hbm = pl.BlockSpec(memory_space=pltpu.HBM)
    kv, kvb, w_near, x_near = call(
        functools.partial(state_kernel, dims),
        [S((rows, dv), F32), S((rows, dv), BF16), S(w.shape, BF16), S(hidden.shape, BF16)],
        [SM] * 2 + [hbm] * 4, 2 * tokens * rows * dv,
        scratch_shapes=[pltpu.VMEM((tokens, rows), BF16), pltpu.VMEM((tokens, nh * dv), BF16),
                        pltpu.SemaphoreType.DMA((4,))])(
                            idx, head_idx, *[pltpu.with_memory_space_constraint(a, pltpu.HBM) for a in (keys, values, w, hidden)])
    send, keep, xt = call(
        functools.partial(project_kernel, head_bits - 1),
        [S((cols // 2, tokens), BF16), S((cols // 2, tokens), F32), S((width, tokens), BF16)], [SM] + [VM] * 2,
        2 * tokens * width * cols)(head_idx, w_near, x_near)

    total, up = kv, kvb
    ups = []
    for bit in range(top):
        partner = swap(up, "seq", bit)
        ups.append(partner)
        if bit < top - 1:
            total = total + partner.astype(F32)
            up = total.astype(BF16)

    got = swap(send, "head", head_bits - 1)
    for bit in reversed(range(head_bits - 1)):
        n = keep.shape[0] // 2
        send, keep = call(
            functools.partial(fold_kernel, bit, n), [S((n, tokens), BF16), S((n, tokens), F32)],
            [SM] + [VM] * 2, n * tokens)(head_idx, keep, got)
        got = swap(send, "head", bit)

    pair_spec = lambda n: pl.BlockSpec((tokens, n), lambda p: (0, p))
    row_spec = lambda n: pl.BlockSpec((n, tokens), lambda p: (p, 0))
    gl = call(
        functools.partial(level_kernel, dims, levels), [S((own, tokens), F32)],
        [pair_spec(2 * dk), pair_spec(2 * dk), pair_spec(2 * dv), pair_spec(2 * dv)],
        2 * tokens * tokens * nh * (dk + dv), grid=(nh // 2,),
        out_specs=[row_spec(2 * levels)])(keys, queries, values, d_out)[0]
    sig, lw, near, qt, gu = call(
        functools.partial(weight_kernel, dims, levels, first, seq_bits),
        [S((own, tokens), F32), S((own, tokens), F32), S((own, tokens), BF16), S((rows, tokens), BF16),
         S((seq_bits, rows, dv), BF16)],
        [VM] * 5, 2 * tokens * rows * dv * seq_bits)(keep, got, gl, queries, d_out)

    up = call(functools.partial(join_kernel, top, top), [S((rows, dv), BF16)], [SM] + [VM] * (top + 2),
              rows * dv)(idx, kv, *ups, gu)[0]
    partner = swap(up, "seq", top)
    ups.append(partner)
    far_rows = call(
        functools.partial(carry_kernel, dims, levels, first, seq_bits), [S((far_own, tokens), BF16)],
        [SM] + [VM] * (seq_bits + 3), 2 * tokens * rows * dv * seq_bits)(idx, *ups, d_out, qt, sig)[0]
    gots = [partner]
    for bit in reversed(range(top)):
        down = call(functools.partial(pend_kernel, bit, top), [S((rows, dv), BF16)], [SM] + [VM] * (len(gots) + 1),
                    rows * dv)(idx, *gots, gu)[0]
        gots.append(swap(down, "seq", bit))

    def reduce(gathered, n_cols):
        send, keep, ordered = call(
            functools.partial(wgrad_kernel, head_bits, per),
            [S((width // 2, n_cols), BF16), S((width // 2, n_cols), F32), S((n_cols, tokens), BF16)],
            [SM] * 2 + [VM] * 2, 2 * tokens * width * n_cols)(idx, head_idx, xt, gathered)
        got = swap(send, "seq", 0)
        for bit in range(1, top):
            n = keep.shape[0] // 2
            send, keep = call(
                functools.partial(fold_kernel, bit, per), [S((n, n_cols), BF16), S((n, n_cols), F32)],
                [SM] + [VM] * 2, n * n_cols)(idx, keep, got)
            got = swap(send, "seq", bit)
        return keep, got, ordered

    near_w, near_got, near_all = reduce(gather_heads(near, head_bits), cols)
    far_w, far_got, far_all = reduce(gather_heads(far_rows, head_bits), far_cols)
    col = jnp.arange(cols, dtype=jnp.int32)[None, :]
    row = jnp.arange(far_cols, dtype=jnp.int32)[:, None]
    within = row % far_own
    at = (row // far_own * nh + within % nh) * levels + first + within // nh
    place = ((at == col) & (within < far)).astype(F32)
    send, keep = call(
        functools.partial(merge_kernel, top), [S((per, cols), BF16), S((per, cols), F32)], [SM] + [VM] * 5,
        4 * per * far_cols * cols)(idx, near_w, near_got, far_w, far_got, place)
    d_w = keep + swap(send, "seq", top).astype(F32)

    half = nh // 4
    local = []
    for part in range(2):
        shift = part * half
        at_col = lambda n, shift=shift: pl.BlockSpec((tokens, n), lambda p: (0, p + shift))
        local.append(call(
            functools.partial(local_kernel, dims, levels),
            [S((nh * dv // 2, tokens), F32), S((rows // 2, tokens), F32), S((tokens, rows // 2), F32),
             S((tokens, nh * dv // 2), F32)],
            [at_col(2 * dk), at_col(2 * dk), at_col(2 * dv), at_col(2 * dv),
             pl.BlockSpec((2 * levels, tokens), lambda p, shift=shift: (p + shift, 0))],
            tokens * tokens * nh * (3 * dk + 3 * dv), grid=(half,),
            out_specs=[row_spec(2 * dv), row_spec(2 * dk), pair_spec(2 * dk), pair_spec(2 * dv)],
        )(keys, queries, values, d_out, lw))
    out_l, dq_l, dk_l, dv_l = [(local[0][n], local[1][n]) for n in range(4)]
    d_queries = call(
        functools.partial(query_kernel, dims, levels, first, seq_bits), [S((tokens, rows), BF16)],
        [SM] + [VM] * (seq_bits + 4), 2 * tokens * rows * dv * seq_bits)(idx, *ups, d_out, lw, *dq_l)[0]
    out = call(
        functools.partial(out_kernel, dims, levels, first, seq_bits),
        [S((tokens, nh * dv), BF16)],
        [SM] + [VM] * (seq_bits + 4), 2 * tokens * rows * dv * seq_bits)(idx, *ups, qt, lw, *out_l)[0]
    d_hidden = call(hidden_kernel, [S((tokens, width), BF16)], [VM] * 4, 2 * tokens * width * cols)(
        near_all, far_all, place, w_near)[0]
    d_keys, d_values = call(
        functools.partial(final_kernel, dims, top),
        [S((tokens, rows), BF16), S((tokens, nh * dv), BF16)], [SM] + [VM] * (top + 8), 4 * tokens * rows * dv)(idx, *gots, d_state.reshape(rows, dv), keys, values, *dk_l, *dv_l)
    return (out, d_queries, d_keys, d_values, d_hidden, d_w)


def solution(mesh):
    two = P("seq", "head")
    return jax.shard_map(
        body, mesh=mesh,
        in_specs=(two, P("head", None), two, two, two, two, P("head", None, None)),
        out_specs=(two, two, two, two, two, P(("head", "seq"), None)),
        check_vma=False)
```

```python
import functools

import jax
import jax.numpy as jnp
from jax import lax
from jax.experimental import pallas as pl
from jax.experimental.pallas import tpu as pltpu
from jax.sharding import PartitionSpec as P


F32 = jnp.float32
BF16 = jnp.bfloat16
LANES = 128
SUB = 8
VM = pl.BlockSpec(memory_space=pltpu.VMEM)
SM = pl.BlockSpec(memory_space=pltpu.SMEM)


def nn(a, b):
    return lax.dot_general(a, b, (((1,), (0,)), ((), ())), preferred_element_type=F32)


def nt(a, b):
    return lax.dot_general(a, b, (((1,), (1,)), ((), ())), preferred_element_type=F32)


def tn(a, b):
    return lax.dot_general(a, b, (((0,), (0,)), ((), ())), preferred_element_type=F32)


def call(kernel, outs, specs, flops, **kwargs):
    size = sum(o.size * o.dtype.itemsize for o in outs)
    return pl.pallas_call(
        kernel,
        out_shape=outs,
        in_specs=specs,
        compiler_params=pltpu.CompilerParams(vmem_limit_bytes=16 << 20),
        cost_estimate=pl.CostEstimate(flops=flops, bytes_accessed=2 * size, transcendentals=0),
        **kwargs,
    )


def leave(buf_ref, hbm_ref, sem, cols):
    copy = pltpu.make_async_copy(buf_ref.at[:, cols], hbm_ref.at[:, cols], sem)
    copy.start()
    return copy


def swap(value, axis, bit):
    mask = 1 << bit
    pairs = [(source, source ^ mask) for source in range(lax.axis_size(axis))]
    return lax.ppermute(value, axis, pairs)


def state_kernel(dims, idx_ref, head_ref, k_hbm, v_hbm, w_hbm, x_hbm, kv_ref, kvb_ref, w_ref, x_ref, k_ref, v_ref, sems):
    nh, dk, dv = dims
    copies = [pltpu.make_async_copy(src, dst, sems.at[n]) for n, (src, dst) in enumerate(
        ((k_hbm, k_ref), (v_hbm, v_ref), (w_hbm, w_ref), (x_hbm, x_ref)))]
    for copy in copies:
        copy.start()
    copies[0].wait()
    copies[1].wait()
    for pair in range(nh // 2):
        turned = k_ref[:, pair * 2 * dk:(pair + 1) * 2 * dk].T
        for j in range(2):
            h = 2 * pair + j
            kv = nn(turned[j * dk:(j + 1) * dk], v_ref[:, h * dv:(h + 1) * dv])
            kv_ref[h * dk:(h + 1) * dk, :] = kv
            kvb_ref[h * dk:(h + 1) * dk, :] = kv.astype(BF16)
    copies[2].wait()
    copies[3].wait()


def part_ways(entries, upper, send_ref, keep_ref, inner):
    n = entries.shape[0] // inner
    for e in range(n // 2):
        low = entries[2 * e * inner:(2 * e + 1) * inner]
        high = entries[(2 * e + 1) * inner:(2 * e + 2) * inner]
        out = slice(e * inner, (e + 1) * inner)
        send_ref[out, :] = jnp.where(upper, low, high).astype(BF16)
        keep_ref[out, :] = jnp.where(upper, high, low)


def project_kernel(bit, idx_ref, w_ref, x_ref, send_ref, keep_ref, xt_ref):
    xt = x_ref[...].T
    xt_ref[...] = xt
    upper = ((idx_ref[0] >> bit) & 1) == 1
    part_ways(tn(w_ref[...], xt), upper, send_ref, keep_ref, keep_ref.shape[0])


def fold_kernel(bit, inner, idx_ref, keep_in, got_ref, send_ref, keep_ref):
    upper = ((idx_ref[0] >> bit) & 1) == 1
    part_ways(keep_in[...] + got_ref[...].astype(F32), upper, send_ref, keep_ref, inner)


def weight_kernel(dims, levels, first, count, keep_ref, got_ref, gl_ref, q_ref, g_ref,
                  sig_ref, lw_ref, near_ref, qt_ref, gu_ref):
    nh, dk, dv = dims
    proj = keep_ref[...] + got_ref[...].astype(F32)
    sig = jax.nn.sigmoid(proj)
    sig_ref[...] = sig
    near_ref[...] = (gl_ref[...] * sig).astype(BF16)
    lw_ref[...] = jnp.maximum(proj, 0.0) + jnp.log1p(jnp.exp(-jnp.abs(proj)))
    for pair in range(nh // 2):
        turned = q_ref[:, pair * 2 * dk:(pair + 1) * 2 * dk].T
        qt_ref[pair * 2 * dk:(pair + 1) * 2 * dk, :] = turned
        wide = turned.astype(F32)
        for j in range(2):
            h = 2 * pair + j
            scaled = jnp.concatenate(
                [wide[j * dk:(j + 1) * dk] * lw_ref[h * levels + first + m:h * levels + first + m + 1, :]
                 for m in range(count)], axis=0)
            grad = nn(scaled.astype(BF16), g_ref[:, h * dv:(h + 1) * dv])
            for m in range(count):
                gu_ref[m, h * dk:(h + 1) * dk, :] = grad[m * dk:(m + 1) * dk].astype(BF16)


def spread_half(rows, lane, low, t_low):
    digits = (low ^ t_low)
    near = jnp.where(digits == 0, rows[0], jnp.where(digits < 2, rows[1], jnp.where(digits < 4, rows[2], rows[3])))
    near = jnp.where(low <= t_low, near, 0.0)
    parts = []
    for a in range(LANES // SUB):
        value = None
        for l in reversed(range(4, 8)):
            if (a >> (l - 4)) & 1 == 0:
                end = (((a >> (l - 3)) + 1) << (l - 3)) * SUB
                value = rows[l] if value is None else jnp.where(lane < end, rows[l], value)
        value = near if value is None else jnp.where(lane < (a + 1) * SUB, near, value)
        if a:
            value = jnp.where(lane < a * SUB, 0.0, value)
        parts.append(value)
    return jnp.concatenate(parts, axis=0)


def level_sums(prod, lane, low, t_low):
    count = LANES // SUB
    group = lane // SUB
    cur = [prod[a * SUB:(a + 1) * SUB] for a in range(count)]
    near = jnp.zeros_like(cur[0])
    for a in range(count):
        near = jnp.where(group == a, cur[a], near)
    near = jnp.where(low <= t_low, near, 0.0)
    digits = low ^ t_low
    sums = []
    for l in range(4):
        lo, hi = (0, 1) if l == 0 else (1 << (l - 1), 1 << l)
        sums.append(jnp.where((digits >= lo) & (digits < hi), near, 0.0))
    for l in range(4, 8):
        total = jnp.zeros_like(near)
        for a in range(0, len(cur), 2):
            total = jnp.where((lane >> (l - 1)) == a + 1, cur[a], total)
        sums.append(total)
        cur = [cur[a] + cur[a + 1] for a in range(0, len(cur), 2)]
    return [jnp.sum(s, axis=0, keepdims=True) for s in sums]


def level_kernel(dims, levels, k_ref, q_ref, v_ref, g_ref, gl_ref):
    nh, dk, dv = dims
    lane = lax.broadcasted_iota(jnp.int32, (SUB, LANES), 1)
    low = lax.broadcasted_iota(jnp.int32, (SUB, LANES), 0)
    t_low = lane % SUB
    gl_ref[...] = jnp.zeros_like(gl_ref)
    for pair in range(nh // 2):
        kp = k_ref[:, pair * 2 * dk:(pair + 1) * 2 * dk]
        qt = q_ref[:, pair * 2 * dk:(pair + 1) * 2 * dk].T
        zero = jnp.zeros_like(qt[:dk])
        for j in range(2):
            h = 2 * pair + j
            base = h * levels
            qz = jnp.concatenate([qt[:dk], zero] if j == 0 else [zero, qt[dk:]], axis=0)
            prod = nn(kp, qz) * nt(v_ref[:, h * dv:(h + 1) * dv], g_ref[:, h * dv:(h + 1) * dv])
            for x in range(2):
                part = slice(x * LANES, (x + 1) * LANES)
                sums = level_sums(prod[part, part], lane, low, t_low)
                for l in range(8):
                    gl_ref[base + l:base + l + 1, part] = sums[l]
            gl_ref[base + 8:base + 9, LANES:] = jnp.sum(prod[:LANES, LANES:], axis=0, keepdims=True)


def local_kernel(dims, levels, pairs, k_ref, q_ref, v_ref, g_ref, lw_ref, out_ref, dq_ref, dk_ref, dv_ref):
    _, dk, dv = dims
    lane = lax.broadcasted_iota(jnp.int32, (SUB, LANES), 1)
    low = lax.broadcasted_iota(jnp.int32, (SUB, LANES), 0)
    t_low = lane % SUB
    for n, pair in enumerate(pairs):
        kp = k_ref[:, pair * 2 * dk:(pair + 1) * 2 * dk]
        qp = q_ref[:, pair * 2 * dk:(pair + 1) * 2 * dk]
        kt, qt = kp.T, qp.T
        zero = jnp.zeros_like(qt[:dk])
        wide_lane = lax.broadcasted_iota(jnp.int32, qp.shape, 1)
        dk_sum = None
        for j in range(2):
            h, m = 2 * pair + j, 2 * n + j
            vj = v_ref[:, h * dv:(h + 1) * dv]
            gj = g_ref[:, h * dv:(h + 1) * dv]
            qz = jnp.concatenate([qt[:dk], zero] if j == 0 else [zero, qt[dk:]], axis=0)
            base = h * levels
            cross = lw_ref[base + 8:base + 9, LANES:]
            halves = []
            for x in range(2):
                rows = [jnp.broadcast_to(lw_ref[base + l:base + l + 1, x * LANES:(x + 1) * LANES], (SUB, LANES))
                        for l in range(8)]
                halves.append(spread_half(rows, lane, low, t_low))

            def weigh(full):
                top = jnp.concatenate([full[:LANES, :LANES] * halves[0], full[:LANES, LANES:] * cross], axis=1)
                bottom = full[LANES:, LANES:] * halves[1]
                bottom = jnp.concatenate([jnp.zeros_like(bottom), bottom], axis=1)
                return jnp.concatenate([top, bottom], axis=0).astype(BF16)

            mixed = weigh(nn(kp, qz))
            grad_scores = weigh(nt(vj, gj))
            out_ref[m * dv:(m + 1) * dv, :] = tn(vj, mixed)
            dq_ref[m * dk:(m + 1) * dk, :] = nn(kt[j * dk:(j + 1) * dk], grad_scores)
            dv_ref[:, m * dv:(m + 1) * dv] = nn(mixed, gj)
            mine = (wide_lane < dk) if j == 0 else (wide_lane >= dk)
            term = nn(grad_scores, jnp.where(mine, qp, jnp.zeros_like(qp)))
            dk_sum = term if dk_sum is None else dk_sum + term
        dk_ref[:, n * 2 * dk:(n + 1) * 2 * dk] = dk_sum


def carry_kernel(dims, levels, first, count, idx_ref, *refs):
    nh, dk, dv = dims
    ups = refs[:count]
    g_ref, qt_ref, sig_ref, far_ref = refs[count:]
    index = idx_ref[0]
    far_ref[...] = jnp.zeros_like(far_ref)
    for m in range(count):
        up = ((index >> m) & 1).astype(F32)
        found = []
        for h in range(nh):
            rows = slice(h * dk, (h + 1) * dk)
            r = h * levels + first + m
            x = nt(ups[m][rows, :], g_ref[:, h * dv:(h + 1) * dv])
            row = jnp.sum(x * qt_ref[rows, :].astype(F32), axis=0, keepdims=True)
            found.append(row * (sig_ref[r:r + 1, :] * up))
        far_ref[m * nh:(m + 1) * nh, :] = jnp.concatenate(found, axis=0).astype(BF16)


def query_kernel(dims, levels, first, count, idx_ref, *refs):
    nh, dk, dv = dims
    ups = refs[:count]
    g_ref, lw_ref, low_ref, high_ref, dq_hbm, dq_ref, sems = refs[count:]
    index = idx_ref[0]
    copies = []
    for pair in range(nh // 2):
        halves = []
        for j in range(2):
            h = 2 * pair + j
            local_ref, n = (low_ref, h) if h < nh // 2 else (high_ref, h - nh // 2)
            total = local_ref[n * dk:(n + 1) * dk, :]
            for m in range(count):
                r = h * levels + first + m
                up = ((index >> m) & 1).astype(F32)
                x = nt(ups[m][h * dk:(h + 1) * dk, :], g_ref[:, h * dv:(h + 1) * dv])
                total = total + x * (lw_ref[r:r + 1, :] * up)
            halves.append(total)
        cols = slice(pair * 2 * dk, (pair + 1) * 2 * dk)
        dq_ref[:, cols] = jnp.concatenate(halves, axis=0).T.astype(BF16)
        copies.append(leave(dq_ref, dq_hbm, sems.at[pair], cols))
    for copy in copies:
        copy.wait()


def out_kernel(dims, levels, first, count, idx_ref, *refs):
    nh, dk, dv = dims
    ups = refs[:count]
    qt_ref, lw_ref, low_ref, high_ref, out_hbm, out_ref, sems = refs[count:]
    index = idx_ref[0]
    copies = []
    for h in range(nh):
        rows = slice(h * dk, (h + 1) * dk)
        local_ref, n = (low_ref, h) if h < nh // 2 else (high_ref, h - nh // 2)
        total = local_ref[n * dv:(n + 1) * dv, :]
        for m in range(count):
            r = h * levels + first + m
            up = ((index >> m) & 1).astype(F32)
            total = total + tn(ups[m][rows, :], qt_ref[rows, :]) * (lw_ref[r:r + 1, :] * up)
        out_ref[:, h * dv:(h + 1) * dv] = total.T.astype(BF16)
        if h % 2:
            copies.append(leave(out_ref, out_hbm, sems.at[h // 2], slice((h - 1) * dv, (h + 1) * dv)))
    for copy in copies:
        copy.wait()


def wgrad_kernel(bits, inner, idx_ref, head_ref, xt_ref, gp_ref, send_ref, keep_ref, sorted_ref):
    count = 1 << bits
    own = gp_ref.shape[0] // count
    for n in range(count):
        away = sum(((n >> k) & 1) << (bits - 1 - k) for k in range(bits))
        at = pl.multiple_of((head_ref[0] ^ away) * own, 16)
        sorted_ref[pl.ds(at, own), :] = gp_ref[n * own:(n + 1) * own, :]
    part_ways(nt(xt_ref[...], sorted_ref[...]), (idx_ref[0] & 1) == 1, send_ref, keep_ref, inner)


def merge_kernel(bit, idx_ref, near_ref, near_got, far_ref, far_got, place_ref, send_ref, keep_ref):
    total = near_ref[...] + near_got[...].astype(F32) + lax.dot_general(
        far_ref[...] + far_got[...].astype(F32), place_ref[...], (((1,), (0,)), ((), ())),
        preferred_element_type=F32, precision=lax.Precision.HIGHEST)
    part_ways(total, ((idx_ref[0] >> bit) & 1) == 1, send_ref, keep_ref, keep_ref.shape[0])


def hidden_kernel(near_ref, far_ref, place_ref, w_ref, dx_hbm, dx_ref, sems):
    gp = (near_ref[...].astype(F32) + tn(place_ref[...].astype(BF16), far_ref[...])).astype(BF16).T
    half = dx_ref.shape[1] // 2
    copies = []
    for n in range(2):
        cols = slice(n * half, (n + 1) * half)
        dx_ref[:, cols] = nt(gp, w_ref[cols, :]).astype(BF16)
        copies.append(leave(dx_ref, dx_hbm, sems.at[n], cols))
    for copy in copies:
        copy.wait()


def join_kernel(top, count, idx_ref, kv_ref, *refs):
    ups = refs[:count]
    gu_ref, send_ref = refs[count:]
    upper = ((idx_ref[0] >> top) & 1) == 1

    @pl.when(upper)
    def _():
        send_ref[...] = gu_ref[top]

    @pl.when(jnp.logical_not(upper))
    def _():
        total = kv_ref[...]
        for up in ups:
            total = total + up[...].astype(F32)
        send_ref[...] = total.astype(BF16)


def pend_kernel(bit, top, idx_ref, *refs):
    gots, (gu_ref, send_ref) = refs[:-2], refs[-2:]
    index = idx_ref[0]
    total = jnp.where(((index >> top) & 1) == 1, 0.0, gots[0][...].astype(F32))
    for got in gots[1:]:
        total = total + got[...].astype(F32)
    send_ref[...] = (total + jnp.where(((index >> bit) & 1) == 1, gu_ref[bit].astype(F32), 0.0)).astype(BF16)


def final_kernel(dims, top, idx_ref, *refs):
    nh, dk, dv = dims
    gots = refs[:top + 1]
    ds_ref, k_ref, v_ref, low_k, high_k, low_v, high_v, dk_hbm, dv_hbm, dk_ref, dv_ref, sems = refs[top + 1:]
    copies = []
    upper = ((idx_ref[0] >> top) & 1) == 1
    zero = jnp.zeros((dk, dv), BF16)
    for pair in range(nh // 2):
        pair_rows = slice(pair * 2 * dk, (pair + 1) * 2 * dk)
        total = ds_ref[pair_rows, :] + jnp.where(upper, 0.0, gots[0][pair_rows, :].astype(F32))
        for got in gots[1:]:
            total = total + got[pair_rows, :].astype(F32)
        adj = [total[:dk].astype(BF16), total[dk:].astype(BF16)]
        kp = k_ref[:, pair * 2 * dk:(pair + 1) * 2 * dk]
        dkl_ref, dvl_ref, p = (low_k, low_v, pair) if pair < nh // 4 else (high_k, high_v, pair - nh // 4)
        total = dkl_ref[:, p * 2 * dk:(p + 1) * 2 * dk]
        for j in range(2):
            h = 2 * pair + j
            padded = jnp.concatenate([adj[j], zero] if j == 0 else [zero, adj[j]], axis=0)
            cols = slice(h * dv, (h + 1) * dv)
            total = total + nt(v_ref[:, cols], padded)
            near = dvl_ref[:, (2 * p + j) * dv:(2 * p + j + 1) * dv]
            dv_ref[:, cols] = (near + nn(kp, padded)).astype(BF16)
        dk_ref[:, pair * 2 * dk:(pair + 1) * 2 * dk] = total.astype(BF16)
        copies.append(leave(dv_ref, dv_hbm, sems.at[2 * pair], slice(2 * pair * dv, (2 * pair + 2) * dv)))
        copies.append(leave(dk_ref, dk_hbm, sems.at[2 * pair + 1], slice(pair * 2 * dk, (pair + 1) * 2 * dk)))
    for copy in copies:
        copy.wait()


def gather_heads(value, head_bits):
    full = value
    for bit in reversed(range(head_bits)):
        full = jnp.concatenate([full, swap(full, "head", bit)], axis=0)
    return full


def body(hidden, w, queries, keys, values, d_out, d_state):
    tokens, width = hidden.shape
    dims = d_state.shape
    nh, dk, dv = dims
    n_seq, n_head = lax.axis_size("seq"), lax.axis_size("head")
    seq_bits, head_bits = n_seq.bit_length() - 1, n_head.bit_length() - 1
    top = seq_bits - 1
    cols = w.shape[1]
    levels = cols // (nh * n_head)
    own = nh * levels
    far = nh * seq_bits
    far_own = -(-far // 16) * 16
    far_cols = far_own * n_head
    first = tokens.bit_length()
    per = width // n_seq
    rows = nh * dk
    S = jax.ShapeDtypeStruct
    idx, head_idx = [jnp.reshape(lax.axis_index(axis), (1,)) for axis in ("seq", "head")]

    hbm = pl.BlockSpec(memory_space=pltpu.HBM)
    kv, kvb, w_near, x_near = call(
        functools.partial(state_kernel, dims),
        [S((rows, dv), F32), S((rows, dv), BF16), S(w.shape, BF16), S(hidden.shape, BF16)],
        [SM] * 2 + [hbm] * 4, 2 * tokens * rows * dv,
        scratch_shapes=[pltpu.VMEM((tokens, rows), BF16), pltpu.VMEM((tokens, nh * dv), BF16),
                        pltpu.SemaphoreType.DMA((4,))])(
                            idx, head_idx, *[pltpu.with_memory_space_constraint(a, pltpu.HBM) for a in (keys, values, w, hidden)])
    send, keep, xt = call(
        functools.partial(project_kernel, head_bits - 1),
        [S((cols // 2, tokens), BF16), S((cols // 2, tokens), F32), S((width, tokens), BF16)], [SM] + [VM] * 2,
        2 * tokens * width * cols)(head_idx, w_near, x_near)

    total, up = kv, kvb
    ups = []
    for bit in range(top):
        partner = swap(up, "seq", bit)
        ups.append(partner)
        if bit < top - 1:
            total = total + partner.astype(F32)
            up = total.astype(BF16)

    got = swap(send, "head", head_bits - 1)
    for bit in reversed(range(head_bits - 1)):
        n = keep.shape[0] // 2
        send, keep = call(
            functools.partial(fold_kernel, bit, n), [S((n, tokens), BF16), S((n, tokens), F32)],
            [SM] + [VM] * 2, n * tokens)(head_idx, keep, got)
        got = swap(send, "head", bit)

    gl = call(
        functools.partial(level_kernel, dims, levels), [S((own, tokens), F32)], [VM] * 4,
        2 * tokens * tokens * nh * (dk + dv))(keys, queries, values, d_out)[0]
    sig, lw, near, qt, gu = call(
        functools.partial(weight_kernel, dims, levels, first, seq_bits),
        [S((own, tokens), F32), S((own, tokens), F32), S((own, tokens), BF16), S((rows, tokens), BF16),
         S((seq_bits, rows, dv), BF16)],
        [VM] * 5, 2 * tokens * rows * dv * seq_bits)(keep, got, gl, queries, d_out)

    up = call(functools.partial(join_kernel, top, top), [S((rows, dv), BF16)], [SM] + [VM] * (top + 2),
              rows * dv)(idx, kv, *ups, gu)[0]
    partner = swap(up, "seq", top)
    ups.append(partner)
    far_rows = call(
        functools.partial(carry_kernel, dims, levels, first, seq_bits), [S((far_own, tokens), BF16)],
        [SM] + [VM] * (seq_bits + 3), 2 * tokens * rows * dv * seq_bits)(idx, *ups, d_out, qt, sig)[0]
    gots = [partner]
    for bit in reversed(range(top)):
        down = call(functools.partial(pend_kernel, bit, top), [S((rows, dv), BF16)], [SM] + [VM] * (len(gots) + 1),
                    rows * dv)(idx, *gots, gu)[0]
        gots.append(swap(down, "seq", bit))

    def reduce(gathered, n_cols):
        send, keep, ordered = call(
            functools.partial(wgrad_kernel, head_bits, per),
            [S((width // 2, n_cols), BF16), S((width // 2, n_cols), F32), S((n_cols, tokens), BF16)],
            [SM] * 2 + [VM] * 2, 2 * tokens * width * n_cols)(idx, head_idx, xt, gathered)
        got = swap(send, "seq", 0)
        for bit in range(1, top):
            n = keep.shape[0] // 2
            send, keep = call(
                functools.partial(fold_kernel, bit, per), [S((n, n_cols), BF16), S((n, n_cols), F32)],
                [SM] + [VM] * 2, n * n_cols)(idx, keep, got)
            got = swap(send, "seq", bit)
        return keep, got, ordered

    near_w, near_got, near_all = reduce(gather_heads(near, head_bits), cols)
    far_w, far_got, far_all = reduce(gather_heads(far_rows, head_bits), far_cols)
    col = jnp.arange(cols, dtype=jnp.int32)[None, :]
    row = jnp.arange(far_cols, dtype=jnp.int32)[:, None]
    within = row % far_own
    at = (row // far_own * nh + within % nh) * levels + first + within // nh
    place = ((at == col) & (within < far)).astype(F32)
    send, keep = call(
        functools.partial(merge_kernel, top), [S((per, cols), BF16), S((per, cols), F32)], [SM] + [VM] * 5,
        4 * per * far_cols * cols)(idx, near_w, near_got, far_w, far_got, place)
    d_w = keep + swap(send, "seq", top).astype(F32)

    half = nh // 4
    local = []
    for part in range(2):
        local.append(call(
            functools.partial(local_kernel, dims, levels, tuple(range(part * half, (part + 1) * half))),
            [S((nh * dv // 2, tokens), F32), S((rows // 2, tokens), F32), S((tokens, rows // 2), F32),
             S((tokens, nh * dv // 2), F32)],
            [VM] * 5, tokens * tokens * nh * (3 * dk + 3 * dv),
        )(keys, queries, values, d_out, lw))
    out_l, dq_l, dk_l, dv_l = [(local[0][n], local[1][n]) for n in range(4)]

    def leaving(shapes, copies):
        return dict(out_specs=[hbm] * len(shapes),
                    scratch_shapes=[pltpu.VMEM(shape, BF16) for shape in shapes] + [pltpu.SemaphoreType.DMA((copies,))])

    def results(*shapes):
        return [S(shape, BF16) for shape in shapes]

    narrow, broad = (tokens, rows), (tokens, nh * dv)
    d_queries = call(
        functools.partial(query_kernel, dims, levels, first, seq_bits), results(narrow),
        [SM] + [VM] * (seq_bits + 4), 2 * tokens * rows * dv * seq_bits, **leaving([narrow], nh // 2))(
            idx, *ups, d_out, lw, *dq_l)[0]
    out = call(
        functools.partial(out_kernel, dims, levels, first, seq_bits), results(broad),
        [SM] + [VM] * (seq_bits + 4), 2 * tokens * rows * dv * seq_bits, **leaving([broad], nh // 2))(
            idx, *ups, qt, lw, *out_l)[0]
    d_hidden = call(
        hidden_kernel, results((tokens, width)), [VM] * 4, 2 * tokens * width * cols,
        **leaving([(tokens, width)], 2))(near_all, far_all, place, w_near)[0]
    d_keys, d_values = call(
        functools.partial(final_kernel, dims, top), results(narrow, broad), [SM] + [VM] * (top + 8),
        4 * tokens * rows * dv, **leaving([narrow, broad], nh))(
            idx, *gots, d_state.reshape(rows, dv), keys, values, *dk_l, *dv_l)
    return (out, d_queries, d_keys, d_values, d_hidden, d_w)


def solution(mesh):
    two = P("seq", "head")
    return jax.shard_map(
        body, mesh=mesh,
        in_specs=(two, P("head", None), two, two, two, two, P("head", None, None)),
        out_specs=(two, two, two, two, two, P(("head", "seq"), None)),
        check_vma=False)
```

```python
import functools

import jax
import jax.numpy as jnp
from jax import lax
from jax.experimental import pallas as pl
from jax.experimental.pallas import tpu as pltpu
from jax.sharding import PartitionSpec as P


F32 = jnp.float32
BF16 = jnp.bfloat16
LANES = 128
SUB = 8
VM = pl.BlockSpec(memory_space=pltpu.VMEM)
SM = pl.BlockSpec(memory_space=pltpu.SMEM)


def nn(a, b):
    return lax.dot_general(a, b, (((1,), (0,)), ((), ())), preferred_element_type=F32)


def nt(a, b):
    return lax.dot_general(a, b, (((1,), (1,)), ((), ())), preferred_element_type=F32)


def tn(a, b):
    return lax.dot_general(a, b, (((0,), (0,)), ((), ())), preferred_element_type=F32)


def call(kernel, outs, specs, flops, **kwargs):
    size = sum(o.size * o.dtype.itemsize for o in outs)
    return pl.pallas_call(
        kernel,
        out_shape=outs,
        in_specs=specs,
        compiler_params=pltpu.CompilerParams(vmem_limit_bytes=16 << 20),
        cost_estimate=pl.CostEstimate(flops=flops, bytes_accessed=2 * size, transcendentals=0),
        **kwargs,
    )


def leave(buf_ref, hbm_ref, sem, cols):
    copy = pltpu.make_async_copy(buf_ref.at[:, cols], hbm_ref.at[:, cols], sem)
    copy.start()
    return copy


def swap(value, axis, bit):
    mask = 1 << bit
    pairs = [(source, source ^ mask) for source in range(lax.axis_size(axis))]
    return lax.ppermute(value, axis, pairs)


def state_kernel(dims, idx_ref, head_ref, k_hbm, v_hbm, w_hbm, x_hbm, kv_ref, kvb_ref, w_ref, x_ref, k_ref, v_ref, sems):
    nh, dk, dv = dims
    copies = [pltpu.make_async_copy(src, dst, sems.at[n]) for n, (src, dst) in enumerate(
        ((k_hbm, k_ref), (v_hbm, v_ref), (w_hbm, w_ref), (x_hbm, x_ref)))]
    for copy in copies:
        copy.start()
    copies[0].wait()
    copies[1].wait()
    for pair in range(nh // 2):
        turned = k_ref[:, pair * 2 * dk:(pair + 1) * 2 * dk].T
        for j in range(2):
            h = 2 * pair + j
            kv = nn(turned[j * dk:(j + 1) * dk], v_ref[:, h * dv:(h + 1) * dv])
            kv_ref[h * dk:(h + 1) * dk, :] = kv
            kvb_ref[h * dk:(h + 1) * dk, :] = kv.astype(BF16)
    copies[2].wait()
    copies[3].wait()


def part_ways(entries, upper, send_ref, keep_ref, inner):
    n = entries.shape[0] // inner
    for e in range(n // 2):
        low = entries[2 * e * inner:(2 * e + 1) * inner]
        high = entries[(2 * e + 1) * inner:(2 * e + 2) * inner]
        out = slice(e * inner, (e + 1) * inner)
        send_ref[out, :] = jnp.where(upper, low, high).astype(BF16)
        keep_ref[out, :] = jnp.where(upper, high, low)


def project_kernel(bit, idx_ref, w_ref, x_ref, send_ref, keep_ref, xt_ref):
    xt = x_ref[...].T
    xt_ref[...] = xt
    upper = ((idx_ref[0] >> bit) & 1) == 1
    part_ways(tn(w_ref[...], xt), upper, send_ref, keep_ref, keep_ref.shape[0])


def fold_kernel(bit, inner, idx_ref, keep_in, got_ref, send_ref, keep_ref):
    upper = ((idx_ref[0] >> bit) & 1) == 1
    part_ways(keep_in[...] + got_ref[...].astype(F32), upper, send_ref, keep_ref, inner)


def weight_kernel(dims, levels, first, count, keep_ref, got_ref, gl_ref, q_ref, g_ref,
                  sig_ref, lw_ref, near_ref, qt_ref, gu_ref):
    nh, dk, dv = dims
    proj = keep_ref[...] + got_ref[...].astype(F32)
    sig = jax.nn.sigmoid(proj)
    sig_ref[...] = sig
    near_ref[...] = (gl_ref[...] * sig).astype(BF16)
    lw_ref[...] = jnp.maximum(proj, 0.0) + jnp.log1p(jnp.exp(-jnp.abs(proj)))
    for pair in range(nh // 2):
        turned = q_ref[:, pair * 2 * dk:(pair + 1) * 2 * dk].T
        qt_ref[pair * 2 * dk:(pair + 1) * 2 * dk, :] = turned
        wide = turned.astype(F32)
        for j in range(2):
            h = 2 * pair + j
            scaled = jnp.concatenate(
                [wide[j * dk:(j + 1) * dk] * lw_ref[h * levels + first + m:h * levels + first + m + 1, :]
                 for m in range(count)], axis=0)
            grad = nn(scaled.astype(BF16), g_ref[:, h * dv:(h + 1) * dv])
            for m in range(count):
                gu_ref[m, h * dk:(h + 1) * dk, :] = grad[m * dk:(m + 1) * dk].astype(BF16)


def spread_half(rows, lane, low, t_low):
    digits = (low ^ t_low)
    near = jnp.where(digits == 0, rows[0], jnp.where(digits < 2, rows[1], jnp.where(digits < 4, rows[2], rows[3])))
    near = jnp.where(low <= t_low, near, 0.0)
    parts = []
    for a in range(LANES // SUB):
        value = None
        for l in reversed(range(4, 8)):
            if (a >> (l - 4)) & 1 == 0:
                end = (((a >> (l - 3)) + 1) << (l - 3)) * SUB
                value = rows[l] if value is None else jnp.where(lane < end, rows[l], value)
        value = near if value is None else jnp.where(lane < (a + 1) * SUB, near, value)
        if a:
            value = jnp.where(lane < a * SUB, 0.0, value)
        parts.append(value)
    return jnp.concatenate(parts, axis=0)


def level_sums(prod, lane, low, t_low):
    count = LANES // SUB
    group = lane // SUB
    cur = [prod[a * SUB:(a + 1) * SUB] for a in range(count)]
    near = jnp.zeros_like(cur[0])
    for a in range(count):
        near = jnp.where(group == a, cur[a], near)
    near = jnp.where(low <= t_low, near, 0.0)
    digits = low ^ t_low
    sums = []
    for l in range(4):
        lo, hi = (0, 1) if l == 0 else (1 << (l - 1), 1 << l)
        sums.append(jnp.where((digits >= lo) & (digits < hi), near, 0.0))
    for l in range(4, 8):
        total = jnp.zeros_like(near)
        for a in range(0, len(cur), 2):
            total = jnp.where((lane >> (l - 1)) == a + 1, cur[a], total)
        sums.append(total)
        cur = [cur[a] + cur[a + 1] for a in range(0, len(cur), 2)]
    return [jnp.sum(s, axis=0, keepdims=True) for s in sums]


def level_kernel(dims, levels, k_ref, q_ref, v_ref, g_ref, gl_ref):
    nh, dk, dv = dims
    lane = lax.broadcasted_iota(jnp.int32, (SUB, LANES), 1)
    low = lax.broadcasted_iota(jnp.int32, (SUB, LANES), 0)
    t_low = lane % SUB
    gl_ref[...] = jnp.zeros_like(gl_ref)
    for pair in range(nh // 2):
        kp = k_ref[:, pair * 2 * dk:(pair + 1) * 2 * dk]
        qt = q_ref[:, pair * 2 * dk:(pair + 1) * 2 * dk].T
        zero = jnp.zeros_like(qt[:dk])
        for j in range(2):
            h = 2 * pair + j
            base = h * levels
            qz = jnp.concatenate([qt[:dk], zero] if j == 0 else [zero, qt[dk:]], axis=0)
            prod = nn(kp, qz) * nt(v_ref[:, h * dv:(h + 1) * dv], g_ref[:, h * dv:(h + 1) * dv])
            for x in range(2):
                part = slice(x * LANES, (x + 1) * LANES)
                sums = level_sums(prod[part, part], lane, low, t_low)
                for l in range(8):
                    gl_ref[base + l:base + l + 1, part] = sums[l]
            gl_ref[base + 8:base + 9, LANES:] = jnp.sum(prod[:LANES, LANES:], axis=0, keepdims=True)


def local_kernel(dims, levels, pairs, k_ref, q_ref, v_ref, g_ref, lw_ref, out_ref, dq_ref, dk_ref, dv_ref):
    _, dk, dv = dims
    lane = lax.broadcasted_iota(jnp.int32, (SUB, LANES), 1)
    low = lax.broadcasted_iota(jnp.int32, (SUB, LANES), 0)
    t_low = lane % SUB
    for n, pair in enumerate(pairs):
        kp = k_ref[:, pair * 2 * dk:(pair + 1) * 2 * dk]
        qp = q_ref[:, pair * 2 * dk:(pair + 1) * 2 * dk]
        kt, qt = kp.T, qp.T
        zero = jnp.zeros_like(qt[:dk])
        wide_lane = lax.broadcasted_iota(jnp.int32, qp.shape, 1)
        dk_sum = None
        for j in range(2):
            h, m = 2 * pair + j, 2 * n + j
            vj = v_ref[:, h * dv:(h + 1) * dv]
            gj = g_ref[:, h * dv:(h + 1) * dv]
            qz = jnp.concatenate([qt[:dk], zero] if j == 0 else [zero, qt[dk:]], axis=0)
            base = h * levels
            cross = lw_ref[base + 8:base + 9, LANES:]
            halves = []
            for x in range(2):
                rows = [jnp.broadcast_to(lw_ref[base + l:base + l + 1, x * LANES:(x + 1) * LANES], (SUB, LANES))
                        for l in range(8)]
                halves.append(spread_half(rows, lane, low, t_low))

            def weigh(full):
                top = jnp.concatenate([full[:LANES, :LANES] * halves[0], full[:LANES, LANES:] * cross], axis=1)
                bottom = full[LANES:, LANES:] * halves[1]
                bottom = jnp.concatenate([jnp.zeros_like(bottom), bottom], axis=1)
                return jnp.concatenate([top, bottom], axis=0).astype(BF16)

            mixed = weigh(nn(kp, qz))
            grad_scores = weigh(nt(vj, gj))
            out_ref[m * dv:(m + 1) * dv, :] = tn(vj, mixed)
            dq_ref[m * dk:(m + 1) * dk, :] = nn(kt[j * dk:(j + 1) * dk], grad_scores)
            dv_ref[:, m * dv:(m + 1) * dv] = nn(mixed, gj)
            mine = (wide_lane < dk) if j == 0 else (wide_lane >= dk)
            term = nn(grad_scores, jnp.where(mine, qp, jnp.zeros_like(qp)))
            dk_sum = term if dk_sum is None else dk_sum + term
        dk_ref[:, n * 2 * dk:(n + 1) * 2 * dk] = dk_sum


def carry_kernel(dims, levels, first, count, idx_ref, *refs):
    nh, dk, dv = dims
    ups = refs[:count]
    g_ref, qt_ref, sig_ref, far_ref = refs[count:]
    index = idx_ref[0]
    far_ref[...] = jnp.zeros_like(far_ref)
    for m in range(count):
        up = ((index >> m) & 1).astype(F32)
        found = []
        for h in range(nh):
            rows = slice(h * dk, (h + 1) * dk)
            r = h * levels + first + m
            x = nt(ups[m][rows, :], g_ref[:, h * dv:(h + 1) * dv])
            row = jnp.sum(x * qt_ref[rows, :].astype(F32), axis=0, keepdims=True)
            found.append(row * (sig_ref[r:r + 1, :] * up))
        far_ref[m * nh:(m + 1) * nh, :] = jnp.concatenate(found, axis=0).astype(BF16)


def query_kernel(dims, levels, first, count, idx_ref, *refs):
    nh, dk, dv = dims
    ups = refs[:count]
    g_ref, lw_ref, low_ref, high_ref, dq_hbm, dq_ref, sems = refs[count:]
    index = idx_ref[0]
    copies = []
    for pair in range(nh // 2):
        halves = []
        for j in range(2):
            h = 2 * pair + j
            local_ref, n = (low_ref, h) if h < nh // 2 else (high_ref, h - nh // 2)
            total = local_ref[n * dk:(n + 1) * dk, :]
            for m in range(count):
                r = h * levels + first + m
                up = ((index >> m) & 1).astype(F32)
                x = nt(ups[m][h * dk:(h + 1) * dk, :], g_ref[:, h * dv:(h + 1) * dv])
                total = total + x * (lw_ref[r:r + 1, :] * up)
            halves.append(total)
        cols = slice(pair * 2 * dk, (pair + 1) * 2 * dk)
        dq_ref[:, cols] = jnp.concatenate(halves, axis=0).astype(BF16).T
        copies.append(leave(dq_ref, dq_hbm, sems.at[pair], cols))
    for copy in copies:
        copy.wait()


def out_kernel(dims, levels, first, count, idx_ref, *refs):
    nh, dk, dv = dims
    ups = refs[:count]
    qt_ref, lw_ref, low_ref, high_ref, out_hbm, out_ref, sems = refs[count:]
    index = idx_ref[0]
    copies = []
    for h in range(nh):
        rows = slice(h * dk, (h + 1) * dk)
        local_ref, n = (low_ref, h) if h < nh // 2 else (high_ref, h - nh // 2)
        total = local_ref[n * dv:(n + 1) * dv, :]
        for m in range(count):
            r = h * levels + first + m
            up = ((index >> m) & 1).astype(F32)
            total = total + tn(ups[m][rows, :], qt_ref[rows, :]) * (lw_ref[r:r + 1, :] * up)
        out_ref[:, h * dv:(h + 1) * dv] = total.astype(BF16).T
        if h % 2:
            copies.append(leave(out_ref, out_hbm, sems.at[h // 2], slice((h - 1) * dv, (h + 1) * dv)))
    for copy in copies:
        copy.wait()


def wgrad_kernel(bits, inner, idx_ref, head_ref, xt_ref, gp_ref, send_ref, keep_ref, sorted_ref):
    count = 1 << bits
    own = gp_ref.shape[0] // count
    for n in range(count):
        away = sum(((n >> k) & 1) << (bits - 1 - k) for k in range(bits))
        at = pl.multiple_of((head_ref[0] ^ away) * own, 16)
        sorted_ref[pl.ds(at, own), :] = gp_ref[n * own:(n + 1) * own, :]
    part_ways(nt(xt_ref[...], sorted_ref[...]), (idx_ref[0] & 1) == 1, send_ref, keep_ref, inner)


def merge_kernel(bit, inner, idx_ref, near_ref, near_got, far_ref, far_got, place_ref, send_ref, keep_ref):
    total = near_ref[...] + near_got[...].astype(F32) + lax.dot_general(
        far_ref[...] + far_got[...].astype(F32), place_ref[...], (((1,), (0,)), ((), ())),
        preferred_element_type=F32, precision=lax.Precision.HIGHEST)
    part_ways(total, ((idx_ref[0] >> bit) & 1) == 1, send_ref, keep_ref, inner)


def join_kernel(top, count, idx_ref, kv_ref, *refs):
    ups = refs[:count]
    gu_ref, send_ref = refs[count:]
    upper = ((idx_ref[0] >> top) & 1) == 1

    @pl.when(upper)
    def _():
        send_ref[...] = gu_ref[top]

    @pl.when(jnp.logical_not(upper))
    def _():
        total = kv_ref[...]
        for up in ups:
            total = total + up[...].astype(F32)
        send_ref[...] = total.astype(BF16)


def pend_kernel(bit, top, idx_ref, *refs):
    gots, (gu_ref, send_ref) = refs[:-2], refs[-2:]
    index = idx_ref[0]
    total = jnp.where(((index >> top) & 1) == 1, 0.0, gots[0][...].astype(F32))
    for got in gots[1:]:
        total = total + got[...].astype(F32)
    send_ref[...] = (total + jnp.where(((index >> bit) & 1) == 1, gu_ref[bit].astype(F32), 0.0)).astype(BF16)


def final_kernel(dims, top, idx_ref, *refs):
    nh, dk, dv = dims
    gots = refs[:top + 1]
    (ds_ref, k_ref, v_ref, low_k, high_k, low_v, high_v, near_ref, far_ref, place_ref, w_ref,
     dx_hbm, dk_hbm, dv_hbm, dx_ref, dk_ref, dv_ref, sems) = refs[top + 1:]
    gp = (near_ref[...].astype(F32) + tn(place_ref[...].astype(BF16), far_ref[...])).astype(BF16)
    dx_ref[...] = lax.dot_general(
        gp, w_ref[...], (((0,), (1,)), ((), ())), preferred_element_type=F32).astype(BF16)
    copies = [leave(dx_ref, dx_hbm, sems.at[nh], slice(0, dx_ref.shape[1]))]
    upper = ((idx_ref[0] >> top) & 1) == 1
    zero = jnp.zeros((dk, dv), BF16)
    for pair in range(nh // 2):
        pair_rows = slice(pair * 2 * dk, (pair + 1) * 2 * dk)
        total = ds_ref[pair_rows, :] + jnp.where(upper, 0.0, gots[0][pair_rows, :].astype(F32))
        for got in gots[1:]:
            total = total + got[pair_rows, :].astype(F32)
        adj = [total[:dk].astype(BF16), total[dk:].astype(BF16)]
        kp = k_ref[:, pair * 2 * dk:(pair + 1) * 2 * dk]
        dkl_ref, dvl_ref, p = (low_k, low_v, pair) if pair < nh // 4 else (high_k, high_v, pair - nh // 4)
        total = dkl_ref[:, p * 2 * dk:(p + 1) * 2 * dk]
        for j in range(2):
            h = 2 * pair + j
            padded = jnp.concatenate([adj[j], zero] if j == 0 else [zero, adj[j]], axis=0)
            cols = slice(h * dv, (h + 1) * dv)
            total = total + nt(v_ref[:, cols], padded)
            near = dvl_ref[:, (2 * p + j) * dv:(2 * p + j + 1) * dv]
            dv_ref[:, cols] = (near + nn(kp, padded)).astype(BF16)
        dk_ref[:, pair * 2 * dk:(pair + 1) * 2 * dk] = total.astype(BF16)
        copies.append(leave(dv_ref, dv_hbm, sems.at[2 * pair], slice(2 * pair * dv, (2 * pair + 2) * dv)))
        copies.append(leave(dk_ref, dk_hbm, sems.at[2 * pair + 1], slice(pair * 2 * dk, (pair + 1) * 2 * dk)))
    for copy in copies:
        copy.wait()


def gather_heads(value, head_bits):
    full = value
    for bit in reversed(range(head_bits)):
        full = jnp.concatenate([full, swap(full, "head", bit)], axis=0)
    return full


def body(hidden, w, queries, keys, values, d_out, d_state):
    tokens, width = hidden.shape
    dims = d_state.shape
    nh, dk, dv = dims
    n_seq, n_head = lax.axis_size("seq"), lax.axis_size("head")
    seq_bits, head_bits = n_seq.bit_length() - 1, n_head.bit_length() - 1
    top = seq_bits - 1
    cols = w.shape[1]
    levels = cols // (nh * n_head)
    own = nh * levels
    far = nh * seq_bits
    far_own = -(-far // 16) * 16
    far_cols = far_own * n_head
    first = tokens.bit_length()
    per = width // n_seq
    rows = nh * dk
    S = jax.ShapeDtypeStruct
    idx, head_idx = [jnp.reshape(lax.axis_index(axis), (1,)) for axis in ("seq", "head")]

    hbm = pl.BlockSpec(memory_space=pltpu.HBM)
    kv, kvb, w_near, x_near = call(
        functools.partial(state_kernel, dims),
        [S((rows, dv), F32), S((rows, dv), BF16), S(w.shape, BF16), S(hidden.shape, BF16)],
        [SM] * 2 + [hbm] * 4, 2 * tokens * rows * dv,
        scratch_shapes=[pltpu.VMEM((tokens, rows), BF16), pltpu.VMEM((tokens, nh * dv), BF16),
                        pltpu.SemaphoreType.DMA((4,))])(
                            idx, head_idx, *[pltpu.with_memory_space_constraint(a, pltpu.HBM) for a in (keys, values, w, hidden)])
    send, keep, xt = call(
        functools.partial(project_kernel, head_bits - 1),
        [S((cols // 2, tokens), BF16), S((cols // 2, tokens), F32), S((width, tokens), BF16)], [SM] + [VM] * 2,
        2 * tokens * width * cols)(head_idx, w_near, x_near)

    total, up = kv, kvb
    ups = []
    for bit in range(top):
        partner = swap(up, "seq", bit)
        ups.append(partner)
        if bit < top - 1:
            total = total + partner.astype(F32)
            up = total.astype(BF16)

    got = swap(send, "head", head_bits - 1)
    for bit in reversed(range(head_bits - 1)):
        n = keep.shape[0] // 2
        send, keep = call(
            functools.partial(fold_kernel, bit, n), [S((n, tokens), BF16), S((n, tokens), F32)],
            [SM] + [VM] * 2, n * tokens)(head_idx, keep, got)
        got = swap(send, "head", bit)

    gl = call(
        functools.partial(level_kernel, dims, levels), [S((own, tokens), F32)], [VM] * 4,
        2 * tokens * tokens * nh * (dk + dv))(keys, queries, values, d_out)[0]
    sig, lw, near, qt, gu = call(
        functools.partial(weight_kernel, dims, levels, first, seq_bits),
        [S((own, tokens), F32), S((own, tokens), F32), S((own, tokens), BF16), S((rows, tokens), BF16),
         S((seq_bits, rows, dv), BF16)],
        [VM] * 5, 2 * tokens * rows * dv * seq_bits)(keep, got, gl, queries, d_out)

    up = call(functools.partial(join_kernel, top, top), [S((rows, dv), BF16)], [SM] + [VM] * (top + 2),
              rows * dv)(idx, kv, *ups, gu)[0]
    partner = swap(up, "seq", top)
    ups.append(partner)
    far_rows = call(
        functools.partial(carry_kernel, dims, levels, first, seq_bits), [S((far_own, tokens), BF16)],
        [SM] + [VM] * (seq_bits + 3), 2 * tokens * rows * dv * seq_bits)(idx, *ups, d_out, qt, sig)[0]
    gots = [partner]
    for bit in reversed(range(top)):
        down = call(functools.partial(pend_kernel, bit, top), [S((rows, dv), BF16)], [SM] + [VM] * (len(gots) + 1),
                    rows * dv)(idx, *gots, gu)[0]
        gots.append(swap(down, "seq", bit))

    def begin(gathered, n_cols):
        send, keep, ordered = call(
            functools.partial(wgrad_kernel, head_bits, per),
            [S((width // 2, n_cols), BF16), S((width // 2, n_cols), F32), S((n_cols, tokens), BF16)],
            [SM] * 2 + [VM] * 2, 2 * tokens * width * n_cols)(idx, head_idx, xt, gathered)
        return keep, swap(send, "seq", 0), ordered

    near_w, near_got, near_all = begin(gather_heads(near, head_bits), cols)
    far_w, far_got, far_all = begin(gather_heads(far_rows, head_bits), far_cols)
    col = jnp.arange(cols, dtype=jnp.int32)[None, :]
    row = jnp.arange(far_cols, dtype=jnp.int32)[:, None]
    within = row % far_own
    at = (row // far_own * nh + within % nh) * levels + first + within // nh
    place = ((at == col) & (within < far)).astype(F32)
    n = width // 4
    send, keep = call(
        functools.partial(merge_kernel, 1, per), [S((n, cols), BF16), S((n, cols), F32)], [SM] + [VM] * 5,
        4 * n * far_cols * cols)(idx, near_w, near_got, far_w, far_got, place)
    got = swap(send, "seq", 1)
    for bit in range(2, seq_bits):
        n = n // 2
        send, keep = call(
            functools.partial(fold_kernel, bit, per), [S((n, cols), BF16), S((n, cols), F32)],
            [SM] + [VM] * 2, n * cols)(idx, keep, got)
        got = swap(send, "seq", bit)
    d_w = keep + got.astype(F32)

    half = nh // 4
    local = []
    for part in range(2):
        local.append(call(
            functools.partial(local_kernel, dims, levels, tuple(range(part * half, (part + 1) * half))),
            [S((nh * dv // 2, tokens), F32), S((rows // 2, tokens), F32), S((tokens, rows // 2), F32),
             S((tokens, nh * dv // 2), F32)],
            [VM] * 5, tokens * tokens * nh * (3 * dk + 3 * dv),
        )(keys, queries, values, d_out, lw))
    out_l, dq_l, dk_l, dv_l = [(local[0][n], local[1][n]) for n in range(4)]

    def leaving(shapes, copies):
        return dict(out_specs=[hbm] * len(shapes),
                    scratch_shapes=[pltpu.VMEM(shape, BF16) for shape in shapes] + [pltpu.SemaphoreType.DMA((copies,))])

    def results(*shapes):
        return [S(shape, BF16) for shape in shapes]

    narrow, broad = (tokens, rows), (tokens, nh * dv)
    d_queries = call(
        functools.partial(query_kernel, dims, levels, first, seq_bits), results(narrow),
        [SM] + [VM] * (seq_bits + 4), 2 * tokens * rows * dv * seq_bits, **leaving([narrow], nh // 2))(
            idx, *ups, d_out, lw, *dq_l)[0]
    out = call(
        functools.partial(out_kernel, dims, levels, first, seq_bits), results(broad),
        [SM] + [VM] * (seq_bits + 4), 2 * tokens * rows * dv * seq_bits, **leaving([broad], nh // 2))(
            idx, *ups, qt, lw, *out_l)[0]
    d_hidden, d_keys, d_values = call(
        functools.partial(final_kernel, dims, top), results((tokens, width), narrow, broad), [SM] + [VM] * (top + 12),
        4 * tokens * rows * dv, **leaving([(tokens, width), narrow, broad], nh + 1))(
            idx, *gots, d_state.reshape(rows, dv), keys, values, *dk_l, *dv_l, near_all, far_all, place, w_near)
    return (out, d_queries, d_keys, d_values, d_hidden, d_w)


def solution(mesh):
    two = P("seq", "head")
    return jax.shard_map(
        body, mesh=mesh,
        in_specs=(two, P("head", None), two, two, two, two, P("head", None, None)),
        out_specs=(two, two, two, two, two, P(("head", "seq"), None)),
        check_vma=False)
```

```python
import functools

import jax
import jax.numpy as jnp
from jax import lax
from jax.experimental import pallas as pl
from jax.experimental.pallas import tpu as pltpu
from jax.sharding import PartitionSpec as P


F32 = jnp.float32
BF16 = jnp.bfloat16
LANES = 128
SUB = 8
VM = pl.BlockSpec(memory_space=pltpu.VMEM)
SM = pl.BlockSpec(memory_space=pltpu.SMEM)


def nn(a, b):
    return lax.dot_general(a, b, (((1,), (0,)), ((), ())), preferred_element_type=F32)


def nt(a, b):
    return lax.dot_general(a, b, (((1,), (1,)), ((), ())), preferred_element_type=F32)


def tn(a, b):
    return lax.dot_general(a, b, (((0,), (0,)), ((), ())), preferred_element_type=F32)


def call(kernel, outs, specs, flops, **kwargs):
    size = sum(o.size * o.dtype.itemsize for o in outs)
    return pl.pallas_call(
        kernel,
        out_shape=outs,
        in_specs=specs,
        compiler_params=pltpu.CompilerParams(vmem_limit_bytes=16 << 20),
        cost_estimate=pl.CostEstimate(flops=flops, bytes_accessed=2 * size, transcendentals=0),
        **kwargs,
    )


def leave(buf_ref, hbm_ref, sem, cols):
    copy = pltpu.make_async_copy(buf_ref.at[:, cols], hbm_ref.at[:, cols], sem)
    copy.start()
    return copy


def exchange(value, axis, mask):
    pairs = [(source, source ^ mask) for source in range(lax.axis_size(axis))]
    return lax.ppermute(value, axis, pairs)


def swap(value, axis, bit):
    return exchange(value, axis, 1 << bit)


def state_kernel(dims, idx_ref, head_ref, k_hbm, v_hbm, w_hbm, x_hbm, kv_ref, kvb_ref, w_ref, x_ref, k_ref, v_ref, sems):
    nh, dk, dv = dims
    copies = [pltpu.make_async_copy(src, dst, sems.at[n]) for n, (src, dst) in enumerate(
        ((k_hbm, k_ref), (v_hbm, v_ref), (w_hbm, w_ref), (x_hbm, x_ref)))]
    for copy in copies:
        copy.start()
    copies[0].wait()
    copies[1].wait()
    for pair in range(nh // 2):
        turned = k_ref[:, pair * 2 * dk:(pair + 1) * 2 * dk].T
        for j in range(2):
            h = 2 * pair + j
            kv = nn(turned[j * dk:(j + 1) * dk], v_ref[:, h * dv:(h + 1) * dv])
            kv_ref[h * dk:(h + 1) * dk, :] = kv
            kvb_ref[h * dk:(h + 1) * dk, :] = kv.astype(BF16)
    copies[2].wait()
    copies[3].wait()


def part_ways(entries, upper, send_ref, keep_ref, inner):
    n = entries.shape[0] // inner
    for e in range(n // 2):
        low = entries[2 * e * inner:(2 * e + 1) * inner]
        high = entries[(2 * e + 1) * inner:(2 * e + 2) * inner]
        out = slice(e * inner, (e + 1) * inner)
        send_ref[out, :] = jnp.where(upper, low, high).astype(BF16)
        keep_ref[out, :] = jnp.where(upper, high, low)


def project_kernel(bit, idx_ref, w_ref, x_ref, send_ref, keep_ref, xt_ref):
    xt = x_ref[...].T
    xt_ref[...] = xt
    upper = ((idx_ref[0] >> bit) & 1) == 1
    part_ways(tn(w_ref[...], xt), upper, send_ref, keep_ref, keep_ref.shape[0])


def fold_kernel(bit, inner, idx_ref, keep_in, got_ref, send_ref, keep_ref):
    upper = ((idx_ref[0] >> bit) & 1) == 1
    part_ways(keep_in[...] + got_ref[...].astype(F32), upper, send_ref, keep_ref, inner)


def weight_kernel(dims, levels, first, count, keep_ref, got_ref, gl_ref, q_ref, g_ref,
                  sig_ref, lw_ref, near_ref, qt_ref, gu_ref):
    nh, dk, dv = dims
    proj = keep_ref[...] + got_ref[...].astype(F32)
    sig = jax.nn.sigmoid(proj)
    sig_ref[...] = sig
    near_ref[...] = (gl_ref[...] * sig).astype(BF16)
    lw_ref[...] = jnp.maximum(proj, 0.0) + jnp.log1p(jnp.exp(-jnp.abs(proj)))
    for pair in range(nh // 2):
        turned = q_ref[:, pair * 2 * dk:(pair + 1) * 2 * dk].T
        qt_ref[pair * 2 * dk:(pair + 1) * 2 * dk, :] = turned
        wide = turned.astype(F32)
        for j in range(2):
            h = 2 * pair + j
            scaled = jnp.concatenate(
                [wide[j * dk:(j + 1) * dk] * lw_ref[h * levels + first + m:h * levels + first + m + 1, :]
                 for m in range(count)], axis=0)
            grad = nn(scaled.astype(BF16), g_ref[:, h * dv:(h + 1) * dv])
            for m in range(count):
                gu_ref[m, h * dk:(h + 1) * dk, :] = grad[m * dk:(m + 1) * dk].astype(BF16)


def spread_half(rows, lane, low, t_low):
    digits = (low ^ t_low)
    near = jnp.where(digits == 0, rows[0], jnp.where(digits < 2, rows[1], jnp.where(digits < 4, rows[2], rows[3])))
    near = jnp.where(low <= t_low, near, 0.0)
    parts = []
    for a in range(LANES // SUB):
        value = None
        for l in reversed(range(4, 8)):
            if (a >> (l - 4)) & 1 == 0:
                end = (((a >> (l - 3)) + 1) << (l - 3)) * SUB
                value = rows[l] if value is None else jnp.where(lane < end, rows[l], value)
        value = near if value is None else jnp.where(lane < (a + 1) * SUB, near, value)
        if a:
            value = jnp.where(lane < a * SUB, 0.0, value)
        parts.append(value)
    return jnp.concatenate(parts, axis=0)


def level_sums(prod, lane, low, t_low):
    count = LANES // SUB
    group = lane // SUB
    cur = [prod[a * SUB:(a + 1) * SUB] for a in range(count)]
    near = jnp.zeros_like(cur[0])
    for a in range(count):
        near = jnp.where(group == a, cur[a], near)
    near = jnp.where(low <= t_low, near, 0.0)
    digits = low ^ t_low
    sums = []
    for l in range(4):
        lo, hi = (0, 1) if l == 0 else (1 << (l - 1), 1 << l)
        sums.append(jnp.where((digits >= lo) & (digits < hi), near, 0.0))
    for l in range(4, 8):
        total = jnp.zeros_like(near)
        for a in range(0, len(cur), 2):
            total = jnp.where((lane >> (l - 1)) == a + 1, cur[a], total)
        sums.append(total)
        cur = [cur[a] + cur[a + 1] for a in range(0, len(cur), 2)]
    return [jnp.sum(s, axis=0, keepdims=True) for s in sums]


def level_kernel(dims, levels, k_ref, q_ref, v_ref, g_ref, gl_ref):
    nh, dk, dv = dims
    lane = lax.broadcasted_iota(jnp.int32, (SUB, LANES), 1)
    low = lax.broadcasted_iota(jnp.int32, (SUB, LANES), 0)
    t_low = lane % SUB
    gl_ref[...] = jnp.zeros_like(gl_ref)
    for pair in range(nh // 2):
        kp = k_ref[:, pair * 2 * dk:(pair + 1) * 2 * dk]
        qt = q_ref[:, pair * 2 * dk:(pair + 1) * 2 * dk].T
        zero = jnp.zeros_like(qt[:dk])
        for j in range(2):
            h = 2 * pair + j
            base = h * levels
            qz = jnp.concatenate([qt[:dk], zero] if j == 0 else [zero, qt[dk:]], axis=0)
            prod = nn(kp, qz) * nt(v_ref[:, h * dv:(h + 1) * dv], g_ref[:, h * dv:(h + 1) * dv])
            for x in range(2):
                part = slice(x * LANES, (x + 1) * LANES)
                sums = level_sums(prod[part, part], lane, low, t_low)
                for l in range(8):
                    gl_ref[base + l:base + l + 1, part] = sums[l]
            gl_ref[base + 8:base + 9, LANES:] = jnp.sum(prod[:LANES, LANES:], axis=0, keepdims=True)


def local_kernel(dims, levels, pairs, k_ref, q_ref, v_ref, g_ref, lw_ref, out_ref, dq_ref, dk_ref, dv_ref):
    _, dk, dv = dims
    lane = lax.broadcasted_iota(jnp.int32, (SUB, LANES), 1)
    low = lax.broadcasted_iota(jnp.int32, (SUB, LANES), 0)
    t_low = lane % SUB
    for n, pair in enumerate(pairs):
        kp = k_ref[:, pair * 2 * dk:(pair + 1) * 2 * dk]
        qp = q_ref[:, pair * 2 * dk:(pair + 1) * 2 * dk]
        kt, qt = kp.T, qp.T
        zero = jnp.zeros_like(qt[:dk])
        wide_lane = lax.broadcasted_iota(jnp.int32, qp.shape, 1)
        dk_sum = None
        for j in range(2):
            h, m = 2 * pair + j, 2 * n + j
            vj = v_ref[:, h * dv:(h + 1) * dv]
            gj = g_ref[:, h * dv:(h + 1) * dv]
            qz = jnp.concatenate([qt[:dk], zero] if j == 0 else [zero, qt[dk:]], axis=0)
            base = h * levels
            cross = lw_ref[base + 8:base + 9, LANES:]
            halves = []
            for x in range(2):
                rows = [jnp.broadcast_to(lw_ref[base + l:base + l + 1, x * LANES:(x + 1) * LANES], (SUB, LANES))
                        for l in range(8)]
                halves.append(spread_half(rows, lane, low, t_low))

            def weigh(full):
                top = jnp.concatenate([full[:LANES, :LANES] * halves[0], full[:LANES, LANES:] * cross], axis=1)
                bottom = full[LANES:, LANES:] * halves[1]
                bottom = jnp.concatenate([jnp.zeros_like(bottom), bottom], axis=1)
                return jnp.concatenate([top, bottom], axis=0).astype(BF16)

            mixed = weigh(nn(kp, qz))
            grad_scores = weigh(nt(vj, gj))
            out_ref[m * dv:(m + 1) * dv, :] = tn(vj, mixed)
            dq_ref[m * dk:(m + 1) * dk, :] = nn(kt[j * dk:(j + 1) * dk], grad_scores)
            dv_ref[:, m * dv:(m + 1) * dv] = nn(mixed, gj)
            mine = (wide_lane < dk) if j == 0 else (wide_lane >= dk)
            term = nn(grad_scores, jnp.where(mine, qp, jnp.zeros_like(qp)))
            dk_sum = term if dk_sum is None else dk_sum + term
        dk_ref[:, n * 2 * dk:(n + 1) * 2 * dk] = dk_sum


def carry_kernel(dims, levels, first, count, idx_ref, *refs):
    nh, dk, dv = dims
    ups = refs[:count]
    g_ref, qt_ref, sig_ref, far_ref = refs[count:]
    index = idx_ref[0]
    far_ref[...] = jnp.zeros_like(far_ref)
    for m in range(count):
        up = ((index >> m) & 1).astype(F32)
        found = []
        for h in range(nh):
            rows = slice(h * dk, (h + 1) * dk)
            r = h * levels + first + m
            x = nt(ups[m][rows, :], g_ref[:, h * dv:(h + 1) * dv])
            row = jnp.sum(x * qt_ref[rows, :].astype(F32), axis=0, keepdims=True)
            found.append(row * (sig_ref[r:r + 1, :] * up))
        far_ref[m * nh:(m + 1) * nh, :] = jnp.concatenate(found, axis=0).astype(BF16)


def put_in_order(bits, head_ref, gp_ref, sorted_ref):
    count = 1 << bits
    own = gp_ref.shape[0] // count
    for n in range(count):
        away = sum(((n >> k) & 1) << (bits - 1 - k) for k in range(bits))
        at = pl.multiple_of((head_ref[0] ^ away) * own, 16)
        sorted_ref[pl.ds(at, own), :] = gp_ref[n * own:(n + 1) * own, :]


def near_wgrad_kernel(bits, inner, idx_ref, head_ref, xt_ref, gp_ref, send_ref, keep_ref, sorted_ref):
    put_in_order(bits, head_ref, gp_ref, sorted_ref)
    part_ways(nt(xt_ref[...], sorted_ref[...]), (idx_ref[0] & 1) == 1, send_ref, keep_ref, inner)


def far_wgrad_kernel(bits, inner, idx_ref, head_ref, xt_ref, gp_ref, keep_ref, one_ref, two_ref, both_ref, sorted_ref):
    put_in_order(bits, head_ref, gp_ref, sorted_ref)
    total = nt(xt_ref[...], sorted_ref[...])
    right, upper = (idx_ref[0] & 1) == 1, ((idx_ref[0] >> 1) & 1) == 1
    for e in range(total.shape[0] // (4 * inner)):
        parts = [total[(4 * e + n) * inner:(4 * e + n + 1) * inner] for n in range(4)]
        kept, sent = jnp.where(right, parts[1], parts[0]), jnp.where(right, parts[0], parts[1])
        kept_up, sent_up = jnp.where(right, parts[3], parts[2]), jnp.where(right, parts[2], parts[3])
        at = slice(e * inner, (e + 1) * inner)
        keep_ref[at, :] = jnp.where(upper, kept_up, kept)
        one_ref[at, :] = jnp.where(upper, sent_up, sent).astype(BF16)
        two_ref[at, :] = jnp.where(upper, kept, kept_up).astype(BF16)
        both_ref[at, :] = jnp.where(upper, sent, sent_up).astype(BF16)


def merge_kernel(bit, inner, idx_ref, near_ref, near_got, far_ref, one_ref, two_ref, both_ref, place_ref,
                 send_ref, keep_ref):
    far = far_ref[...] + one_ref[...].astype(F32) + two_ref[...].astype(F32) + both_ref[...].astype(F32)
    total = near_ref[...] + near_got[...].astype(F32) + lax.dot_general(
        far, place_ref[...], (((1,), (0,)), ((), ())), preferred_element_type=F32, precision=lax.Precision.HIGHEST)
    part_ways(total, ((idx_ref[0] >> bit) & 1) == 1, send_ref, keep_ref, inner)


def join_kernel(top, count, idx_ref, kv_ref, *refs):
    ups = refs[:count]
    gu_ref, send_ref = refs[count:]
    upper = ((idx_ref[0] >> top) & 1) == 1

    @pl.when(upper)
    def _():
        send_ref[...] = gu_ref[top]

    @pl.when(jnp.logical_not(upper))
    def _():
        total = kv_ref[...]
        for up in ups:
            total = total + up[...].astype(F32)
        send_ref[...] = total.astype(BF16)


def pend_kernel(bit, top, idx_ref, *refs):
    gots, (gu_ref, send_ref) = refs[:-2], refs[-2:]
    index = idx_ref[0]
    total = jnp.where(((index >> top) & 1) == 1, 0.0, gots[0][...].astype(F32))
    for got in gots[1:]:
        total = total + got[...].astype(F32)
    send_ref[...] = (total + jnp.where(((index >> bit) & 1) == 1, gu_ref[bit].astype(F32), 0.0)).astype(BF16)


def final_kernel(dims, levels, first, count, idx_ref, *refs):
    nh, dk, dv = dims
    top = count - 1
    ups, gots = refs[:count], refs[count:2 * count]
    (qt_ref, lw_ref, g_ref, ds_ref, k_ref, v_ref, low_o, low_q, low_k, low_v, high_o, high_q, high_k, high_v,
     near_ref, far_ref, place_ref, w_ref, out_hbm, dq_hbm, dx_hbm, dk_hbm, dv_hbm,
     out_ref, dq_ref, dx_ref, dk_ref, dv_ref, sems) = refs[2 * count:]
    index = idx_ref[0]
    copies = []

    def send(buf_ref, hbm_ref, cols):
        copies.append(leave(buf_ref, hbm_ref, sems.at[len(copies)], cols))

    def weights(h, m):
        r = h * levels + first + m
        return lw_ref[r:r + 1, :] * ((index >> m) & 1).astype(F32)

    for h in range(nh):
        rows = slice(h * dk, (h + 1) * dk)
        local_ref, n = (low_o, h) if h < nh // 2 else (high_o, h - nh // 2)
        total = local_ref[n * dv:(n + 1) * dv, :]
        for m in range(count):
            total = total + tn(ups[m][rows, :], qt_ref[rows, :]) * weights(h, m)
        out_ref[:, h * dv:(h + 1) * dv] = total.astype(BF16).T
        if h % 2:
            send(out_ref, out_hbm, slice((h - 1) * dv, (h + 1) * dv))
    for pair in range(nh // 2):
        halves = []
        for j in range(2):
            h = 2 * pair + j
            local_ref, n = (low_q, h) if h < nh // 2 else (high_q, h - nh // 2)
            total = local_ref[n * dk:(n + 1) * dk, :]
            for m in range(count):
                total = total + nt(ups[m][h * dk:(h + 1) * dk, :], g_ref[:, h * dv:(h + 1) * dv]) * weights(h, m)
            halves.append(total)
        cols = slice(pair * 2 * dk, (pair + 1) * 2 * dk)
        dq_ref[:, cols] = jnp.concatenate(halves, axis=0).astype(BF16).T
        send(dq_ref, dq_hbm, cols)
    gp = (near_ref[...].astype(F32) + tn(place_ref[...].astype(BF16), far_ref[...])).astype(BF16)
    dx_ref[...] = lax.dot_general(
        gp, w_ref[...], (((0,), (1,)), ((), ())), preferred_element_type=F32).astype(BF16)
    send(dx_ref, dx_hbm, slice(0, dx_ref.shape[1]))
    upper = ((index >> top) & 1) == 1
    zero = jnp.zeros((dk, dv), BF16)
    for pair in range(nh // 2):
        pair_rows = slice(pair * 2 * dk, (pair + 1) * 2 * dk)
        total = ds_ref[pair_rows, :] + jnp.where(upper, 0.0, gots[0][pair_rows, :].astype(F32))
        for got in gots[1:]:
            total = total + got[pair_rows, :].astype(F32)
        adj = [total[:dk].astype(BF16), total[dk:].astype(BF16)]
        kp = k_ref[:, pair * 2 * dk:(pair + 1) * 2 * dk]
        dkl_ref, dvl_ref, p = (low_k, low_v, pair) if pair < nh // 4 else (high_k, high_v, pair - nh // 4)
        total = dkl_ref[:, p * 2 * dk:(p + 1) * 2 * dk]
        for j in range(2):
            h = 2 * pair + j
            padded = jnp.concatenate([adj[j], zero] if j == 0 else [zero, adj[j]], axis=0)
            cols = slice(h * dv, (h + 1) * dv)
            total = total + nt(v_ref[:, cols], padded)
            near = dvl_ref[:, (2 * p + j) * dv:(2 * p + j + 1) * dv]
            dv_ref[:, cols] = (near + nn(kp, padded)).astype(BF16)
        dk_ref[:, pair * 2 * dk:(pair + 1) * 2 * dk] = total.astype(BF16)
        send(dv_ref, dv_hbm, slice(2 * pair * dv, (2 * pair + 2) * dv))
        send(dk_ref, dk_hbm, slice(pair * 2 * dk, (pair + 1) * 2 * dk))
    for copy in copies:
        copy.wait()


def gather_heads(value, head_bits):
    full = value
    for bit in reversed(range(head_bits)):
        full = jnp.concatenate([full, swap(full, "head", bit)], axis=0)
    return full


def body(hidden, w, queries, keys, values, d_out, d_state):
    tokens, width = hidden.shape
    dims = d_state.shape
    nh, dk, dv = dims
    n_seq, n_head = lax.axis_size("seq"), lax.axis_size("head")
    seq_bits, head_bits = n_seq.bit_length() - 1, n_head.bit_length() - 1
    top = seq_bits - 1
    cols = w.shape[1]
    levels = cols // (nh * n_head)
    own = nh * levels
    far = nh * seq_bits
    far_own = -(-far // 16) * 16
    far_cols = far_own * n_head
    first = tokens.bit_length()
    per = width // n_seq
    rows = nh * dk
    S = jax.ShapeDtypeStruct
    idx, head_idx = [jnp.reshape(lax.axis_index(axis), (1,)) for axis in ("seq", "head")]

    hbm = pl.BlockSpec(memory_space=pltpu.HBM)
    kv, kvb, w_near, x_near = call(
        functools.partial(state_kernel, dims),
        [S((rows, dv), F32), S((rows, dv), BF16), S(w.shape, BF16), S(hidden.shape, BF16)],
        [SM] * 2 + [hbm] * 4, 2 * tokens * rows * dv,
        scratch_shapes=[pltpu.VMEM((tokens, rows), BF16), pltpu.VMEM((tokens, nh * dv), BF16),
                        pltpu.SemaphoreType.DMA((4,))])(
                            idx, head_idx, *[pltpu.with_memory_space_constraint(a, pltpu.HBM) for a in (keys, values, w, hidden)])
    send, keep, xt = call(
        functools.partial(project_kernel, head_bits - 1),
        [S((cols // 2, tokens), BF16), S((cols // 2, tokens), F32), S((width, tokens), BF16)], [SM] + [VM] * 2,
        2 * tokens * width * cols)(head_idx, w_near, x_near)

    total, up = kv, kvb
    ups = []
    for bit in range(top):
        partner = swap(up, "seq", bit)
        ups.append(partner)
        if bit < top - 1:
            total = total + partner.astype(F32)
            up = total.astype(BF16)

    got = swap(send, "head", head_bits - 1)
    for bit in reversed(range(head_bits - 1)):
        n = keep.shape[0] // 2
        send, keep = call(
            functools.partial(fold_kernel, bit, n), [S((n, tokens), BF16), S((n, tokens), F32)],
            [SM] + [VM] * 2, n * tokens)(head_idx, keep, got)
        got = swap(send, "head", bit)

    gl = call(
        functools.partial(level_kernel, dims, levels), [S((own, tokens), F32)], [VM] * 4,
        2 * tokens * tokens * nh * (dk + dv))(keys, queries, values, d_out)[0]
    sig, lw, near, qt, gu = call(
        functools.partial(weight_kernel, dims, levels, first, seq_bits),
        [S((own, tokens), F32), S((own, tokens), F32), S((own, tokens), BF16), S((rows, tokens), BF16),
         S((seq_bits, rows, dv), BF16)],
        [VM] * 5, 2 * tokens * rows * dv * seq_bits)(keep, got, gl, queries, d_out)

    up = call(functools.partial(join_kernel, top, top), [S((rows, dv), BF16)], [SM] + [VM] * (top + 2),
              rows * dv)(idx, kv, *ups, gu)[0]
    partner = swap(up, "seq", top)
    ups.append(partner)
    far_rows = call(
        functools.partial(carry_kernel, dims, levels, first, seq_bits), [S((far_own, tokens), BF16)],
        [SM] + [VM] * (seq_bits + 3), 2 * tokens * rows * dv * seq_bits)(idx, *ups, d_out, qt, sig)[0]
    gots = [partner]
    for bit in reversed(range(top)):
        down = call(functools.partial(pend_kernel, bit, top), [S((rows, dv), BF16)], [SM] + [VM] * (len(gots) + 1),
                    rows * dv)(idx, *gots, gu)[0]
        gots.append(swap(down, "seq", bit))

    near_all = gather_heads(near, head_bits)
    n = width // 2
    send, near_w, near_all = call(
        functools.partial(near_wgrad_kernel, head_bits, per),
        [S((n, cols), BF16), S((n, cols), F32), S((cols, tokens), BF16)],
        [SM] * 2 + [VM] * 2, 2 * tokens * width * cols)(idx, head_idx, xt, near_all)
    got = swap(send, "seq", 0)
    n = n // 2
    send, near_w = call(
        functools.partial(fold_kernel, 1, per), [S((n, cols), BF16), S((n, cols), F32)],
        [SM] + [VM] * 2, n * cols)(idx, near_w, got)
    near_got = swap(send, "seq", 1)

    far_all = gather_heads(far_rows, head_bits)
    far_w, one, two, both, far_all = call(
        functools.partial(far_wgrad_kernel, head_bits, per),
        [S((n, far_cols), F32)] + [S((n, far_cols), BF16)] * 3 + [S((far_cols, tokens), BF16)],
        [SM] * 2 + [VM] * 2, 2 * tokens * width * far_cols)(idx, head_idx, xt, far_all)
    far_gots = [exchange(one, "seq", 1), exchange(two, "seq", 2),
                exchange(both, "seq", 3)]

    col = jnp.arange(cols, dtype=jnp.int32)[None, :]
    row = jnp.arange(far_cols, dtype=jnp.int32)[:, None]
    within = row % far_own
    at = (row // far_own * nh + within % nh) * levels + first + within // nh
    place = ((at == col) & (within < far)).astype(F32)
    n = n // 2
    send, keep = call(
        functools.partial(merge_kernel, 2, per), [S((n, cols), BF16), S((n, cols), F32)], [SM] + [VM] * 7,
        4 * n * far_cols * cols)(idx, near_w, near_got, far_w, *far_gots, place)
    got = swap(send, "seq", 2)
    for bit in range(3, seq_bits):
        n = n // 2
        send, keep = call(
            functools.partial(fold_kernel, bit, per), [S((n, cols), BF16), S((n, cols), F32)],
            [SM] + [VM] * 2, n * cols)(idx, keep, got)
        got = swap(send, "seq", bit)
    d_w = keep + got.astype(F32)

    half = nh // 4
    local = []
    for part in range(2):
        local.append(call(
            functools.partial(local_kernel, dims, levels, tuple(range(part * half, (part + 1) * half))),
            [S((nh * dv // 2, tokens), F32), S((rows // 2, tokens), F32), S((tokens, rows // 2), F32),
             S((tokens, nh * dv // 2), F32)],
            [VM] * 5, tokens * tokens * nh * (3 * dk + 3 * dv),
        )(keys, queries, values, d_out, lw))
    shapes = [(tokens, nh * dv), (tokens, rows), (tokens, width), (tokens, rows), (tokens, nh * dv)]
    out, d_queries, d_hidden, d_keys, d_values = call(
        functools.partial(final_kernel, dims, levels, first, seq_bits), [S(shape, BF16) for shape in shapes],
        [SM] + [VM] * (2 * seq_bits + 18), 8 * tokens * rows * dv * seq_bits, out_specs=[hbm] * len(shapes),
        scratch_shapes=[pltpu.VMEM(shape, BF16) for shape in shapes] + [pltpu.SemaphoreType.DMA((2 * nh + 1,))])(
            idx, *ups, *gots, qt, lw, d_out, d_state.reshape(rows, dv), keys, values, *local[0], *local[1],
            near_all, far_all, place, w_near)
    return (out, d_queries, d_keys, d_values, d_hidden, d_w)


def solution(mesh):
    two = P("seq", "head")
    return jax.shard_map(
        body, mesh=mesh,
        in_specs=(two, P("head", None), two, two, two, two, P("head", None, None)),
        out_specs=(two, two, two, two, two, P(("head", "seq"), None)),
        check_vma=False)
```

```python
import functools

import jax
import jax.numpy as jnp
from jax import lax
from jax.experimental import pallas as pl
from jax.experimental.pallas import tpu as pltpu
from jax.sharding import PartitionSpec as P


F32 = jnp.float32
BF16 = jnp.bfloat16
LANES = 128
SUB = 8
VM = pl.BlockSpec(memory_space=pltpu.VMEM)
SM = pl.BlockSpec(memory_space=pltpu.SMEM)


def nn(a, b):
    return lax.dot_general(a, b, (((1,), (0,)), ((), ())), preferred_element_type=F32)


def nt(a, b):
    return lax.dot_general(a, b, (((1,), (1,)), ((), ())), preferred_element_type=F32)


def tn(a, b):
    return lax.dot_general(a, b, (((0,), (0,)), ((), ())), preferred_element_type=F32)


def call(kernel, outs, specs, flops, **kwargs):
    size = sum(o.size * o.dtype.itemsize for o in outs)
    return pl.pallas_call(
        kernel,
        out_shape=outs,
        in_specs=specs,
        compiler_params=pltpu.CompilerParams(vmem_limit_bytes=16 << 20),
        cost_estimate=pl.CostEstimate(flops=flops, bytes_accessed=2 * size, transcendentals=0),
        **kwargs,
    )


def leave(buf_ref, hbm_ref, sem, cols):
    copy = pltpu.make_async_copy(buf_ref.at[:, cols], hbm_ref.at[:, cols], sem)
    copy.start()
    return copy


def exchange(value, axis, mask):
    pairs = [(source, source ^ mask) for source in range(lax.axis_size(axis))]
    return lax.ppermute(value, axis, pairs)


def swap(value, axis, bit):
    return exchange(value, axis, 1 << bit)


def state_kernel(dims, idx_ref, head_ref, k_hbm, v_hbm, w_hbm, x_hbm, kv_ref, kvb_ref, w_ref, x_ref, k_ref, v_ref, sems):
    nh, dk, dv = dims
    copies = []
    for pair in range(nh // 2):
        for src, dst, n in ((k_hbm, k_ref, 2 * dk), (v_hbm, v_ref, 2 * dv)):
            cols = slice(pair * n, (pair + 1) * n)
            copies.append(pltpu.make_async_copy(src.at[:, cols], dst.at[:, cols], sems.at[len(copies)]))
    copies.append(pltpu.make_async_copy(w_hbm, w_ref, sems.at[nh]))
    copies.append(pltpu.make_async_copy(x_hbm, x_ref, sems.at[nh + 1]))
    for copy in copies:
        copy.start()
    for pair in range(nh // 2):
        copies[2 * pair].wait()
        copies[2 * pair + 1].wait()
        turned = k_ref[:, pair * 2 * dk:(pair + 1) * 2 * dk].T
        for j in range(2):
            h = 2 * pair + j
            kv = nn(turned[j * dk:(j + 1) * dk], v_ref[:, h * dv:(h + 1) * dv])
            kv_ref[h * dk:(h + 1) * dk, :] = kv
            kvb_ref[h * dk:(h + 1) * dk, :] = kv.astype(BF16)
    copies[nh].wait()
    copies[nh + 1].wait()


def part_ways(entries, upper, send_ref, keep_ref, inner):
    n = entries.shape[0] // inner
    for e in range(n // 2):
        low = entries[2 * e * inner:(2 * e + 1) * inner]
        high = entries[(2 * e + 1) * inner:(2 * e + 2) * inner]
        out = slice(e * inner, (e + 1) * inner)
        send_ref[out, :] = jnp.where(upper, low, high).astype(BF16)
        keep_ref[out, :] = jnp.where(upper, high, low)


def project_kernel(bit, idx_ref, w_ref, x_ref, send_ref, keep_ref, xt_ref):
    xt = x_ref[...].T
    xt_ref[...] = xt
    upper = ((idx_ref[0] >> bit) & 1) == 1
    part_ways(tn(w_ref[...], xt), upper, send_ref, keep_ref, keep_ref.shape[0])


def fold_kernel(bit, inner, idx_ref, keep_in, got_ref, send_ref, keep_ref):
    upper = ((idx_ref[0] >> bit) & 1) == 1
    part_ways(keep_in[...] + got_ref[...].astype(F32), upper, send_ref, keep_ref, inner)


def weight_kernel(dims, levels, first, count, keep_ref, got_ref, gl_ref, q_ref, g_ref,
                  sig_ref, lw_ref, near_ref, qt_ref, gu_ref):
    nh, dk, dv = dims
    proj = keep_ref[...] + got_ref[...].astype(F32)
    sig = jax.nn.sigmoid(proj)
    sig_ref[...] = sig
    near_ref[...] = (gl_ref[...] * sig).astype(BF16)
    lw_ref[...] = jnp.maximum(proj, 0.0) + jnp.log1p(jnp.exp(-jnp.abs(proj)))
    for pair in range(nh // 2):
        turned = q_ref[:, pair * 2 * dk:(pair + 1) * 2 * dk].T
        qt_ref[pair * 2 * dk:(pair + 1) * 2 * dk, :] = turned
        wide = turned.astype(F32)
        for j in range(2):
            h = 2 * pair + j
            scaled = jnp.concatenate(
                [wide[j * dk:(j + 1) * dk] * lw_ref[h * levels + first + m:h * levels + first + m + 1, :]
                 for m in range(count)], axis=0)
            grad = nn(scaled.astype(BF16), g_ref[:, h * dv:(h + 1) * dv])
            for m in range(count):
                gu_ref[m, h * dk:(h + 1) * dk, :] = grad[m * dk:(m + 1) * dk].astype(BF16)


def spread_half(rows, lane, low, t_low):
    digits = (low ^ t_low)
    near = jnp.where(digits == 0, rows[0], jnp.where(digits < 2, rows[1], jnp.where(digits < 4, rows[2], rows[3])))
    near = jnp.where(low <= t_low, near, 0.0)
    parts = []
    for a in range(LANES // SUB):
        value = None
        for l in reversed(range(4, 8)):
            if (a >> (l - 4)) & 1 == 0:
                end = (((a >> (l - 3)) + 1) << (l - 3)) * SUB
                value = rows[l] if value is None else jnp.where(lane < end, rows[l], value)
        value = near if value is None else jnp.where(lane < (a + 1) * SUB, near, value)
        if a:
            value = jnp.where(lane < a * SUB, 0.0, value)
        parts.append(value)
    return jnp.concatenate(parts, axis=0)


def level_sums(prod, lane, low, t_low):
    count = LANES // SUB
    group = lane // SUB
    cur = [prod[a * SUB:(a + 1) * SUB] for a in range(count)]
    near = jnp.zeros_like(cur[0])
    for a in range(count):
        near = jnp.where(group == a, cur[a], near)
    near = jnp.where(low <= t_low, near, 0.0)
    digits = low ^ t_low
    sums = []
    for l in range(4):
        lo, hi = (0, 1) if l == 0 else (1 << (l - 1), 1 << l)
        sums.append(jnp.where((digits >= lo) & (digits < hi), near, 0.0))
    for l in range(4, 8):
        total = jnp.zeros_like(near)
        for a in range(0, len(cur), 2):
            total = jnp.where((lane >> (l - 1)) == a + 1, cur[a], total)
        sums.append(total)
        cur = [cur[a] + cur[a + 1] for a in range(0, len(cur), 2)]
    return [jnp.sum(s, axis=0, keepdims=True) for s in sums]


def level_kernel(dims, levels, k_ref, q_ref, v_ref, g_ref, gl_ref):
    nh, dk, dv = dims
    lane = lax.broadcasted_iota(jnp.int32, (SUB, LANES), 1)
    low = lax.broadcasted_iota(jnp.int32, (SUB, LANES), 0)
    t_low = lane % SUB
    gl_ref[...] = jnp.zeros_like(gl_ref)
    for pair in range(nh // 2):
        kp = k_ref[:, pair * 2 * dk:(pair + 1) * 2 * dk]
        qt = q_ref[:, pair * 2 * dk:(pair + 1) * 2 * dk].T
        zero = jnp.zeros_like(qt[:dk])
        for j in range(2):
            h = 2 * pair + j
            base = h * levels
            qz = jnp.concatenate([qt[:dk], zero] if j == 0 else [zero, qt[dk:]], axis=0)
            prod = nn(kp, qz) * nt(v_ref[:, h * dv:(h + 1) * dv], g_ref[:, h * dv:(h + 1) * dv])
            for x in range(2):
                part = slice(x * LANES, (x + 1) * LANES)
                sums = level_sums(prod[part, part], lane, low, t_low)
                for l in range(8):
                    gl_ref[base + l:base + l + 1, part] = sums[l]
            gl_ref[base + 8:base + 9, LANES:] = jnp.sum(prod[:LANES, LANES:], axis=0, keepdims=True)


def local_kernel(dims, levels, pairs, k_ref, q_ref, v_ref, g_ref, lw_ref, out_ref, dq_ref, dk_ref, dv_ref):
    _, dk, dv = dims
    lane = lax.broadcasted_iota(jnp.int32, (SUB, LANES), 1)
    low = lax.broadcasted_iota(jnp.int32, (SUB, LANES), 0)
    t_low = lane % SUB
    for n, pair in enumerate(pairs):
        kp = k_ref[:, pair * 2 * dk:(pair + 1) * 2 * dk]
        qp = q_ref[:, pair * 2 * dk:(pair + 1) * 2 * dk]
        kt, qt = kp.T, qp.T
        zero = jnp.zeros_like(qt[:dk])
        wide_lane = lax.broadcasted_iota(jnp.int32, qp.shape, 1)
        dk_sum = None
        for j in range(2):
            h, m = 2 * pair + j, 2 * n + j
            vj = v_ref[:, h * dv:(h + 1) * dv]
            gj = g_ref[:, h * dv:(h + 1) * dv]
            qz = jnp.concatenate([qt[:dk], zero] if j == 0 else [zero, qt[dk:]], axis=0)
            base = h * levels
            cross = lw_ref[base + 8:base + 9, LANES:]
            halves = []
            for x in range(2):
                rows = [jnp.broadcast_to(lw_ref[base + l:base + l + 1, x * LANES:(x + 1) * LANES], (SUB, LANES))
                        for l in range(8)]
                halves.append(spread_half(rows, lane, low, t_low))

            def weigh(full):
                top = jnp.concatenate([full[:LANES, :LANES] * halves[0], full[:LANES, LANES:] * cross], axis=1)
                bottom = full[LANES:, LANES:] * halves[1]
                bottom = jnp.concatenate([jnp.zeros_like(bottom), bottom], axis=1)
                return jnp.concatenate([top, bottom], axis=0).astype(BF16)

            mixed = weigh(nn(kp, qz))
            grad_scores = weigh(nt(vj, gj))
            out_ref[m * dv:(m + 1) * dv, :] = tn(vj, mixed)
            dq_ref[m * dk:(m + 1) * dk, :] = nn(kt[j * dk:(j + 1) * dk], grad_scores)
            dv_ref[:, m * dv:(m + 1) * dv] = nn(mixed, gj)
            mine = (wide_lane < dk) if j == 0 else (wide_lane >= dk)
            term = nn(grad_scores, jnp.where(mine, qp, jnp.zeros_like(qp)))
            dk_sum = term if dk_sum is None else dk_sum + term
        dk_ref[:, n * 2 * dk:(n + 1) * 2 * dk] = dk_sum


def carry_kernel(dims, levels, first, count, idx_ref, *refs):
    nh, dk, dv = dims
    ups = refs[:count]
    g_ref, qt_ref, sig_ref, far_ref = refs[count:]
    index = idx_ref[0]
    far_ref[...] = jnp.zeros_like(far_ref)
    for m in range(count):
        up = ((index >> m) & 1).astype(F32)
        found = []
        for h in range(nh):
            rows = slice(h * dk, (h + 1) * dk)
            r = h * levels + first + m
            x = nt(ups[m][rows, :], g_ref[:, h * dv:(h + 1) * dv])
            row = jnp.sum(x * qt_ref[rows, :].astype(F32), axis=0, keepdims=True)
            found.append(row * (sig_ref[r:r + 1, :] * up))
        far_ref[m * nh:(m + 1) * nh, :] = jnp.concatenate(found, axis=0).astype(BF16)


def put_in_order(bits, head_ref, gp_ref, sorted_ref):
    count = 1 << bits
    own = gp_ref.shape[0] // count
    for n in range(count):
        away = sum(((n >> k) & 1) << (bits - 1 - k) for k in range(bits))
        at = pl.multiple_of((head_ref[0] ^ away) * own, 16)
        sorted_ref[pl.ds(at, own), :] = gp_ref[n * own:(n + 1) * own, :]


def near_wgrad_kernel(bits, inner, idx_ref, head_ref, xt_ref, gp_ref, send_ref, keep_ref, sorted_ref):
    put_in_order(bits, head_ref, gp_ref, sorted_ref)
    part_ways(nt(xt_ref[...], sorted_ref[...]), (idx_ref[0] & 1) == 1, send_ref, keep_ref, inner)


def far_wgrad_kernel(inner, idx_ref, head_ref, xt_ref, *refs):
    gathered, (keep_ref, one_ref, two_ref, both_ref, sorted_ref) = refs[:-5], refs[-5:]
    for away, gp_ref in enumerate(gathered):
        own = gp_ref.shape[0]
        sorted_ref[pl.ds(pl.multiple_of((head_ref[0] ^ away) * own, 16), own), :] = gp_ref[...]
    total = nt(xt_ref[...], sorted_ref[...])
    right, upper = (idx_ref[0] & 1) == 1, ((idx_ref[0] >> 1) & 1) == 1
    for e in range(total.shape[0] // (4 * inner)):
        parts = [total[(4 * e + n) * inner:(4 * e + n + 1) * inner] for n in range(4)]
        kept, sent = jnp.where(right, parts[1], parts[0]), jnp.where(right, parts[0], parts[1])
        kept_up, sent_up = jnp.where(right, parts[3], parts[2]), jnp.where(right, parts[2], parts[3])
        at = slice(e * inner, (e + 1) * inner)
        keep_ref[at, :] = jnp.where(upper, kept_up, kept)
        one_ref[at, :] = jnp.where(upper, sent_up, sent).astype(BF16)
        two_ref[at, :] = jnp.where(upper, kept, kept_up).astype(BF16)
        both_ref[at, :] = jnp.where(upper, sent, sent_up).astype(BF16)


def merge_kernel(bit, inner, idx_ref, near_ref, near_got, far_ref, one_ref, two_ref, both_ref, place_ref,
                 send_ref, keep_ref):
    far = far_ref[...] + one_ref[...].astype(F32) + two_ref[...].astype(F32) + both_ref[...].astype(F32)
    n, width = near_ref.shape
    below = near_got.shape[0] - n * (width // LANES)
    got = jnp.concatenate([near_got[below + c * n:below + (c + 1) * n, :] for c in range(width // LANES)], axis=1)
    total = near_ref[...] + got.astype(F32) + lax.dot_general(
        far, place_ref[...], (((1,), (0,)), ((), ())), preferred_element_type=F32, precision=lax.Precision.HIGHEST)
    part_ways(total, ((idx_ref[0] >> bit) & 1) == 1, send_ref, keep_ref, inner)


def join_kernel(top, count, idx_ref, kv_ref, *refs):
    ups = refs[:count]
    gu_ref, send_ref = refs[count:]
    upper = ((idx_ref[0] >> top) & 1) == 1

    @pl.when(upper)
    def _():
        send_ref[...] = gu_ref[top]

    @pl.when(jnp.logical_not(upper))
    def _():
        total = kv_ref[...]
        for up in ups:
            total = total + up[...].astype(F32)
        send_ref[...] = total.astype(BF16)


def pending(bit, top, index, gots, gu_ref):
    rows = gu_ref.shape[1]
    total = jnp.where(((index >> top) & 1) == 1, 0.0, gots[0][...].astype(F32))
    for got in gots[1:]:
        total = total + got[:rows, :].astype(F32)
    return (total + jnp.where(((index >> bit) & 1) == 1, gu_ref[bit].astype(F32), 0.0)).astype(BF16)


def pend_kernel(bit, top, idx_ref, *refs):
    gots, (gu_ref, send_ref) = refs[:-2], refs[-2:]
    send_ref[...] = pending(bit, top, idx_ref[0], gots, gu_ref)


def pack_kernel(bit, top, inner, idx_ref, *refs):
    gots, (gu_ref, keep_in, got_ref, send_ref, keep_ref, part_ref) = refs[:-6], refs[-6:]
    rows = gu_ref.shape[1]
    send_ref[:rows, :] = pending(bit, top, idx_ref[0], gots, gu_ref)
    upper = ((idx_ref[0] >> bit) & 1) == 1
    part_ways(keep_in[...] + got_ref[...].astype(F32), upper, part_ref, keep_ref, inner)
    n = part_ref.shape[0]
    for c in range(part_ref.shape[1] // LANES):
        send_ref[rows + c * n:rows + (c + 1) * n, :] = part_ref[:, c * LANES:(c + 1) * LANES]


def final_kernel(dims, levels, first, count, idx_ref, *refs):
    nh, dk, dv = dims
    top = count - 1
    ups, gots = refs[:count], refs[count:2 * count]
    (qt_ref, lw_ref, g_ref, ds_ref, k_ref, v_ref, low_o, low_q, low_k, low_v, high_o, high_q, high_k, high_v,
     near_ref, far_ref, place_ref, w_ref, out_hbm, dq_hbm, dx_hbm, dk_hbm, dv_hbm,
     out_ref, dq_ref, dx_ref, dk_ref, dv_ref, sems) = refs[2 * count:]
    index = idx_ref[0]
    copies = []

    def send(buf_ref, hbm_ref, cols):
        copies.append(leave(buf_ref, hbm_ref, sems.at[len(copies)], cols))

    def weights(h, m):
        r = h * levels + first + m
        return lw_ref[r:r + 1, :] * ((index >> m) & 1).astype(F32)

    for h in range(nh):
        rows = slice(h * dk, (h + 1) * dk)
        local_ref, n = (low_o, h) if h < nh // 2 else (high_o, h - nh // 2)
        total = local_ref[n * dv:(n + 1) * dv, :]
        for m in range(count):
            total = total + tn(ups[m][rows, :], qt_ref[rows, :]) * weights(h, m)
        out_ref[:, h * dv:(h + 1) * dv] = total.astype(BF16).T
        if h % 2:
            send(out_ref, out_hbm, slice((h - 1) * dv, (h + 1) * dv))
    for pair in range(nh // 2):
        halves = []
        for j in range(2):
            h = 2 * pair + j
            local_ref, n = (low_q, h) if h < nh // 2 else (high_q, h - nh // 2)
            total = local_ref[n * dk:(n + 1) * dk, :]
            for m in range(count):
                total = total + nt(ups[m][h * dk:(h + 1) * dk, :], g_ref[:, h * dv:(h + 1) * dv]) * weights(h, m)
            halves.append(total)
        cols = slice(pair * 2 * dk, (pair + 1) * 2 * dk)
        dq_ref[:, cols] = jnp.concatenate(halves, axis=0).astype(BF16).T
        send(dq_ref, dq_hbm, cols)
    gp = (near_ref[...].astype(F32) + tn(place_ref[...].astype(BF16), far_ref[...])).astype(BF16)
    dx_ref[...] = lax.dot_general(
        gp, w_ref[...], (((0,), (1,)), ((), ())), preferred_element_type=F32).astype(BF16)
    send(dx_ref, dx_hbm, slice(0, dx_ref.shape[1]))
    upper = ((index >> top) & 1) == 1
    zero = jnp.zeros((dk, dv), BF16)
    for pair in range(nh // 2):
        pair_rows = slice(pair * 2 * dk, (pair + 1) * 2 * dk)
        total = ds_ref[pair_rows, :] + jnp.where(upper, 0.0, gots[0][pair_rows, :].astype(F32))
        for got in gots[1:]:
            total = total + got[pair_rows, :].astype(F32)
        adj = [total[:dk].astype(BF16), total[dk:].astype(BF16)]
        kp = k_ref[:, pair * 2 * dk:(pair + 1) * 2 * dk]
        dkl_ref, dvl_ref, p = (low_k, low_v, pair) if pair < nh // 4 else (high_k, high_v, pair - nh // 4)
        total = dkl_ref[:, p * 2 * dk:(p + 1) * 2 * dk]
        for j in range(2):
            h = 2 * pair + j
            padded = jnp.concatenate([adj[j], zero] if j == 0 else [zero, adj[j]], axis=0)
            cols = slice(h * dv, (h + 1) * dv)
            total = total + nt(v_ref[:, cols], padded)
            near = dvl_ref[:, (2 * p + j) * dv:(2 * p + j + 1) * dv]
            dv_ref[:, cols] = (near + nn(kp, padded)).astype(BF16)
        dk_ref[:, pair * 2 * dk:(pair + 1) * 2 * dk] = total.astype(BF16)
        send(dv_ref, dv_hbm, slice(2 * pair * dv, (2 * pair + 2) * dv))
        send(dk_ref, dk_hbm, slice(pair * 2 * dk, (pair + 1) * 2 * dk))
    for copy in copies:
        copy.wait()


def gather_heads(value, head_bits):
    full = value
    for bit in reversed(range(head_bits)):
        full = jnp.concatenate([full, swap(full, "head", bit)], axis=0)
    return full


def body(hidden, w, queries, keys, values, d_out, d_state):
    tokens, width = hidden.shape
    dims = d_state.shape
    nh, dk, dv = dims
    n_seq, n_head = lax.axis_size("seq"), lax.axis_size("head")
    seq_bits, head_bits = n_seq.bit_length() - 1, n_head.bit_length() - 1
    top = seq_bits - 1
    cols = w.shape[1]
    levels = cols // (nh * n_head)
    own = nh * levels
    far = nh * seq_bits
    far_own = -(-far // 16) * 16
    far_cols = far_own * n_head
    first = tokens.bit_length()
    per = width // n_seq
    rows = nh * dk
    S = jax.ShapeDtypeStruct
    idx, head_idx = [jnp.reshape(lax.axis_index(axis), (1,)) for axis in ("seq", "head")]

    hbm = pl.BlockSpec(memory_space=pltpu.HBM)
    kv, kvb, w_near, x_near = call(
        functools.partial(state_kernel, dims),
        [S((rows, dv), F32), S((rows, dv), BF16), S(w.shape, BF16), S(hidden.shape, BF16)],
        [SM] * 2 + [hbm] * 4, 2 * tokens * rows * dv,
        scratch_shapes=[pltpu.VMEM((tokens, rows), BF16), pltpu.VMEM((tokens, nh * dv), BF16),
                        pltpu.SemaphoreType.DMA((nh + 2,))])(
                            idx, head_idx, *[pltpu.with_memory_space_constraint(a, pltpu.HBM) for a in (keys, values, w, hidden)])
    send, keep, xt = call(
        functools.partial(project_kernel, head_bits - 1),
        [S((cols // 2, tokens), BF16), S((cols // 2, tokens), F32), S((width, tokens), BF16)], [SM] + [VM] * 2,
        2 * tokens * width * cols)(head_idx, w_near, x_near)

    total, up = kv, kvb
    ups = []
    for bit in range(top):
        partner = swap(up, "seq", bit)
        ups.append(partner)
        if bit < top - 1:
            total = total + partner.astype(F32)
            up = total.astype(BF16)

    got = swap(send, "head", head_bits - 1)
    for bit in reversed(range(head_bits - 1)):
        n = keep.shape[0] // 2
        send, keep = call(
            functools.partial(fold_kernel, bit, n), [S((n, tokens), BF16), S((n, tokens), F32)],
            [SM] + [VM] * 2, n * tokens)(head_idx, keep, got)
        got = swap(send, "head", bit)

    gl = call(
        functools.partial(level_kernel, dims, levels), [S((own, tokens), F32)], [VM] * 4,
        2 * tokens * tokens * nh * (dk + dv))(keys, queries, values, d_out)[0]
    sig, lw, near, qt, gu = call(
        functools.partial(weight_kernel, dims, levels, first, seq_bits),
        [S((own, tokens), F32), S((own, tokens), F32), S((own, tokens), BF16), S((rows, tokens), BF16),
         S((seq_bits, rows, dv), BF16)],
        [VM] * 5, 2 * tokens * rows * dv * seq_bits)(keep, got, gl, queries, d_out)

    up = call(functools.partial(join_kernel, top, top), [S((rows, dv), BF16)], [SM] + [VM] * (top + 2),
              rows * dv)(idx, kv, *ups, gu)[0]
    partner = swap(up, "seq", top)
    ups.append(partner)
    far_rows = call(
        functools.partial(carry_kernel, dims, levels, first, seq_bits), [S((far_own, tokens), BF16)],
        [SM] + [VM] * (seq_bits + 3), 2 * tokens * rows * dv * seq_bits)(idx, *ups, d_out, qt, sig)[0]
    near_all = gather_heads(near, head_bits)
    n = width // 2
    send, near_w, near_all = call(
        functools.partial(near_wgrad_kernel, head_bits, per),
        [S((n, cols), BF16), S((n, cols), F32), S((cols, tokens), BF16)],
        [SM] * 2 + [VM] * 2, 2 * tokens * width * cols)(idx, head_idx, xt, near_all)
    near_first = swap(send, "seq", 0)
    n = n // 2

    gots = [partner]
    for bit in reversed(range(top)):
        if bit == 1:
            down, near_w = call(
                functools.partial(pack_kernel, bit, top, per),
                [S((rows + n * (cols // LANES), dv), BF16), S((n, cols), F32)], [SM] + [VM] * (len(gots) + 3),
                rows * dv + n * cols, scratch_shapes=[pltpu.VMEM((n, cols), BF16)])(
                    idx, *gots, gu, near_w, near_first)
        else:
            down = call(functools.partial(pend_kernel, bit, top), [S((rows, dv), BF16)], [SM] + [VM] * (len(gots) + 1),
                        rows * dv)(idx, *gots, gu)[0]
        gots.append(swap(down, "seq", bit))
    near_got = gots[top - 1]

    far_all = [far_rows] + [exchange(far_rows, "head", away) for away in range(1, n_head)]
    far_w, one, two, both, far_all = call(
        functools.partial(far_wgrad_kernel, per),
        [S((n, far_cols), F32)] + [S((n, far_cols), BF16)] * 3 + [S((far_cols, tokens), BF16)],
        [SM] * 2 + [VM] * (n_head + 1), 2 * tokens * width * far_cols)(idx, head_idx, xt, *far_all)
    far_gots = [exchange(one, "seq", 1), exchange(two, "seq", 2),
                exchange(both, "seq", 3)]

    col = jnp.arange(cols, dtype=jnp.int32)[None, :]
    row = jnp.arange(far_cols, dtype=jnp.int32)[:, None]
    within = row % far_own
    at = (row // far_own * nh + within % nh) * levels + first + within // nh
    place = ((at == col) & (within < far)).astype(F32)
    n = n // 2
    send, keep = call(
        functools.partial(merge_kernel, 2, per), [S((n, cols), BF16), S((n, cols), F32)], [SM] + [VM] * 7,
        4 * n * far_cols * cols)(idx, near_w, near_got, far_w, *far_gots, place)
    got = swap(send, "seq", 2)
    for bit in range(3, seq_bits):
        n = n // 2
        send, keep = call(
            functools.partial(fold_kernel, bit, per), [S((n, cols), BF16), S((n, cols), F32)],
            [SM] + [VM] * 2, n * cols)(idx, keep, got)
        got = swap(send, "seq", bit)
    d_w = keep + got.astype(F32)

    half = nh // 4
    local = []
    for part in range(2):
        local.append(call(
            functools.partial(local_kernel, dims, levels, tuple(range(part * half, (part + 1) * half))),
            [S((nh * dv // 2, tokens), F32), S((rows // 2, tokens), F32), S((tokens, rows // 2), F32),
             S((tokens, nh * dv // 2), F32)],
            [VM] * 5, tokens * tokens * nh * (3 * dk + 3 * dv),
        )(keys, queries, values, d_out, lw))
    shapes = [(tokens, nh * dv), (tokens, rows), (tokens, width), (tokens, rows), (tokens, nh * dv)]
    out, d_queries, d_hidden, d_keys, d_values = call(
        functools.partial(final_kernel, dims, levels, first, seq_bits), [S(shape, BF16) for shape in shapes],
        [SM] + [VM] * (2 * seq_bits + 18), 8 * tokens * rows * dv * seq_bits, out_specs=[hbm] * len(shapes),
        scratch_shapes=[pltpu.VMEM(shape, BF16) for shape in shapes] + [pltpu.SemaphoreType.DMA((2 * nh + 1,))])(
            idx, *ups, *gots, qt, lw, d_out, d_state.reshape(rows, dv), keys, values, *local[0], *local[1],
            near_all, far_all, place, w_near)
    return (out, d_queries, d_keys, d_values, d_hidden, d_w)


def solution(mesh):
    two = P("seq", "head")
    return jax.shard_map(
        body, mesh=mesh,
        in_specs=(two, P("head", None), two, two, two, two, P("head", None, None)),
        out_specs=(two, two, two, two, two, P(("head", "seq"), None)),
        check_vma=False)
```

```python
import functools

import jax
import jax.numpy as jnp
from jax import lax
from jax.experimental import pallas as pl
from jax.experimental.pallas import tpu as pltpu
from jax.sharding import PartitionSpec as P


F32 = jnp.float32
BF16 = jnp.bfloat16
LANES = 128
SUB = 8
VM = pl.BlockSpec(memory_space=pltpu.VMEM)
SM = pl.BlockSpec(memory_space=pltpu.SMEM)


def nn(a, b):
    return lax.dot_general(a, b, (((1,), (0,)), ((), ())), preferred_element_type=F32)


def nt(a, b):
    return lax.dot_general(a, b, (((1,), (1,)), ((), ())), preferred_element_type=F32)


def tn(a, b):
    return lax.dot_general(a, b, (((0,), (0,)), ((), ())), preferred_element_type=F32)


def call(kernel, outs, specs, flops, **kwargs):
    size = sum(o.size * o.dtype.itemsize for o in outs)
    return pl.pallas_call(
        kernel,
        out_shape=outs,
        in_specs=specs,
        compiler_params=pltpu.CompilerParams(vmem_limit_bytes=16 << 20),
        cost_estimate=pl.CostEstimate(flops=flops, bytes_accessed=2 * size, transcendentals=0),
        **kwargs,
    )


def leave(buf_ref, hbm_ref, sem, cols):
    copy = pltpu.make_async_copy(buf_ref.at[:, cols], hbm_ref.at[:, cols], sem)
    copy.start()
    return copy


def exchange(value, axis, mask):
    pairs = [(source, source ^ mask) for source in range(lax.axis_size(axis))]
    return lax.ppermute(value, axis, pairs)


def swap(value, axis, bit):
    return exchange(value, axis, 1 << bit)


def state_kernel(dims, idx_ref, head_ref, k_hbm, v_hbm, w_hbm, x_hbm, kv_ref, kvb_ref, w_ref, x_ref, k_ref, v_ref, sems):
    nh, dk, dv = dims
    copies = [pltpu.make_async_copy(src, dst, sems.at[n]) for n, (src, dst) in enumerate(
        ((k_hbm, k_ref), (v_hbm, v_ref), (w_hbm, w_ref), (x_hbm, x_ref)))]
    for copy in copies:
        copy.start()
    copies[0].wait()
    copies[1].wait()
    for pair in range(nh // 2):
        turned = k_ref[:, pair * 2 * dk:(pair + 1) * 2 * dk].T
        for j in range(2):
            h = 2 * pair + j
            kv = nn(turned[j * dk:(j + 1) * dk], v_ref[:, h * dv:(h + 1) * dv])
            kv_ref[h * dk:(h + 1) * dk, :] = kv
            kvb_ref[h * dk:(h + 1) * dk, :] = kv.astype(BF16)
    copies[2].wait()
    copies[3].wait()


def part_ways(entries, upper, send_ref, keep_ref, inner):
    n = entries.shape[0] // inner
    for e in range(n // 2):
        low = entries[2 * e * inner:(2 * e + 1) * inner]
        high = entries[(2 * e + 1) * inner:(2 * e + 2) * inner]
        out = slice(e * inner, (e + 1) * inner)
        send_ref[out, :] = jnp.where(upper, low, high).astype(BF16)
        keep_ref[out, :] = jnp.where(upper, high, low)


def project_kernel(bit, idx_ref, w_ref, x_ref, send_ref, keep_ref, xt_ref):
    xt = x_ref[...].T
    xt_ref[...] = xt
    upper = ((idx_ref[0] >> bit) & 1) == 1
    part_ways(tn(w_ref[...], xt), upper, send_ref, keep_ref, keep_ref.shape[0])


def fold_kernel(bit, inner, idx_ref, keep_in, got_ref, send_ref, keep_ref):
    upper = ((idx_ref[0] >> bit) & 1) == 1
    part_ways(keep_in[...] + got_ref[...].astype(F32), upper, send_ref, keep_ref, inner)


def weight_kernel(dims, levels, first, count, keep_ref, got_ref, gl_ref, q_ref, g_ref,
                  sig_ref, lw_ref, near_ref, qt_ref, gu_ref):
    nh, dk, dv = dims
    proj = keep_ref[...] + got_ref[...].astype(F32)
    sig = jax.nn.sigmoid(proj)
    sig_ref[...] = sig
    near_ref[...] = (gl_ref[...] * sig).astype(BF16)
    lw_ref[...] = jnp.maximum(proj, 0.0) + jnp.log1p(jnp.exp(-jnp.abs(proj)))
    for pair in range(nh // 2):
        turned = q_ref[:, pair * 2 * dk:(pair + 1) * 2 * dk].T
        qt_ref[pair * 2 * dk:(pair + 1) * 2 * dk, :] = turned
        wide = turned.astype(F32)
        for j in range(2):
            h = 2 * pair + j
            scaled = jnp.concatenate(
                [wide[j * dk:(j + 1) * dk] * lw_ref[h * levels + first + m:h * levels + first + m + 1, :]
                 for m in range(count)], axis=0)
            grad = nn(scaled.astype(BF16), g_ref[:, h * dv:(h + 1) * dv])
            for m in range(count):
                gu_ref[m, h * dk:(h + 1) * dk, :] = grad[m * dk:(m + 1) * dk].astype(BF16)


def spread_half(rows, lane, low, t_low):
    digits = (low ^ t_low)
    near = jnp.where(digits == 0, rows[0], jnp.where(digits < 2, rows[1], jnp.where(digits < 4, rows[2], rows[3])))
    near = jnp.where(low <= t_low, near, 0.0)
    parts = []
    for a in range(LANES // SUB):
        value = None
        for l in reversed(range(4, 8)):
            if (a >> (l - 4)) & 1 == 0:
                end = (((a >> (l - 3)) + 1) << (l - 3)) * SUB
                value = rows[l] if value is None else jnp.where(lane < end, rows[l], value)
        value = near if value is None else jnp.where(lane < (a + 1) * SUB, near, value)
        if a:
            value = jnp.where(lane < a * SUB, 0.0, value)
        parts.append(value)
    return jnp.concatenate(parts, axis=0)


def level_sums(prod, lane, low, t_low):
    count = LANES // SUB
    group = lane // SUB
    cur = [prod[a * SUB:(a + 1) * SUB] for a in range(count)]
    near = jnp.zeros_like(cur[0])
    for a in range(count):
        near = jnp.where(group == a, cur[a], near)
    near = jnp.where(low <= t_low, near, 0.0)
    digits = low ^ t_low
    sums = []
    for l in range(4):
        lo, hi = (0, 1) if l == 0 else (1 << (l - 1), 1 << l)
        sums.append(jnp.where((digits >= lo) & (digits < hi), near, 0.0))
    for l in range(4, 8):
        total = jnp.zeros_like(near)
        for a in range(0, len(cur), 2):
            total = jnp.where((lane >> (l - 1)) == a + 1, cur[a], total)
        sums.append(total)
        cur = [cur[a] + cur[a + 1] for a in range(0, len(cur), 2)]
    return [jnp.sum(s, axis=0, keepdims=True) for s in sums]


def level_kernel(dims, levels, k_ref, q_ref, v_ref, g_ref, gl_ref):
    nh, dk, dv = dims
    lane = lax.broadcasted_iota(jnp.int32, (SUB, LANES), 1)
    low = lax.broadcasted_iota(jnp.int32, (SUB, LANES), 0)
    t_low = lane % SUB
    gl_ref[...] = jnp.zeros_like(gl_ref)
    for pair in range(nh // 2):
        kp = k_ref[:, pair * 2 * dk:(pair + 1) * 2 * dk]
        qt = q_ref[:, pair * 2 * dk:(pair + 1) * 2 * dk].T
        zero = jnp.zeros_like(qt[:dk])
        for j in range(2):
            h = 2 * pair + j
            base = h * levels
            qz = jnp.concatenate([qt[:dk], zero] if j == 0 else [zero, qt[dk:]], axis=0)
            prod = nn(kp, qz) * nt(v_ref[:, h * dv:(h + 1) * dv], g_ref[:, h * dv:(h + 1) * dv])
            for x in range(2):
                part = slice(x * LANES, (x + 1) * LANES)
                sums = level_sums(prod[part, part], lane, low, t_low)
                for l in range(8):
                    gl_ref[base + l:base + l + 1, part] = sums[l]
            gl_ref[base + 8:base + 9, LANES:] = jnp.sum(prod[:LANES, LANES:], axis=0, keepdims=True)


def local_kernel(dims, levels, pairs, k_ref, q_ref, v_ref, g_ref, lw_ref, out_ref, dq_ref, dk_ref, dv_ref):
    _, dk, dv = dims
    lane = lax.broadcasted_iota(jnp.int32, (SUB, LANES), 1)
    low = lax.broadcasted_iota(jnp.int32, (SUB, LANES), 0)
    t_low = lane % SUB
    for n, pair in enumerate(pairs):
        kp = k_ref[:, pair * 2 * dk:(pair + 1) * 2 * dk]
        qp = q_ref[:, pair * 2 * dk:(pair + 1) * 2 * dk]
        kt, qt = kp.T, qp.T
        zero = jnp.zeros_like(qt[:dk])
        wide_lane = lax.broadcasted_iota(jnp.int32, qp.shape, 1)
        dk_sum = None
        for j in range(2):
            h, m = 2 * pair + j, 2 * n + j
            vj = v_ref[:, h * dv:(h + 1) * dv]
            gj = g_ref[:, h * dv:(h + 1) * dv]
            qz = jnp.concatenate([qt[:dk], zero] if j == 0 else [zero, qt[dk:]], axis=0)
            base = h * levels
            cross = lw_ref[base + 8:base + 9, LANES:]
            halves = []
            for x in range(2):
                rows = [jnp.broadcast_to(lw_ref[base + l:base + l + 1, x * LANES:(x + 1) * LANES], (SUB, LANES))
                        for l in range(8)]
                halves.append(spread_half(rows, lane, low, t_low))

            def weigh(full):
                top = jnp.concatenate([full[:LANES, :LANES] * halves[0], full[:LANES, LANES:] * cross], axis=1)
                bottom = full[LANES:, LANES:] * halves[1]
                bottom = jnp.concatenate([jnp.zeros_like(bottom), bottom], axis=1)
                return jnp.concatenate([top, bottom], axis=0).astype(BF16)

            mixed = weigh(nn(kp, qz))
            grad_scores = weigh(nt(vj, gj))
            out_ref[m * dv:(m + 1) * dv, :] = tn(vj, mixed)
            dq_ref[m * dk:(m + 1) * dk, :] = nn(kt[j * dk:(j + 1) * dk], grad_scores)
            dv_ref[:, m * dv:(m + 1) * dv] = nn(mixed, gj)
            mine = (wide_lane < dk) if j == 0 else (wide_lane >= dk)
            term = nn(grad_scores, jnp.where(mine, qp, jnp.zeros_like(qp)))
            dk_sum = term if dk_sum is None else dk_sum + term
        dk_ref[:, n * 2 * dk:(n + 1) * 2 * dk] = dk_sum


def carry_kernel(dims, levels, first, count, idx_ref, *refs):
    nh, dk, dv = dims
    ups = refs[:count]
    g_ref, qt_ref, sig_ref, far_ref = refs[count:]
    index = idx_ref[0]
    far_ref[...] = jnp.zeros_like(far_ref)
    for m in range(count):
        up = ((index >> m) & 1).astype(F32)
        found = []
        for h in range(nh):
            rows = slice(h * dk, (h + 1) * dk)
            r = h * levels + first + m
            x = nt(ups[m][rows, :], g_ref[:, h * dv:(h + 1) * dv])
            row = jnp.sum(x * qt_ref[rows, :].astype(F32), axis=0, keepdims=True)
            found.append(row * (sig_ref[r:r + 1, :] * up))
        far_ref[m * nh:(m + 1) * nh, :] = jnp.concatenate(found, axis=0).astype(BF16)


def put_in_order(bits, head_ref, gp_ref, sorted_ref):
    count = 1 << bits
    own = gp_ref.shape[0] // count
    for n in range(count):
        away = sum(((n >> k) & 1) << (bits - 1 - k) for k in range(bits))
        at = pl.multiple_of((head_ref[0] ^ away) * own, 16)
        sorted_ref[pl.ds(at, own), :] = gp_ref[n * own:(n + 1) * own, :]


def near_wgrad_kernel(bits, inner, idx_ref, head_ref, xt_ref, gp_ref, send_ref, keep_ref, sorted_ref):
    put_in_order(bits, head_ref, gp_ref, sorted_ref)
    part_ways(nt(xt_ref[...], sorted_ref[...]), (idx_ref[0] & 1) == 1, send_ref, keep_ref, inner)


def far_wgrad_kernel(inner, idx_ref, head_ref, xt_ref, near_in, near_got, *refs):
    gathered, (keep_ref, one_ref, two_ref, both_ref, near_ref, sorted_ref) = refs[:-6], refs[-6:]
    for away, gp_ref in enumerate(gathered):
        own = gp_ref.shape[0]
        sorted_ref[pl.ds(pl.multiple_of((head_ref[0] ^ away) * own, 16), own), :] = gp_ref[...]
    total = nt(xt_ref[...], sorted_ref[...])
    right, upper = (idx_ref[0] & 1) == 1, ((idx_ref[0] >> 1) & 1) == 1
    cols = near_ref.shape[1]
    part_ways(near_in[...] + near_got[...].astype(F32), upper, two_ref.at[:, :cols], near_ref, inner)
    for e in range(total.shape[0] // (4 * inner)):
        parts = [total[(4 * e + n) * inner:(4 * e + n + 1) * inner] for n in range(4)]
        kept, sent = jnp.where(right, parts[1], parts[0]), jnp.where(right, parts[0], parts[1])
        kept_up, sent_up = jnp.where(right, parts[3], parts[2]), jnp.where(right, parts[2], parts[3])
        at = slice(e * inner, (e + 1) * inner)
        keep_ref[at, :] = jnp.where(upper, kept_up, kept)
        one_ref[at, :] = jnp.where(upper, sent_up, sent).astype(BF16)
        two_ref[at, cols:] = jnp.where(upper, kept, kept_up).astype(BF16)
        both_ref[at, :] = jnp.where(upper, sent, sent_up).astype(BF16)


def merge_kernel(bit, inner, idx_ref, near_ref, far_ref, one_ref, two_ref, both_ref, place_ref, send_ref, keep_ref):
    cols = near_ref.shape[1]
    far = far_ref[...] + one_ref[...].astype(F32) + two_ref[:, cols:].astype(F32) + both_ref[...].astype(F32)
    total = near_ref[...] + two_ref[:, :cols].astype(F32) + lax.dot_general(
        far, place_ref[...], (((1,), (0,)), ((), ())), preferred_element_type=F32, precision=lax.Precision.HIGHEST)
    part_ways(total, ((idx_ref[0] >> bit) & 1) == 1, send_ref, keep_ref, inner)


def join_kernel(top, count, idx_ref, kv_ref, *refs):
    ups = refs[:count]
    gu_ref, send_ref = refs[count:]
    upper = ((idx_ref[0] >> top) & 1) == 1

    @pl.when(upper)
    def _():
        send_ref[...] = gu_ref[top]

    @pl.when(jnp.logical_not(upper))
    def _():
        total = kv_ref[...]
        for up in ups:
            total = total + up[...].astype(F32)
        send_ref[...] = total.astype(BF16)


def pend_kernel(bit, top, idx_ref, *refs):
    gots, (gu_ref, send_ref) = refs[:-2], refs[-2:]
    index = idx_ref[0]
    total = jnp.where(((index >> top) & 1) == 1, 0.0, gots[0][...].astype(F32))
    for got in gots[1:]:
        total = total + got[...].astype(F32)
    send_ref[...] = (total + jnp.where(((index >> bit) & 1) == 1, gu_ref[bit].astype(F32), 0.0)).astype(BF16)


def final_kernel(dims, levels, first, count, idx_ref, *refs):
    nh, dk, dv = dims
    top = count - 1
    ups, gots = refs[:count], refs[count:2 * count]
    (qt_ref, lw_ref, g_ref, ds_ref, k_ref, v_ref, low_o, low_q, low_k, low_v, high_o, high_q, high_k, high_v,
     near_ref, far_ref, place_ref, w_ref, out_hbm, dq_hbm, dx_hbm, dk_hbm, dv_hbm,
     out_ref, dq_ref, dx_ref, dk_ref, dv_ref, sems) = refs[2 * count:]
    index = idx_ref[0]
    copies = []

    def send(buf_ref, hbm_ref, cols):
        copies.append(leave(buf_ref, hbm_ref, sems.at[len(copies)], cols))

    def weights(h, m):
        r = h * levels + first + m
        return lw_ref[r:r + 1, :] * ((index >> m) & 1).astype(F32)

    for h in range(nh):
        rows = slice(h * dk, (h + 1) * dk)
        local_ref, n = (low_o, h) if h < nh // 2 else (high_o, h - nh // 2)
        total = local_ref[n * dv:(n + 1) * dv, :]
        for m in range(count):
            total = total + tn(ups[m][rows, :], qt_ref[rows, :]) * weights(h, m)
        out_ref[:, h * dv:(h + 1) * dv] = total.astype(BF16).T
        if h % 2:
            send(out_ref, out_hbm, slice((h - 1) * dv, (h + 1) * dv))
    for pair in range(nh // 2):
        halves = []
        for j in range(2):
            h = 2 * pair + j
            local_ref, n = (low_q, h) if h < nh // 2 else (high_q, h - nh // 2)
            total = local_ref[n * dk:(n + 1) * dk, :]
            for m in range(count):
                total = total + nt(ups[m][h * dk:(h + 1) * dk, :], g_ref[:, h * dv:(h + 1) * dv]) * weights(h, m)
            halves.append(total)
        cols = slice(pair * 2 * dk, (pair + 1) * 2 * dk)
        dq_ref[:, cols] = jnp.concatenate(halves, axis=0).astype(BF16).T
        send(dq_ref, dq_hbm, cols)
    gp = (near_ref[...].astype(F32) + tn(place_ref[...].astype(BF16), far_ref[...])).astype(BF16)
    dx_ref[...] = lax.dot_general(
        gp, w_ref[...], (((0,), (1,)), ((), ())), preferred_element_type=F32).astype(BF16)
    send(dx_ref, dx_hbm, slice(0, dx_ref.shape[1]))
    upper = ((index >> top) & 1) == 1
    zero = jnp.zeros((dk, dv), BF16)
    for pair in range(nh // 2):
        pair_rows = slice(pair * 2 * dk, (pair + 1) * 2 * dk)
        total = ds_ref[pair_rows, :] + jnp.where(upper, 0.0, gots[0][pair_rows, :].astype(F32))
        for got in gots[1:]:
            total = total + got[pair_rows, :].astype(F32)
        adj = [total[:dk].astype(BF16), total[dk:].astype(BF16)]
        kp = k_ref[:, pair * 2 * dk:(pair + 1) * 2 * dk]
        dkl_ref, dvl_ref, p = (low_k, low_v, pair) if pair < nh // 4 else (high_k, high_v, pair - nh // 4)
        total = dkl_ref[:, p * 2 * dk:(p + 1) * 2 * dk]
        for j in range(2):
            h = 2 * pair + j
            padded = jnp.concatenate([adj[j], zero] if j == 0 else [zero, adj[j]], axis=0)
            cols = slice(h * dv, (h + 1) * dv)
            total = total + nt(v_ref[:, cols], padded)
            near = dvl_ref[:, (2 * p + j) * dv:(2 * p + j + 1) * dv]
            dv_ref[:, cols] = (near + nn(kp, padded)).astype(BF16)
        dk_ref[:, pair * 2 * dk:(pair + 1) * 2 * dk] = total.astype(BF16)
        send(dv_ref, dv_hbm, slice(2 * pair * dv, (2 * pair + 2) * dv))
        send(dk_ref, dk_hbm, slice(pair * 2 * dk, (pair + 1) * 2 * dk))
    for copy in copies:
        copy.wait()


def gather_heads(value, head_bits):
    full = value
    for bit in reversed(range(head_bits)):
        full = jnp.concatenate([full, swap(full, "head", bit)], axis=0)
    return full


def body(hidden, w, queries, keys, values, d_out, d_state):
    tokens, width = hidden.shape
    dims = d_state.shape
    nh, dk, dv = dims
    n_seq, n_head = lax.axis_size("seq"), lax.axis_size("head")
    seq_bits, head_bits = n_seq.bit_length() - 1, n_head.bit_length() - 1
    top = seq_bits - 1
    cols = w.shape[1]
    levels = cols // (nh * n_head)
    own = nh * levels
    far = nh * seq_bits
    far_own = -(-far // 16) * 16
    far_cols = far_own * n_head
    first = tokens.bit_length()
    per = width // n_seq
    rows = nh * dk
    S = jax.ShapeDtypeStruct
    idx, head_idx = [jnp.reshape(lax.axis_index(axis), (1,)) for axis in ("seq", "head")]

    hbm = pl.BlockSpec(memory_space=pltpu.HBM)
    kv, kvb, w_near, x_near = call(
        functools.partial(state_kernel, dims),
        [S((rows, dv), F32), S((rows, dv), BF16), S(w.shape, BF16), S(hidden.shape, BF16)],
        [SM] * 2 + [hbm] * 4, 2 * tokens * rows * dv,
        scratch_shapes=[pltpu.VMEM((tokens, rows), BF16), pltpu.VMEM((tokens, nh * dv), BF16),
                        pltpu.SemaphoreType.DMA((4,))])(
                            idx, head_idx, *[pltpu.with_memory_space_constraint(a, pltpu.HBM) for a in (keys, values, w, hidden)])
    send, keep, xt = call(
        functools.partial(project_kernel, head_bits - 1),
        [S((cols // 2, tokens), BF16), S((cols // 2, tokens), F32), S((width, tokens), BF16)], [SM] + [VM] * 2,
        2 * tokens * width * cols)(head_idx, w_near, x_near)

    total, up = kv, kvb
    ups = []
    for bit in range(top):
        partner = swap(up, "seq", bit)
        ups.append(partner)
        if bit < top - 1:
            total = total + partner.astype(F32)
            up = total.astype(BF16)

    got = swap(send, "head", head_bits - 1)
    for bit in reversed(range(head_bits - 1)):
        n = keep.shape[0] // 2
        send, keep = call(
            functools.partial(fold_kernel, bit, n), [S((n, tokens), BF16), S((n, tokens), F32)],
            [SM] + [VM] * 2, n * tokens)(head_idx, keep, got)
        got = swap(send, "head", bit)

    gl = call(
        functools.partial(level_kernel, dims, levels), [S((own, tokens), F32)], [VM] * 4,
        2 * tokens * tokens * nh * (dk + dv))(keys, queries, values, d_out)[0]
    sig, lw, near, qt, gu = call(
        functools.partial(weight_kernel, dims, levels, first, seq_bits),
        [S((own, tokens), F32), S((own, tokens), F32), S((own, tokens), BF16), S((rows, tokens), BF16),
         S((seq_bits, rows, dv), BF16)],
        [VM] * 5, 2 * tokens * rows * dv * seq_bits)(keep, got, gl, queries, d_out)

    up = call(functools.partial(join_kernel, top, top), [S((rows, dv), BF16)], [SM] + [VM] * (top + 2),
              rows * dv)(idx, kv, *ups, gu)[0]
    partner = swap(up, "seq", top)
    ups.append(partner)
    far_rows = call(
        functools.partial(carry_kernel, dims, levels, first, seq_bits), [S((far_own, tokens), BF16)],
        [SM] + [VM] * (seq_bits + 3), 2 * tokens * rows * dv * seq_bits)(idx, *ups, d_out, qt, sig)[0]
    gots = [partner]
    for bit in reversed(range(top)):
        down = call(functools.partial(pend_kernel, bit, top), [S((rows, dv), BF16)], [SM] + [VM] * (len(gots) + 1),
                    rows * dv)(idx, *gots, gu)[0]
        gots.append(swap(down, "seq", bit))

    near_all = gather_heads(near, head_bits)
    n = width // 2
    send, near_w, near_all = call(
        functools.partial(near_wgrad_kernel, head_bits, per),
        [S((n, cols), BF16), S((n, cols), F32), S((cols, tokens), BF16)],
        [SM] * 2 + [VM] * 2, 2 * tokens * width * cols)(idx, head_idx, xt, near_all)
    near_got = swap(send, "seq", 0)

    far_all = [far_rows] + [exchange(far_rows, "head", away) for away in range(1, n_head)]
    n = n // 2
    part, joined = S((n, far_cols), BF16), S((n, cols + far_cols), BF16)
    far_w, one, two, both, near_w, far_all = call(
        functools.partial(far_wgrad_kernel, per),
        [S((n, far_cols), F32), part, joined, part, S((n, cols), F32), S((far_cols, tokens), BF16)],
        [SM] * 2 + [VM] * (n_head + 3), 2 * tokens * width * far_cols)(
            idx, head_idx, xt, near_w, near_got, *far_all)
    far_gots = [exchange(one, "seq", 1), exchange(two, "seq", 2),
                exchange(both, "seq", 3)]

    col = jnp.arange(cols, dtype=jnp.int32)[None, :]
    row = jnp.arange(far_cols, dtype=jnp.int32)[:, None]
    within = row % far_own
    at = (row // far_own * nh + within % nh) * levels + first + within // nh
    place = ((at == col) & (within < far)).astype(F32)
    n = n // 2
    send, keep = call(
        functools.partial(merge_kernel, 2, per), [S((n, cols), BF16), S((n, cols), F32)], [SM] + [VM] * 6,
        4 * n * far_cols * cols)(idx, near_w, far_w, *far_gots, place)
    got = swap(send, "seq", 2)
    for bit in range(3, seq_bits):
        n = n // 2
        send, keep = call(
            functools.partial(fold_kernel, bit, per), [S((n, cols), BF16), S((n, cols), F32)],
            [SM] + [VM] * 2, n * cols)(idx, keep, got)
        got = swap(send, "seq", bit)
    d_w = keep + got.astype(F32)

    half = nh // 4
    local = []
    for part in range(2):
        local.append(call(
            functools.partial(local_kernel, dims, levels, tuple(range(part * half, (part + 1) * half))),
            [S((nh * dv // 2, tokens), F32), S((rows // 2, tokens), F32), S((tokens, rows // 2), F32),
             S((tokens, nh * dv // 2), F32)],
            [VM] * 5, tokens * tokens * nh * (3 * dk + 3 * dv),
        )(keys, queries, values, d_out, lw))
    shapes = [(tokens, nh * dv), (tokens, rows), (tokens, width), (tokens, rows), (tokens, nh * dv)]
    out, d_queries, d_hidden, d_keys, d_values = call(
        functools.partial(final_kernel, dims, levels, first, seq_bits), [S(shape, BF16) for shape in shapes],
        [SM] + [VM] * (2 * seq_bits + 18), 8 * tokens * rows * dv * seq_bits, out_specs=[hbm] * len(shapes),
        scratch_shapes=[pltpu.VMEM(shape, BF16) for shape in shapes] + [pltpu.SemaphoreType.DMA((2 * nh + 1,))])(
            idx, *ups, *gots, qt, lw, d_out, d_state.reshape(rows, dv), keys, values, *local[0], *local[1],
            near_all, far_all, place, w_near)
    return (out, d_queries, d_keys, d_values, d_hidden, d_w)


def solution(mesh):
    two = P("seq", "head")
    return jax.shard_map(
        body, mesh=mesh,
        in_specs=(two, P("head", None), two, two, two, two, P("head", None, None)),
        out_specs=(two, two, two, two, two, P(("head", "seq"), None)),
        check_vma=False)
```

```python
import functools

import jax
import jax.numpy as jnp
from jax import lax
from jax.experimental import pallas as pl
from jax.experimental.pallas import tpu as pltpu
from jax.sharding import PartitionSpec as P


F32 = jnp.float32
BF16 = jnp.bfloat16
LANES = 128
SUB = 8
VM = pl.BlockSpec(memory_space=pltpu.VMEM)
SM = pl.BlockSpec(memory_space=pltpu.SMEM)


def nn(a, b):
    return lax.dot_general(a, b, (((1,), (0,)), ((), ())), preferred_element_type=F32)


def nt(a, b):
    return lax.dot_general(a, b, (((1,), (1,)), ((), ())), preferred_element_type=F32)


def tn(a, b):
    return lax.dot_general(a, b, (((0,), (0,)), ((), ())), preferred_element_type=F32)


def call(kernel, outs, specs, flops, **kwargs):
    size = sum(o.size * o.dtype.itemsize for o in outs)
    return pl.pallas_call(
        kernel,
        out_shape=outs,
        in_specs=specs,
        compiler_params=pltpu.CompilerParams(vmem_limit_bytes=16 << 20),
        cost_estimate=pl.CostEstimate(flops=flops, bytes_accessed=2 * size, transcendentals=0),
        **kwargs,
    )


def leave(buf_ref, hbm_ref, sem, cols):
    copy = pltpu.make_async_copy(buf_ref.at[:, cols], hbm_ref.at[:, cols], sem)
    copy.start()
    return copy


def exchange(value, axis, mask):
    pairs = [(source, source ^ mask) for source in range(lax.axis_size(axis))]
    return lax.ppermute(value, axis, pairs)


def swap(value, axis, bit):
    return exchange(value, axis, 1 << bit)


def state_kernel(dims, idx_ref, head_ref, k_hbm, v_hbm, w_hbm, x_hbm, kv_ref, kvb_ref, w_ref, x_ref, k_ref, v_ref, sems):
    nh, dk, dv = dims
    copies = [pltpu.make_async_copy(src, dst, sems.at[n]) for n, (src, dst) in enumerate(
        ((k_hbm, k_ref), (v_hbm, v_ref), (w_hbm, w_ref), (x_hbm, x_ref)))]
    for copy in copies:
        copy.start()
    copies[0].wait()
    copies[1].wait()
    for pair in range(nh // 2):
        turned = k_ref[:, pair * 2 * dk:(pair + 1) * 2 * dk].T
        for j in range(2):
            h = 2 * pair + j
            kv = nn(turned[j * dk:(j + 1) * dk], v_ref[:, h * dv:(h + 1) * dv])
            kv_ref[h * dk:(h + 1) * dk, :] = kv
            kvb_ref[h * dk:(h + 1) * dk, :] = kv.astype(BF16)
    copies[2].wait()
    copies[3].wait()


def part_ways(entries, upper, send_ref, keep_ref, inner):
    n = entries.shape[0] // inner
    for e in range(n // 2):
        low = entries[2 * e * inner:(2 * e + 1) * inner]
        high = entries[(2 * e + 1) * inner:(2 * e + 2) * inner]
        out = slice(e * inner, (e + 1) * inner)
        send_ref[out, :] = jnp.where(upper, low, high).astype(BF16)
        keep_ref[out, :] = jnp.where(upper, high, low)


def project_kernel(bit, idx_ref, w_ref, x_ref, send_ref, keep_ref, xt_ref):
    xt = x_ref[...].T
    xt_ref[...] = xt
    upper = ((idx_ref[0] >> bit) & 1) == 1
    part_ways(tn(w_ref[...], xt), upper, send_ref, keep_ref, keep_ref.shape[0])


def fold_kernel(bit, inner, idx_ref, keep_in, got_ref, send_ref, keep_ref):
    upper = ((idx_ref[0] >> bit) & 1) == 1
    part_ways(keep_in[...] + got_ref[...].astype(F32), upper, send_ref, keep_ref, inner)


def weight_kernel(dims, levels, first, count, keep_ref, got_ref, gl_ref, q_ref, g_ref,
                  sig_ref, lw_ref, near_ref, qt_ref, gu_ref):
    nh, dk, dv = dims
    proj = keep_ref[...] + got_ref[...].astype(F32)
    sig = jax.nn.sigmoid(proj)
    sig_ref[...] = sig
    near_ref[...] = (gl_ref[...] * sig).astype(BF16)
    lw_ref[...] = jnp.maximum(proj, 0.0) + jnp.log1p(jnp.exp(-jnp.abs(proj)))
    for pair in range(nh // 2):
        turned = q_ref[:, pair * 2 * dk:(pair + 1) * 2 * dk].T
        qt_ref[pair * 2 * dk:(pair + 1) * 2 * dk, :] = turned
        wide = turned.astype(F32)
        for j in range(2):
            h = 2 * pair + j
            scaled = jnp.concatenate(
                [wide[j * dk:(j + 1) * dk] * lw_ref[h * levels + first + m:h * levels + first + m + 1, :]
                 for m in range(count)], axis=0)
            grad = nn(scaled.astype(BF16), g_ref[:, h * dv:(h + 1) * dv])
            for m in range(count):
                gu_ref[m, h * dk:(h + 1) * dk, :] = grad[m * dk:(m + 1) * dk].astype(BF16)


def spread_half(rows, lane, low, t_low):
    digits = (low ^ t_low)
    near = jnp.where(digits == 0, rows[0], jnp.where(digits < 2, rows[1], jnp.where(digits < 4, rows[2], rows[3])))
    near = jnp.where(low <= t_low, near, 0.0)
    parts = []
    for a in range(LANES // SUB):
        value = None
        for l in reversed(range(4, 8)):
            if (a >> (l - 4)) & 1 == 0:
                end = (((a >> (l - 3)) + 1) << (l - 3)) * SUB
                value = rows[l] if value is None else jnp.where(lane < end, rows[l], value)
        value = near if value is None else jnp.where(lane < (a + 1) * SUB, near, value)
        if a:
            value = jnp.where(lane < a * SUB, 0.0, value)
        parts.append(value)
    return jnp.concatenate(parts, axis=0)


def level_sums(prod, lane, low, t_low):
    count = LANES // SUB
    group = lane // SUB
    cur = [prod[a * SUB:(a + 1) * SUB] for a in range(count)]
    near = jnp.zeros_like(cur[0])
    for a in range(count):
        near = jnp.where(group == a, cur[a], near)
    near = jnp.where(low <= t_low, near, 0.0)
    digits = low ^ t_low
    sums = []
    for l in range(4):
        lo, hi = (0, 1) if l == 0 else (1 << (l - 1), 1 << l)
        sums.append(jnp.where((digits >= lo) & (digits < hi), near, 0.0))
    for l in range(4, 8):
        total = jnp.zeros_like(near)
        for a in range(0, len(cur), 2):
            total = jnp.where((lane >> (l - 1)) == a + 1, cur[a], total)
        sums.append(total)
        cur = [cur[a] + cur[a + 1] for a in range(0, len(cur), 2)]
    return [jnp.sum(s, axis=0, keepdims=True) for s in sums]


def level_kernel(dims, levels, k_ref, q_ref, v_ref, g_ref, gl_ref):
    nh, dk, dv = dims
    lane = lax.broadcasted_iota(jnp.int32, (SUB, LANES), 1)
    low = lax.broadcasted_iota(jnp.int32, (SUB, LANES), 0)
    t_low = lane % SUB
    gl_ref[...] = jnp.zeros_like(gl_ref)
    for pair in range(nh // 2):
        kp = k_ref[:, pair * 2 * dk:(pair + 1) * 2 * dk]
        qt = q_ref[:, pair * 2 * dk:(pair + 1) * 2 * dk].T
        zero = jnp.zeros_like(qt[:dk])
        for j in range(2):
            h = 2 * pair + j
            base = h * levels
            qz = jnp.concatenate([qt[:dk], zero] if j == 0 else [zero, qt[dk:]], axis=0)
            prod = nn(kp, qz) * nt(v_ref[:, h * dv:(h + 1) * dv], g_ref[:, h * dv:(h + 1) * dv])
            for x in range(2):
                part = slice(x * LANES, (x + 1) * LANES)
                sums = level_sums(prod[part, part], lane, low, t_low)
                for l in range(8):
                    gl_ref[base + l:base + l + 1, part] = sums[l]
            gl_ref[base + 8:base + 9, LANES:] = jnp.sum(prod[:LANES, LANES:], axis=0, keepdims=True)


def local_kernel(dims, levels, pairs, k_ref, q_ref, v_ref, g_ref, lw_ref, out_ref, dq_ref, dk_ref, dv_ref):
    _, dk, dv = dims
    lane = lax.broadcasted_iota(jnp.int32, (SUB, LANES), 1)
    low = lax.broadcasted_iota(jnp.int32, (SUB, LANES), 0)
    t_low = lane % SUB
    for n, pair in enumerate(pairs):
        kp = k_ref[:, pair * 2 * dk:(pair + 1) * 2 * dk]
        qp = q_ref[:, pair * 2 * dk:(pair + 1) * 2 * dk]
        kt, qt = kp.T, qp.T
        zero = jnp.zeros_like(qt[:dk])
        wide_lane = lax.broadcasted_iota(jnp.int32, qp.shape, 1)
        dk_sum = None
        for j in range(2):
            h, m = 2 * pair + j, 2 * n + j
            vj = v_ref[:, h * dv:(h + 1) * dv]
            gj = g_ref[:, h * dv:(h + 1) * dv]
            qz = jnp.concatenate([qt[:dk], zero] if j == 0 else [zero, qt[dk:]], axis=0)
            base = h * levels
            cross = lw_ref[base + 8:base + 9, LANES:]
            halves = []
            for x in range(2):
                rows = [jnp.broadcast_to(lw_ref[base + l:base + l + 1, x * LANES:(x + 1) * LANES], (SUB, LANES))
                        for l in range(8)]
                halves.append(spread_half(rows, lane, low, t_low))

            def weigh(full):
                top = jnp.concatenate([full[:LANES, :LANES] * halves[0], full[:LANES, LANES:] * cross], axis=1)
                bottom = full[LANES:, LANES:] * halves[1]
                bottom = jnp.concatenate([jnp.zeros_like(bottom), bottom], axis=1)
                return jnp.concatenate([top, bottom], axis=0).astype(BF16)

            mixed = weigh(nn(kp, qz))
            grad_scores = weigh(nt(vj, gj))
            out_ref[m * dv:(m + 1) * dv, :] = tn(vj, mixed)
            dq_ref[m * dk:(m + 1) * dk, :] = nn(kt[j * dk:(j + 1) * dk], grad_scores)
            dv_ref[:, m * dv:(m + 1) * dv] = nn(mixed, gj)
            mine = (wide_lane < dk) if j == 0 else (wide_lane >= dk)
            term = nn(grad_scores, jnp.where(mine, qp, jnp.zeros_like(qp)))
            dk_sum = term if dk_sum is None else dk_sum + term
        dk_ref[:, n * 2 * dk:(n + 1) * 2 * dk] = dk_sum


def carry_kernel(dims, levels, first, count, idx_ref, *refs):
    nh, dk, dv = dims
    ups = refs[:count]
    g_ref, qt_ref, sig_ref, far_ref = refs[count:]
    index = idx_ref[0]
    far_ref[...] = jnp.zeros_like(far_ref)
    for m in range(count):
        up = ((index >> m) & 1).astype(F32)
        found = []
        for h in range(nh):
            rows = slice(h * dk, (h + 1) * dk)
            r = h * levels + first + m
            x = nt(ups[m][rows, :], g_ref[:, h * dv:(h + 1) * dv])
            row = jnp.sum(x * qt_ref[rows, :].astype(F32), axis=0, keepdims=True)
            found.append(row * (sig_ref[r:r + 1, :] * up))
        far_ref[m * nh:(m + 1) * nh, :] = jnp.concatenate(found, axis=0).astype(BF16)


def put_in_order(bits, head_ref, gp_ref, sorted_ref):
    count = 1 << bits
    own = gp_ref.shape[0] // count
    for n in range(count):
        away = sum(((n >> k) & 1) << (bits - 1 - k) for k in range(bits))
        at = pl.multiple_of((head_ref[0] ^ away) * own, 16)
        sorted_ref[pl.ds(at, own), :] = gp_ref[n * own:(n + 1) * own, :]


def near_wgrad_kernel(bits, inner, idx_ref, head_ref, xt_ref, gp_ref, send_ref, keep_ref, sorted_ref):
    put_in_order(bits, head_ref, gp_ref, sorted_ref)
    part_ways(nt(xt_ref[...], sorted_ref[...]), (idx_ref[0] & 1) == 1, send_ref, keep_ref, inner)


def far_wgrad_kernel(inner, idx_ref, head_ref, xt_ref, *refs):
    gathered, (keep_ref, one_ref, two_ref, both_ref, sorted_ref) = refs[:-5], refs[-5:]
    for away, gp_ref in enumerate(gathered):
        own = gp_ref.shape[0]
        sorted_ref[pl.ds(pl.multiple_of((head_ref[0] ^ away) * own, 16), own), :] = gp_ref[...]
    total = nt(xt_ref[...], sorted_ref[...])
    right, upper = (idx_ref[0] & 1) == 1, ((idx_ref[0] >> 1) & 1) == 1
    for e in range(total.shape[0] // (4 * inner)):
        parts = [total[(4 * e + n) * inner:(4 * e + n + 1) * inner] for n in range(4)]
        kept, sent = jnp.where(right, parts[1], parts[0]), jnp.where(right, parts[0], parts[1])
        kept_up, sent_up = jnp.where(right, parts[3], parts[2]), jnp.where(right, parts[2], parts[3])
        at = slice(e * inner, (e + 1) * inner)
        keep_ref[at, :] = jnp.where(upper, kept_up, kept)
        one_ref[at, :] = jnp.where(upper, sent_up, sent).astype(BF16)
        two_ref[at, :] = jnp.where(upper, kept, kept_up).astype(BF16)
        both_ref[at, :] = jnp.where(upper, sent, sent_up).astype(BF16)


def merge_kernel(bit, inner, idx_ref, near_ref, near_got, far_ref, one_ref, two_ref, both_ref, place_ref,
                 send_ref, keep_ref):
    far = far_ref[...] + one_ref[...].astype(F32) + two_ref[...].astype(F32) + both_ref[...].astype(F32)
    total = near_ref[...] + near_got[...].astype(F32) + lax.dot_general(
        far, place_ref[...], (((1,), (0,)), ((), ())), preferred_element_type=F32, precision=lax.Precision.HIGHEST)
    part_ways(total, ((idx_ref[0] >> bit) & 1) == 1, send_ref, keep_ref, inner)


def join_kernel(top, count, idx_ref, kv_ref, *refs):
    ups = refs[:count]
    gu_ref, send_ref = refs[count:]
    upper = ((idx_ref[0] >> top) & 1) == 1

    @pl.when(upper)
    def _():
        send_ref[...] = gu_ref[top]

    @pl.when(jnp.logical_not(upper))
    def _():
        total = kv_ref[...]
        for up in ups:
            total = total + up[...].astype(F32)
        send_ref[...] = total.astype(BF16)


def pend_kernel(bit, top, idx_ref, *refs):
    gots, (gu_ref, send_ref) = refs[:-2], refs[-2:]
    index = idx_ref[0]
    total = jnp.where(((index >> top) & 1) == 1, 0.0, gots[0][...].astype(F32))
    for got in gots[1:]:
        total = total + got[...].astype(F32)
    send_ref[...] = (total + jnp.where(((index >> bit) & 1) == 1, gu_ref[bit].astype(F32), 0.0)).astype(BF16)


def final_kernel(dims, levels, first, count, idx_ref, *refs):
    nh, dk, dv = dims
    top = count - 1
    ups, gots = refs[:count], refs[count:2 * count]
    (qt_ref, lw_ref, g_ref, ds_ref, k_ref, v_ref, low_o, low_q, low_k, low_v, high_o, high_q, high_k, high_v,
     near_ref, far_ref, place_ref, w_ref, out_hbm, dq_hbm, dx_hbm, dk_hbm, dv_hbm,
     out_ref, dq_ref, dx_ref, dk_ref, dv_ref, sems) = refs[2 * count:]
    index = idx_ref[0]
    copies = []

    def send(buf_ref, hbm_ref, cols):
        copies.append(leave(buf_ref, hbm_ref, sems.at[len(copies)], cols))

    def weights(h, m):
        r = h * levels + first + m
        return lw_ref[r:r + 1, :] * ((index >> m) & 1).astype(F32)

    for h in range(nh):
        rows = slice(h * dk, (h + 1) * dk)
        local_ref, n = (low_o, h) if h < nh // 2 else (high_o, h - nh // 2)
        total = local_ref[n * dv:(n + 1) * dv, :]
        for m in range(count):
            total = total + tn(ups[m][rows, :], qt_ref[rows, :]) * weights(h, m)
        out_ref[:, h * dv:(h + 1) * dv] = total.astype(BF16).T
        if h % 2:
            send(out_ref, out_hbm, slice((h - 1) * dv, (h + 1) * dv))
    for pair in range(nh // 2):
        halves = []
        for j in range(2):
            h = 2 * pair + j
            local_ref, n = (low_q, h) if h < nh // 2 else (high_q, h - nh // 2)
            total = local_ref[n * dk:(n + 1) * dk, :]
            for m in range(count):
                total = total + nt(ups[m][h * dk:(h + 1) * dk, :], g_ref[:, h * dv:(h + 1) * dv]) * weights(h, m)
            halves.append(total)
        cols = slice(pair * 2 * dk, (pair + 1) * 2 * dk)
        dq_ref[:, cols] = jnp.concatenate(halves, axis=0).astype(BF16).T
        send(dq_ref, dq_hbm, cols)
    gp = (near_ref[...].astype(F32) + tn(place_ref[...].astype(BF16), far_ref[...])).astype(BF16)
    dx_ref[...] = lax.dot_general(
        gp, w_ref[...], (((0,), (1,)), ((), ())), preferred_element_type=F32).astype(BF16)
    send(dx_ref, dx_hbm, slice(0, dx_ref.shape[1]))
    upper = ((index >> top) & 1) == 1
    zero = jnp.zeros((dk, dv), BF16)
    for pair in range(nh // 2):
        pair_rows = slice(pair * 2 * dk, (pair + 1) * 2 * dk)
        total = ds_ref[pair_rows, :] + jnp.where(upper, 0.0, gots[0][pair_rows, :].astype(F32))
        for got in gots[1:]:
            total = total + got[pair_rows, :].astype(F32)
        adj = [total[:dk].astype(BF16), total[dk:].astype(BF16)]
        kp = k_ref[:, pair * 2 * dk:(pair + 1) * 2 * dk]
        dkl_ref, dvl_ref, p = (low_k, low_v, pair) if pair < nh // 4 else (high_k, high_v, pair - nh // 4)
        total = dkl_ref[:, p * 2 * dk:(p + 1) * 2 * dk]
        for j in range(2):
            h = 2 * pair + j
            padded = jnp.concatenate([adj[j], zero] if j == 0 else [zero, adj[j]], axis=0)
            cols = slice(h * dv, (h + 1) * dv)
            total = total + nt(v_ref[:, cols], padded)
            near = dvl_ref[:, (2 * p + j) * dv:(2 * p + j + 1) * dv]
            dv_ref[:, cols] = (near + nn(kp, padded)).astype(BF16)
        dk_ref[:, pair * 2 * dk:(pair + 1) * 2 * dk] = total.astype(BF16)
        send(dv_ref, dv_hbm, slice(2 * pair * dv, (2 * pair + 2) * dv))
        send(dk_ref, dk_hbm, slice(pair * 2 * dk, (pair + 1) * 2 * dk))
    for copy in copies:
        copy.wait()


def gather_heads(value, head_bits):
    full = value
    for bit in reversed(range(head_bits)):
        full = jnp.concatenate([full, swap(full, "head", bit)], axis=0)
    return full


def body(hidden, w, queries, keys, values, d_out, d_state):
    tokens, width = hidden.shape
    dims = d_state.shape
    nh, dk, dv = dims
    n_seq, n_head = lax.axis_size("seq"), lax.axis_size("head")
    seq_bits, head_bits = n_seq.bit_length() - 1, n_head.bit_length() - 1
    top = seq_bits - 1
    cols = w.shape[1]
    levels = cols // (nh * n_head)
    own = nh * levels
    far = nh * seq_bits
    far_own = -(-far // 16) * 16
    far_cols = far_own * n_head
    first = tokens.bit_length()
    per = width // n_seq
    rows = nh * dk
    S = jax.ShapeDtypeStruct
    idx, head_idx = [jnp.reshape(lax.axis_index(axis), (1,)) for axis in ("seq", "head")]

    hbm = pl.BlockSpec(memory_space=pltpu.HBM)
    kv, kvb, w_near, x_near = call(
        functools.partial(state_kernel, dims),
        [S((rows, dv), F32), S((rows, dv), BF16), S(w.shape, BF16), S(hidden.shape, BF16)],
        [SM] * 2 + [hbm] * 4, 2 * tokens * rows * dv,
        scratch_shapes=[pltpu.VMEM((tokens, rows), BF16), pltpu.VMEM((tokens, nh * dv), BF16),
                        pltpu.SemaphoreType.DMA((4,))])(
                            idx, head_idx, *[pltpu.with_memory_space_constraint(a, pltpu.HBM) for a in (keys, values, w, hidden)])
    send, keep, xt = call(
        functools.partial(project_kernel, head_bits - 1),
        [S((cols // 2, tokens), BF16), S((cols // 2, tokens), F32), S((width, tokens), BF16)], [SM] + [VM] * 2,
        2 * tokens * width * cols)(head_idx, w_near, x_near)

    total, up = kv, kvb
    ups = []
    for bit in range(top):
        partner = swap(up, "seq", bit)
        ups.append(partner)
        if bit < top - 1:
            total = total + partner.astype(F32)
            up = total.astype(BF16)

    got = swap(send, "head", head_bits - 1)
    for bit in reversed(range(head_bits - 1)):
        n = keep.shape[0] // 2
        send, keep = call(
            functools.partial(fold_kernel, bit, n), [S((n, tokens), BF16), S((n, tokens), F32)],
            [SM] + [VM] * 2, n * tokens)(head_idx, keep, got)
        got = swap(send, "head", bit)

    gl = call(
        functools.partial(level_kernel, dims, levels), [S((own, tokens), F32)], [VM] * 4,
        2 * tokens * tokens * nh * (dk + dv))(keys, queries, values, d_out)[0]
    sig, lw, near, qt, gu = call(
        functools.partial(weight_kernel, dims, levels, first, seq_bits),
        [S((own, tokens), F32), S((own, tokens), F32), S((own, tokens), BF16), S((rows, tokens), BF16),
         S((seq_bits, rows, dv), BF16)],
        [VM] * 5, 2 * tokens * rows * dv * seq_bits)(keep, got, gl, queries, d_out)

    up = call(functools.partial(join_kernel, top, top), [S((rows, dv), BF16)], [SM] + [VM] * (top + 2),
              rows * dv)(idx, kv, *ups, gu)[0]
    partner = swap(up, "seq", top)
    ups.append(partner)
    far_rows = call(
        functools.partial(carry_kernel, dims, levels, first, seq_bits), [S((far_own, tokens), BF16)],
        [SM] + [VM] * (seq_bits + 3), 2 * tokens * rows * dv * seq_bits)(idx, *ups, d_out, qt, sig)[0]
    gots = [partner]
    for bit in reversed(range(top)):
        down = call(functools.partial(pend_kernel, bit, top), [S((rows, dv), BF16)], [SM] + [VM] * (len(gots) + 1),
                    rows * dv)(idx, *gots, gu)[0]
        gots.append(swap(down, "seq", bit))

    near_all = gather_heads(near, head_bits)
    n = width // 2
    send, near_w, near_all = call(
        functools.partial(near_wgrad_kernel, head_bits, per),
        [S((n, cols), BF16), S((n, cols), F32), S((cols, tokens), BF16)],
        [SM] * 2 + [VM] * 2, 2 * tokens * width * cols)(idx, head_idx, xt, near_all)
    got = swap(send, "seq", 0)
    n = n // 2
    send, near_w = call(
        functools.partial(fold_kernel, 1, per), [S((n, cols), BF16), S((n, cols), F32)],
        [SM] + [VM] * 2, n * cols)(idx, near_w, got)
    near_got = swap(send, "seq", 1)

    far_all = [far_rows] + [exchange(far_rows, "head", away) for away in range(1, n_head)]
    far_w, one, two, both, far_all = call(
        functools.partial(far_wgrad_kernel, per),
        [S((n, far_cols), F32)] + [S((n, far_cols), BF16)] * 3 + [S((far_cols, tokens), BF16)],
        [SM] * 2 + [VM] * (n_head + 1), 2 * tokens * width * far_cols)(idx, head_idx, xt, *far_all)
    far_gots = [exchange(one, "seq", 1), exchange(two, "seq", 2),
                exchange(both, "seq", 3)]

    col = jnp.arange(cols, dtype=jnp.int32)[None, :]
    row = jnp.arange(far_cols, dtype=jnp.int32)[:, None]
    within = row % far_own
    at = (row // far_own * nh + within % nh) * levels + first + within // nh
    place = ((at == col) & (within < far)).astype(F32)
    n = n // 2
    send, keep = call(
        functools.partial(merge_kernel, 2, per), [S((n, cols), BF16), S((n, cols), F32)], [SM] + [VM] * 7,
        4 * n * far_cols * cols)(idx, near_w, near_got, far_w, *far_gots, place)
    got = swap(send, "seq", 2)
    for bit in range(3, seq_bits):
        n = n // 2
        send, keep = call(
            functools.partial(fold_kernel, bit, per), [S((n, cols), BF16), S((n, cols), F32)],
            [SM] + [VM] * 2, n * cols)(idx, keep, got)
        got = swap(send, "seq", bit)
    d_w = keep + got.astype(F32)

    half = nh // 4
    local = []
    for part in range(2):
        local.append(call(
            functools.partial(local_kernel, dims, levels, tuple(range(part * half, (part + 1) * half))),
            [S((nh * dv // 2, tokens), F32), S((rows // 2, tokens), F32), S((tokens, rows // 2), F32),
             S((tokens, nh * dv // 2), F32)],
            [VM] * 5, tokens * tokens * nh * (3 * dk + 3 * dv),
        )(keys, queries, values, d_out, lw))
    shapes = [(tokens, nh * dv), (tokens, rows), (tokens, width), (tokens, rows), (tokens, nh * dv)]
    out, d_queries, d_hidden, d_keys, d_values = call(
        functools.partial(final_kernel, dims, levels, first, seq_bits), [S(shape, BF16) for shape in shapes],
        [SM] + [VM] * (2 * seq_bits + 18), 8 * tokens * rows * dv * seq_bits, out_specs=[hbm] * len(shapes),
        scratch_shapes=[pltpu.VMEM(shape, BF16) for shape in shapes] + [pltpu.SemaphoreType.DMA((2 * nh + 1,))])(
            idx, *ups, *gots, qt, lw, d_out, d_state.reshape(rows, dv), keys, values, *local[0], *local[1],
            near_all, far_all, place, w_near)
    return (out, d_queries, d_keys, d_values, d_hidden, d_w)


def solution(mesh):
    two = P("seq", "head")
    return jax.shard_map(
        body, mesh=mesh,
        in_specs=(two, P("head", None), two, two, two, two, P("head", None, None)),
        out_specs=(two, two, two, two, two, P(("head", "seq"), None)),
        check_vma=False)
```

```python
import functools

import jax
import jax.numpy as jnp
from jax import lax
from jax.experimental import pallas as pl
from jax.experimental.pallas import tpu as pltpu
from jax.sharding import PartitionSpec as P


F32 = jnp.float32
BF16 = jnp.bfloat16
LANES = 128
SUB = 8
VM = pl.BlockSpec(memory_space=pltpu.VMEM)
SM = pl.BlockSpec(memory_space=pltpu.SMEM)


def nn(a, b):
    return lax.dot_general(a, b, (((1,), (0,)), ((), ())), preferred_element_type=F32)


def nt(a, b):
    return lax.dot_general(a, b, (((1,), (1,)), ((), ())), preferred_element_type=F32)


def tn(a, b):
    return lax.dot_general(a, b, (((0,), (0,)), ((), ())), preferred_element_type=F32)


def call(kernel, outs, specs, flops, **kwargs):
    size = sum(o.size * o.dtype.itemsize for o in outs)
    return pl.pallas_call(
        kernel,
        out_shape=outs,
        in_specs=specs,
        compiler_params=pltpu.CompilerParams(vmem_limit_bytes=16 << 20),
        cost_estimate=pl.CostEstimate(flops=flops, bytes_accessed=2 * size, transcendentals=0),
        **kwargs,
    )


def leave(buf_ref, hbm_ref, sem, cols):
    copy = pltpu.make_async_copy(buf_ref.at[:, cols], hbm_ref.at[:, cols], sem)
    copy.start()
    return copy


def exchange(value, axis, mask):
    pairs = [(source, source ^ mask) for source in range(lax.axis_size(axis))]
    return lax.ppermute(value, axis, pairs)


def swap(value, axis, bit):
    return exchange(value, axis, 1 << bit)


def state_kernel(dims, idx_ref, head_ref, k_hbm, v_hbm, w_hbm, x_hbm, kv_ref, kvb_ref, w_ref, x_ref, k_ref, v_ref, sems):
    nh, dk, dv = dims
    copies = [pltpu.make_async_copy(src, dst, sems.at[n]) for n, (src, dst) in enumerate(
        ((k_hbm, k_ref), (v_hbm, v_ref), (w_hbm, w_ref), (x_hbm, x_ref)))]
    for copy in copies:
        copy.start()
    copies[0].wait()
    copies[1].wait()
    for pair in range(nh // 2):
        turned = k_ref[:, pair * 2 * dk:(pair + 1) * 2 * dk].T
        for j in range(2):
            h = 2 * pair + j
            kv = nn(turned[j * dk:(j + 1) * dk], v_ref[:, h * dv:(h + 1) * dv])
            kv_ref[h * dk:(h + 1) * dk, :] = kv
            kvb_ref[h * dk:(h + 1) * dk, :] = kv.astype(BF16)
    copies[2].wait()
    copies[3].wait()


def part_ways(entries, upper, send_ref, keep_ref, inner):
    n = entries.shape[0] // inner
    for e in range(n // 2):
        low = entries[2 * e * inner:(2 * e + 1) * inner]
        high = entries[(2 * e + 1) * inner:(2 * e + 2) * inner]
        out = slice(e * inner, (e + 1) * inner)
        send_ref[out, :] = jnp.where(upper, low, high).astype(BF16)
        keep_ref[out, :] = jnp.where(upper, high, low)


def project_kernel(bit, idx_ref, w_ref, x_ref, send_ref, keep_ref, xt_ref):
    xt = x_ref[...].T
    xt_ref[...] = xt
    upper = ((idx_ref[0] >> bit) & 1) == 1
    part_ways(tn(w_ref[...], xt), upper, send_ref, keep_ref, keep_ref.shape[0])


def fold_kernel(bit, inner, idx_ref, keep_in, *refs):
    gots, (send_ref, keep_ref) = refs[:-2], refs[-2:]
    upper = ((idx_ref[0] >> bit) & 1) == 1
    total = keep_in[...]
    for got in gots:
        total = total + got[...].astype(F32)
    part_ways(total, upper, send_ref, keep_ref, inner)


def weight_kernel(dims, levels, first, count, keep_ref, got_ref, gl_ref, q_ref, g_ref,
                  sig_ref, lw_ref, near_ref, qt_ref, gu_ref):
    nh, dk, dv = dims
    proj = keep_ref[...] + got_ref[...].astype(F32)
    sig = jax.nn.sigmoid(proj)
    sig_ref[...] = sig
    near_ref[...] = (gl_ref[...] * sig).astype(BF16)
    lw_ref[...] = jnp.maximum(proj, 0.0) + jnp.log1p(jnp.exp(-jnp.abs(proj)))
    for pair in range(nh // 2):
        turned = q_ref[:, pair * 2 * dk:(pair + 1) * 2 * dk].T
        qt_ref[pair * 2 * dk:(pair + 1) * 2 * dk, :] = turned
        wide = turned.astype(F32)
        for j in range(2):
            h = 2 * pair + j
            scaled = jnp.concatenate(
                [wide[j * dk:(j + 1) * dk] * lw_ref[h * levels + first + m:h * levels + first + m + 1, :]
                 for m in range(count)], axis=0)
            grad = nn(scaled.astype(BF16), g_ref[:, h * dv:(h + 1) * dv])
            for m in range(count):
                gu_ref[m, h * dk:(h + 1) * dk, :] = grad[m * dk:(m + 1) * dk].astype(BF16)


def spread_half(rows, lane, low, t_low):
    digits = (low ^ t_low)
    near = jnp.where(digits == 0, rows[0], jnp.where(digits < 2, rows[1], jnp.where(digits < 4, rows[2], rows[3])))
    near = jnp.where(low <= t_low, near, 0.0)
    parts = []
    for a in range(LANES // SUB):
        value = None
        for l in reversed(range(4, 8)):
            if (a >> (l - 4)) & 1 == 0:
                end = (((a >> (l - 3)) + 1) << (l - 3)) * SUB
                value = rows[l] if value is None else jnp.where(lane < end, rows[l], value)
        value = near if value is None else jnp.where(lane < (a + 1) * SUB, near, value)
        if a:
            value = jnp.where(lane < a * SUB, 0.0, value)
        parts.append(value)
    return jnp.concatenate(parts, axis=0)


def level_sums(prod, lane, low, t_low):
    count = LANES // SUB
    group = lane // SUB
    cur = [prod[a * SUB:(a + 1) * SUB] for a in range(count)]
    near = jnp.zeros_like(cur[0])
    for a in range(count):
        near = jnp.where(group == a, cur[a], near)
    near = jnp.where(low <= t_low, near, 0.0)
    digits = low ^ t_low
    sums = []
    for l in range(4):
        lo, hi = (0, 1) if l == 0 else (1 << (l - 1), 1 << l)
        sums.append(jnp.where((digits >= lo) & (digits < hi), near, 0.0))
    for l in range(4, 8):
        total = jnp.zeros_like(near)
        for a in range(0, len(cur), 2):
            total = jnp.where((lane >> (l - 1)) == a + 1, cur[a], total)
        sums.append(total)
        cur = [cur[a] + cur[a + 1] for a in range(0, len(cur), 2)]
    return [jnp.sum(s, axis=0, keepdims=True) for s in sums]


def level_kernel(dims, levels, k_ref, q_ref, v_ref, g_ref, gl_ref):
    nh, dk, dv = dims
    lane = lax.broadcasted_iota(jnp.int32, (SUB, LANES), 1)
    low = lax.broadcasted_iota(jnp.int32, (SUB, LANES), 0)
    t_low = lane % SUB
    gl_ref[...] = jnp.zeros_like(gl_ref)
    for pair in range(nh // 2):
        kp = k_ref[:, pair * 2 * dk:(pair + 1) * 2 * dk]
        qt = q_ref[:, pair * 2 * dk:(pair + 1) * 2 * dk].T
        zero = jnp.zeros_like(qt[:dk])
        for j in range(2):
            h = 2 * pair + j
            base = h * levels
            qz = jnp.concatenate([qt[:dk], zero] if j == 0 else [zero, qt[dk:]], axis=0)
            prod = nn(kp, qz) * nt(v_ref[:, h * dv:(h + 1) * dv], g_ref[:, h * dv:(h + 1) * dv])
            for x in range(2):
                part = slice(x * LANES, (x + 1) * LANES)
                sums = level_sums(prod[part, part], lane, low, t_low)
                for l in range(8):
                    gl_ref[base + l:base + l + 1, part] = sums[l]
            gl_ref[base + 8:base + 9, LANES:] = jnp.sum(prod[:LANES, LANES:], axis=0, keepdims=True)


def local_kernel(dims, levels, pairs, k_ref, q_ref, v_ref, g_ref, lw_ref, out_ref, dq_ref, dk_ref, dv_ref):
    _, dk, dv = dims
    lane = lax.broadcasted_iota(jnp.int32, (SUB, LANES), 1)
    low = lax.broadcasted_iota(jnp.int32, (SUB, LANES), 0)
    t_low = lane % SUB
    for n, pair in enumerate(pairs):
        kp = k_ref[:, pair * 2 * dk:(pair + 1) * 2 * dk]
        qp = q_ref[:, pair * 2 * dk:(pair + 1) * 2 * dk]
        kt, qt = kp.T, qp.T
        zero = jnp.zeros_like(qt[:dk])
        wide_lane = lax.broadcasted_iota(jnp.int32, qp.shape, 1)
        dk_sum = None
        for j in range(2):
            h, m = 2 * pair + j, 2 * n + j
            vj = v_ref[:, h * dv:(h + 1) * dv]
            gj = g_ref[:, h * dv:(h + 1) * dv]
            qz = jnp.concatenate([qt[:dk], zero] if j == 0 else [zero, qt[dk:]], axis=0)
            base = h * levels
            cross = lw_ref[base + 8:base + 9, LANES:]
            halves = []
            for x in range(2):
                rows = [jnp.broadcast_to(lw_ref[base + l:base + l + 1, x * LANES:(x + 1) * LANES], (SUB, LANES))
                        for l in range(8)]
                halves.append(spread_half(rows, lane, low, t_low))

            def weigh(full):
                top = jnp.concatenate([full[:LANES, :LANES] * halves[0], full[:LANES, LANES:] * cross], axis=1)
                bottom = full[LANES:, LANES:] * halves[1]
                bottom = jnp.concatenate([jnp.zeros_like(bottom), bottom], axis=1)
                return jnp.concatenate([top, bottom], axis=0).astype(BF16)

            mixed = weigh(nn(kp, qz))
            grad_scores = weigh(nt(vj, gj))
            out_ref[m * dv:(m + 1) * dv, :] = tn(vj, mixed)
            dq_ref[m * dk:(m + 1) * dk, :] = nn(kt[j * dk:(j + 1) * dk], grad_scores)
            dv_ref[:, m * dv:(m + 1) * dv] = nn(mixed, gj)
            mine = (wide_lane < dk) if j == 0 else (wide_lane >= dk)
            term = nn(grad_scores, jnp.where(mine, qp, jnp.zeros_like(qp)))
            dk_sum = term if dk_sum is None else dk_sum + term
        dk_ref[:, n * 2 * dk:(n + 1) * 2 * dk] = dk_sum


def carry_kernel(dims, levels, first, count, idx_ref, *refs):
    nh, dk, dv = dims
    ups = refs[:count]
    g_ref, qt_ref, sig_ref, far_ref = refs[count:]
    index = idx_ref[0]
    far_ref[...] = jnp.zeros_like(far_ref)
    for m in range(count):
        up = ((index >> m) & 1).astype(F32)
        found = []
        for h in range(nh):
            rows = slice(h * dk, (h + 1) * dk)
            r = h * levels + first + m
            x = nt(ups[m][rows, :], g_ref[:, h * dv:(h + 1) * dv])
            row = jnp.sum(x * qt_ref[rows, :].astype(F32), axis=0, keepdims=True)
            found.append(row * (sig_ref[r:r + 1, :] * up))
        far_ref[m * nh:(m + 1) * nh, :] = jnp.concatenate(found, axis=0).astype(BF16)


def wgrad_kernel(bits, inner, idx_ref, head_ref, xt_ref, place_ref, near_ref, *refs):
    gathered, (keep_ref, one_ref, two_ref, both_ref, gp_ref, far_ref) = refs[:-6], refs[-6:]
    own = near_ref.shape[0] >> bits
    for n, rows_ref in enumerate(gathered):
        away = sum(((n >> k) & 1) << (bits - 1 - k) for k in range(bits))
        at = pl.multiple_of((head_ref[0] ^ away) * own, 16)
        gp_ref[pl.ds(at, own), :] = near_ref[n * own:(n + 1) * own, :]
        some = rows_ref.shape[0]
        far_ref[pl.ds(pl.multiple_of((head_ref[0] ^ n) * some, 16), some), :] = rows_ref[...]
    gp = (gp_ref[...].astype(F32) + tn(place_ref[...], far_ref[...])).astype(BF16)
    gp_ref[...] = gp
    total = nt(xt_ref[...], gp)
    right, upper = (idx_ref[0] & 1) == 1, ((idx_ref[0] >> 1) & 1) == 1
    for e in range(total.shape[0] // (4 * inner)):
        parts = [total[(4 * e + n) * inner:(4 * e + n + 1) * inner] for n in range(4)]
        kept, sent = jnp.where(right, parts[1], parts[0]), jnp.where(right, parts[0], parts[1])
        kept_up, sent_up = jnp.where(right, parts[3], parts[2]), jnp.where(right, parts[2], parts[3])
        at = slice(e * inner, (e + 1) * inner)
        keep_ref[at, :] = jnp.where(upper, kept_up, kept)
        one_ref[at, :] = jnp.where(upper, sent_up, sent).astype(BF16)
        two_ref[at, :] = jnp.where(upper, kept, kept_up).astype(BF16)
        both_ref[at, :] = jnp.where(upper, sent, sent_up).astype(BF16)


def join_kernel(top, count, idx_ref, kv_ref, *refs):
    ups = refs[:count]
    gu_ref, send_ref = refs[count:]
    upper = ((idx_ref[0] >> top) & 1) == 1

    @pl.when(upper)
    def _():
        send_ref[...] = gu_ref[top]

    @pl.when(jnp.logical_not(upper))
    def _():
        total = kv_ref[...]
        for up in ups:
            total = total + up[...].astype(F32)
        send_ref[...] = total.astype(BF16)


def pend_kernel(bit, top, idx_ref, *refs):
    gots, (gu_ref, send_ref) = refs[:-2], refs[-2:]
    index = idx_ref[0]
    total = jnp.where(((index >> top) & 1) == 1, 0.0, gots[0][...].astype(F32))
    for got in gots[1:]:
        total = total + got[...].astype(F32)
    send_ref[...] = (total + jnp.where(((index >> bit) & 1) == 1, gu_ref[bit].astype(F32), 0.0)).astype(BF16)


def final_kernel(dims, levels, first, count, idx_ref, *refs):
    nh, dk, dv = dims
    top = count - 1
    ups, gots = refs[:count], refs[count:2 * count]
    (qt_ref, lw_ref, g_ref, ds_ref, k_ref, v_ref, low_o, low_q, low_k, low_v, high_o, high_q, high_k, high_v,
     gp_ref, w_ref, out_hbm, dq_hbm, dx_hbm, dk_hbm, dv_hbm,
     out_ref, dq_ref, dx_ref, dk_ref, dv_ref, sems) = refs[2 * count:]
    index = idx_ref[0]
    copies = []

    def send(buf_ref, hbm_ref, cols):
        copies.append(leave(buf_ref, hbm_ref, sems.at[len(copies)], cols))

    def weights(h, m):
        r = h * levels + first + m
        return lw_ref[r:r + 1, :] * ((index >> m) & 1).astype(F32)

    for h in range(nh):
        rows = slice(h * dk, (h + 1) * dk)
        local_ref, n = (low_o, h) if h < nh // 2 else (high_o, h - nh // 2)
        total = local_ref[n * dv:(n + 1) * dv, :]
        for m in range(count):
            total = total + tn(ups[m][rows, :], qt_ref[rows, :]) * weights(h, m)
        out_ref[:, h * dv:(h + 1) * dv] = total.astype(BF16).T
        if h % 2:
            send(out_ref, out_hbm, slice((h - 1) * dv, (h + 1) * dv))
    for pair in range(nh // 2):
        halves = []
        for j in range(2):
            h = 2 * pair + j
            local_ref, n = (low_q, h) if h < nh // 2 else (high_q, h - nh // 2)
            total = local_ref[n * dk:(n + 1) * dk, :]
            for m in range(count):
                total = total + nt(ups[m][h * dk:(h + 1) * dk, :], g_ref[:, h * dv:(h + 1) * dv]) * weights(h, m)
            halves.append(total)
        cols = slice(pair * 2 * dk, (pair + 1) * 2 * dk)
        dq_ref[:, cols] = jnp.concatenate(halves, axis=0).astype(BF16).T
        send(dq_ref, dq_hbm, cols)
    dx_ref[...] = lax.dot_general(
        gp_ref[...], w_ref[...], (((0,), (1,)), ((), ())), preferred_element_type=F32).astype(BF16)
    send(dx_ref, dx_hbm, slice(0, dx_ref.shape[1]))
    upper = ((index >> top) & 1) == 1
    zero = jnp.zeros((dk, dv), BF16)
    for pair in range(nh // 2):
        pair_rows = slice(pair * 2 * dk, (pair + 1) * 2 * dk)
        total = ds_ref[pair_rows, :] + jnp.where(upper, 0.0, gots[0][pair_rows, :].astype(F32))
        for got in gots[1:]:
            total = total + got[pair_rows, :].astype(F32)
        adj = [total[:dk].astype(BF16), total[dk:].astype(BF16)]
        kp = k_ref[:, pair * 2 * dk:(pair + 1) * 2 * dk]
        dkl_ref, dvl_ref, p = (low_k, low_v, pair) if pair < nh // 4 else (high_k, high_v, pair - nh // 4)
        total = dkl_ref[:, p * 2 * dk:(p + 1) * 2 * dk]
        for j in range(2):
            h = 2 * pair + j
            padded = jnp.concatenate([adj[j], zero] if j == 0 else [zero, adj[j]], axis=0)
            cols = slice(h * dv, (h + 1) * dv)
            total = total + nt(v_ref[:, cols], padded)
            near = dvl_ref[:, (2 * p + j) * dv:(2 * p + j + 1) * dv]
            dv_ref[:, cols] = (near + nn(kp, padded)).astype(BF16)
        dk_ref[:, pair * 2 * dk:(pair + 1) * 2 * dk] = total.astype(BF16)
        send(dv_ref, dv_hbm, slice(2 * pair * dv, (2 * pair + 2) * dv))
        send(dk_ref, dk_hbm, slice(pair * 2 * dk, (pair + 1) * 2 * dk))
    for copy in copies:
        copy.wait()


def gather_heads(value, head_bits):
    full = value
    for bit in reversed(range(head_bits)):
        full = jnp.concatenate([full, swap(full, "head", bit)], axis=0)
    return full


def body(hidden, w, queries, keys, values, d_out, d_state):
    tokens, width = hidden.shape
    dims = d_state.shape
    nh, dk, dv = dims
    n_seq, n_head = lax.axis_size("seq"), lax.axis_size("head")
    seq_bits, head_bits = n_seq.bit_length() - 1, n_head.bit_length() - 1
    top = seq_bits - 1
    cols = w.shape[1]
    levels = cols // (nh * n_head)
    own = nh * levels
    far = nh * seq_bits
    far_own = -(-far // 16) * 16
    far_cols = far_own * n_head
    first = tokens.bit_length()
    per = width // n_seq
    rows = nh * dk
    S = jax.ShapeDtypeStruct
    idx, head_idx = [jnp.reshape(lax.axis_index(axis), (1,)) for axis in ("seq", "head")]

    hbm = pl.BlockSpec(memory_space=pltpu.HBM)
    kv, kvb, w_near, x_near = call(
        functools.partial(state_kernel, dims),
        [S((rows, dv), F32), S((rows, dv), BF16), S(w.shape, BF16), S(hidden.shape, BF16)],
        [SM] * 2 + [hbm] * 4, 2 * tokens * rows * dv,
        scratch_shapes=[pltpu.VMEM((tokens, rows), BF16), pltpu.VMEM((tokens, nh * dv), BF16),
                        pltpu.SemaphoreType.DMA((4,))])(
                            idx, head_idx, *[pltpu.with_memory_space_constraint(a, pltpu.HBM) for a in (keys, values, w, hidden)])
    send, keep, xt = call(
        functools.partial(project_kernel, head_bits - 1),
        [S((cols // 2, tokens), BF16), S((cols // 2, tokens), F32), S((width, tokens), BF16)], [SM] + [VM] * 2,
        2 * tokens * width * cols)(head_idx, w_near, x_near)

    total, up = kv, kvb
    ups = []
    for bit in range(top):
        partner = swap(up, "seq", bit)
        ups.append(partner)
        if bit < top - 1:
            total = total + partner.astype(F32)
            up = total.astype(BF16)

    got = swap(send, "head", head_bits - 1)
    for bit in reversed(range(head_bits - 1)):
        n = keep.shape[0] // 2
        send, keep = call(
            functools.partial(fold_kernel, bit, n), [S((n, tokens), BF16), S((n, tokens), F32)],
            [SM] + [VM] * 2, n * tokens)(head_idx, keep, got)
        got = swap(send, "head", bit)

    gl = call(
        functools.partial(level_kernel, dims, levels), [S((own, tokens), F32)], [VM] * 4,
        2 * tokens * tokens * nh * (dk + dv))(keys, queries, values, d_out)[0]
    sig, lw, near, qt, gu = call(
        functools.partial(weight_kernel, dims, levels, first, seq_bits),
        [S((own, tokens), F32), S((own, tokens), F32), S((own, tokens), BF16), S((rows, tokens), BF16),
         S((seq_bits, rows, dv), BF16)],
        [VM] * 5, 2 * tokens * rows * dv * seq_bits)(keep, got, gl, queries, d_out)

    up = call(functools.partial(join_kernel, top, top), [S((rows, dv), BF16)], [SM] + [VM] * (top + 2),
              rows * dv)(idx, kv, *ups, gu)[0]
    partner = swap(up, "seq", top)
    ups.append(partner)
    far_rows = call(
        functools.partial(carry_kernel, dims, levels, first, seq_bits), [S((far_own, tokens), BF16)],
        [SM] + [VM] * (seq_bits + 3), 2 * tokens * rows * dv * seq_bits)(idx, *ups, d_out, qt, sig)[0]
    gots = [partner]
    for bit in reversed(range(top)):
        down = call(functools.partial(pend_kernel, bit, top), [S((rows, dv), BF16)], [SM] + [VM] * (len(gots) + 1),
                    rows * dv)(idx, *gots, gu)[0]
        gots.append(swap(down, "seq", bit))

    near_all = gather_heads(near, head_bits)
    far_all = [far_rows] + [exchange(far_rows, "head", away) for away in range(1, n_head)]
    col = jnp.arange(cols, dtype=jnp.int32)[None, :]
    row = jnp.arange(far_cols, dtype=jnp.int32)[:, None]
    within = row % far_own
    at = (row // far_own * nh + within % nh) * levels + first + within // nh
    place = ((at == col) & (within < far)).astype(BF16)

    n = width // 4
    keep, one, two, both, gp = call(
        functools.partial(wgrad_kernel, head_bits, per),
        [S((n, cols), F32)] + [S((n, cols), BF16)] * 3 + [S((cols, tokens), BF16)],
        [SM] * 2 + [VM] * (n_head + 3), 2 * tokens * width * cols,
        scratch_shapes=[pltpu.VMEM((far_cols, tokens), BF16)])(idx, head_idx, xt, place, near_all, *far_all)
    got = [exchange(one, "seq", 1), exchange(two, "seq", 2), exchange(both, "seq", 3)]
    for bit in range(2, seq_bits):
        n = n // 2
        send, keep = call(
            functools.partial(fold_kernel, bit, per), [S((n, cols), BF16), S((n, cols), F32)],
            [SM] + [VM] * (1 + len(got)), n * cols)(idx, keep, *got)
        got = [swap(send, "seq", bit)]
    d_w = keep + got[0].astype(F32)

    half = nh // 4
    local = []
    for part in range(2):
        local.append(call(
            functools.partial(local_kernel, dims, levels, tuple(range(part * half, (part + 1) * half))),
            [S((nh * dv // 2, tokens), F32), S((rows // 2, tokens), F32), S((tokens, rows // 2), F32),
             S((tokens, nh * dv // 2), F32)],
            [VM] * 5, tokens * tokens * nh * (3 * dk + 3 * dv),
        )(keys, queries, values, d_out, lw))
    shapes = [(tokens, nh * dv), (tokens, rows), (tokens, width), (tokens, rows), (tokens, nh * dv)]
    out, d_queries, d_hidden, d_keys, d_values = call(
        functools.partial(final_kernel, dims, levels, first, seq_bits), [S(shape, BF16) for shape in shapes],
        [SM] + [VM] * (2 * seq_bits + 16), 8 * tokens * rows * dv * seq_bits, out_specs=[hbm] * len(shapes),
        scratch_shapes=[pltpu.VMEM(shape, BF16) for shape in shapes] + [pltpu.SemaphoreType.DMA((2 * nh + 1,))])(
            idx, *ups, *gots, qt, lw, d_out, d_state.reshape(rows, dv), keys, values, *local[0], *local[1],
            gp, w_near)
    return (out, d_queries, d_keys, d_values, d_hidden, d_w)


def solution(mesh):
    two = P("seq", "head")
    return jax.shard_map(
        body, mesh=mesh,
        in_specs=(two, P("head", None), two, two, two, two, P("head", None, None)),
        out_specs=(two, two, two, two, two, P(("head", "seq"), None)),
        check_vma=False)
```

```python
import functools

import jax
import jax.numpy as jnp
from jax import lax
from jax.experimental import pallas as pl
from jax.experimental.pallas import tpu as pltpu
from jax.sharding import PartitionSpec as P


F32 = jnp.float32
BF16 = jnp.bfloat16
LANES = 128
SUB = 8
VM = pl.BlockSpec(memory_space=pltpu.VMEM)
SM = pl.BlockSpec(memory_space=pltpu.SMEM)


def nn(a, b):
    return lax.dot_general(a, b, (((1,), (0,)), ((), ())), preferred_element_type=F32)


def nt(a, b):
    return lax.dot_general(a, b, (((1,), (1,)), ((), ())), preferred_element_type=F32)


def tn(a, b):
    return lax.dot_general(a, b, (((0,), (0,)), ((), ())), preferred_element_type=F32)


def call(kernel, outs, specs, flops, **kwargs):
    size = sum(o.size * o.dtype.itemsize for o in outs)
    return pl.pallas_call(
        kernel,
        out_shape=outs,
        in_specs=specs,
        compiler_params=pltpu.CompilerParams(vmem_limit_bytes=16 << 20),
        cost_estimate=pl.CostEstimate(flops=flops, bytes_accessed=2 * size, transcendentals=0),
        **kwargs,
    )


def leave(buf_ref, hbm_ref, sem, cols):
    copy = pltpu.make_async_copy(buf_ref.at[:, cols], hbm_ref.at[:, cols], sem)
    copy.start()
    return copy


def exchange(value, axis, mask, only=None):
    pairs = [(source, source ^ mask) for source in range(lax.axis_size(axis))
             if only is None or bool(source & mask) == only]
    return lax.ppermute(value, axis, pairs)


def swap(value, axis, bit):
    return exchange(value, axis, 1 << bit)


def state_kernel(dims, idx_ref, head_ref, k_hbm, v_hbm, w_hbm, x_hbm, kv_ref, kvb_ref, w_ref, x_ref, k_ref, v_ref, sems):
    nh, dk, dv = dims
    copies = [pltpu.make_async_copy(src, dst, sems.at[n]) for n, (src, dst) in enumerate(
        ((k_hbm, k_ref), (v_hbm, v_ref), (w_hbm, w_ref), (x_hbm, x_ref)))]
    for copy in copies:
        copy.start()
    copies[0].wait()
    copies[1].wait()
    for pair in range(nh // 2):
        turned = k_ref[:, pair * 2 * dk:(pair + 1) * 2 * dk].T
        for j in range(2):
            h = 2 * pair + j
            kv = nn(turned[j * dk:(j + 1) * dk], v_ref[:, h * dv:(h + 1) * dv])
            kv_ref[h * dk:(h + 1) * dk, :] = kv
            kvb_ref[h * dk:(h + 1) * dk, :] = kv.astype(BF16)
    copies[2].wait()
    copies[3].wait()


def part_ways(entries, upper, send_ref, keep_ref, inner):
    n = entries.shape[0] // inner
    for e in range(n // 2):
        low = entries[2 * e * inner:(2 * e + 1) * inner]
        high = entries[(2 * e + 1) * inner:(2 * e + 2) * inner]
        out = slice(e * inner, (e + 1) * inner)
        send_ref[out, :] = jnp.where(upper, low, high).astype(BF16)
        keep_ref[out, :] = jnp.where(upper, high, low)


def project_kernel(bit, idx_ref, w_ref, x_ref, send_ref, keep_ref, xt_ref):
    xt = x_ref[...].T
    xt_ref[...] = xt
    upper = ((idx_ref[0] >> bit) & 1) == 1
    part_ways(tn(w_ref[...], xt), upper, send_ref, keep_ref, keep_ref.shape[0])


def fold_kernel(bit, inner, idx_ref, keep_in, *refs):
    gots, (send_ref, keep_ref) = refs[:-2], refs[-2:]
    upper = ((idx_ref[0] >> bit) & 1) == 1
    total = keep_in[...]
    for got in gots:
        total = total + got[...].astype(F32)
    part_ways(total, upper, send_ref, keep_ref, inner)


def weight_kernel(dims, levels, first, count, keep_ref, got_ref, gl_ref, q_ref, g_ref,
                  sig_ref, lw_ref, near_ref, qt_ref, gu_ref, gu_top_ref):
    nh, dk, dv = dims
    proj = keep_ref[...] + got_ref[...].astype(F32)
    sig = jax.nn.sigmoid(proj)
    sig_ref[...] = sig
    near_ref[...] = (gl_ref[...] * sig).astype(BF16)
    lw_ref[...] = jnp.maximum(proj, 0.0) + jnp.log1p(jnp.exp(-jnp.abs(proj)))
    for pair in range(nh // 2):
        turned = q_ref[:, pair * 2 * dk:(pair + 1) * 2 * dk].T
        qt_ref[pair * 2 * dk:(pair + 1) * 2 * dk, :] = turned
        wide = turned.astype(F32)
        for j in range(2):
            h = 2 * pair + j
            scaled = jnp.concatenate(
                [wide[j * dk:(j + 1) * dk] * lw_ref[h * levels + first + m:h * levels + first + m + 1, :]
                 for m in range(count)], axis=0)
            grad = nn(scaled.astype(BF16), g_ref[:, h * dv:(h + 1) * dv])
            for m in range(count - 1):
                gu_ref[m, h * dk:(h + 1) * dk, :] = grad[m * dk:(m + 1) * dk].astype(BF16)
            gu_top_ref[h * dk:(h + 1) * dk, :] = grad[(count - 1) * dk:].astype(BF16)


def spread_half(rows, lane, low, t_low):
    digits = (low ^ t_low)
    near = jnp.where(digits == 0, rows[0], jnp.where(digits < 2, rows[1], jnp.where(digits < 4, rows[2], rows[3])))
    near = jnp.where(low <= t_low, near, 0.0)
    parts = []
    for a in range(LANES // SUB):
        value = None
        for l in reversed(range(4, 8)):
            if (a >> (l - 4)) & 1 == 0:
                end = (((a >> (l - 3)) + 1) << (l - 3)) * SUB
                value = rows[l] if value is None else jnp.where(lane < end, rows[l], value)
        value = near if value is None else jnp.where(lane < (a + 1) * SUB, near, value)
        if a:
            value = jnp.where(lane < a * SUB, 0.0, value)
        parts.append(value)
    return jnp.concatenate(parts, axis=0)


def level_sums(prod, lane, low, t_low):
    count = LANES // SUB
    group = lane // SUB
    cur = [prod[a * SUB:(a + 1) * SUB] for a in range(count)]
    near = jnp.zeros_like(cur[0])
    for a in range(count):
        near = jnp.where(group == a, cur[a], near)
    near = jnp.where(low <= t_low, near, 0.0)
    digits = low ^ t_low
    sums = []
    for l in range(4):
        lo, hi = (0, 1) if l == 0 else (1 << (l - 1), 1 << l)
        sums.append(jnp.where((digits >= lo) & (digits < hi), near, 0.0))
    for l in range(4, 8):
        total = jnp.zeros_like(near)
        for a in range(0, len(cur), 2):
            total = jnp.where((lane >> (l - 1)) == a + 1, cur[a], total)
        sums.append(total)
        cur = [cur[a] + cur[a + 1] for a in range(0, len(cur), 2)]
    return [jnp.sum(s, axis=0, keepdims=True) for s in sums]


def level_kernel(dims, levels, k_ref, q_ref, v_ref, g_ref, gl_ref):
    nh, dk, dv = dims
    lane = lax.broadcasted_iota(jnp.int32, (SUB, LANES), 1)
    low = lax.broadcasted_iota(jnp.int32, (SUB, LANES), 0)
    t_low = lane % SUB
    gl_ref[...] = jnp.zeros_like(gl_ref)
    for pair in range(nh // 2):
        kp = k_ref[:, pair * 2 * dk:(pair + 1) * 2 * dk]
        qt = q_ref[:, pair * 2 * dk:(pair + 1) * 2 * dk].T
        zero = jnp.zeros_like(qt[:dk])
        for j in range(2):
            h = 2 * pair + j
            base = h * levels
            qz = jnp.concatenate([qt[:dk], zero] if j == 0 else [zero, qt[dk:]], axis=0)
            prod = nn(kp, qz) * nt(v_ref[:, h * dv:(h + 1) * dv], g_ref[:, h * dv:(h + 1) * dv])
            for x in range(2):
                part = slice(x * LANES, (x + 1) * LANES)
                sums = level_sums(prod[part, part], lane, low, t_low)
                for l in range(8):
                    gl_ref[base + l:base + l + 1, part] = sums[l]
            gl_ref[base + 8:base + 9, LANES:] = jnp.sum(prod[:LANES, LANES:], axis=0, keepdims=True)


def local_kernel(dims, levels, pairs, k_ref, q_ref, v_ref, g_ref, lw_ref, out_ref, dq_ref, dk_ref, dv_ref):
    _, dk, dv = dims
    lane = lax.broadcasted_iota(jnp.int32, (SUB, LANES), 1)
    low = lax.broadcasted_iota(jnp.int32, (SUB, LANES), 0)
    t_low = lane % SUB
    for n, pair in enumerate(pairs):
        kp = k_ref[:, pair * 2 * dk:(pair + 1) * 2 * dk]
        qp = q_ref[:, pair * 2 * dk:(pair + 1) * 2 * dk]
        kt, qt = kp.T, qp.T
        zero = jnp.zeros_like(qt[:dk])
        wide_lane = lax.broadcasted_iota(jnp.int32, qp.shape, 1)
        dk_sum = None
        for j in range(2):
            h, m = 2 * pair + j, 2 * n + j
            vj = v_ref[:, h * dv:(h + 1) * dv]
            gj = g_ref[:, h * dv:(h + 1) * dv]
            qz = jnp.concatenate([qt[:dk], zero] if j == 0 else [zero, qt[dk:]], axis=0)
            base = h * levels
            cross = lw_ref[base + 8:base + 9, LANES:]
            halves = []
            for x in range(2):
                rows = [jnp.broadcast_to(lw_ref[base + l:base + l + 1, x * LANES:(x + 1) * LANES], (SUB, LANES))
                        for l in range(8)]
                halves.append(spread_half(rows, lane, low, t_low))

            def weigh(full):
                top = jnp.concatenate([full[:LANES, :LANES] * halves[0], full[:LANES, LANES:] * cross], axis=1)
                bottom = full[LANES:, LANES:] * halves[1]
                bottom = jnp.concatenate([jnp.zeros_like(bottom), bottom], axis=1)
                return jnp.concatenate([top, bottom], axis=0).astype(BF16)

            mixed = weigh(nn(kp, qz))
            grad_scores = weigh(nt(vj, gj))
            out_ref[m * dv:(m + 1) * dv, :] = tn(vj, mixed)
            dq_ref[m * dk:(m + 1) * dk, :] = nn(kt[j * dk:(j + 1) * dk], grad_scores)
            dv_ref[:, m * dv:(m + 1) * dv] = nn(mixed, gj)
            mine = (wide_lane < dk) if j == 0 else (wide_lane >= dk)
            term = nn(grad_scores, jnp.where(mine, qp, jnp.zeros_like(qp)))
            dk_sum = term if dk_sum is None else dk_sum + term
        dk_ref[:, n * 2 * dk:(n + 1) * 2 * dk] = dk_sum


def carry_kernel(dims, levels, first, count, idx_ref, *refs):
    nh, dk, dv = dims
    ups = refs[:count]
    g_ref, qt_ref, sig_ref, far_ref = refs[count:]
    index = idx_ref[0]
    far_ref[...] = jnp.zeros_like(far_ref)
    for m in range(count):
        up = ((index >> m) & 1).astype(F32)
        found = []
        for h in range(nh):
            rows = slice(h * dk, (h + 1) * dk)
            r = h * levels + first + m
            x = nt(ups[m][rows, :], g_ref[:, h * dv:(h + 1) * dv])
            row = jnp.sum(x * qt_ref[rows, :].astype(F32), axis=0, keepdims=True)
            found.append(row * (sig_ref[r:r + 1, :] * up))
        far_ref[m * nh:(m + 1) * nh, :] = jnp.concatenate(found, axis=0).astype(BF16)


def wgrad_kernel(bits, inner, idx_ref, head_ref, xt_ref, place_ref, near_ref, *refs):
    gathered, (keep_ref, one_ref, two_ref, both_ref, gp_ref, far_ref) = refs[:-6], refs[-6:]
    own = near_ref.shape[0] >> bits
    for n, rows_ref in enumerate(gathered):
        away = sum(((n >> k) & 1) << (bits - 1 - k) for k in range(bits))
        at = pl.multiple_of((head_ref[0] ^ away) * own, 16)
        gp_ref[pl.ds(at, own), :] = near_ref[n * own:(n + 1) * own, :]
        some = rows_ref.shape[0]
        far_ref[pl.ds(pl.multiple_of((head_ref[0] ^ n) * some, 16), some), :] = rows_ref[...]
    gp = (gp_ref[...].astype(F32) + tn(place_ref[...], far_ref[...])).astype(BF16)
    gp_ref[...] = gp
    total = nt(xt_ref[...], gp)
    right, upper = (idx_ref[0] & 1) == 1, ((idx_ref[0] >> 1) & 1) == 1
    for e in range(total.shape[0] // (4 * inner)):
        parts = [total[(4 * e + n) * inner:(4 * e + n + 1) * inner] for n in range(4)]
        kept, sent = jnp.where(right, parts[1], parts[0]), jnp.where(right, parts[0], parts[1])
        kept_up, sent_up = jnp.where(right, parts[3], parts[2]), jnp.where(right, parts[2], parts[3])
        at = slice(e * inner, (e + 1) * inner)
        keep_ref[at, :] = jnp.where(upper, kept_up, kept)
        one_ref[at, :] = jnp.where(upper, sent_up, sent).astype(BF16)
        two_ref[at, :] = jnp.where(upper, kept, kept_up).astype(BF16)
        both_ref[at, :] = jnp.where(upper, sent, sent_up).astype(BF16)


def quad_kernel(kv_ref, one_ref, two_ref, both_ref, upper_ref, sum_ref, send_ref):
    upper = two_ref[...].astype(F32) + both_ref[...].astype(F32)
    upper_ref[...] = upper.astype(BF16)
    total = kv_ref[...] + one_ref[...].astype(F32) + upper
    sum_ref[...] = total
    send_ref[...] = total.astype(BF16)


def pend_kernel(bit, top, idx_ref, *refs):
    gots, (gu_ref, send_ref) = refs[:-2], refs[-2:]
    index = idx_ref[0]
    total = jnp.where(((index >> top) & 1) == 1, 0.0, gots[0][...].astype(F32))
    for got in gots[1:]:
        total = total + got[...].astype(F32)
    send_ref[...] = (total + jnp.where(((index >> bit) & 1) == 1, gu_ref[bit].astype(F32), 0.0)).astype(BF16)


def final_kernel(dims, levels, first, count, idx_ref, *refs):
    nh, dk, dv = dims
    top = count - 1
    ups, gots = refs[:count], refs[count:2 * count]
    (qt_ref, lw_ref, g_ref, ds_ref, k_ref, v_ref, low_o, low_q, low_k, low_v, high_o, high_q, high_k, high_v,
     gp_ref, w_ref, out_hbm, dq_hbm, dx_hbm, dk_hbm, dv_hbm,
     out_ref, dq_ref, dx_ref, dk_ref, dv_ref, sems) = refs[2 * count:]
    index = idx_ref[0]
    copies = []

    def send(buf_ref, hbm_ref, cols):
        copies.append(leave(buf_ref, hbm_ref, sems.at[len(copies)], cols))

    def weights(h, m):
        r = h * levels + first + m
        return lw_ref[r:r + 1, :] * ((index >> m) & 1).astype(F32)

    for h in range(nh):
        rows = slice(h * dk, (h + 1) * dk)
        local_ref, n = (low_o, h) if h < nh // 2 else (high_o, h - nh // 2)
        total = local_ref[n * dv:(n + 1) * dv, :]
        for m in range(count):
            total = total + tn(ups[m][rows, :], qt_ref[rows, :]) * weights(h, m)
        out_ref[:, h * dv:(h + 1) * dv] = total.astype(BF16).T
        if h % 2:
            send(out_ref, out_hbm, slice((h - 1) * dv, (h + 1) * dv))
    for pair in range(nh // 2):
        halves = []
        for j in range(2):
            h = 2 * pair + j
            local_ref, n = (low_q, h) if h < nh // 2 else (high_q, h - nh // 2)
            total = local_ref[n * dk:(n + 1) * dk, :]
            for m in range(count):
                total = total + nt(ups[m][h * dk:(h + 1) * dk, :], g_ref[:, h * dv:(h + 1) * dv]) * weights(h, m)
            halves.append(total)
        cols = slice(pair * 2 * dk, (pair + 1) * 2 * dk)
        dq_ref[:, cols] = jnp.concatenate(halves, axis=0).astype(BF16).T
        send(dq_ref, dq_hbm, cols)
    dx_ref[...] = lax.dot_general(
        gp_ref[...], w_ref[...], (((0,), (1,)), ((), ())), preferred_element_type=F32).astype(BF16)
    send(dx_ref, dx_hbm, slice(0, dx_ref.shape[1]))
    upper = ((index >> top) & 1) == 1
    zero = jnp.zeros((dk, dv), BF16)
    for pair in range(nh // 2):
        pair_rows = slice(pair * 2 * dk, (pair + 1) * 2 * dk)
        total = ds_ref[pair_rows, :] + jnp.where(upper, 0.0, gots[0][pair_rows, :].astype(F32))
        for got in gots[1:]:
            total = total + got[pair_rows, :].astype(F32)
        adj = [total[:dk].astype(BF16), total[dk:].astype(BF16)]
        kp = k_ref[:, pair * 2 * dk:(pair + 1) * 2 * dk]
        dkl_ref, dvl_ref, p = (low_k, low_v, pair) if pair < nh // 4 else (high_k, high_v, pair - nh // 4)
        total = dkl_ref[:, p * 2 * dk:(p + 1) * 2 * dk]
        for j in range(2):
            h = 2 * pair + j
            padded = jnp.concatenate([adj[j], zero] if j == 0 else [zero, adj[j]], axis=0)
            cols = slice(h * dv, (h + 1) * dv)
            total = total + nt(v_ref[:, cols], padded)
            near = dvl_ref[:, (2 * p + j) * dv:(2 * p + j + 1) * dv]
            dv_ref[:, cols] = (near + nn(kp, padded)).astype(BF16)
        dk_ref[:, pair * 2 * dk:(pair + 1) * 2 * dk] = total.astype(BF16)
        send(dv_ref, dv_hbm, slice(2 * pair * dv, (2 * pair + 2) * dv))
        send(dk_ref, dk_hbm, slice(pair * 2 * dk, (pair + 1) * 2 * dk))
    for copy in copies:
        copy.wait()


def gather_heads(value, head_bits):
    full = value
    for bit in reversed(range(head_bits)):
        full = jnp.concatenate([full, swap(full, "head", bit)], axis=0)
    return full


def body(hidden, w, queries, keys, values, d_out, d_state):
    tokens, width = hidden.shape
    dims = d_state.shape
    nh, dk, dv = dims
    n_seq, n_head = lax.axis_size("seq"), lax.axis_size("head")
    seq_bits, head_bits = n_seq.bit_length() - 1, n_head.bit_length() - 1
    top = seq_bits - 1
    cols = w.shape[1]
    levels = cols // (nh * n_head)
    own = nh * levels
    far = nh * seq_bits
    far_own = -(-far // 16) * 16
    far_cols = far_own * n_head
    first = tokens.bit_length()
    per = width // n_seq
    rows = nh * dk
    S = jax.ShapeDtypeStruct
    idx, head_idx = [jnp.reshape(lax.axis_index(axis), (1,)) for axis in ("seq", "head")]

    hbm = pl.BlockSpec(memory_space=pltpu.HBM)
    kv, kvb, w_near, x_near = call(
        functools.partial(state_kernel, dims),
        [S((rows, dv), F32), S((rows, dv), BF16), S(w.shape, BF16), S(hidden.shape, BF16)],
        [SM] * 2 + [hbm] * 4, 2 * tokens * rows * dv,
        scratch_shapes=[pltpu.VMEM((tokens, rows), BF16), pltpu.VMEM((tokens, nh * dv), BF16),
                        pltpu.SemaphoreType.DMA((4,))])(
                            idx, head_idx, *[pltpu.with_memory_space_constraint(a, pltpu.HBM) for a in (keys, values, w, hidden)])
    send, keep, xt = call(
        functools.partial(project_kernel, head_bits - 1),
        [S((cols // 2, tokens), BF16), S((cols // 2, tokens), F32), S((width, tokens), BF16)], [SM] + [VM] * 2,
        2 * tokens * width * cols)(head_idx, w_near, x_near)

    quad = [exchange(kvb, "seq", 1), exchange(kvb, "seq", 2), exchange(kvb, "seq", 3)]

    got = swap(send, "head", head_bits - 1)
    for bit in reversed(range(head_bits - 1)):
        n = keep.shape[0] // 2
        send, keep = call(
            functools.partial(fold_kernel, bit, n), [S((n, tokens), BF16), S((n, tokens), F32)],
            [SM] + [VM] * 2, n * tokens)(head_idx, keep, got)
        got = swap(send, "head", bit)

    gl = call(
        functools.partial(level_kernel, dims, levels), [S((own, tokens), F32)], [VM] * 4,
        2 * tokens * tokens * nh * (dk + dv))(keys, queries, values, d_out)[0]
    sig, lw, near, qt, gu, gu_top = call(
        functools.partial(weight_kernel, dims, levels, first, seq_bits),
        [S((own, tokens), F32), S((own, tokens), F32), S((own, tokens), BF16), S((rows, tokens), BF16),
         S((top, rows, dv), BF16), S((rows, dv), BF16)],
        [VM] * 5, 2 * tokens * rows * dv * seq_bits)(keep, got, gl, queries, d_out)

    second, total, up = call(
        quad_kernel, [S((rows, dv), BF16), S((rows, dv), F32), S((rows, dv), BF16)], [VM] * 4, 4 * rows * dv)(
            kv, *quad)
    ups = [quad[0], second]
    for bit in range(2, top):
        ups.append(swap(up, "seq", bit))
        total = total + ups[-1].astype(F32)
        up = total.astype(BF16)
    ups.append(exchange(up, "seq", 1 << top, only=False))
    far_rows = call(
        functools.partial(carry_kernel, dims, levels, first, seq_bits), [S((far_own, tokens), BF16)],
        [SM] + [VM] * (seq_bits + 3), 2 * tokens * rows * dv * seq_bits)(idx, *ups, d_out, qt, sig)[0]
    gots = [exchange(gu_top, "seq", 1 << top, only=True)]
    for bit in reversed(range(top)):
        down = call(functools.partial(pend_kernel, bit, top), [S((rows, dv), BF16)], [SM] + [VM] * (len(gots) + 1),
                    rows * dv)(idx, *gots, gu)[0]
        gots.append(swap(down, "seq", bit))

    near_all = gather_heads(near, head_bits)
    far_all = [far_rows] + [exchange(far_rows, "head", away) for away in range(1, n_head)]
    col = jnp.arange(cols, dtype=jnp.int32)[None, :]
    row = jnp.arange(far_cols, dtype=jnp.int32)[:, None]
    within = row % far_own
    at = (row // far_own * nh + within % nh) * levels + first + within // nh
    place = ((at == col) & (within < far)).astype(BF16)

    n = width // 4
    keep, one, two, both, gp = call(
        functools.partial(wgrad_kernel, head_bits, per),
        [S((n, cols), F32)] + [S((n, cols), BF16)] * 3 + [S((cols, tokens), BF16)],
        [SM] * 2 + [VM] * (n_head + 3), 2 * tokens * width * cols,
        scratch_shapes=[pltpu.VMEM((far_cols, tokens), BF16)])(idx, head_idx, xt, place, near_all, *far_all)
    got = [exchange(one, "seq", 1), exchange(two, "seq", 2), exchange(both, "seq", 3)]
    for bit in range(2, seq_bits):
        n = n // 2
        send, keep = call(
            functools.partial(fold_kernel, bit, per), [S((n, cols), BF16), S((n, cols), F32)],
            [SM] + [VM] * (1 + len(got)), n * cols)(idx, keep, *got)
        got = [swap(send, "seq", bit)]
    d_w = keep + got[0].astype(F32)

    half = nh // 4
    local = []
    for part in range(2):
        local.append(call(
            functools.partial(local_kernel, dims, levels, tuple(range(part * half, (part + 1) * half))),
            [S((nh * dv // 2, tokens), F32), S((rows // 2, tokens), F32), S((tokens, rows // 2), F32),
             S((tokens, nh * dv // 2), F32)],
            [VM] * 5, tokens * tokens * nh * (3 * dk + 3 * dv),
        )(keys, queries, values, d_out, lw))
    shapes = [(tokens, nh * dv), (tokens, rows), (tokens, width), (tokens, rows), (tokens, nh * dv)]
    out, d_queries, d_hidden, d_keys, d_values = call(
        functools.partial(final_kernel, dims, levels, first, seq_bits), [S(shape, BF16) for shape in shapes],
        [SM] + [VM] * (2 * seq_bits + 16), 8 * tokens * rows * dv * seq_bits, out_specs=[hbm] * len(shapes),
        scratch_shapes=[pltpu.VMEM(shape, BF16) for shape in shapes] + [pltpu.SemaphoreType.DMA((2 * nh + 1,))])(
            idx, *ups, *gots, qt, lw, d_out, d_state.reshape(rows, dv), keys, values, *local[0], *local[1],
            gp, w_near)
    return (out, d_queries, d_keys, d_values, d_hidden, d_w)


def solution(mesh):
    two = P("seq", "head")
    return jax.shard_map(
        body, mesh=mesh,
        in_specs=(two, P("head", None), two, two, two, two, P("head", None, None)),
        out_specs=(two, two, two, two, two, P(("head", "seq"), None)),
        check_vma=False)
```

```python
import functools

import jax
import jax.numpy as jnp
from jax import lax
from jax.experimental import pallas as pl
from jax.experimental.pallas import tpu as pltpu
from jax.sharding import PartitionSpec as P


F32 = jnp.float32
BF16 = jnp.bfloat16
LANES = 128
SUB = 8
VM = pl.BlockSpec(memory_space=pltpu.VMEM)
SM = pl.BlockSpec(memory_space=pltpu.SMEM)


def nn(a, b):
    return lax.dot_general(a, b, (((1,), (0,)), ((), ())), preferred_element_type=F32)


def nt(a, b):
    return lax.dot_general(a, b, (((1,), (1,)), ((), ())), preferred_element_type=F32)


def tn(a, b):
    return lax.dot_general(a, b, (((0,), (0,)), ((), ())), preferred_element_type=F32)


def call(kernel, outs, specs, flops, **kwargs):
    size = sum(o.size * o.dtype.itemsize for o in outs)
    return pl.pallas_call(
        kernel,
        out_shape=outs,
        in_specs=specs,
        compiler_params=pltpu.CompilerParams(vmem_limit_bytes=16 << 20),
        cost_estimate=pl.CostEstimate(flops=flops, bytes_accessed=2 * size, transcendentals=0),
        **kwargs,
    )


def leave(buf_ref, hbm_ref, sem, cols):
    copy = pltpu.make_async_copy(buf_ref.at[:, cols], hbm_ref.at[:, cols], sem)
    copy.start()
    return copy


def exchange(value, axis, mask):
    pairs = [(source, source ^ mask) for source in range(lax.axis_size(axis))]
    return lax.ppermute(value, axis, pairs)


def swap(value, axis, bit):
    return exchange(value, axis, 1 << bit)


def state_kernel(dims, idx_ref, head_ref, k_hbm, v_hbm, w_hbm, x_hbm, kv_ref, kvb_ref, w_ref, x_ref, k_ref, v_ref, sems):
    nh, dk, dv = dims
    copies = [pltpu.make_async_copy(src, dst, sems.at[n]) for n, (src, dst) in enumerate(
        ((k_hbm, k_ref), (v_hbm, v_ref), (w_hbm, w_ref), (x_hbm, x_ref)))]
    for copy in copies:
        copy.start()
    copies[0].wait()
    copies[1].wait()
    for pair in range(nh // 2):
        turned = k_ref[:, pair * 2 * dk:(pair + 1) * 2 * dk].T
        for j in range(2):
            h = 2 * pair + j
            kv = nn(turned[j * dk:(j + 1) * dk], v_ref[:, h * dv:(h + 1) * dv])
            kv_ref[h * dk:(h + 1) * dk, :] = kv
            kvb_ref[h * dk:(h + 1) * dk, :] = kv.astype(BF16)
    copies[2].wait()
    copies[3].wait()


def part_ways(entries, upper, send_ref, keep_ref, inner):
    n = entries.shape[0] // inner
    for e in range(n // 2):
        low = entries[2 * e * inner:(2 * e + 1) * inner]
        high = entries[(2 * e + 1) * inner:(2 * e + 2) * inner]
        out = slice(e * inner, (e + 1) * inner)
        send_ref[out, :] = jnp.where(upper, low, high).astype(BF16)
        keep_ref[out, :] = jnp.where(upper, high, low)


def project_kernel(bit, idx_ref, w_ref, x_ref, send_ref, keep_ref, xt_ref):
    xt = x_ref[...].T
    xt_ref[...] = xt
    upper = ((idx_ref[0] >> bit) & 1) == 1
    part_ways(tn(w_ref[...], xt), upper, send_ref, keep_ref, keep_ref.shape[0])


def fold_kernel(bit, inner, idx_ref, keep_in, got_ref, send_ref, keep_ref):
    upper = ((idx_ref[0] >> bit) & 1) == 1
    part_ways(keep_in[...] + got_ref[...].astype(F32), upper, send_ref, keep_ref, inner)


def weight_kernel(dims, levels, first, count, keep_ref, got_ref, gl_ref, q_ref, g_ref,
                  sig_ref, lw_ref, near_ref, qt_ref, gu_ref):
    nh, dk, dv = dims
    proj = keep_ref[...] + got_ref[...].astype(F32)
    sig = jax.nn.sigmoid(proj)
    sig_ref[...] = sig
    near_ref[...] = (gl_ref[...] * sig).astype(BF16)
    lw_ref[...] = jnp.maximum(proj, 0.0) + jnp.log1p(jnp.exp(-jnp.abs(proj)))
    for pair in range(nh // 2):
        turned = q_ref[:, pair * 2 * dk:(pair + 1) * 2 * dk].T
        qt_ref[pair * 2 * dk:(pair + 1) * 2 * dk, :] = turned
        wide = turned.astype(F32)
        for j in range(2):
            h = 2 * pair + j
            scaled = jnp.concatenate(
                [wide[j * dk:(j + 1) * dk] * lw_ref[h * levels + first + m:h * levels + first + m + 1, :]
                 for m in range(count)], axis=0)
            grad = nn(scaled.astype(BF16), g_ref[:, h * dv:(h + 1) * dv])
            for m in range(count):
                gu_ref[m, h * dk:(h + 1) * dk, :] = grad[m * dk:(m + 1) * dk].astype(BF16)


def spread_half(rows, lane, low, t_low):
    digits = (low ^ t_low)
    near = jnp.where(digits == 0, rows[0], jnp.where(digits < 2, rows[1], jnp.where(digits < 4, rows[2], rows[3])))
    near = jnp.where(low <= t_low, near, 0.0)
    parts = []
    for a in range(LANES // SUB):
        value = None
        for l in reversed(range(4, 8)):
            if (a >> (l - 4)) & 1 == 0:
                end = (((a >> (l - 3)) + 1) << (l - 3)) * SUB
                value = rows[l] if value is None else jnp.where(lane < end, rows[l], value)
        value = near if value is None else jnp.where(lane < (a + 1) * SUB, near, value)
        if a:
            value = jnp.where(lane < a * SUB, 0.0, value)
        parts.append(value)
    return jnp.concatenate(parts, axis=0)


def level_sums(prod, lane, low, t_low):
    count = LANES // SUB
    group = lane // SUB
    cur = [prod[a * SUB:(a + 1) * SUB] for a in range(count)]
    near = jnp.zeros_like(cur[0])
    for a in range(count):
        near = jnp.where(group == a, cur[a], near)
    near = jnp.where(low <= t_low, near, 0.0)
    digits = low ^ t_low
    sums = []
    for l in range(4):
        lo, hi = (0, 1) if l == 0 else (1 << (l - 1), 1 << l)
        sums.append(jnp.where((digits >= lo) & (digits < hi), near, 0.0))
    for l in range(4, 8):
        total = jnp.zeros_like(near)
        for a in range(0, len(cur), 2):
            total = jnp.where((lane >> (l - 1)) == a + 1, cur[a], total)
        sums.append(total)
        cur = [cur[a] + cur[a + 1] for a in range(0, len(cur), 2)]
    return [jnp.sum(s, axis=0, keepdims=True) for s in sums]


def level_kernel(dims, levels, k_ref, q_ref, v_ref, g_ref, gl_ref):
    nh, dk, dv = dims
    lane = lax.broadcasted_iota(jnp.int32, (SUB, LANES), 1)
    low = lax.broadcasted_iota(jnp.int32, (SUB, LANES), 0)
    t_low = lane % SUB
    gl_ref[...] = jnp.zeros_like(gl_ref)
    for pair in range(nh // 2):
        kp = k_ref[:, pair * 2 * dk:(pair + 1) * 2 * dk]
        qt = q_ref[:, pair * 2 * dk:(pair + 1) * 2 * dk].T
        zero = jnp.zeros_like(qt[:dk])
        for j in range(2):
            h = 2 * pair + j
            base = h * levels
            qz = jnp.concatenate([qt[:dk], zero] if j == 0 else [zero, qt[dk:]], axis=0)
            prod = nn(kp, qz) * nt(v_ref[:, h * dv:(h + 1) * dv], g_ref[:, h * dv:(h + 1) * dv])
            for x in range(2):
                part = slice(x * LANES, (x + 1) * LANES)
                sums = level_sums(prod[part, part], lane, low, t_low)
                for l in range(8):
                    gl_ref[base + l:base + l + 1, part] = sums[l]
            gl_ref[base + 8:base + 9, LANES:] = jnp.sum(prod[:LANES, LANES:], axis=0, keepdims=True)


def local_kernel(dims, levels, pairs, k_ref, q_ref, v_ref, g_ref, lw_ref, out_ref, dq_ref, dk_ref, dv_ref):
    _, dk, dv = dims
    lane = lax.broadcasted_iota(jnp.int32, (SUB, LANES), 1)
    low = lax.broadcasted_iota(jnp.int32, (SUB, LANES), 0)
    t_low = lane % SUB
    for n, pair in enumerate(pairs):
        kp = k_ref[:, pair * 2 * dk:(pair + 1) * 2 * dk]
        qp = q_ref[:, pair * 2 * dk:(pair + 1) * 2 * dk]
        kt, qt = kp.T, qp.T
        zero = jnp.zeros_like(qt[:dk])
        wide_lane = lax.broadcasted_iota(jnp.int32, qp.shape, 1)
        dk_sum = None
        for j in range(2):
            h, m = 2 * pair + j, 2 * n + j
            vj = v_ref[:, h * dv:(h + 1) * dv]
            gj = g_ref[:, h * dv:(h + 1) * dv]
            qz = jnp.concatenate([qt[:dk], zero] if j == 0 else [zero, qt[dk:]], axis=0)
            base = h * levels
            cross = lw_ref[base + 8:base + 9, LANES:]
            halves = []
            for x in range(2):
                rows = [jnp.broadcast_to(lw_ref[base + l:base + l + 1, x * LANES:(x + 1) * LANES], (SUB, LANES))
                        for l in range(8)]
                halves.append(spread_half(rows, lane, low, t_low))

            def weigh(full):
                top = jnp.concatenate([full[:LANES, :LANES] * halves[0], full[:LANES, LANES:] * cross], axis=1)
                bottom = full[LANES:, LANES:] * halves[1]
                bottom = jnp.concatenate([jnp.zeros_like(bottom), bottom], axis=1)
                return jnp.concatenate([top, bottom], axis=0).astype(BF16)

            mixed = weigh(nn(kp, qz))
            grad_scores = weigh(nt(vj, gj))
            out_ref[m * dv:(m + 1) * dv, :] = tn(vj, mixed)
            dq_ref[m * dk:(m + 1) * dk, :] = nn(kt[j * dk:(j + 1) * dk], grad_scores)
            dv_ref[:, m * dv:(m + 1) * dv] = nn(mixed, gj)
            mine = (wide_lane < dk) if j == 0 else (wide_lane >= dk)
            term = nn(grad_scores, jnp.where(mine, qp, jnp.zeros_like(qp)))
            dk_sum = term if dk_sum is None else dk_sum + term
        dk_ref[:, n * 2 * dk:(n + 1) * 2 * dk] = dk_sum


def carry_kernel(dims, levels, first, some, idx_ref, *refs):
    nh, dk, dv = dims
    count = len(some)
    ups = refs[:count]
    g_ref, qt_ref, sig_ref = refs[count:count + 3]
    far_ref = refs[-1]
    far_ref[...] = refs[count + 3][...] if len(refs) > count + 4 else jnp.zeros_like(far_ref)
    index = idx_ref[0]
    for m, up_ref in zip(some, ups):
        up = ((index >> m) & 1).astype(F32)
        found = []
        for h in range(nh):
            rows = slice(h * dk, (h + 1) * dk)
            r = h * levels + first + m
            x = nt(up_ref[rows, :], g_ref[:, h * dv:(h + 1) * dv])
            row = jnp.sum(x * qt_ref[rows, :].astype(F32), axis=0, keepdims=True)
            found.append(row * (sig_ref[r:r + 1, :] * up))
        far_ref[m * nh:(m + 1) * nh, :] = jnp.concatenate(found, axis=0).astype(BF16)


def put_in_order(bits, head_ref, gp_ref, sorted_ref):
    count = 1 << bits
    own = gp_ref.shape[0] // count
    for n in range(count):
        away = sum(((n >> k) & 1) << (bits - 1 - k) for k in range(bits))
        at = pl.multiple_of((head_ref[0] ^ away) * own, 16)
        sorted_ref[pl.ds(at, own), :] = gp_ref[n * own:(n + 1) * own, :]


def near_wgrad_kernel(bits, inner, idx_ref, head_ref, xt_ref, gp_ref, send_ref, keep_ref, sorted_ref):
    put_in_order(bits, head_ref, gp_ref, sorted_ref)
    part_ways(nt(xt_ref[...], sorted_ref[...]), (idx_ref[0] & 1) == 1, send_ref, keep_ref, inner)


def far_wgrad_kernel(inner, idx_ref, head_ref, xt_ref, *refs):
    gathered, (keep_ref, one_ref, two_ref, both_ref, sorted_ref) = refs[:-5], refs[-5:]
    for away, gp_ref in enumerate(gathered):
        own = gp_ref.shape[0]
        sorted_ref[pl.ds(pl.multiple_of((head_ref[0] ^ away) * own, 16), own), :] = gp_ref[...]
    total = nt(xt_ref[...], sorted_ref[...])
    right, upper = (idx_ref[0] & 1) == 1, ((idx_ref[0] >> 1) & 1) == 1
    for e in range(total.shape[0] // (4 * inner)):
        parts = [total[(4 * e + n) * inner:(4 * e + n + 1) * inner] for n in range(4)]
        kept, sent = jnp.where(right, parts[1], parts[0]), jnp.where(right, parts[0], parts[1])
        kept_up, sent_up = jnp.where(right, parts[3], parts[2]), jnp.where(right, parts[2], parts[3])
        at = slice(e * inner, (e + 1) * inner)
        keep_ref[at, :] = jnp.where(upper, kept_up, kept)
        one_ref[at, :] = jnp.where(upper, sent_up, sent).astype(BF16)
        two_ref[at, :] = jnp.where(upper, kept, kept_up).astype(BF16)
        both_ref[at, :] = jnp.where(upper, sent, sent_up).astype(BF16)


def merge_kernel(bit, inner, idx_ref, near_ref, near_got, far_ref, one_ref, two_ref, both_ref, place_ref,
                 send_ref, keep_ref):
    far = far_ref[...] + one_ref[...].astype(F32) + two_ref[...].astype(F32) + both_ref[...].astype(F32)
    total = near_ref[...] + near_got[...].astype(F32) + lax.dot_general(
        far, place_ref[...], (((1,), (0,)), ((), ())), preferred_element_type=F32, precision=lax.Precision.HIGHEST)
    part_ways(total, ((idx_ref[0] >> bit) & 1) == 1, send_ref, keep_ref, inner)


def join_kernel(top, count, idx_ref, kv_ref, *refs):
    ups = refs[:count]
    gu_ref, send_ref = refs[count:]
    upper = ((idx_ref[0] >> top) & 1) == 1

    @pl.when(upper)
    def _():
        send_ref[...] = gu_ref[top]

    @pl.when(jnp.logical_not(upper))
    def _():
        total = kv_ref[...]
        for up in ups:
            total = total + up[...].astype(F32)
        send_ref[...] = total.astype(BF16)


def pend_kernel(bit, top, idx_ref, *refs):
    gots, (gu_ref, send_ref) = refs[:-2], refs[-2:]
    index = idx_ref[0]
    total = jnp.where(((index >> top) & 1) == 1, 0.0, gots[0][...].astype(F32))
    for got in gots[1:]:
        total = total + got[...].astype(F32)
    send_ref[...] = (total + jnp.where(((index >> bit) & 1) == 1, gu_ref[bit].astype(F32), 0.0)).astype(BF16)


def final_kernel(dims, levels, first, count, cuts, idx_ref, *refs):
    nh, dk, dv = dims
    top = count - 1
    ups, gots = refs[:count], refs[count:2 * count]
    qt_ref, lw_ref, g_ref, ds_ref, k_ref, v_ref = refs[2 * count:2 * count + 6]
    at = 2 * count + 6 + 4 * (len(cuts) - 1)
    local = refs[2 * count + 6:at]
    (near_ref, far_ref, place_ref, w_ref, out_hbm, dq_hbm, dx_hbm, dk_hbm, dv_hbm,
     out_ref, dq_ref, dx_ref, dk_ref, dv_ref, sems) = refs[at:]
    index = idx_ref[0]
    copies = []

    def send(buf_ref, hbm_ref, cols):
        copies.append(leave(buf_ref, hbm_ref, sems.at[len(copies)], cols))

    def piece(kind, pair):
        part = sum(pair >= cut for cut in cuts) - 1
        return local[4 * part + kind], pair - cuts[part]

    def weights(h, m):
        r = h * levels + first + m
        return lw_ref[r:r + 1, :] * ((index >> m) & 1).astype(F32)

    for h in range(nh):
        rows = slice(h * dk, (h + 1) * dk)
        local_ref, n = piece(0, h // 2)
        n = 2 * n + h % 2
        total = local_ref[n * dv:(n + 1) * dv, :]
        for m in range(count):
            total = total + tn(ups[m][rows, :], qt_ref[rows, :]) * weights(h, m)
        out_ref[:, h * dv:(h + 1) * dv] = total.astype(BF16).T
        if h % 2:
            send(out_ref, out_hbm, slice((h - 1) * dv, (h + 1) * dv))
    for pair in range(nh // 2):
        halves = []
        for j in range(2):
            h = 2 * pair + j
            local_ref, n = piece(1, pair)
            n = 2 * n + j
            total = local_ref[n * dk:(n + 1) * dk, :]
            for m in range(count):
                total = total + nt(ups[m][h * dk:(h + 1) * dk, :], g_ref[:, h * dv:(h + 1) * dv]) * weights(h, m)
            halves.append(total)
        cols = slice(pair * 2 * dk, (pair + 1) * 2 * dk)
        dq_ref[:, cols] = jnp.concatenate(halves, axis=0).astype(BF16).T
        send(dq_ref, dq_hbm, cols)
    gp = (near_ref[...].astype(F32) + tn(place_ref[...].astype(BF16), far_ref[...])).astype(BF16)
    dx_ref[...] = lax.dot_general(
        gp, w_ref[...], (((0,), (1,)), ((), ())), preferred_element_type=F32).astype(BF16)
    send(dx_ref, dx_hbm, slice(0, dx_ref.shape[1]))
    upper = ((index >> top) & 1) == 1
    zero = jnp.zeros((dk, dv), BF16)
    for pair in range(nh // 2):
        pair_rows = slice(pair * 2 * dk, (pair + 1) * 2 * dk)
        total = ds_ref[pair_rows, :] + jnp.where(upper, 0.0, gots[0][pair_rows, :].astype(F32))
        for got in gots[1:]:
            total = total + got[pair_rows, :].astype(F32)
        adj = [total[:dk].astype(BF16), total[dk:].astype(BF16)]
        kp = k_ref[:, pair * 2 * dk:(pair + 1) * 2 * dk]
        dkl_ref, p = piece(2, pair)
        dvl_ref, p = piece(3, pair)
        total = dkl_ref[:, p * 2 * dk:(p + 1) * 2 * dk]
        for j in range(2):
            h = 2 * pair + j
            padded = jnp.concatenate([adj[j], zero] if j == 0 else [zero, adj[j]], axis=0)
            cols = slice(h * dv, (h + 1) * dv)
            total = total + nt(v_ref[:, cols], padded)
            near = dvl_ref[:, (2 * p + j) * dv:(2 * p + j + 1) * dv]
            dv_ref[:, cols] = (near + nn(kp, padded)).astype(BF16)
        dk_ref[:, pair * 2 * dk:(pair + 1) * 2 * dk] = total.astype(BF16)
        send(dv_ref, dv_hbm, slice(2 * pair * dv, (2 * pair + 2) * dv))
        send(dk_ref, dk_hbm, slice(pair * 2 * dk, (pair + 1) * 2 * dk))
    for copy in copies:
        copy.wait()


def gather_heads(value, head_bits):
    full = value
    for bit in reversed(range(head_bits)):
        full = jnp.concatenate([full, swap(full, "head", bit)], axis=0)
    return full


def body(hidden, w, queries, keys, values, d_out, d_state):
    tokens, width = hidden.shape
    dims = d_state.shape
    nh, dk, dv = dims
    n_seq, n_head = lax.axis_size("seq"), lax.axis_size("head")
    seq_bits, head_bits = n_seq.bit_length() - 1, n_head.bit_length() - 1
    top = seq_bits - 1
    cols = w.shape[1]
    levels = cols // (nh * n_head)
    own = nh * levels
    far = nh * seq_bits
    far_own = -(-far // 16) * 16
    far_cols = far_own * n_head
    first = tokens.bit_length()
    per = width // n_seq
    rows = nh * dk
    S = jax.ShapeDtypeStruct
    idx, head_idx = [jnp.reshape(lax.axis_index(axis), (1,)) for axis in ("seq", "head")]

    hbm = pl.BlockSpec(memory_space=pltpu.HBM)
    kv, kvb, w_near, x_near = call(
        functools.partial(state_kernel, dims),
        [S((rows, dv), F32), S((rows, dv), BF16), S(w.shape, BF16), S(hidden.shape, BF16)],
        [SM] * 2 + [hbm] * 4, 2 * tokens * rows * dv,
        scratch_shapes=[pltpu.VMEM((tokens, rows), BF16), pltpu.VMEM((tokens, nh * dv), BF16),
                        pltpu.SemaphoreType.DMA((4,))])(
                            idx, head_idx, *[pltpu.with_memory_space_constraint(a, pltpu.HBM) for a in (keys, values, w, hidden)])
    send, keep, xt = call(
        functools.partial(project_kernel, head_bits - 1),
        [S((cols // 2, tokens), BF16), S((cols // 2, tokens), F32), S((width, tokens), BF16)], [SM] + [VM] * 2,
        2 * tokens * width * cols)(head_idx, w_near, x_near)

    total, up = kv, kvb
    ups = []
    for bit in range(top):
        partner = swap(up, "seq", bit)
        ups.append(partner)
        if bit < top - 1:
            total = total + partner.astype(F32)
            up = total.astype(BF16)

    got = swap(send, "head", head_bits - 1)
    for bit in reversed(range(head_bits - 1)):
        n = keep.shape[0] // 2
        send, keep = call(
            functools.partial(fold_kernel, bit, n), [S((n, tokens), BF16), S((n, tokens), F32)],
            [SM] + [VM] * 2, n * tokens)(head_idx, keep, got)
        got = swap(send, "head", bit)

    gl = call(
        functools.partial(level_kernel, dims, levels), [S((own, tokens), F32)], [VM] * 4,
        2 * tokens * tokens * nh * (dk + dv))(keys, queries, values, d_out)[0]
    sig, lw, near, qt, gu = call(
        functools.partial(weight_kernel, dims, levels, first, seq_bits),
        [S((own, tokens), F32), S((own, tokens), F32), S((own, tokens), BF16), S((rows, tokens), BF16),
         S((seq_bits, rows, dv), BF16)],
        [VM] * 5, 2 * tokens * rows * dv * seq_bits)(keep, got, gl, queries, d_out)

    up = call(functools.partial(join_kernel, top, top), [S((rows, dv), BF16)], [SM] + [VM] * (top + 2),
              rows * dv)(idx, kv, *ups, gu)[0]
    partner = swap(up, "seq", top)
    ups.append(partner)
    far_rows = []
    for some in (tuple(range(top)), (top,)):
        far_rows = call(
            functools.partial(carry_kernel, dims, levels, first, some), [S((far_own, tokens), BF16)],
            [SM] + [VM] * (len(some) + 3 + len(far_rows)), 2 * tokens * rows * dv * len(some))(
                idx, *[ups[m] for m in some], d_out, qt, sig, *far_rows)
    far_rows = far_rows[0]
    gots = [partner]
    for bit in reversed(range(top)):
        down = call(functools.partial(pend_kernel, bit, top), [S((rows, dv), BF16)], [SM] + [VM] * (len(gots) + 1),
                    rows * dv)(idx, *gots, gu)[0]
        gots.append(swap(down, "seq", bit))

    near_all = gather_heads(near, head_bits)
    n = width // 2
    send, near_w, near_all = call(
        functools.partial(near_wgrad_kernel, head_bits, per),
        [S((n, cols), BF16), S((n, cols), F32), S((cols, tokens), BF16)],
        [SM] * 2 + [VM] * 2, 2 * tokens * width * cols)(idx, head_idx, xt, near_all)
    got = swap(send, "seq", 0)
    n = n // 2
    send, near_w = call(
        functools.partial(fold_kernel, 1, per), [S((n, cols), BF16), S((n, cols), F32)],
        [SM] + [VM] * 2, n * cols)(idx, near_w, got)
    near_got = swap(send, "seq", 1)

    far_all = [far_rows] + [exchange(far_rows, "head", away) for away in range(1, n_head)]
    far_w, one, two, both, far_all = call(
        functools.partial(far_wgrad_kernel, per),
        [S((n, far_cols), F32)] + [S((n, far_cols), BF16)] * 3 + [S((far_cols, tokens), BF16)],
        [SM] * 2 + [VM] * (n_head + 1), 2 * tokens * width * far_cols)(idx, head_idx, xt, *far_all)
    far_gots = [exchange(one, "seq", 1), exchange(two, "seq", 2),
                exchange(both, "seq", 3)]

    col = jnp.arange(cols, dtype=jnp.int32)[None, :]
    row = jnp.arange(far_cols, dtype=jnp.int32)[:, None]
    within = row % far_own
    at = (row // far_own * nh + within % nh) * levels + first + within // nh
    place = ((at == col) & (within < far)).astype(F32)
    n = n // 2
    send, keep = call(
        functools.partial(merge_kernel, 2, per), [S((n, cols), BF16), S((n, cols), F32)], [SM] + [VM] * 7,
        4 * n * far_cols * cols)(idx, near_w, near_got, far_w, *far_gots, place)
    got = swap(send, "seq", 2)
    for bit in range(3, seq_bits):
        n = n // 2
        send, keep = call(
            functools.partial(fold_kernel, bit, per), [S((n, cols), BF16), S((n, cols), F32)],
            [SM] + [VM] * 2, n * cols)(idx, keep, got)
        got = swap(send, "seq", bit)
    d_w = keep + got.astype(F32)

    local = []
    cuts = (0, nh // 8, nh // 4, nh // 2)
    for part in range(3):
        pairs = tuple(range(cuts[part], cuts[part + 1]))
        heads = 2 * len(pairs)
        local += call(
            functools.partial(local_kernel, dims, levels, pairs),
            [S((heads * dv, tokens), F32), S((heads * dk, tokens), F32), S((tokens, heads * dk), F32),
             S((tokens, heads * dv), F32)],
            [VM] * 5, 2 * tokens * tokens * heads * (3 * dk + 3 * dv),
        )(keys, queries, values, d_out, lw)
    shapes = [(tokens, nh * dv), (tokens, rows), (tokens, width), (tokens, rows), (tokens, nh * dv)]
    out, d_queries, d_hidden, d_keys, d_values = call(
        functools.partial(final_kernel, dims, levels, first, seq_bits, cuts), [S(shape, BF16) for shape in shapes],
        [SM] + [VM] * (2 * seq_bits + 10 + len(local)), 8 * tokens * rows * dv * seq_bits, out_specs=[hbm] * len(shapes),
        scratch_shapes=[pltpu.VMEM(shape, BF16) for shape in shapes] + [pltpu.SemaphoreType.DMA((2 * nh + 1,))])(
            idx, *ups, *gots, qt, lw, d_out, d_state.reshape(rows, dv), keys, values, *local,
            near_all, far_all, place, w_near)
    return (out, d_queries, d_keys, d_values, d_hidden, d_w)


def solution(mesh):
    two = P("seq", "head")
    return jax.shard_map(
        body, mesh=mesh,
        in_specs=(two, P("head", None), two, two, two, two, P("head", None, None)),
        out_specs=(two, two, two, two, two, P(("head", "seq"), None)),
        check_vma=False)
```

```python
import functools

import jax
import jax.numpy as jnp
from jax import lax
from jax.experimental import pallas as pl
from jax.experimental.pallas import tpu as pltpu
from jax.sharding import PartitionSpec as P


F32 = jnp.float32
BF16 = jnp.bfloat16
LANES = 128
SUB = 8
VM = pl.BlockSpec(memory_space=pltpu.VMEM)
SM = pl.BlockSpec(memory_space=pltpu.SMEM)


def nn(a, b):
    return lax.dot_general(a, b, (((1,), (0,)), ((), ())), preferred_element_type=F32)


def nt(a, b):
    return lax.dot_general(a, b, (((1,), (1,)), ((), ())), preferred_element_type=F32)


def tn(a, b):
    return lax.dot_general(a, b, (((0,), (0,)), ((), ())), preferred_element_type=F32)


def call(kernel, outs, specs, flops, **kwargs):
    size = sum(o.size * o.dtype.itemsize for o in outs)
    return pl.pallas_call(
        kernel,
        out_shape=outs,
        in_specs=specs,
        compiler_params=pltpu.CompilerParams(vmem_limit_bytes=16 << 20),
        cost_estimate=pl.CostEstimate(flops=flops, bytes_accessed=2 * size, transcendentals=0),
        **kwargs,
    )


def leave(buf_ref, hbm_ref, sem, cols):
    copy = pltpu.make_async_copy(buf_ref.at[:, cols], hbm_ref.at[:, cols], sem)
    copy.start()
    return copy


def exchange(value, axis, mask):
    pairs = [(source, source ^ mask) for source in range(lax.axis_size(axis))]
    return lax.ppermute(value, axis, pairs)


def swap(value, axis, bit):
    return exchange(value, axis, 1 << bit)


def state_kernel(dims, idx_ref, head_ref, k_hbm, v_hbm, w_hbm, x_hbm, kv_ref, kvb_ref, w_ref, x_ref, k_ref, v_ref, sems):
    nh, dk, dv = dims
    copies = [pltpu.make_async_copy(src, dst, sems.at[n]) for n, (src, dst) in enumerate(
        ((k_hbm, k_ref), (v_hbm, v_ref), (w_hbm, w_ref), (x_hbm, x_ref)))]
    for copy in copies:
        copy.start()
    copies[0].wait()
    copies[1].wait()
    for pair in range(nh // 2):
        turned = k_ref[:, pair * 2 * dk:(pair + 1) * 2 * dk].T
        for j in range(2):
            h = 2 * pair + j
            kv = nn(turned[j * dk:(j + 1) * dk], v_ref[:, h * dv:(h + 1) * dv])
            kv_ref[h * dk:(h + 1) * dk, :] = kv
            kvb_ref[h * dk:(h + 1) * dk, :] = kv.astype(BF16)
    copies[2].wait()
    copies[3].wait()


def part_ways(entries, upper, send_ref, keep_ref, inner):
    n = entries.shape[0] // inner
    for e in range(n // 2):
        low = entries[2 * e * inner:(2 * e + 1) * inner]
        high = entries[(2 * e + 1) * inner:(2 * e + 2) * inner]
        out = slice(e * inner, (e + 1) * inner)
        send_ref[out, :] = jnp.where(upper, low, high).astype(BF16)
        keep_ref[out, :] = jnp.where(upper, high, low)


def project_kernel(bit, idx_ref, w_ref, x_ref, send_ref, keep_ref, xt_ref):
    xt = x_ref[...].T
    xt_ref[...] = xt
    upper = ((idx_ref[0] >> bit) & 1) == 1
    part_ways(tn(w_ref[...], xt), upper, send_ref, keep_ref, keep_ref.shape[0])


def fold_kernel(bit, inner, idx_ref, keep_in, got_ref, send_ref, keep_ref):
    upper = ((idx_ref[0] >> bit) & 1) == 1
    part_ways(keep_in[...] + got_ref[...].astype(F32), upper, send_ref, keep_ref, inner)


def weight_kernel(dims, levels, first, count, keep_ref, got_ref, gl_ref, q_ref, g_ref,
                  sig_ref, lw_ref, near_ref, qt_ref, gu_ref):
    nh, dk, dv = dims
    proj = keep_ref[...] + got_ref[...].astype(F32)
    sig = jax.nn.sigmoid(proj)
    sig_ref[...] = sig
    near_ref[...] = (gl_ref[...] * sig).astype(BF16)
    lw_ref[...] = jnp.maximum(proj, 0.0) + jnp.log1p(jnp.exp(-jnp.abs(proj)))
    for pair in range(nh // 2):
        turned = q_ref[:, pair * 2 * dk:(pair + 1) * 2 * dk].T
        qt_ref[pair * 2 * dk:(pair + 1) * 2 * dk, :] = turned
        wide = turned.astype(F32)
        for j in range(2):
            h = 2 * pair + j
            scaled = jnp.concatenate(
                [wide[j * dk:(j + 1) * dk] * lw_ref[h * levels + first + m:h * levels + first + m + 1, :]
                 for m in range(count)], axis=0)
            grad = nn(scaled.astype(BF16), g_ref[:, h * dv:(h + 1) * dv])
            for m in range(count):
                gu_ref[m, h * dk:(h + 1) * dk, :] = grad[m * dk:(m + 1) * dk].astype(BF16)


def spread_half(rows, lane, low, t_low):
    digits = (low ^ t_low)
    near = jnp.where(digits == 0, rows[0], jnp.where(digits < 2, rows[1], jnp.where(digits < 4, rows[2], rows[3])))
    near = jnp.where(low <= t_low, near, 0.0)
    parts = []
    for a in range(LANES // SUB):
        value = None
        for l in reversed(range(4, 8)):
            if (a >> (l - 4)) & 1 == 0:
                end = (((a >> (l - 3)) + 1) << (l - 3)) * SUB
                value = rows[l] if value is None else jnp.where(lane < end, rows[l], value)
        value = near if value is None else jnp.where(lane < (a + 1) * SUB, near, value)
        if a:
            value = jnp.where(lane < a * SUB, 0.0, value)
        parts.append(value)
    return jnp.concatenate(parts, axis=0)


def level_sums(prod, lane, low, t_low):
    count = LANES // SUB
    group = lane // SUB
    cur = [prod[a * SUB:(a + 1) * SUB] for a in range(count)]
    near = jnp.zeros_like(cur[0])
    for a in range(count):
        near = jnp.where(group == a, cur[a], near)
    near = jnp.where(low <= t_low, near, 0.0)
    digits = low ^ t_low
    sums = []
    for l in range(4):
        lo, hi = (0, 1) if l == 0 else (1 << (l - 1), 1 << l)
        sums.append(jnp.where((digits >= lo) & (digits < hi), near, 0.0))
    for l in range(4, 8):
        total = jnp.zeros_like(near)
        for a in range(0, len(cur), 2):
            total = jnp.where((lane >> (l - 1)) == a + 1, cur[a], total)
        sums.append(total)
        cur = [cur[a] + cur[a + 1] for a in range(0, len(cur), 2)]
    return [jnp.sum(s, axis=0, keepdims=True) for s in sums]


def level_kernel(dims, levels, k_ref, q_ref, v_ref, g_ref, gl_ref):
    nh, dk, dv = dims
    lane = lax.broadcasted_iota(jnp.int32, (SUB, LANES), 1)
    low = lax.broadcasted_iota(jnp.int32, (SUB, LANES), 0)
    t_low = lane % SUB
    gl_ref[...] = jnp.zeros_like(gl_ref)
    for pair in range(nh // 2):
        kp = k_ref[:, pair * 2 * dk:(pair + 1) * 2 * dk]
        qt = q_ref[:, pair * 2 * dk:(pair + 1) * 2 * dk].T
        zero = jnp.zeros_like(qt[:dk])
        for j in range(2):
            h = 2 * pair + j
            base = h * levels
            qz = jnp.concatenate([qt[:dk], zero] if j == 0 else [zero, qt[dk:]], axis=0)
            prod = nn(kp, qz) * nt(v_ref[:, h * dv:(h + 1) * dv], g_ref[:, h * dv:(h + 1) * dv])
            for x in range(2):
                part = slice(x * LANES, (x + 1) * LANES)
                sums = level_sums(prod[part, part], lane, low, t_low)
                for l in range(8):
                    gl_ref[base + l:base + l + 1, part] = sums[l]
            gl_ref[base + 8:base + 9, LANES:] = jnp.sum(prod[:LANES, LANES:], axis=0, keepdims=True)


def local_kernel(dims, levels, pairs, k_ref, q_ref, v_ref, g_ref, lw_ref, out_ref, dq_ref, dk_ref, dv_ref):
    _, dk, dv = dims
    lane = lax.broadcasted_iota(jnp.int32, (SUB, LANES), 1)
    low = lax.broadcasted_iota(jnp.int32, (SUB, LANES), 0)
    t_low = lane % SUB
    for n, pair in enumerate(pairs):
        kp = k_ref[:, pair * 2 * dk:(pair + 1) * 2 * dk]
        qp = q_ref[:, pair * 2 * dk:(pair + 1) * 2 * dk]
        kt, qt = kp.T, qp.T
        zero = jnp.zeros_like(qt[:dk])
        wide_lane = lax.broadcasted_iota(jnp.int32, qp.shape, 1)
        dk_sum = None
        for j in range(2):
            h, m = 2 * pair + j, 2 * n + j
            vj = v_ref[:, h * dv:(h + 1) * dv]
            gj = g_ref[:, h * dv:(h + 1) * dv]
            qz = jnp.concatenate([qt[:dk], zero] if j == 0 else [zero, qt[dk:]], axis=0)
            base = h * levels
            cross = lw_ref[base + 8:base + 9, LANES:]
            halves = []
            for x in range(2):
                rows = [jnp.broadcast_to(lw_ref[base + l:base + l + 1, x * LANES:(x + 1) * LANES], (SUB, LANES))
                        for l in range(8)]
                halves.append(spread_half(rows, lane, low, t_low))

            def weigh(full):
                top = jnp.concatenate([full[:LANES, :LANES] * halves[0], full[:LANES, LANES:] * cross], axis=1)
                bottom = full[LANES:, LANES:] * halves[1]
                bottom = jnp.concatenate([jnp.zeros_like(bottom), bottom], axis=1)
                return jnp.concatenate([top, bottom], axis=0).astype(BF16)

            mixed = weigh(nn(kp, qz))
            grad_scores = weigh(nt(vj, gj))
            out_ref[m * dv:(m + 1) * dv, :] = tn(vj, mixed)
            dq_ref[m * dk:(m + 1) * dk, :] = nn(kt[j * dk:(j + 1) * dk], grad_scores)
            dv_ref[:, m * dv:(m + 1) * dv] = nn(mixed, gj)
            mine = (wide_lane < dk) if j == 0 else (wide_lane >= dk)
            term = nn(grad_scores, jnp.where(mine, qp, jnp.zeros_like(qp)))
            dk_sum = term if dk_sum is None else dk_sum + term
        dk_ref[:, n * 2 * dk:(n + 1) * 2 * dk] = dk_sum


def carry_kernel(dims, levels, first, some, idx_ref, *refs):
    nh, dk, dv = dims
    count = len(some)
    ups = refs[:count]
    g_ref, qt_ref, sig_ref = refs[count:count + 3]
    far_ref = refs[-1]
    far_ref[...] = refs[count + 3][...] if len(refs) > count + 4 else jnp.zeros_like(far_ref)
    index = idx_ref[0]
    for m, up_ref in zip(some, ups):
        up = ((index >> m) & 1).astype(F32)
        found = []
        for h in range(nh):
            rows = slice(h * dk, (h + 1) * dk)
            r = h * levels + first + m
            x = nt(up_ref[rows, :], g_ref[:, h * dv:(h + 1) * dv])
            row = jnp.sum(x * qt_ref[rows, :].astype(F32), axis=0, keepdims=True)
            found.append(row * (sig_ref[r:r + 1, :] * up))
        far_ref[m * nh:(m + 1) * nh, :] = jnp.concatenate(found, axis=0).astype(BF16)


def put_in_order(bits, head_ref, gp_ref, sorted_ref):
    count = 1 << bits
    own = gp_ref.shape[0] // count
    for n in range(count):
        away = sum(((n >> k) & 1) << (bits - 1 - k) for k in range(bits))
        at = pl.multiple_of((head_ref[0] ^ away) * own, 16)
        sorted_ref[pl.ds(at, own), :] = gp_ref[n * own:(n + 1) * own, :]


def near_wgrad_kernel(bits, inner, idx_ref, head_ref, xt_ref, gp_ref, send_ref, keep_ref, sorted_ref):
    put_in_order(bits, head_ref, gp_ref, sorted_ref)
    part_ways(nt(xt_ref[...], sorted_ref[...]), (idx_ref[0] & 2) == 2, send_ref, keep_ref, inner)


def far_wgrad_kernel(inner, idx_ref, head_ref, xt_ref, *refs):
    gathered, (keep_ref, one_ref, two_ref, both_ref, sorted_ref) = refs[:-5], refs[-5:]
    for away, gp_ref in enumerate(gathered):
        own = gp_ref.shape[0]
        sorted_ref[pl.ds(pl.multiple_of((head_ref[0] ^ away) * own, 16), own), :] = gp_ref[...]
    total = nt(xt_ref[...], sorted_ref[...])
    right, upper = (idx_ref[0] & 1) == 1, ((idx_ref[0] >> 1) & 1) == 1
    for e in range(total.shape[0] // (4 * inner)):
        parts = [total[(4 * e + n) * inner:(4 * e + n + 1) * inner] for n in range(4)]
        kept, sent = jnp.where(right, parts[1], parts[0]), jnp.where(right, parts[0], parts[1])
        kept_up, sent_up = jnp.where(right, parts[3], parts[2]), jnp.where(right, parts[2], parts[3])
        at = slice(e * inner, (e + 1) * inner)
        keep_ref[at, :] = jnp.where(upper, kept_up, kept)
        one_ref[at, :] = jnp.where(upper, sent_up, sent).astype(BF16)
        two_ref[at, :] = jnp.where(upper, kept, kept_up).astype(BF16)
        both_ref[at, :] = jnp.where(upper, sent, sent_up).astype(BF16)


def merge_kernel(bit, inner, idx_ref, near_ref, near_got, far_ref, one_ref, two_ref, both_ref, place_ref,
                 send_ref, keep_ref):
    far = far_ref[...] + one_ref[...].astype(F32) + two_ref[...].astype(F32) + both_ref[...].astype(F32)
    total = near_ref[...] + near_got[...].astype(F32) + lax.dot_general(
        far, place_ref[...], (((1,), (0,)), ((), ())), preferred_element_type=F32, precision=lax.Precision.HIGHEST)
    part_ways(total, ((idx_ref[0] >> bit) & 1) == 1, send_ref, keep_ref, inner)


def join_kernel(top, count, idx_ref, kv_ref, *refs):
    ups = refs[:count]
    gu_ref, send_ref = refs[count:]
    upper = ((idx_ref[0] >> top) & 1) == 1

    @pl.when(upper)
    def _():
        send_ref[...] = gu_ref[top]

    @pl.when(jnp.logical_not(upper))
    def _():
        total = kv_ref[...]
        for up in ups:
            total = total + up[...].astype(F32)
        send_ref[...] = total.astype(BF16)


def pend_kernel(bit, top, idx_ref, *refs):
    gots, (gu_ref, send_ref) = refs[:-2], refs[-2:]
    index = idx_ref[0]
    total = jnp.where(((index >> top) & 1) == 1, 0.0, gots[0][...].astype(F32))
    for got in gots[1:]:
        total = total + got[...].astype(F32)
    send_ref[...] = (total + jnp.where(((index >> bit) & 1) == 1, gu_ref[bit].astype(F32), 0.0)).astype(BF16)


def final_kernel(dims, levels, first, count, cuts, idx_ref, *refs):
    nh, dk, dv = dims
    top = count - 1
    ups, gots = refs[:count], refs[count:2 * count]
    qt_ref, lw_ref, g_ref, ds_ref, k_ref, v_ref = refs[2 * count:2 * count + 6]
    at = 2 * count + 6 + 4 * (len(cuts) - 1)
    local = refs[2 * count + 6:at]
    (near_ref, far_ref, place_ref, w_ref, out_hbm, dq_hbm, dx_hbm, dk_hbm, dv_hbm,
     out_ref, dq_ref, dx_ref, dk_ref, dv_ref, sems) = refs[at:]
    index = idx_ref[0]
    copies = []

    def send(buf_ref, hbm_ref, cols):
        copies.append(leave(buf_ref, hbm_ref, sems.at[len(copies)], cols))

    def piece(kind, pair):
        part = sum(pair >= cut for cut in cuts) - 1
        return local[4 * part + kind], pair - cuts[part]

    def weights(h, m):
        r = h * levels + first + m
        return lw_ref[r:r + 1, :] * ((index >> m) & 1).astype(F32)

    for h in range(nh):
        rows = slice(h * dk, (h + 1) * dk)
        local_ref, n = piece(0, h // 2)
        n = 2 * n + h % 2
        total = local_ref[n * dv:(n + 1) * dv, :]
        for m in range(count):
            total = total + tn(ups[m][rows, :], qt_ref[rows, :]) * weights(h, m)
        out_ref[:, h * dv:(h + 1) * dv] = total.astype(BF16).T
        if h % 2:
            send(out_ref, out_hbm, slice((h - 1) * dv, (h + 1) * dv))
    for pair in range(nh // 2):
        halves = []
        for j in range(2):
            h = 2 * pair + j
            local_ref, n = piece(1, pair)
            n = 2 * n + j
            total = local_ref[n * dk:(n + 1) * dk, :]
            for m in range(count):
                total = total + nt(ups[m][h * dk:(h + 1) * dk, :], g_ref[:, h * dv:(h + 1) * dv]) * weights(h, m)
            halves.append(total)
        cols = slice(pair * 2 * dk, (pair + 1) * 2 * dk)
        dq_ref[:, cols] = jnp.concatenate(halves, axis=0).astype(BF16).T
        send(dq_ref, dq_hbm, cols)
    gp = (near_ref[...].astype(F32) + tn(place_ref[...].astype(BF16), far_ref[...])).astype(BF16)
    dx_ref[...] = lax.dot_general(
        gp, w_ref[...], (((0,), (1,)), ((), ())), preferred_element_type=F32).astype(BF16)
    send(dx_ref, dx_hbm, slice(0, dx_ref.shape[1]))
    upper = ((index >> top) & 1) == 1
    zero = jnp.zeros((dk, dv), BF16)
    for pair in range(nh // 2):
        pair_rows = slice(pair * 2 * dk, (pair + 1) * 2 * dk)
        total = ds_ref[pair_rows, :] + jnp.where(upper, 0.0, gots[0][pair_rows, :].astype(F32))
        for got in gots[1:]:
            total = total + got[pair_rows, :].astype(F32)
        adj = [total[:dk].astype(BF16), total[dk:].astype(BF16)]
        kp = k_ref[:, pair * 2 * dk:(pair + 1) * 2 * dk]
        dkl_ref, p = piece(2, pair)
        dvl_ref, p = piece(3, pair)
        total = dkl_ref[:, p * 2 * dk:(p + 1) * 2 * dk]
        for j in range(2):
            h = 2 * pair + j
            padded = jnp.concatenate([adj[j], zero] if j == 0 else [zero, adj[j]], axis=0)
            cols = slice(h * dv, (h + 1) * dv)
            total = total + nt(v_ref[:, cols], padded)
            near = dvl_ref[:, (2 * p + j) * dv:(2 * p + j + 1) * dv]
            dv_ref[:, cols] = (near + nn(kp, padded)).astype(BF16)
        dk_ref[:, pair * 2 * dk:(pair + 1) * 2 * dk] = total.astype(BF16)
        send(dv_ref, dv_hbm, slice(2 * pair * dv, (2 * pair + 2) * dv))
        send(dk_ref, dk_hbm, slice(pair * 2 * dk, (pair + 1) * 2 * dk))
    for copy in copies:
        copy.wait()


def gather_heads(value, head_bits):
    full = value
    for bit in reversed(range(head_bits)):
        full = jnp.concatenate([full, swap(full, "head", bit)], axis=0)
    return full


def body(hidden, w, queries, keys, values, d_out, d_state):
    tokens, width = hidden.shape
    dims = d_state.shape
    nh, dk, dv = dims
    n_seq, n_head = lax.axis_size("seq"), lax.axis_size("head")
    seq_bits, head_bits = n_seq.bit_length() - 1, n_head.bit_length() - 1
    top = seq_bits - 1
    cols = w.shape[1]
    levels = cols // (nh * n_head)
    own = nh * levels
    far = nh * seq_bits
    far_own = -(-far // 16) * 16
    far_cols = far_own * n_head
    first = tokens.bit_length()
    per = width // n_seq
    rows = nh * dk
    S = jax.ShapeDtypeStruct
    idx, head_idx = [jnp.reshape(lax.axis_index(axis), (1,)) for axis in ("seq", "head")]

    hbm = pl.BlockSpec(memory_space=pltpu.HBM)
    kv, kvb, w_near, x_near = call(
        functools.partial(state_kernel, dims),
        [S((rows, dv), F32), S((rows, dv), BF16), S(w.shape, BF16), S(hidden.shape, BF16)],
        [SM] * 2 + [hbm] * 4, 2 * tokens * rows * dv,
        scratch_shapes=[pltpu.VMEM((tokens, rows), BF16), pltpu.VMEM((tokens, nh * dv), BF16),
                        pltpu.SemaphoreType.DMA((4,))])(
                            idx, head_idx, *[pltpu.with_memory_space_constraint(a, pltpu.HBM) for a in (keys, values, w, hidden)])
    send, keep, xt = call(
        functools.partial(project_kernel, head_bits - 1),
        [S((cols // 2, tokens), BF16), S((cols // 2, tokens), F32), S((width, tokens), BF16)], [SM] + [VM] * 2,
        2 * tokens * width * cols)(head_idx, w_near, x_near)

    total, up = kv, kvb
    ups = []
    for bit in range(top):
        partner = swap(up, "seq", bit)
        ups.append(partner)
        if bit < top - 1:
            total = total + partner.astype(F32)
            up = total.astype(BF16)

    got = swap(send, "head", head_bits - 1)
    for bit in reversed(range(head_bits - 1)):
        n = keep.shape[0] // 2
        send, keep = call(
            functools.partial(fold_kernel, bit, n), [S((n, tokens), BF16), S((n, tokens), F32)],
            [SM] + [VM] * 2, n * tokens)(head_idx, keep, got)
        got = swap(send, "head", bit)

    gl = call(
        functools.partial(level_kernel, dims, levels), [S((own, tokens), F32)], [VM] * 4,
        2 * tokens * tokens * nh * (dk + dv))(keys, queries, values, d_out)[0]
    sig, lw, near, qt, gu = call(
        functools.partial(weight_kernel, dims, levels, first, seq_bits),
        [S((own, tokens), F32), S((own, tokens), F32), S((own, tokens), BF16), S((rows, tokens), BF16),
         S((seq_bits, rows, dv), BF16)],
        [VM] * 5, 2 * tokens * rows * dv * seq_bits)(keep, got, gl, queries, d_out)

    up = call(functools.partial(join_kernel, top, top), [S((rows, dv), BF16)], [SM] + [VM] * (top + 2),
              rows * dv)(idx, kv, *ups, gu)[0]
    partner = swap(up, "seq", top)
    ups.append(partner)
    far_rows = []
    for some in (tuple(range(top)), (top,)):
        far_rows = call(
            functools.partial(carry_kernel, dims, levels, first, some), [S((far_own, tokens), BF16)],
            [SM] + [VM] * (len(some) + 3 + len(far_rows)), 2 * tokens * rows * dv * len(some))(
                idx, *[ups[m] for m in some], d_out, qt, sig, *far_rows)
    far_rows = far_rows[0]
    gots = [partner]
    for bit in reversed(range(top)):
        down = call(functools.partial(pend_kernel, bit, top), [S((rows, dv), BF16)], [SM] + [VM] * (len(gots) + 1),
                    rows * dv)(idx, *gots, gu)[0]
        gots.append(swap(down, "seq", bit))

    near_all = gather_heads(near, head_bits)
    n = width // 2
    send, near_w, near_all = call(
        functools.partial(near_wgrad_kernel, head_bits, 2 * per),
        [S((n, cols), BF16), S((n, cols), F32), S((cols, tokens), BF16)],
        [SM] * 2 + [VM] * 2, 2 * tokens * width * cols)(idx, head_idx, xt, near_all)
    got = swap(send, "seq", 1)
    n = n // 2
    send, near_w = call(
        functools.partial(fold_kernel, 0, per), [S((n, cols), BF16), S((n, cols), F32)],
        [SM] + [VM] * 2, n * cols)(idx, near_w, got)
    near_got = swap(send, "seq", 0)

    far_all = [far_rows] + [exchange(far_rows, "head", away) for away in range(1, n_head)]
    far_w, one, two, both, far_all = call(
        functools.partial(far_wgrad_kernel, per),
        [S((n, far_cols), F32)] + [S((n, far_cols), BF16)] * 3 + [S((far_cols, tokens), BF16)],
        [SM] * 2 + [VM] * (n_head + 1), 2 * tokens * width * far_cols)(idx, head_idx, xt, *far_all)
    far_gots = [exchange(one, "seq", 1), exchange(two, "seq", 2),
                exchange(both, "seq", 3)]

    col = jnp.arange(cols, dtype=jnp.int32)[None, :]
    row = jnp.arange(far_cols, dtype=jnp.int32)[:, None]
    within = row % far_own
    at = (row // far_own * nh + within % nh) * levels + first + within // nh
    place = ((at == col) & (within < far)).astype(F32)
    n = n // 2
    send, keep = call(
        functools.partial(merge_kernel, 2, per), [S((n, cols), BF16), S((n, cols), F32)], [SM] + [VM] * 7,
        4 * n * far_cols * cols)(idx, near_w, near_got, far_w, *far_gots, place)
    got = swap(send, "seq", 2)
    for bit in range(3, seq_bits):
        n = n // 2
        send, keep = call(
            functools.partial(fold_kernel, bit, per), [S((n, cols), BF16), S((n, cols), F32)],
            [SM] + [VM] * 2, n * cols)(idx, keep, got)
        got = swap(send, "seq", bit)
    d_w = keep + got.astype(F32)

    local = []
    cuts = (0, nh // 8, nh // 4, nh // 2)
    for part in range(3):
        pairs = tuple(range(cuts[part], cuts[part + 1]))
        heads = 2 * len(pairs)
        local += call(
            functools.partial(local_kernel, dims, levels, pairs),
            [S((heads * dv, tokens), F32), S((heads * dk, tokens), F32), S((tokens, heads * dk), F32),
             S((tokens, heads * dv), F32)],
            [VM] * 5, 2 * tokens * tokens * heads * (3 * dk + 3 * dv),
        )(keys, queries, values, d_out, lw)
    shapes = [(tokens, nh * dv), (tokens, rows), (tokens, width), (tokens, rows), (tokens, nh * dv)]
    out, d_queries, d_hidden, d_keys, d_values = call(
        functools.partial(final_kernel, dims, levels, first, seq_bits, cuts), [S(shape, BF16) for shape in shapes],
        [SM] + [VM] * (2 * seq_bits + 10 + len(local)), 8 * tokens * rows * dv * seq_bits, out_specs=[hbm] * len(shapes),
        scratch_shapes=[pltpu.VMEM(shape, BF16) for shape in shapes] + [pltpu.SemaphoreType.DMA((2 * nh + 1,))])(
            idx, *ups, *gots, qt, lw, d_out, d_state.reshape(rows, dv), keys, values, *local,
            near_all, far_all, place, w_near)
    return (out, d_queries, d_keys, d_values, d_hidden, d_w)


def solution(mesh):
    two = P("seq", "head")
    return jax.shard_map(
        body, mesh=mesh,
        in_specs=(two, P("head", None), two, two, two, two, P("head", None, None)),
        out_specs=(two, two, two, two, two, P(("head", "seq"), None)),
        check_vma=False)
```

```python
import functools

import jax
import jax.numpy as jnp
from jax import lax
from jax.experimental import pallas as pl
from jax.experimental.pallas import tpu as pltpu
from jax.sharding import PartitionSpec as P


F32 = jnp.float32
BF16 = jnp.bfloat16
LANES = 128
SUB = 8
VM = pl.BlockSpec(memory_space=pltpu.VMEM)
SM = pl.BlockSpec(memory_space=pltpu.SMEM)


def nn(a, b):
    return lax.dot_general(a, b, (((1,), (0,)), ((), ())), preferred_element_type=F32)


def nt(a, b):
    return lax.dot_general(a, b, (((1,), (1,)), ((), ())), preferred_element_type=F32)


def tn(a, b):
    return lax.dot_general(a, b, (((0,), (0,)), ((), ())), preferred_element_type=F32)


def call(kernel, outs, specs, flops, **kwargs):
    size = sum(o.size * o.dtype.itemsize for o in outs)
    return pl.pallas_call(
        kernel,
        out_shape=outs,
        in_specs=specs,
        compiler_params=pltpu.CompilerParams(vmem_limit_bytes=16 << 20),
        cost_estimate=pl.CostEstimate(flops=flops, bytes_accessed=2 * size, transcendentals=0),
        **kwargs,
    )


def leave(buf_ref, hbm_ref, sem, cols):
    copy = pltpu.make_async_copy(buf_ref.at[:, cols], hbm_ref.at[:, cols], sem)
    copy.start()
    return copy


def exchange(value, axis, mask):
    pairs = [(source, source ^ mask) for source in range(lax.axis_size(axis))]
    return lax.ppermute(value, axis, pairs)


def swap(value, axis, bit):
    return exchange(value, axis, 1 << bit)


def state_kernel(dims, idx_ref, head_ref, k_hbm, v_hbm, w_hbm, x_hbm, kv_ref, kvb_ref, w_ref, x_ref, k_ref, v_ref, sems):
    nh, dk, dv = dims
    copies = [pltpu.make_async_copy(src, dst, sems.at[n]) for n, (src, dst) in enumerate(
        ((k_hbm, k_ref), (v_hbm, v_ref), (w_hbm, w_ref), (x_hbm, x_ref)))]
    for copy in copies:
        copy.start()
    copies[0].wait()
    copies[1].wait()
    for pair in range(nh // 2):
        turned = k_ref[:, pair * 2 * dk:(pair + 1) * 2 * dk].T
        for j in range(2):
            h = 2 * pair + j
            kv = nn(turned[j * dk:(j + 1) * dk], v_ref[:, h * dv:(h + 1) * dv])
            kv_ref[h * dk:(h + 1) * dk, :] = kv
            kvb_ref[h * dk:(h + 1) * dk, :] = kv.astype(BF16)
    copies[2].wait()
    copies[3].wait()


def part_ways(entries, upper, send_ref, keep_ref, inner):
    n = entries.shape[0] // inner
    for e in range(n // 2):
        low = entries[2 * e * inner:(2 * e + 1) * inner]
        high = entries[(2 * e + 1) * inner:(2 * e + 2) * inner]
        out = slice(e * inner, (e + 1) * inner)
        send_ref[out, :] = jnp.where(upper, low, high).astype(BF16)
        keep_ref[out, :] = jnp.where(upper, high, low)


def project_kernel(bit, idx_ref, w_ref, x_ref, send_ref, keep_ref, xt_ref):
    xt = x_ref[...].T
    xt_ref[...] = xt
    upper = ((idx_ref[0] >> bit) & 1) == 1
    part_ways(tn(w_ref[...], xt), upper, send_ref, keep_ref, keep_ref.shape[0])


def fold_kernel(bit, inner, idx_ref, keep_in, got_ref, send_ref, keep_ref):
    upper = ((idx_ref[0] >> bit) & 1) == 1
    part_ways(keep_in[...] + got_ref[...].astype(F32), upper, send_ref, keep_ref, inner)


def weight_kernel(dims, levels, first, count, keep_ref, got_ref, gl_ref, q_ref, g_ref,
                  sig_ref, lw_ref, near_ref, qt_ref, gu_ref):
    nh, dk, dv = dims
    proj = keep_ref[...] + got_ref[...].astype(F32)
    sig = jax.nn.sigmoid(proj)
    sig_ref[...] = sig
    near_ref[...] = (gl_ref[...] * sig).astype(BF16)
    lw_ref[...] = jnp.maximum(proj, 0.0) + jnp.log1p(jnp.exp(-jnp.abs(proj)))
    for pair in range(nh // 2):
        turned = q_ref[:, pair * 2 * dk:(pair + 1) * 2 * dk].T
        qt_ref[pair * 2 * dk:(pair + 1) * 2 * dk, :] = turned
        wide = turned.astype(F32)
        for j in range(2):
            h = 2 * pair + j
            scaled = jnp.concatenate(
                [wide[j * dk:(j + 1) * dk] * lw_ref[h * levels + first + m:h * levels + first + m + 1, :]
                 for m in range(count)], axis=0)
            grad = nn(scaled.astype(BF16), g_ref[:, h * dv:(h + 1) * dv])
            for m in range(count):
                gu_ref[m, h * dk:(h + 1) * dk, :] = grad[m * dk:(m + 1) * dk].astype(BF16)


def spread_half(rows, lane, low, t_low):
    digits = (low ^ t_low)
    near = jnp.where(digits == 0, rows[0], jnp.where(digits < 2, rows[1], jnp.where(digits < 4, rows[2], rows[3])))
    near = jnp.where(low <= t_low, near, 0.0)
    parts = []
    for a in range(LANES // SUB):
        value = None
        for l in reversed(range(4, 8)):
            if (a >> (l - 4)) & 1 == 0:
                end = (((a >> (l - 3)) + 1) << (l - 3)) * SUB
                value = rows[l] if value is None else jnp.where(lane < end, rows[l], value)
        value = near if value is None else jnp.where(lane < (a + 1) * SUB, near, value)
        if a:
            value = jnp.where(lane < a * SUB, 0.0, value)
        parts.append(value)
    return jnp.concatenate(parts, axis=0)


def level_sums(prod, lane, low, t_low):
    count = LANES // SUB
    group = lane // SUB
    cur = [prod[a * SUB:(a + 1) * SUB] for a in range(count)]
    near = jnp.zeros_like(cur[0])
    for a in range(count):
        near = jnp.where(group == a, cur[a], near)
    near = jnp.where(low <= t_low, near, 0.0)
    digits = low ^ t_low
    sums = []
    for l in range(4):
        lo, hi = (0, 1) if l == 0 else (1 << (l - 1), 1 << l)
        sums.append(jnp.where((digits >= lo) & (digits < hi), near, 0.0))
    for l in range(4, 8):
        total = jnp.zeros_like(near)
        for a in range(0, len(cur), 2):
            total = jnp.where((lane >> (l - 1)) == a + 1, cur[a], total)
        sums.append(total)
        cur = [cur[a] + cur[a + 1] for a in range(0, len(cur), 2)]
    return [jnp.sum(s, axis=0, keepdims=True) for s in sums]


def level_kernel(dims, levels, k_ref, q_ref, v_ref, g_ref, gl_ref):
    nh, dk, dv = dims
    lane = lax.broadcasted_iota(jnp.int32, (SUB, LANES), 1)
    low = lax.broadcasted_iota(jnp.int32, (SUB, LANES), 0)
    t_low = lane % SUB
    gl_ref[...] = jnp.zeros_like(gl_ref)
    for pair in range(nh // 2):
        kp = k_ref[:, pair * 2 * dk:(pair + 1) * 2 * dk]
        qt = q_ref[:, pair * 2 * dk:(pair + 1) * 2 * dk].T
        zero = jnp.zeros_like(qt[:dk])
        for j in range(2):
            h = 2 * pair + j
            base = h * levels
            qz = jnp.concatenate([qt[:dk], zero] if j == 0 else [zero, qt[dk:]], axis=0)
            prod = nn(kp, qz) * nt(v_ref[:, h * dv:(h + 1) * dv], g_ref[:, h * dv:(h + 1) * dv])
            for x in range(2):
                part = slice(x * LANES, (x + 1) * LANES)
                sums = level_sums(prod[part, part], lane, low, t_low)
                for l in range(8):
                    gl_ref[base + l:base + l + 1, part] = sums[l]
            gl_ref[base + 8:base + 9, LANES:] = jnp.sum(prod[:LANES, LANES:], axis=0, keepdims=True)


def local_kernel(dims, levels, pairs, k_ref, q_ref, v_ref, g_ref, lw_ref, out_ref, dq_ref, dk_ref, dv_ref):
    _, dk, dv = dims
    lane = lax.broadcasted_iota(jnp.int32, (SUB, LANES), 1)
    low = lax.broadcasted_iota(jnp.int32, (SUB, LANES), 0)
    t_low = lane % SUB
    for n, pair in enumerate(pairs):
        kp = k_ref[:, pair * 2 * dk:(pair + 1) * 2 * dk]
        qp = q_ref[:, pair * 2 * dk:(pair + 1) * 2 * dk]
        kt, qt = kp.T, qp.T
        zero = jnp.zeros_like(qt[:dk])
        wide_lane = lax.broadcasted_iota(jnp.int32, qp.shape, 1)
        dk_sum = None
        for j in range(2):
            h, m = 2 * pair + j, 2 * n + j
            vj = v_ref[:, h * dv:(h + 1) * dv]
            gj = g_ref[:, h * dv:(h + 1) * dv]
            qz = jnp.concatenate([qt[:dk], zero] if j == 0 else [zero, qt[dk:]], axis=0)
            base = h * levels
            cross = lw_ref[base + 8:base + 9, LANES:]
            halves = []
            for x in range(2):
                rows = [jnp.broadcast_to(lw_ref[base + l:base + l + 1, x * LANES:(x + 1) * LANES], (SUB, LANES))
                        for l in range(8)]
                halves.append(spread_half(rows, lane, low, t_low))

            def weigh(full):
                top = jnp.concatenate([full[:LANES, :LANES] * halves[0], full[:LANES, LANES:] * cross], axis=1)
                bottom = full[LANES:, LANES:] * halves[1]
                bottom = jnp.concatenate([jnp.zeros_like(bottom), bottom], axis=1)
                return jnp.concatenate([top, bottom], axis=0).astype(BF16)

            mixed = weigh(nn(kp, qz))
            grad_scores = weigh(nt(vj, gj))
            out_ref[m * dv:(m + 1) * dv, :] = tn(vj, mixed)
            dq_ref[m * dk:(m + 1) * dk, :] = nn(kt[j * dk:(j + 1) * dk], grad_scores)
            dv_ref[:, m * dv:(m + 1) * dv] = nn(mixed, gj)
            mine = (wide_lane < dk) if j == 0 else (wide_lane >= dk)
            term = nn(grad_scores, jnp.where(mine, qp, jnp.zeros_like(qp)))
            dk_sum = term if dk_sum is None else dk_sum + term
        dk_ref[:, n * 2 * dk:(n + 1) * 2 * dk] = dk_sum


def carry_kernel(dims, levels, first, some, idx_ref, *refs):
    nh, dk, dv = dims
    count = len(some)
    ups = refs[:count]
    g_ref, qt_ref, sig_ref = refs[count:count + 3]
    far_ref = refs[-1]
    far_ref[...] = refs[count + 3][...] if len(refs) > count + 4 else jnp.zeros_like(far_ref)
    index = idx_ref[0]
    for m, up_ref in zip(some, ups):
        up = ((index >> m) & 1).astype(F32)
        found = []
        for h in range(nh):
            rows = slice(h * dk, (h + 1) * dk)
            r = h * levels + first + m
            x = nt(up_ref[rows, :], g_ref[:, h * dv:(h + 1) * dv])
            row = jnp.sum(x * qt_ref[rows, :].astype(F32), axis=0, keepdims=True)
            found.append(row * (sig_ref[r:r + 1, :] * up))
        far_ref[m * nh:(m + 1) * nh, :] = jnp.concatenate(found, axis=0).astype(BF16)


def put_in_order(bits, head_ref, gp_ref, sorted_ref):
    count = 1 << bits
    own = gp_ref.shape[0] // count
    for n in range(count):
        away = sum(((n >> k) & 1) << (bits - 1 - k) for k in range(bits))
        at = pl.multiple_of((head_ref[0] ^ away) * own, 16)
        sorted_ref[pl.ds(at, own), :] = gp_ref[n * own:(n + 1) * own, :]


def near_wgrad_kernel(bits, inner, idx_ref, head_ref, xt_ref, gp_ref, send_ref, keep_ref, sorted_ref):
    put_in_order(bits, head_ref, gp_ref, sorted_ref)
    part_ways(nt(xt_ref[...], sorted_ref[...]), (idx_ref[0] & 2) == 2, send_ref, keep_ref, inner)


def far_wgrad_kernel(inner, idx_ref, head_ref, xt_ref, near_in, near_got, *refs):
    gathered, (keep_ref, one_ref, two_ref, both_ref, near_ref, sorted_ref) = refs[:-6], refs[-6:]
    for away, gp_ref in enumerate(gathered):
        own = gp_ref.shape[0]
        sorted_ref[pl.ds(pl.multiple_of((head_ref[0] ^ away) * own, 16), own), :] = gp_ref[...]
    total = nt(xt_ref[...], sorted_ref[...])
    right, upper = (idx_ref[0] & 1) == 1, ((idx_ref[0] >> 1) & 1) == 1
    cols = near_ref.shape[1]
    part_ways(near_in[...] + near_got[...].astype(F32), right, one_ref.at[:, :cols], near_ref, inner)
    for e in range(total.shape[0] // (4 * inner)):
        parts = [total[(4 * e + n) * inner:(4 * e + n + 1) * inner] for n in range(4)]
        kept, sent = jnp.where(right, parts[1], parts[0]), jnp.where(right, parts[0], parts[1])
        kept_up, sent_up = jnp.where(right, parts[3], parts[2]), jnp.where(right, parts[2], parts[3])
        at = slice(e * inner, (e + 1) * inner)
        keep_ref[at, :] = jnp.where(upper, kept_up, kept)
        one_ref[at, cols:] = jnp.where(upper, sent_up, sent).astype(BF16)
        two_ref[at, :] = jnp.where(upper, kept, kept_up).astype(BF16)
        both_ref[at, :] = jnp.where(upper, sent, sent_up).astype(BF16)


def merge_kernel(bit, inner, idx_ref, near_ref, far_ref, one_ref, two_ref, both_ref, place_ref, send_ref, keep_ref):
    cols = near_ref.shape[1]
    far = far_ref[...] + one_ref[:, cols:].astype(F32) + two_ref[...].astype(F32) + both_ref[...].astype(F32)
    total = near_ref[...] + one_ref[:, :cols].astype(F32) + lax.dot_general(
        far, place_ref[...], (((1,), (0,)), ((), ())), preferred_element_type=F32, precision=lax.Precision.HIGHEST)
    part_ways(total, ((idx_ref[0] >> bit) & 1) == 1, send_ref, keep_ref, inner)


def join_kernel(top, count, idx_ref, kv_ref, *refs):
    ups = refs[:count]
    gu_ref, send_ref = refs[count:]
    upper = ((idx_ref[0] >> top) & 1) == 1

    @pl.when(upper)
    def _():
        send_ref[...] = gu_ref[top]

    @pl.when(jnp.logical_not(upper))
    def _():
        total = kv_ref[...]
        for up in ups:
            total = total + up[...].astype(F32)
        send_ref[...] = total.astype(BF16)


def pend_kernel(bit, top, idx_ref, *refs):
    gots, (gu_ref, send_ref) = refs[:-2], refs[-2:]
    index = idx_ref[0]
    total = jnp.where(((index >> top) & 1) == 1, 0.0, gots[0][...].astype(F32))
    for got in gots[1:]:
        total = total + got[...].astype(F32)
    send_ref[...] = (total + jnp.where(((index >> bit) & 1) == 1, gu_ref[bit].astype(F32), 0.0)).astype(BF16)


def final_kernel(dims, levels, first, count, cuts, idx_ref, *refs):
    nh, dk, dv = dims
    top = count - 1
    ups, gots = refs[:count], refs[count:2 * count]
    qt_ref, lw_ref, g_ref, ds_ref, k_ref, v_ref = refs[2 * count:2 * count + 6]
    at = 2 * count + 6 + 4 * (len(cuts) - 1)
    local = refs[2 * count + 6:at]
    (near_ref, far_ref, place_ref, w_ref, out_hbm, dq_hbm, dx_hbm, dk_hbm, dv_hbm,
     out_ref, dq_ref, dx_ref, dk_ref, dv_ref, sems) = refs[at:]
    index = idx_ref[0]
    copies = []

    def send(buf_ref, hbm_ref, cols):
        copies.append(leave(buf_ref, hbm_ref, sems.at[len(copies)], cols))

    def piece(kind, pair):
        part = sum(pair >= cut for cut in cuts) - 1
        return local[4 * part + kind], pair - cuts[part]

    def weights(h, m):
        r = h * levels + first + m
        return lw_ref[r:r + 1, :] * ((index >> m) & 1).astype(F32)

    for h in range(nh):
        rows = slice(h * dk, (h + 1) * dk)
        local_ref, n = piece(0, h // 2)
        n = 2 * n + h % 2
        total = local_ref[n * dv:(n + 1) * dv, :]
        for m in range(count):
            total = total + tn(ups[m][rows, :], qt_ref[rows, :]) * weights(h, m)
        out_ref[:, h * dv:(h + 1) * dv] = total.astype(BF16).T
        if h % 2:
            send(out_ref, out_hbm, slice((h - 1) * dv, (h + 1) * dv))
    for pair in range(nh // 2):
        halves = []
        for j in range(2):
            h = 2 * pair + j
            local_ref, n = piece(1, pair)
            n = 2 * n + j
            total = local_ref[n * dk:(n + 1) * dk, :]
            for m in range(count):
                total = total + nt(ups[m][h * dk:(h + 1) * dk, :], g_ref[:, h * dv:(h + 1) * dv]) * weights(h, m)
            halves.append(total)
        cols = slice(pair * 2 * dk, (pair + 1) * 2 * dk)
        dq_ref[:, cols] = jnp.concatenate(halves, axis=0).astype(BF16).T
        send(dq_ref, dq_hbm, cols)
    gp = (near_ref[...].astype(F32) + tn(place_ref[...].astype(BF16), far_ref[...])).astype(BF16)
    dx_ref[...] = lax.dot_general(
        gp, w_ref[...], (((0,), (1,)), ((), ())), preferred_element_type=F32).astype(BF16)
    send(dx_ref, dx_hbm, slice(0, dx_ref.shape[1]))
    upper = ((index >> top) & 1) == 1
    zero = jnp.zeros((dk, dv), BF16)
    for pair in range(nh // 2):
        pair_rows = slice(pair * 2 * dk, (pair + 1) * 2 * dk)
        total = ds_ref[pair_rows, :] + jnp.where(upper, 0.0, gots[0][pair_rows, :].astype(F32))
        for got in gots[1:]:
            total = total + got[pair_rows, :].astype(F32)
        adj = [total[:dk].astype(BF16), total[dk:].astype(BF16)]
        kp = k_ref[:, pair * 2 * dk:(pair + 1) * 2 * dk]
        dkl_ref, p = piece(2, pair)
        dvl_ref, p = piece(3, pair)
        total = dkl_ref[:, p * 2 * dk:(p + 1) * 2 * dk]
        for j in range(2):
            h = 2 * pair + j
            padded = jnp.concatenate([adj[j], zero] if j == 0 else [zero, adj[j]], axis=0)
            cols = slice(h * dv, (h + 1) * dv)
            total = total + nt(v_ref[:, cols], padded)
            near = dvl_ref[:, (2 * p + j) * dv:(2 * p + j + 1) * dv]
            dv_ref[:, cols] = (near + nn(kp, padded)).astype(BF16)
        dk_ref[:, pair * 2 * dk:(pair + 1) * 2 * dk] = total.astype(BF16)
        send(dv_ref, dv_hbm, slice(2 * pair * dv, (2 * pair + 2) * dv))
        send(dk_ref, dk_hbm, slice(pair * 2 * dk, (pair + 1) * 2 * dk))
    for copy in copies:
        copy.wait()


def gather_heads(value, head_bits):
    full = value
    for bit in reversed(range(head_bits)):
        full = jnp.concatenate([full, swap(full, "head", bit)], axis=0)
    return full


def body(hidden, w, queries, keys, values, d_out, d_state):
    tokens, width = hidden.shape
    dims = d_state.shape
    nh, dk, dv = dims
    n_seq, n_head = lax.axis_size("seq"), lax.axis_size("head")
    seq_bits, head_bits = n_seq.bit_length() - 1, n_head.bit_length() - 1
    top = seq_bits - 1
    cols = w.shape[1]
    levels = cols // (nh * n_head)
    own = nh * levels
    far = nh * seq_bits
    far_own = -(-far // 16) * 16
    far_cols = far_own * n_head
    first = tokens.bit_length()
    per = width // n_seq
    rows = nh * dk
    S = jax.ShapeDtypeStruct
    idx, head_idx = [jnp.reshape(lax.axis_index(axis), (1,)) for axis in ("seq", "head")]

    hbm = pl.BlockSpec(memory_space=pltpu.HBM)
    kv, kvb, w_near, x_near = call(
        functools.partial(state_kernel, dims),
        [S((rows, dv), F32), S((rows, dv), BF16), S(w.shape, BF16), S(hidden.shape, BF16)],
        [SM] * 2 + [hbm] * 4, 2 * tokens * rows * dv,
        scratch_shapes=[pltpu.VMEM((tokens, rows), BF16), pltpu.VMEM((tokens, nh * dv), BF16),
                        pltpu.SemaphoreType.DMA((4,))])(
                            idx, head_idx, *[pltpu.with_memory_space_constraint(a, pltpu.HBM) for a in (keys, values, w, hidden)])
    send, keep, xt = call(
        functools.partial(project_kernel, head_bits - 1),
        [S((cols // 2, tokens), BF16), S((cols // 2, tokens), F32), S((width, tokens), BF16)], [SM] + [VM] * 2,
        2 * tokens * width * cols)(head_idx, w_near, x_near)

    total, up = kv, kvb
    ups = []
    for bit in range(top):
        partner = swap(up, "seq", bit)
        ups.append(partner)
        if bit < top - 1:
            total = total + partner.astype(F32)
            up = total.astype(BF16)

    got = swap(send, "head", head_bits - 1)
    for bit in reversed(range(head_bits - 1)):
        n = keep.shape[0] // 2
        send, keep = call(
            functools.partial(fold_kernel, bit, n), [S((n, tokens), BF16), S((n, tokens), F32)],
            [SM] + [VM] * 2, n * tokens)(head_idx, keep, got)
        got = swap(send, "head", bit)

    gl = call(
        functools.partial(level_kernel, dims, levels), [S((own, tokens), F32)], [VM] * 4,
        2 * tokens * tokens * nh * (dk + dv))(keys, queries, values, d_out)[0]
    sig, lw, near, qt, gu = call(
        functools.partial(weight_kernel, dims, levels, first, seq_bits),
        [S((own, tokens), F32), S((own, tokens), F32), S((own, tokens), BF16), S((rows, tokens), BF16),
         S((seq_bits, rows, dv), BF16)],
        [VM] * 5, 2 * tokens * rows * dv * seq_bits)(keep, got, gl, queries, d_out)

    up = call(functools.partial(join_kernel, top, top), [S((rows, dv), BF16)], [SM] + [VM] * (top + 2),
              rows * dv)(idx, kv, *ups, gu)[0]
    partner = swap(up, "seq", top)
    ups.append(partner)
    far_rows = []
    for some in (tuple(range(top)), (top,)):
        far_rows = call(
            functools.partial(carry_kernel, dims, levels, first, some), [S((far_own, tokens), BF16)],
            [SM] + [VM] * (len(some) + 3 + len(far_rows)), 2 * tokens * rows * dv * len(some))(
                idx, *[ups[m] for m in some], d_out, qt, sig, *far_rows)
    far_rows = far_rows[0]
    gots = [partner]
    for bit in reversed(range(top)):
        down = call(functools.partial(pend_kernel, bit, top), [S((rows, dv), BF16)], [SM] + [VM] * (len(gots) + 1),
                    rows * dv)(idx, *gots, gu)[0]
        gots.append(swap(down, "seq", bit))

    near_all = gather_heads(near, head_bits)
    n = width // 2
    send, near_w, near_all = call(
        functools.partial(near_wgrad_kernel, head_bits, 2 * per),
        [S((n, cols), BF16), S((n, cols), F32), S((cols, tokens), BF16)],
        [SM] * 2 + [VM] * 2, 2 * tokens * width * cols)(idx, head_idx, xt, near_all)
    near_got = swap(send, "seq", 1)

    far_all = [far_rows] + [exchange(far_rows, "head", away) for away in range(1, n_head)]
    n = n // 2
    part, joined = S((n, far_cols), BF16), S((n, cols + far_cols), BF16)
    far_w, one, two, both, near_w, far_all = call(
        functools.partial(far_wgrad_kernel, per),
        [S((n, far_cols), F32), joined, part, part, S((n, cols), F32), S((far_cols, tokens), BF16)],
        [SM] * 2 + [VM] * (n_head + 3), 2 * tokens * width * far_cols)(
            idx, head_idx, xt, near_w, near_got, *far_all)
    far_gots = [exchange(one, "seq", 1), exchange(two, "seq", 2),
                exchange(both, "seq", 3)]

    col = jnp.arange(cols, dtype=jnp.int32)[None, :]
    row = jnp.arange(far_cols, dtype=jnp.int32)[:, None]
    within = row % far_own
    at = (row // far_own * nh + within % nh) * levels + first + within // nh
    place = ((at == col) & (within < far)).astype(F32)
    n = n // 2
    send, keep = call(
        functools.partial(merge_kernel, 2, per), [S((n, cols), BF16), S((n, cols), F32)], [SM] + [VM] * 6,
        4 * n * far_cols * cols)(idx, near_w, far_w, *far_gots, place)
    got = swap(send, "seq", 2)
    for bit in range(3, seq_bits):
        n = n // 2
        send, keep = call(
            functools.partial(fold_kernel, bit, per), [S((n, cols), BF16), S((n, cols), F32)],
            [SM] + [VM] * 2, n * cols)(idx, keep, got)
        got = swap(send, "seq", bit)
    d_w = keep + got.astype(F32)

    local = []
    cuts = (0, nh // 8, nh // 4, nh // 2)
    for part in range(3):
        pairs = tuple(range(cuts[part], cuts[part + 1]))
        heads = 2 * len(pairs)
        local += call(
            functools.partial(local_kernel, dims, levels, pairs),
            [S((heads * dv, tokens), F32), S((heads * dk, tokens), F32), S((tokens, heads * dk), F32),
             S((tokens, heads * dv), F32)],
            [VM] * 5, 2 * tokens * tokens * heads * (3 * dk + 3 * dv),
        )(keys, queries, values, d_out, lw)
    shapes = [(tokens, nh * dv), (tokens, rows), (tokens, width), (tokens, rows), (tokens, nh * dv)]
    out, d_queries, d_hidden, d_keys, d_values = call(
        functools.partial(final_kernel, dims, levels, first, seq_bits, cuts), [S(shape, BF16) for shape in shapes],
        [SM] + [VM] * (2 * seq_bits + 10 + len(local)), 8 * tokens * rows * dv * seq_bits, out_specs=[hbm] * len(shapes),
        scratch_shapes=[pltpu.VMEM(shape, BF16) for shape in shapes] + [pltpu.SemaphoreType.DMA((2 * nh + 1,))])(
            idx, *ups, *gots, qt, lw, d_out, d_state.reshape(rows, dv), keys, values, *local,
            near_all, far_all, place, w_near)
    return (out, d_queries, d_keys, d_values, d_hidden, d_w)


def solution(mesh):
    two = P("seq", "head")
    return jax.shard_map(
        body, mesh=mesh,
        in_specs=(two, P("head", None), two, two, two, two, P("head", None, None)),
        out_specs=(two, two, two, two, two, P(("head", "seq"), None)),
        check_vma=False)
```

```python
import functools

import jax
import jax.numpy as jnp
from jax import lax
from jax.experimental import pallas as pl
from jax.experimental.pallas import tpu as pltpu
from jax.sharding import PartitionSpec as P


F32 = jnp.float32
BF16 = jnp.bfloat16
LANES = 128
SUB = 8
VM = pl.BlockSpec(memory_space=pltpu.VMEM)
SM = pl.BlockSpec(memory_space=pltpu.SMEM)


def nn(a, b):
    return lax.dot_general(a, b, (((1,), (0,)), ((), ())), preferred_element_type=F32)


def nt(a, b):
    return lax.dot_general(a, b, (((1,), (1,)), ((), ())), preferred_element_type=F32)


def tn(a, b):
    return lax.dot_general(a, b, (((0,), (0,)), ((), ())), preferred_element_type=F32)


def call(kernel, outs, specs, flops, **kwargs):
    size = sum(o.size * o.dtype.itemsize for o in outs)
    return pl.pallas_call(
        kernel,
        out_shape=outs,
        in_specs=specs,
        compiler_params=pltpu.CompilerParams(vmem_limit_bytes=16 << 20),
        cost_estimate=pl.CostEstimate(flops=flops, bytes_accessed=2 * size, transcendentals=0),
        **kwargs,
    )


def leave(buf_ref, hbm_ref, sem, cols):
    copy = pltpu.make_async_copy(buf_ref.at[:, cols], hbm_ref.at[:, cols], sem)
    copy.start()
    return copy


def exchange(value, axis, mask):
    pairs = [(source, source ^ mask) for source in range(lax.axis_size(axis))]
    return lax.ppermute(value, axis, pairs)


def swap(value, axis, bit):
    return exchange(value, axis, 1 << bit)


def state_kernel(dims, idx_ref, head_ref, k_hbm, v_hbm, w_hbm, x_hbm, kv_ref, kvb_ref, w_ref, x_ref, k_ref, v_ref, sems):
    nh, dk, dv = dims
    copies = [pltpu.make_async_copy(src, dst, sems.at[n]) for n, (src, dst) in enumerate(
        ((k_hbm, k_ref), (v_hbm, v_ref), (w_hbm, w_ref), (x_hbm, x_ref)))]
    for copy in copies:
        copy.start()
    copies[0].wait()
    copies[1].wait()
    for pair in range(nh // 2):
        turned = k_ref[:, pair * 2 * dk:(pair + 1) * 2 * dk].T
        for j in range(2):
            h = 2 * pair + j
            kv = nn(turned[j * dk:(j + 1) * dk], v_ref[:, h * dv:(h + 1) * dv])
            kv_ref[h * dk:(h + 1) * dk, :] = kv
            kvb_ref[h * dk:(h + 1) * dk, :] = kv.astype(BF16)
    copies[2].wait()
    copies[3].wait()


def part_ways(entries, upper, send_ref, keep_ref, inner):
    n = entries.shape[0] // inner
    for e in range(n // 2):
        low = entries[2 * e * inner:(2 * e + 1) * inner]
        high = entries[(2 * e + 1) * inner:(2 * e + 2) * inner]
        out = slice(e * inner, (e + 1) * inner)
        send_ref[out, :] = jnp.where(upper, low, high).astype(BF16)
        keep_ref[out, :] = jnp.where(upper, high, low)


def project_kernel(bit, idx_ref, w_ref, x_ref, send_ref, keep_ref, xt_ref):
    xt = x_ref[...].T
    xt_ref[...] = xt
    upper = ((idx_ref[0] >> bit) & 1) == 1
    part_ways(tn(w_ref[...], xt), upper, send_ref, keep_ref, keep_ref.shape[0])


def fold_kernel(bit, inner, idx_ref, keep_in, got_ref, send_ref, keep_ref):
    upper = ((idx_ref[0] >> bit) & 1) == 1
    part_ways(keep_in[...] + got_ref[...].astype(F32), upper, send_ref, keep_ref, inner)


def weight_kernel(dims, levels, first, count, keep_ref, got_ref, gl_ref, q_ref, g_ref,
                  sig_ref, lw_ref, near_ref, qt_ref, gu_ref):
    nh, dk, dv = dims
    proj = keep_ref[...] + got_ref[...].astype(F32)
    sig = jax.nn.sigmoid(proj)
    sig_ref[...] = sig
    near_ref[...] = (gl_ref[...] * sig).astype(BF16)
    lw_ref[...] = jnp.maximum(proj, 0.0) + jnp.log1p(jnp.exp(-jnp.abs(proj)))
    for pair in range(nh // 2):
        turned = q_ref[:, pair * 2 * dk:(pair + 1) * 2 * dk].T
        qt_ref[pair * 2 * dk:(pair + 1) * 2 * dk, :] = turned
        wide = turned.astype(F32)
        for j in range(2):
            h = 2 * pair + j
            scaled = jnp.concatenate(
                [wide[j * dk:(j + 1) * dk] * lw_ref[h * levels + first + m:h * levels + first + m + 1, :]
                 for m in range(count)], axis=0)
            grad = nn(scaled.astype(BF16), g_ref[:, h * dv:(h + 1) * dv])
            for m in range(count):
                gu_ref[m, h * dk:(h + 1) * dk, :] = grad[m * dk:(m + 1) * dk].astype(BF16)


def spread_half(rows, lane, low, t_low):
    digits = (low ^ t_low)
    near = jnp.where(digits == 0, rows[0], jnp.where(digits < 2, rows[1], jnp.where(digits < 4, rows[2], rows[3])))
    near = jnp.where(low <= t_low, near, 0.0)
    parts = []
    for a in range(LANES // SUB):
        value = None
        for l in reversed(range(4, 8)):
            if (a >> (l - 4)) & 1 == 0:
                end = (((a >> (l - 3)) + 1) << (l - 3)) * SUB
                value = rows[l] if value is None else jnp.where(lane < end, rows[l], value)
        value = near if value is None else jnp.where(lane < (a + 1) * SUB, near, value)
        if a:
            value = jnp.where(lane < a * SUB, 0.0, value)
        parts.append(value)
    return jnp.concatenate(parts, axis=0)


def level_sums(prod, lane, low, t_low):
    count = LANES // SUB
    group = lane // SUB
    cur = [prod[a * SUB:(a + 1) * SUB] for a in range(count)]
    near = jnp.zeros_like(cur[0])
    for a in range(count):
        near = jnp.where(group == a, cur[a], near)
    near = jnp.where(low <= t_low, near, 0.0)
    digits = low ^ t_low
    sums = []
    for l in range(4):
        lo, hi = (0, 1) if l == 0 else (1 << (l - 1), 1 << l)
        sums.append(jnp.where((digits >= lo) & (digits < hi), near, 0.0))
    for l in range(4, 8):
        total = jnp.zeros_like(near)
        for a in range(0, len(cur), 2):
            total = jnp.where((lane >> (l - 1)) == a + 1, cur[a], total)
        sums.append(total)
        cur = [cur[a] + cur[a + 1] for a in range(0, len(cur), 2)]
    return [jnp.sum(s, axis=0, keepdims=True) for s in sums]


def level_kernel(dims, levels, k_ref, q_ref, v_ref, g_ref, gl_ref):
    nh, dk, dv = dims
    lane = lax.broadcasted_iota(jnp.int32, (SUB, LANES), 1)
    low = lax.broadcasted_iota(jnp.int32, (SUB, LANES), 0)
    t_low = lane % SUB
    gl_ref[...] = jnp.zeros_like(gl_ref)
    for pair in range(nh // 2):
        kp = k_ref[:, pair * 2 * dk:(pair + 1) * 2 * dk]
        qt = q_ref[:, pair * 2 * dk:(pair + 1) * 2 * dk].T
        zero = jnp.zeros_like(qt[:dk])
        for j in range(2):
            h = 2 * pair + j
            base = h * levels
            qz = jnp.concatenate([qt[:dk], zero] if j == 0 else [zero, qt[dk:]], axis=0)
            prod = nn(kp, qz) * nt(v_ref[:, h * dv:(h + 1) * dv], g_ref[:, h * dv:(h + 1) * dv])
            for x in range(2):
                part = slice(x * LANES, (x + 1) * LANES)
                sums = level_sums(prod[part, part], lane, low, t_low)
                for l in range(8):
                    gl_ref[base + l:base + l + 1, part] = sums[l]
            gl_ref[base + 8:base + 9, LANES:] = jnp.sum(prod[:LANES, LANES:], axis=0, keepdims=True)


def local_kernel(dims, levels, pairs, k_ref, q_ref, v_ref, g_ref, lw_ref, out_ref, dq_ref, dk_ref, dv_ref):
    _, dk, dv = dims
    lane = lax.broadcasted_iota(jnp.int32, (SUB, LANES), 1)
    low = lax.broadcasted_iota(jnp.int32, (SUB, LANES), 0)
    t_low = lane % SUB
    for n, pair in enumerate(pairs):
        kp = k_ref[:, pair * 2 * dk:(pair + 1) * 2 * dk]
        qp = q_ref[:, pair * 2 * dk:(pair + 1) * 2 * dk]
        kt, qt = kp.T, qp.T
        zero = jnp.zeros_like(qt[:dk])
        wide_lane = lax.broadcasted_iota(jnp.int32, qp.shape, 1)
        dk_sum = None
        for j in range(2):
            h, m = 2 * pair + j, 2 * n + j
            vj = v_ref[:, h * dv:(h + 1) * dv]
            gj = g_ref[:, h * dv:(h + 1) * dv]
            qz = jnp.concatenate([qt[:dk], zero] if j == 0 else [zero, qt[dk:]], axis=0)
            base = h * levels
            cross = lw_ref[base + 8:base + 9, LANES:]
            halves = []
            for x in range(2):
                rows = [jnp.broadcast_to(lw_ref[base + l:base + l + 1, x * LANES:(x + 1) * LANES], (SUB, LANES))
                        for l in range(8)]
                halves.append(spread_half(rows, lane, low, t_low))

            def weigh(full):
                top = jnp.concatenate([full[:LANES, :LANES] * halves[0], full[:LANES, LANES:] * cross], axis=1)
                bottom = full[LANES:, LANES:] * halves[1]
                bottom = jnp.concatenate([jnp.zeros_like(bottom), bottom], axis=1)
                return jnp.concatenate([top, bottom], axis=0).astype(BF16)

            mixed = weigh(nn(kp, qz))
            grad_scores = weigh(nt(vj, gj))
            out_ref[m * dv:(m + 1) * dv, :] = tn(vj, mixed)
            dq_ref[m * dk:(m + 1) * dk, :] = nn(kt[j * dk:(j + 1) * dk], grad_scores)
            dv_ref[:, m * dv:(m + 1) * dv] = nn(mixed, gj)
            mine = (wide_lane < dk) if j == 0 else (wide_lane >= dk)
            term = nn(grad_scores, jnp.where(mine, qp, jnp.zeros_like(qp)))
            dk_sum = term if dk_sum is None else dk_sum + term
        dk_ref[:, n * 2 * dk:(n + 1) * 2 * dk] = dk_sum


def carry_kernel(dims, levels, first, some, idx_ref, *refs):
    nh, dk, dv = dims
    count = len(some)
    ups = refs[:count]
    g_ref, qt_ref, sig_ref = refs[count:count + 3]
    far_ref = refs[-1]
    far_ref[...] = refs[count + 3][...] if len(refs) > count + 4 else jnp.zeros_like(far_ref)
    index = idx_ref[0]
    for m, up_ref in zip(some, ups):
        up = ((index >> m) & 1).astype(F32)
        found = []
        for h in range(nh):
            rows = slice(h * dk, (h + 1) * dk)
            r = h * levels + first + m
            x = nt(up_ref[rows, :], g_ref[:, h * dv:(h + 1) * dv])
            row = jnp.sum(x * qt_ref[rows, :].astype(F32), axis=0, keepdims=True)
            found.append(row * (sig_ref[r:r + 1, :] * up))
        far_ref[m * nh:(m + 1) * nh, :] = jnp.concatenate(found, axis=0).astype(BF16)


def put_in_order(bits, head_ref, gp_ref, sorted_ref):
    count = 1 << bits
    own = gp_ref.shape[0] // count
    for n in range(count):
        away = sum(((n >> k) & 1) << (bits - 1 - k) for k in range(bits))
        at = pl.multiple_of((head_ref[0] ^ away) * own, 16)
        sorted_ref[pl.ds(at, own), :] = gp_ref[n * own:(n + 1) * own, :]


def near_wgrad_kernel(bits, inner, idx_ref, head_ref, xt_ref, gp_ref, send_ref, keep_ref, sorted_ref):
    put_in_order(bits, head_ref, gp_ref, sorted_ref)
    part_ways(nt(xt_ref[...], sorted_ref[...]), (idx_ref[0] & 2) == 2, send_ref, keep_ref, inner)


def far_wgrad_kernel(inner, idx_ref, head_ref, xt_ref, near_in, near_got, *refs):
    gathered, (keep_ref, one_ref, two_ref, both_ref, near_ref, sorted_ref) = refs[:-6], refs[-6:]
    for away, gp_ref in enumerate(gathered):
        own = gp_ref.shape[0]
        sorted_ref[pl.ds(pl.multiple_of((head_ref[0] ^ away) * own, 16), own), :] = gp_ref[...]
    total = nt(xt_ref[...], sorted_ref[...])
    right, upper = (idx_ref[0] & 1) == 1, ((idx_ref[0] >> 1) & 1) == 1
    cols = near_ref.shape[1]
    part_ways(near_in[...] + near_got[...].astype(F32), right, one_ref.at[:, :cols], near_ref, inner)
    for e in range(total.shape[0] // (4 * inner)):
        parts = [total[(4 * e + n) * inner:(4 * e + n + 1) * inner] for n in range(4)]
        kept, sent = jnp.where(right, parts[1], parts[0]), jnp.where(right, parts[0], parts[1])
        kept_up, sent_up = jnp.where(right, parts[3], parts[2]), jnp.where(right, parts[2], parts[3])
        at = slice(e * inner, (e + 1) * inner)
        keep_ref[at, :] = jnp.where(upper, kept_up, kept)
        one_ref[at, cols:] = jnp.where(upper, sent_up, sent).astype(BF16)
        two_ref[at, :] = jnp.where(upper, kept, kept_up).astype(BF16)
        both_ref[at, :] = jnp.where(upper, sent, sent_up).astype(BF16)


def merge_kernel(bit, inner, idx_ref, near_ref, far_ref, one_ref, two_ref, both_ref, place_ref, send_ref, keep_ref):
    cols = near_ref.shape[1]
    far = far_ref[...] + one_ref[:, cols:].astype(F32) + two_ref[...].astype(F32) + both_ref[...].astype(F32)
    place = place_ref[...].astype(BF16)
    high = far.astype(BF16)
    total = near_ref[...] + one_ref[:, :cols].astype(F32) + nn(high, place) + nn((far - high.astype(F32)).astype(BF16), place)
    part_ways(total, ((idx_ref[0] >> bit) & 1) == 1, send_ref, keep_ref, inner)


def join_kernel(top, count, idx_ref, kv_ref, *refs):
    ups = refs[:count]
    gu_ref, send_ref = refs[count:]
    upper = ((idx_ref[0] >> top) & 1) == 1

    @pl.when(upper)
    def _():
        send_ref[...] = gu_ref[top]

    @pl.when(jnp.logical_not(upper))
    def _():
        total = kv_ref[...]
        for up in ups:
            total = total + up[...].astype(F32)
        send_ref[...] = total.astype(BF16)


def pend_kernel(bit, top, idx_ref, *refs):
    gots, (gu_ref, send_ref) = refs[:-2], refs[-2:]
    index = idx_ref[0]
    total = jnp.where(((index >> top) & 1) == 1, 0.0, gots[0][...].astype(F32))
    for got in gots[1:]:
        total = total + got[...].astype(F32)
    send_ref[...] = (total + jnp.where(((index >> bit) & 1) == 1, gu_ref[bit].astype(F32), 0.0)).astype(BF16)


def final_kernel(dims, levels, first, count, cuts, idx_ref, *refs):
    nh, dk, dv = dims
    top = count - 1
    ups, gots = refs[:count], refs[count:2 * count]
    qt_ref, lw_ref, g_ref, ds_ref, k_ref, v_ref = refs[2 * count:2 * count + 6]
    at = 2 * count + 6 + 4 * (len(cuts) - 1)
    local = refs[2 * count + 6:at]
    (near_ref, far_ref, place_ref, w_ref, out_hbm, dq_hbm, dx_hbm, dk_hbm, dv_hbm,
     out_ref, dq_ref, dx_ref, dk_ref, dv_ref, sems) = refs[at:]
    index = idx_ref[0]
    copies = []

    def send(buf_ref, hbm_ref, cols):
        copies.append(leave(buf_ref, hbm_ref, sems.at[len(copies)], cols))

    def piece(kind, pair):
        part = sum(pair >= cut for cut in cuts) - 1
        return local[4 * part + kind], pair - cuts[part]

    def weights(h, m):
        r = h * levels + first + m
        return lw_ref[r:r + 1, :] * ((index >> m) & 1).astype(F32)

    for h in range(nh):
        rows = slice(h * dk, (h + 1) * dk)
        local_ref, n = piece(0, h // 2)
        n = 2 * n + h % 2
        total = local_ref[n * dv:(n + 1) * dv, :]
        for m in range(count):
            total = total + tn(ups[m][rows, :], qt_ref[rows, :]) * weights(h, m)
        out_ref[:, h * dv:(h + 1) * dv] = total.astype(BF16).T
        if h % 2:
            send(out_ref, out_hbm, slice((h - 1) * dv, (h + 1) * dv))
    for pair in range(nh // 2):
        halves = []
        for j in range(2):
            h = 2 * pair + j
            local_ref, n = piece(1, pair)
            n = 2 * n + j
            total = local_ref[n * dk:(n + 1) * dk, :]
            for m in range(count):
                total = total + nt(ups[m][h * dk:(h + 1) * dk, :], g_ref[:, h * dv:(h + 1) * dv]) * weights(h, m)
            halves.append(total)
        cols = slice(pair * 2 * dk, (pair + 1) * 2 * dk)
        dq_ref[:, cols] = jnp.concatenate(halves, axis=0).astype(BF16).T
        send(dq_ref, dq_hbm, cols)
    gp = (near_ref[...].astype(F32) + tn(place_ref[...].astype(BF16), far_ref[...])).astype(BF16)
    dx_ref[...] = lax.dot_general(
        gp, w_ref[...], (((0,), (1,)), ((), ())), preferred_element_type=F32).astype(BF16)
    send(dx_ref, dx_hbm, slice(0, dx_ref.shape[1]))
    upper = ((index >> top) & 1) == 1
    zero = jnp.zeros((dk, dv), BF16)
    for pair in range(nh // 2):
        pair_rows = slice(pair * 2 * dk, (pair + 1) * 2 * dk)
        total = ds_ref[pair_rows, :] + jnp.where(upper, 0.0, gots[0][pair_rows, :].astype(F32))
        for got in gots[1:]:
            total = total + got[pair_rows, :].astype(F32)
        adj = [total[:dk].astype(BF16), total[dk:].astype(BF16)]
        kp = k_ref[:, pair * 2 * dk:(pair + 1) * 2 * dk]
        dkl_ref, p = piece(2, pair)
        dvl_ref, p = piece(3, pair)
        total = dkl_ref[:, p * 2 * dk:(p + 1) * 2 * dk]
        for j in range(2):
            h = 2 * pair + j
            padded = jnp.concatenate([adj[j], zero] if j == 0 else [zero, adj[j]], axis=0)
            cols = slice(h * dv, (h + 1) * dv)
            total = total + nt(v_ref[:, cols], padded)
            near = dvl_ref[:, (2 * p + j) * dv:(2 * p + j + 1) * dv]
            dv_ref[:, cols] = (near + nn(kp, padded)).astype(BF16)
        dk_ref[:, pair * 2 * dk:(pair + 1) * 2 * dk] = total.astype(BF16)
        send(dv_ref, dv_hbm, slice(2 * pair * dv, (2 * pair + 2) * dv))
        send(dk_ref, dk_hbm, slice(pair * 2 * dk, (pair + 1) * 2 * dk))
    for copy in copies:
        copy.wait()


def gather_heads(value, head_bits):
    full = value
    for bit in reversed(range(head_bits)):
        full = jnp.concatenate([full, swap(full, "head", bit)], axis=0)
    return full


def body(hidden, w, queries, keys, values, d_out, d_state):
    tokens, width = hidden.shape
    dims = d_state.shape
    nh, dk, dv = dims
    n_seq, n_head = lax.axis_size("seq"), lax.axis_size("head")
    seq_bits, head_bits = n_seq.bit_length() - 1, n_head.bit_length() - 1
    top = seq_bits - 1
    cols = w.shape[1]
    levels = cols // (nh * n_head)
    own = nh * levels
    far = nh * seq_bits
    far_own = -(-far // 16) * 16
    far_cols = far_own * n_head
    first = tokens.bit_length()
    per = width // n_seq
    rows = nh * dk
    S = jax.ShapeDtypeStruct
    idx, head_idx = [jnp.reshape(lax.axis_index(axis), (1,)) for axis in ("seq", "head")]

    hbm = pl.BlockSpec(memory_space=pltpu.HBM)
    kv, kvb, w_near, x_near = call(
        functools.partial(state_kernel, dims),
        [S((rows, dv), F32), S((rows, dv), BF16), S(w.shape, BF16), S(hidden.shape, BF16)],
        [SM] * 2 + [hbm] * 4, 2 * tokens * rows * dv,
        scratch_shapes=[pltpu.VMEM((tokens, rows), BF16), pltpu.VMEM((tokens, nh * dv), BF16),
                        pltpu.SemaphoreType.DMA((4,))])(
                            idx, head_idx, *[pltpu.with_memory_space_constraint(a, pltpu.HBM) for a in (keys, values, w, hidden)])
    send, keep, xt = call(
        functools.partial(project_kernel, head_bits - 1),
        [S((cols // 2, tokens), BF16), S((cols // 2, tokens), F32), S((width, tokens), BF16)], [SM] + [VM] * 2,
        2 * tokens * width * cols)(head_idx, w_near, x_near)

    total, up = kv, kvb
    ups = []
    for bit in range(top):
        partner = swap(up, "seq", bit)
        ups.append(partner)
        if bit < top - 1:
            total = total + partner.astype(F32)
            up = total.astype(BF16)

    got = swap(send, "head", head_bits - 1)
    for bit in reversed(range(head_bits - 1)):
        n = keep.shape[0] // 2
        send, keep = call(
            functools.partial(fold_kernel, bit, n), [S((n, tokens), BF16), S((n, tokens), F32)],
            [SM] + [VM] * 2, n * tokens)(head_idx, keep, got)
        got = swap(send, "head", bit)

    gl = call(
        functools.partial(level_kernel, dims, levels), [S((own, tokens), F32)], [VM] * 4,
        2 * tokens * tokens * nh * (dk + dv))(keys, queries, values, d_out)[0]
    sig, lw, near, qt, gu = call(
        functools.partial(weight_kernel, dims, levels, first, seq_bits),
        [S((own, tokens), F32), S((own, tokens), F32), S((own, tokens), BF16), S((rows, tokens), BF16),
         S((seq_bits, rows, dv), BF16)],
        [VM] * 5, 2 * tokens * rows * dv * seq_bits)(keep, got, gl, queries, d_out)

    up = call(functools.partial(join_kernel, top, top), [S((rows, dv), BF16)], [SM] + [VM] * (top + 2),
              rows * dv)(idx, kv, *ups, gu)[0]
    partner = swap(up, "seq", top)
    ups.append(partner)
    far_rows = []
    for some in (tuple(range(top)), (top,)):
        far_rows = call(
            functools.partial(carry_kernel, dims, levels, first, some), [S((far_own, tokens), BF16)],
            [SM] + [VM] * (len(some) + 3 + len(far_rows)), 2 * tokens * rows * dv * len(some))(
                idx, *[ups[m] for m in some], d_out, qt, sig, *far_rows)
    far_rows = far_rows[0]
    gots = [partner]
    for bit in reversed(range(top)):
        down = call(functools.partial(pend_kernel, bit, top), [S((rows, dv), BF16)], [SM] + [VM] * (len(gots) + 1),
                    rows * dv)(idx, *gots, gu)[0]
        gots.append(swap(down, "seq", bit))

    near_all = gather_heads(near, head_bits)
    n = width // 2
    send, near_w, near_all = call(
        functools.partial(near_wgrad_kernel, head_bits, 2 * per),
        [S((n, cols), BF16), S((n, cols), F32), S((cols, tokens), BF16)],
        [SM] * 2 + [VM] * 2, 2 * tokens * width * cols)(idx, head_idx, xt, near_all)
    near_got = swap(send, "seq", 1)

    far_all = [far_rows] + [exchange(far_rows, "head", away) for away in range(1, n_head)]
    n = n // 2
    part, joined = S((n, far_cols), BF16), S((n, cols + far_cols), BF16)
    far_w, one, two, both, near_w, far_all = call(
        functools.partial(far_wgrad_kernel, per),
        [S((n, far_cols), F32), joined, part, part, S((n, cols), F32), S((far_cols, tokens), BF16)],
        [SM] * 2 + [VM] * (n_head + 3), 2 * tokens * width * far_cols)(
            idx, head_idx, xt, near_w, near_got, *far_all)
    far_gots = [exchange(one, "seq", 1), exchange(two, "seq", 2),
                exchange(both, "seq", 3)]

    col = jnp.arange(cols, dtype=jnp.int32)[None, :]
    row = jnp.arange(far_cols, dtype=jnp.int32)[:, None]
    within = row % far_own
    at = (row // far_own * nh + within % nh) * levels + first + within // nh
    place = ((at == col) & (within < far)).astype(F32)
    n = n // 2
    send, keep = call(
        functools.partial(merge_kernel, 2, per), [S((n, cols), BF16), S((n, cols), F32)], [SM] + [VM] * 6,
        4 * n * far_cols * cols)(idx, near_w, far_w, *far_gots, place)
    got = swap(send, "seq", 2)
    for bit in range(3, seq_bits):
        n = n // 2
        send, keep = call(
            functools.partial(fold_kernel, bit, per), [S((n, cols), BF16), S((n, cols), F32)],
            [SM] + [VM] * 2, n * cols)(idx, keep, got)
        got = swap(send, "seq", bit)
    d_w = keep + got.astype(F32)

    local = []
    cuts = (0, nh // 8, nh // 4, nh // 2)
    for part in range(3):
        pairs = tuple(range(cuts[part], cuts[part + 1]))
        heads = 2 * len(pairs)
        local += call(
            functools.partial(local_kernel, dims, levels, pairs),
            [S((heads * dv, tokens), F32), S((heads * dk, tokens), F32), S((tokens, heads * dk), F32),
             S((tokens, heads * dv), F32)],
            [VM] * 5, 2 * tokens * tokens * heads * (3 * dk + 3 * dv),
        )(keys, queries, values, d_out, lw)
    shapes = [(tokens, nh * dv), (tokens, rows), (tokens, width), (tokens, rows), (tokens, nh * dv)]
    out, d_queries, d_hidden, d_keys, d_values = call(
        functools.partial(final_kernel, dims, levels, first, seq_bits, cuts), [S(shape, BF16) for shape in shapes],
        [SM] + [VM] * (2 * seq_bits + 10 + len(local)), 8 * tokens * rows * dv * seq_bits, out_specs=[hbm] * len(shapes),
        scratch_shapes=[pltpu.VMEM(shape, BF16) for shape in shapes] + [pltpu.SemaphoreType.DMA((2 * nh + 1,))])(
            idx, *ups, *gots, qt, lw, d_out, d_state.reshape(rows, dv), keys, values, *local,
            near_all, far_all, place, w_near)
    return (out, d_queries, d_keys, d_values, d_hidden, d_w)


def solution(mesh):
    two = P("seq", "head")
    return jax.shard_map(
        body, mesh=mesh,
        in_specs=(two, P("head", None), two, two, two, two, P("head", None, None)),
        out_specs=(two, two, two, two, two, P(("head", "seq"), None)),
        check_vma=False)
```

```python
import functools

import jax
import jax.numpy as jnp
from jax import lax
from jax.experimental import pallas as pl
from jax.experimental.pallas import tpu as pltpu
from jax.sharding import PartitionSpec as P


F32 = jnp.float32
BF16 = jnp.bfloat16
LANES = 128
SUB = 8
VM = pl.BlockSpec(memory_space=pltpu.VMEM)
SM = pl.BlockSpec(memory_space=pltpu.SMEM)


def nn(a, b):
    return lax.dot_general(a, b, (((1,), (0,)), ((), ())), preferred_element_type=F32)


def nt(a, b):
    return lax.dot_general(a, b, (((1,), (1,)), ((), ())), preferred_element_type=F32)


def tn(a, b):
    return lax.dot_general(a, b, (((0,), (0,)), ((), ())), preferred_element_type=F32)


def call(kernel, outs, specs, flops, **kwargs):
    size = sum(o.size * o.dtype.itemsize for o in outs)
    return pl.pallas_call(
        kernel,
        out_shape=outs,
        in_specs=specs,
        compiler_params=pltpu.CompilerParams(vmem_limit_bytes=16 << 20),
        cost_estimate=pl.CostEstimate(flops=flops, bytes_accessed=2 * size, transcendentals=0),
        **kwargs,
    )


def leave(buf_ref, hbm_ref, sem, cols):
    copy = pltpu.make_async_copy(buf_ref.at[:, cols], hbm_ref.at[:, cols], sem)
    copy.start()
    return copy


def exchange(value, axis, mask):
    pairs = [(source, source ^ mask) for source in range(lax.axis_size(axis))]
    return lax.ppermute(value, axis, pairs)


def swap(value, axis, bit):
    return exchange(value, axis, 1 << bit)


def state_kernel(dims, idx_ref, head_ref, k_hbm, v_hbm, w_hbm, x_hbm, kv_ref, kvb_ref, w_ref, x_ref, k_ref, v_ref, sems):
    nh, dk, dv = dims
    copies = [pltpu.make_async_copy(src, dst, sems.at[n]) for n, (src, dst) in enumerate(
        ((k_hbm, k_ref), (v_hbm, v_ref), (w_hbm, w_ref), (x_hbm, x_ref)))]
    for copy in copies:
        copy.start()
    copies[0].wait()
    copies[1].wait()
    for pair in range(nh // 2):
        turned = k_ref[:, pair * 2 * dk:(pair + 1) * 2 * dk].T
        for j in range(2):
            h = 2 * pair + j
            kv = nn(turned[j * dk:(j + 1) * dk], v_ref[:, h * dv:(h + 1) * dv])
            kv_ref[h * dk:(h + 1) * dk, :] = kv
            kvb_ref[h * dk:(h + 1) * dk, :] = kv.astype(BF16)
    copies[2].wait()
    copies[3].wait()


def part_ways(entries, upper, send_ref, keep_ref, inner):
    n = entries.shape[0] // inner
    for e in range(n // 2):
        low = entries[2 * e * inner:(2 * e + 1) * inner]
        high = entries[(2 * e + 1) * inner:(2 * e + 2) * inner]
        out = slice(e * inner, (e + 1) * inner)
        send_ref[out, :] = jnp.where(upper, low, high).astype(BF16)
        keep_ref[out, :] = jnp.where(upper, high, low)


def project_kernel(bit, idx_ref, w_ref, x_ref, send_ref, keep_ref, xt_ref):
    xt = x_ref[...].T
    xt_ref[...] = xt
    upper = ((idx_ref[0] >> bit) & 1) == 1
    part_ways(tn(w_ref[...], xt), upper, send_ref, keep_ref, keep_ref.shape[0])


def fold_kernel(bit, inner, idx_ref, keep_in, got_ref, send_ref, keep_ref):
    upper = ((idx_ref[0] >> bit) & 1) == 1
    part_ways(keep_in[...] + got_ref[...].astype(F32), upper, send_ref, keep_ref, inner)


def weight_kernel(dims, levels, first, count, keep_ref, got_ref, gl_ref, q_ref, g_ref,
                  sig_ref, lw_ref, near_ref, qt_ref, gu_ref):
    nh, dk, dv = dims
    proj = keep_ref[...] + got_ref[...].astype(F32)
    sig = jax.nn.sigmoid(proj)
    sig_ref[...] = sig
    near_ref[...] = (gl_ref[...] * sig).astype(BF16)
    lw_ref[...] = jnp.maximum(proj, 0.0) + jnp.log1p(jnp.exp(-jnp.abs(proj)))
    for pair in range(nh // 2):
        turned = q_ref[:, pair * 2 * dk:(pair + 1) * 2 * dk].T
        qt_ref[pair * 2 * dk:(pair + 1) * 2 * dk, :] = turned
        wide = turned.astype(F32)
        for j in range(2):
            h = 2 * pair + j
            scaled = jnp.concatenate(
                [wide[j * dk:(j + 1) * dk] * lw_ref[h * levels + first + m:h * levels + first + m + 1, :]
                 for m in range(count)], axis=0)
            high = scaled.astype(BF16)
            gh = g_ref[:, h * dv:(h + 1) * dv]
            grad = nn(high, gh) + nn((scaled - high.astype(F32)).astype(BF16), gh)
            for m in range(count):
                gu_ref[m, h * dk:(h + 1) * dk, :] = grad[m * dk:(m + 1) * dk].astype(BF16)


def spread_half(rows, lane, low, t_low):
    digits = (low ^ t_low)
    near = jnp.where(digits == 0, rows[0], jnp.where(digits < 2, rows[1], jnp.where(digits < 4, rows[2], rows[3])))
    near = jnp.where(low <= t_low, near, 0.0)
    parts = []
    for a in range(LANES // SUB):
        value = None
        for l in reversed(range(4, 8)):
            if (a >> (l - 4)) & 1 == 0:
                end = (((a >> (l - 3)) + 1) << (l - 3)) * SUB
                value = rows[l] if value is None else jnp.where(lane < end, rows[l], value)
        value = near if value is None else jnp.where(lane < (a + 1) * SUB, near, value)
        if a:
            value = jnp.where(lane < a * SUB, 0.0, value)
        parts.append(value)
    return jnp.concatenate(parts, axis=0)


def level_sums(prod, lane, low, t_low):
    count = LANES // SUB
    group = lane // SUB
    cur = [prod[a * SUB:(a + 1) * SUB] for a in range(count)]
    near = jnp.zeros_like(cur[0])
    for a in range(count):
        near = jnp.where(group == a, cur[a], near)
    near = jnp.where(low <= t_low, near, 0.0)
    digits = low ^ t_low
    sums = []
    for l in range(4):
        lo, hi = (0, 1) if l == 0 else (1 << (l - 1), 1 << l)
        sums.append(jnp.where((digits >= lo) & (digits < hi), near, 0.0))
    for l in range(4, 8):
        total = jnp.zeros_like(near)
        for a in range(0, len(cur), 2):
            total = jnp.where((lane >> (l - 1)) == a + 1, cur[a], total)
        sums.append(total)
        cur = [cur[a] + cur[a + 1] for a in range(0, len(cur), 2)]
    return [jnp.sum(s, axis=0, keepdims=True) for s in sums]


def level_kernel(dims, levels, k_ref, q_ref, v_ref, g_ref, gl_ref):
    nh, dk, dv = dims
    lane = lax.broadcasted_iota(jnp.int32, (SUB, LANES), 1)
    low = lax.broadcasted_iota(jnp.int32, (SUB, LANES), 0)
    t_low = lane % SUB
    gl_ref[...] = jnp.zeros_like(gl_ref)
    for pair in range(nh // 2):
        kp = k_ref[:, pair * 2 * dk:(pair + 1) * 2 * dk]
        qt = q_ref[:, pair * 2 * dk:(pair + 1) * 2 * dk].T
        zero = jnp.zeros_like(qt[:dk])
        for j in range(2):
            h = 2 * pair + j
            base = h * levels
            qz = jnp.concatenate([qt[:dk], zero] if j == 0 else [zero, qt[dk:]], axis=0)
            prod = nn(kp, qz) * nt(v_ref[:, h * dv:(h + 1) * dv], g_ref[:, h * dv:(h + 1) * dv])
            for x in range(2):
                part = slice(x * LANES, (x + 1) * LANES)
                sums = level_sums(prod[part, part], lane, low, t_low)
                for l in range(8):
                    gl_ref[base + l:base + l + 1, part] = sums[l]
            gl_ref[base + 8:base + 9, LANES:] = jnp.sum(prod[:LANES, LANES:], axis=0, keepdims=True)


def local_kernel(dims, levels, pairs, k_ref, q_ref, v_ref, g_ref, lw_ref, out_ref, dq_ref, dk_ref, dv_ref):
    _, dk, dv = dims
    lane = lax.broadcasted_iota(jnp.int32, (SUB, LANES), 1)
    low = lax.broadcasted_iota(jnp.int32, (SUB, LANES), 0)
    t_low = lane % SUB
    for n, pair in enumerate(pairs):
        kp = k_ref[:, pair * 2 * dk:(pair + 1) * 2 * dk]
        qp = q_ref[:, pair * 2 * dk:(pair + 1) * 2 * dk]
        kt, qt = kp.T, qp.T
        zero = jnp.zeros_like(qt[:dk])
        wide_lane = lax.broadcasted_iota(jnp.int32, qp.shape, 1)
        dk_sum = None
        for j in range(2):
            h, m = 2 * pair + j, 2 * n + j
            vj = v_ref[:, h * dv:(h + 1) * dv]
            gj = g_ref[:, h * dv:(h + 1) * dv]
            qz = jnp.concatenate([qt[:dk], zero] if j == 0 else [zero, qt[dk:]], axis=0)
            base = h * levels
            cross = lw_ref[base + 8:base + 9, LANES:]
            halves = []
            for x in range(2):
                rows = [jnp.broadcast_to(lw_ref[base + l:base + l + 1, x * LANES:(x + 1) * LANES], (SUB, LANES))
                        for l in range(8)]
                halves.append(spread_half(rows, lane, low, t_low))

            def weigh(full):
                top = jnp.concatenate([full[:LANES, :LANES] * halves[0], full[:LANES, LANES:] * cross], axis=1)
                bottom = full[LANES:, LANES:] * halves[1]
                bottom = jnp.concatenate([jnp.zeros_like(bottom), bottom], axis=1)
                return jnp.concatenate([top, bottom], axis=0).astype(BF16)

            mixed = weigh(nn(kp, qz))
            grad_scores = weigh(nt(vj, gj))
            out_ref[m * dv:(m + 1) * dv, :] = tn(vj, mixed)
            dq_ref[m * dk:(m + 1) * dk, :] = nn(kt[j * dk:(j + 1) * dk], grad_scores)
            dv_ref[:, m * dv:(m + 1) * dv] = nn(mixed, gj)
            mine = (wide_lane < dk) if j == 0 else (wide_lane >= dk)
            term = nn(grad_scores, jnp.where(mine, qp, jnp.zeros_like(qp)))
            dk_sum = term if dk_sum is None else dk_sum + term
        dk_ref[:, n * 2 * dk:(n + 1) * 2 * dk] = dk_sum


def carry_kernel(dims, levels, first, some, idx_ref, *refs):
    nh, dk, dv = dims
    count = len(some)
    ups = refs[:count]
    g_ref, qt_ref, sig_ref = refs[count:count + 3]
    far_ref = refs[-1]
    far_ref[...] = refs[count + 3][...] if len(refs) > count + 4 else jnp.zeros_like(far_ref)
    index = idx_ref[0]
    for m, up_ref in zip(some, ups):
        up = ((index >> m) & 1).astype(F32)
        found = []
        for h in range(nh):
            rows = slice(h * dk, (h + 1) * dk)
            r = h * levels + first + m
            x = nt(up_ref[rows, :], g_ref[:, h * dv:(h + 1) * dv])
            row = jnp.sum(x * qt_ref[rows, :].astype(F32), axis=0, keepdims=True)
            found.append(row * (sig_ref[r:r + 1, :] * up))
        far_ref[m * nh:(m + 1) * nh, :] = jnp.concatenate(found, axis=0).astype(BF16)


def put_in_order(bits, head_ref, gp_ref, sorted_ref):
    count = 1 << bits
    own = gp_ref.shape[0] // count
    for n in range(count):
        away = sum(((n >> k) & 1) << (bits - 1 - k) for k in range(bits))
        at = pl.multiple_of((head_ref[0] ^ away) * own, 16)
        sorted_ref[pl.ds(at, own), :] = gp_ref[n * own:(n + 1) * own, :]


def near_wgrad_kernel(bits, inner, idx_ref, head_ref, xt_ref, gp_ref, send_ref, keep_ref, sorted_ref):
    put_in_order(bits, head_ref, gp_ref, sorted_ref)
    part_ways(nt(xt_ref[...], sorted_ref[...]), (idx_ref[0] & 2) == 2, send_ref, keep_ref, inner)


def far_wgrad_kernel(inner, idx_ref, head_ref, xt_ref, near_in, near_got, *refs):
    gathered, (keep_ref, one_ref, two_ref, both_ref, near_ref, sorted_ref) = refs[:-6], refs[-6:]
    for away, gp_ref in enumerate(gathered):
        own = gp_ref.shape[0]
        sorted_ref[pl.ds(pl.multiple_of((head_ref[0] ^ away) * own, 16), own), :] = gp_ref[...]
    total = nt(xt_ref[...], sorted_ref[...])
    right, upper = (idx_ref[0] & 1) == 1, ((idx_ref[0] >> 1) & 1) == 1
    cols = near_ref.shape[1]
    part_ways(near_in[...] + near_got[...].astype(F32), right, one_ref.at[:, :cols], near_ref, inner)
    for e in range(total.shape[0] // (4 * inner)):
        parts = [total[(4 * e + n) * inner:(4 * e + n + 1) * inner] for n in range(4)]
        kept, sent = jnp.where(right, parts[1], parts[0]), jnp.where(right, parts[0], parts[1])
        kept_up, sent_up = jnp.where(right, parts[3], parts[2]), jnp.where(right, parts[2], parts[3])
        at = slice(e * inner, (e + 1) * inner)
        keep_ref[at, :] = jnp.where(upper, kept_up, kept)
        one_ref[at, cols:] = jnp.where(upper, sent_up, sent).astype(BF16)
        two_ref[at, :] = jnp.where(upper, kept, kept_up).astype(BF16)
        both_ref[at, :] = jnp.where(upper, sent, sent_up).astype(BF16)


def merge_kernel(bit, inner, idx_ref, near_ref, far_ref, one_ref, two_ref, both_ref, place_ref, send_ref, keep_ref):
    cols = near_ref.shape[1]
    far = far_ref[...] + one_ref[:, cols:].astype(F32) + two_ref[...].astype(F32) + both_ref[...].astype(F32)
    place = place_ref[...].astype(BF16)
    high = far.astype(BF16)
    total = near_ref[...] + one_ref[:, :cols].astype(F32) + nn(high, place) + nn((far - high.astype(F32)).astype(BF16), place)
    part_ways(total, ((idx_ref[0] >> bit) & 1) == 1, send_ref, keep_ref, inner)


def join_kernel(top, count, idx_ref, kv_ref, *refs):
    ups = refs[:count]
    gu_ref, send_ref = refs[count:]
    upper = ((idx_ref[0] >> top) & 1) == 1

    @pl.when(upper)
    def _():
        send_ref[...] = gu_ref[top]

    @pl.when(jnp.logical_not(upper))
    def _():
        total = kv_ref[...]
        for up in ups:
            total = total + up[...].astype(F32)
        send_ref[...] = total.astype(BF16)


def pend_kernel(bit, top, idx_ref, *refs):
    gots, (gu_ref, send_ref) = refs[:-2], refs[-2:]
    index = idx_ref[0]
    total = jnp.where(((index >> top) & 1) == 1, 0.0, gots[0][...].astype(F32))
    for got in gots[1:]:
        total = total + got[...].astype(F32)
    send_ref[...] = (total + jnp.where(((index >> bit) & 1) == 1, gu_ref[bit].astype(F32), 0.0)).astype(BF16)


def final_kernel(dims, levels, first, count, cuts, idx_ref, *refs):
    nh, dk, dv = dims
    top = count - 1
    ups, gots = refs[:count], refs[count:2 * count]
    qt_ref, lw_ref, g_ref, ds_ref, k_ref, v_ref = refs[2 * count:2 * count + 6]
    at = 2 * count + 6 + 4 * (len(cuts) - 1)
    local = refs[2 * count + 6:at]
    (near_ref, far_ref, place_ref, w_ref, out_hbm, dq_hbm, dx_hbm, dk_hbm, dv_hbm,
     out_ref, dq_ref, dx_ref, dk_ref, dv_ref, sems) = refs[at:]
    index = idx_ref[0]
    copies = []

    def send(buf_ref, hbm_ref, cols):
        copies.append(leave(buf_ref, hbm_ref, sems.at[len(copies)], cols))

    def piece(kind, pair):
        part = sum(pair >= cut for cut in cuts) - 1
        return local[4 * part + kind], pair - cuts[part]

    def weights(h, m):
        r = h * levels + first + m
        return lw_ref[r:r + 1, :] * ((index >> m) & 1).astype(F32)

    for h in range(nh):
        rows = slice(h * dk, (h + 1) * dk)
        local_ref, n = piece(0, h // 2)
        n = 2 * n + h % 2
        total = local_ref[n * dv:(n + 1) * dv, :]
        for m in range(count):
            total = total + tn(ups[m][rows, :], qt_ref[rows, :]) * weights(h, m)
        out_ref[:, h * dv:(h + 1) * dv] = total.astype(BF16).T
        if h % 2:
            send(out_ref, out_hbm, slice((h - 1) * dv, (h + 1) * dv))
    for pair in range(nh // 2):
        halves = []
        for j in range(2):
            h = 2 * pair + j
            local_ref, n = piece(1, pair)
            n = 2 * n + j
            total = local_ref[n * dk:(n + 1) * dk, :]
            for m in range(count):
                total = total + nt(ups[m][h * dk:(h + 1) * dk, :], g_ref[:, h * dv:(h + 1) * dv]) * weights(h, m)
            halves.append(total)
        cols = slice(pair * 2 * dk, (pair + 1) * 2 * dk)
        dq_ref[:, cols] = jnp.concatenate(halves, axis=0).astype(BF16).T
        send(dq_ref, dq_hbm, cols)
    gp = (near_ref[...].astype(F32) + tn(place_ref[...].astype(BF16), far_ref[...])).astype(BF16)
    dx_ref[...] = lax.dot_general(
        gp, w_ref[...], (((0,), (1,)), ((), ())), preferred_element_type=F32).astype(BF16)
    send(dx_ref, dx_hbm, slice(0, dx_ref.shape[1]))
    upper = ((index >> top) & 1) == 1
    zero = jnp.zeros((dk, dv), BF16)
    for pair in range(nh // 2):
        pair_rows = slice(pair * 2 * dk, (pair + 1) * 2 * dk)
        total = ds_ref[pair_rows, :] + jnp.where(upper, 0.0, gots[0][pair_rows, :].astype(F32))
        for got in gots[1:]:
            total = total + got[pair_rows, :].astype(F32)
        high = total.astype(BF16)
        low = (total - high.astype(F32)).astype(BF16)
        kp = k_ref[:, pair * 2 * dk:(pair + 1) * 2 * dk]
        dkl_ref, p = piece(2, pair)
        dvl_ref, p = piece(3, pair)
        total = dkl_ref[:, p * 2 * dk:(p + 1) * 2 * dk]
        for j in range(2):
            h = 2 * pair + j
            padded, rest = [jnp.concatenate([adj[:dk], zero] if j == 0 else [zero, adj[dk:]], axis=0)
                            for adj in (high, low)]
            cols = slice(h * dv, (h + 1) * dv)
            total = total + nt(v_ref[:, cols], padded) + nt(v_ref[:, cols], rest)
            near = dvl_ref[:, (2 * p + j) * dv:(2 * p + j + 1) * dv]
            dv_ref[:, cols] = (near + nn(kp, padded) + nn(kp, rest)).astype(BF16)
        dk_ref[:, pair * 2 * dk:(pair + 1) * 2 * dk] = total.astype(BF16)
        send(dv_ref, dv_hbm, slice(2 * pair * dv, (2 * pair + 2) * dv))
        send(dk_ref, dk_hbm, slice(pair * 2 * dk, (pair + 1) * 2 * dk))
    for copy in copies:
        copy.wait()


def gather_heads(value, head_bits):
    full = value
    for bit in reversed(range(head_bits)):
        full = jnp.concatenate([full, swap(full, "head", bit)], axis=0)
    return full


def body(hidden, w, queries, keys, values, d_out, d_state):
    tokens, width = hidden.shape
    dims = d_state.shape
    nh, dk, dv = dims
    n_seq, n_head = lax.axis_size("seq"), lax.axis_size("head")
    seq_bits, head_bits = n_seq.bit_length() - 1, n_head.bit_length() - 1
    top = seq_bits - 1
    cols = w.shape[1]
    levels = cols // (nh * n_head)
    own = nh * levels
    far = nh * seq_bits
    far_own = -(-far // 16) * 16
    far_cols = far_own * n_head
    first = tokens.bit_length()
    per = width // n_seq
    rows = nh * dk
    S = jax.ShapeDtypeStruct
    idx, head_idx = [jnp.reshape(lax.axis_index(axis), (1,)) for axis in ("seq", "head")]

    hbm = pl.BlockSpec(memory_space=pltpu.HBM)
    kv, kvb, w_near, x_near = call(
        functools.partial(state_kernel, dims),
        [S((rows, dv), F32), S((rows, dv), BF16), S(w.shape, BF16), S(hidden.shape, BF16)],
        [SM] * 2 + [hbm] * 4, 2 * tokens * rows * dv,
        scratch_shapes=[pltpu.VMEM((tokens, rows), BF16), pltpu.VMEM((tokens, nh * dv), BF16),
                        pltpu.SemaphoreType.DMA((4,))])(
                            idx, head_idx, *[pltpu.with_memory_space_constraint(a, pltpu.HBM) for a in (keys, values, w, hidden)])
    send, keep, xt = call(
        functools.partial(project_kernel, head_bits - 1),
        [S((cols // 2, tokens), BF16), S((cols // 2, tokens), F32), S((width, tokens), BF16)], [SM] + [VM] * 2,
        2 * tokens * width * cols)(head_idx, w_near, x_near)

    total, up = kv, kvb
    ups = []
    for bit in range(top):
        partner = swap(up, "seq", bit)
        ups.append(partner)
        if bit < top - 1:
            total = total + partner.astype(F32)
            up = total.astype(BF16)

    got = swap(send, "head", head_bits - 1)
    for bit in reversed(range(head_bits - 1)):
        n = keep.shape[0] // 2
        send, keep = call(
            functools.partial(fold_kernel, bit, n), [S((n, tokens), BF16), S((n, tokens), F32)],
            [SM] + [VM] * 2, n * tokens)(head_idx, keep, got)
        got = swap(send, "head", bit)

    gl = call(
        functools.partial(level_kernel, dims, levels), [S((own, tokens), F32)], [VM] * 4,
        2 * tokens * tokens * nh * (dk + dv))(keys, queries, values, d_out)[0]
    sig, lw, near, qt, gu = call(
        functools.partial(weight_kernel, dims, levels, first, seq_bits),
        [S((own, tokens), F32), S((own, tokens), F32), S((own, tokens), BF16), S((rows, tokens), BF16),
         S((seq_bits, rows, dv), BF16)],
        [VM] * 5, 2 * tokens * rows * dv * seq_bits)(keep, got, gl, queries, d_out)

    up = call(functools.partial(join_kernel, top, top), [S((rows, dv), BF16)], [SM] + [VM] * (top + 2),
              rows * dv)(idx, kv, *ups, gu)[0]
    partner = swap(up, "seq", top)
    ups.append(partner)
    far_rows = []
    for some in (tuple(range(top)), (top,)):
        far_rows = call(
            functools.partial(carry_kernel, dims, levels, first, some), [S((far_own, tokens), BF16)],
            [SM] + [VM] * (len(some) + 3 + len(far_rows)), 2 * tokens * rows * dv * len(some))(
                idx, *[ups[m] for m in some], d_out, qt, sig, *far_rows)
    far_rows = far_rows[0]
    gots = [partner]
    for bit in reversed(range(top)):
        down = call(functools.partial(pend_kernel, bit, top), [S((rows, dv), BF16)], [SM] + [VM] * (len(gots) + 1),
                    rows * dv)(idx, *gots, gu)[0]
        gots.append(swap(down, "seq", bit))

    near_all = gather_heads(near, head_bits)
    n = width // 2
    send, near_w, near_all = call(
        functools.partial(near_wgrad_kernel, head_bits, 2 * per),
        [S((n, cols), BF16), S((n, cols), F32), S((cols, tokens), BF16)],
        [SM] * 2 + [VM] * 2, 2 * tokens * width * cols)(idx, head_idx, xt, near_all)
    near_got = swap(send, "seq", 1)

    far_all = [far_rows] + [exchange(far_rows, "head", away) for away in range(1, n_head)]
    n = n // 2
    part, joined = S((n, far_cols), BF16), S((n, cols + far_cols), BF16)
    far_w, one, two, both, near_w, far_all = call(
        functools.partial(far_wgrad_kernel, per),
        [S((n, far_cols), F32), joined, part, part, S((n, cols), F32), S((far_cols, tokens), BF16)],
        [SM] * 2 + [VM] * (n_head + 3), 2 * tokens * width * far_cols)(
            idx, head_idx, xt, near_w, near_got, *far_all)
    far_gots = [exchange(one, "seq", 1), exchange(two, "seq", 2),
                exchange(both, "seq", 3)]

    col = jnp.arange(cols, dtype=jnp.int32)[None, :]
    row = jnp.arange(far_cols, dtype=jnp.int32)[:, None]
    within = row % far_own
    at = (row // far_own * nh + within % nh) * levels + first + within // nh
    place = ((at == col) & (within < far)).astype(F32)
    n = n // 2
    send, keep = call(
        functools.partial(merge_kernel, 2, per), [S((n, cols), BF16), S((n, cols), F32)], [SM] + [VM] * 6,
        4 * n * far_cols * cols)(idx, near_w, far_w, *far_gots, place)
    got = swap(send, "seq", 2)
    for bit in range(3, seq_bits):
        n = n // 2
        send, keep = call(
            functools.partial(fold_kernel, bit, per), [S((n, cols), BF16), S((n, cols), F32)],
            [SM] + [VM] * 2, n * cols)(idx, keep, got)
        got = swap(send, "seq", bit)
    d_w = keep + got.astype(F32)

    local = []
    cuts = (0, nh // 8, nh // 4, nh // 2)
    for part in range(3):
        pairs = tuple(range(cuts[part], cuts[part + 1]))
        heads = 2 * len(pairs)
        local += call(
            functools.partial(local_kernel, dims, levels, pairs),
            [S((heads * dv, tokens), F32), S((heads * dk, tokens), F32), S((tokens, heads * dk), F32),
             S((tokens, heads * dv), F32)],
            [VM] * 5, 2 * tokens * tokens * heads * (3 * dk + 3 * dv),
        )(keys, queries, values, d_out, lw)
    shapes = [(tokens, nh * dv), (tokens, rows), (tokens, width), (tokens, rows), (tokens, nh * dv)]
    out, d_queries, d_hidden, d_keys, d_values = call(
        functools.partial(final_kernel, dims, levels, first, seq_bits, cuts), [S(shape, BF16) for shape in shapes],
        [SM] + [VM] * (2 * seq_bits + 10 + len(local)), 8 * tokens * rows * dv * seq_bits, out_specs=[hbm] * len(shapes),
        scratch_shapes=[pltpu.VMEM(shape, BF16) for shape in shapes] + [pltpu.SemaphoreType.DMA((2 * nh + 1,))])(
            idx, *ups, *gots, qt, lw, d_out, d_state.reshape(rows, dv), keys, values, *local,
            near_all, far_all, place, w_near)
    return (out, d_queries, d_keys, d_values, d_hidden, d_w)


def solution(mesh):
    two = P("seq", "head")
    return jax.shard_map(
        body, mesh=mesh,
        in_specs=(two, P("head", None), two, two, two, two, P("head", None, None)),
        out_specs=(two, two, two, two, two, P(("head", "seq"), None)),
        check_vma=False)
```
